32 devices in a mesh: section: 2 (over core), dp: 8 (over z, x), mp: 2 (over y).
Axes of the slice: x: 2, y: 2, z: 4, core: 2. Of those that a mesh axis runs over, the one named last changes fastest.
Arguments:
- block_input: bfloat16 [2, 256, 16, 1024], P('section', 'dp'), may hold values from -6 to 6
- norm_gain: float32 [2, 1024], P('section'), may hold values from 0.5 to 1.5
- lstm_in: bfloat16 [2, 1024, 4, 1024], P('section', 'dp', None, 'mp'), may hold values from -0.1875 to 0.1875
- lstm_rec: bfloat16 [2, 1024, 4, 1024], P('section', 'dp', None, 'mp'), may hold values from -0.4375 to 0.4375
- lstm_bias: bfloat16 [2, 4, 1024], P('section', None, 'mp'), may hold values from -1.25 to 2.75
- mono_mem: bfloat16 [1024, 1024], P('dp', ('section', 'mp')), may hold values from -0.1875 to 0.1875
- mono_dec: bfloat16 [1024, 1024], P('dp', ('section', 'mp')), may hold values from -0.1875 to 0.1875
- mono_bias: float32 [1024], P(('section', 'mp')), may hold values from -3 to 3
- mono_vec: float32 [1024], P(('section', 'mp')), may hold values from -0.6 to 0.6
- span_mem: bfloat16 [1024, 1024], P('dp', ('section', 'mp')), may hold values from -0.1875 to 0.1875
- span_dec: bfloat16 [1024, 1024], P('dp', ('section', 'mp')), may hold values from -0.1875 to 0.1875
- span_bias: float32 [1024], P(('section', 'mp')), may hold values from -3 to 3
- span_vec: float32 [1024], P(('section', 'mp')), may hold values from -0.6 to 0.6
- out_weight: bfloat16 [2, 1024, 1024], P(None, 'dp', ('section', 'mp')), may hold values from -0.125 to 0.125
- out_bias: float32 [1024], P(('section', 'mp')), may hold values from -2 to 2
- vocab_weight: bfloat16 [1024, 1000], P(('section', 'mp')), may hold values from -1 to 1
- vocab_bias: float32 [1000], replicated, may hold values from -3 to 3
- noise: float32 [256, 16, 16], P('dp'), may hold values from 0 to 4
- enc_lengths: int32 [256], P('dp'), may hold values from 1 to 16, as said below
- label_lengths: int32 [256], P('dp'), may hold values from 1 to 16, as said below
- labels: int32 [256, 16], P('dp'), may hold values from 0 to 999
Outputs:
- input_grad: float32 [2, 256, 16, 1024], P('section', 'dp')
- norm_gain_grad: float32 [2, 1024], P('section')
- lstm_in_grad: float32 [2, 1024, 4, 1024], P('section', 'dp', None, 'mp')
- lstm_rec_grad: float32 [2, 1024, 4, 1024], P('section', 'dp', None, 'mp')
- lstm_bias_grad: float32 [2, 4, 1024], P('section', None, 'mp')
- mono_mem_grad: float32 [1024, 1024], P('dp', ('section', 'mp'))
- mono_dec_grad: float32 [1024, 1024], P('dp', ('section', 'mp'))
- mono_bias_grad: float32 [1024], P(('section', 'mp'))
- mono_vec_grad: float32 [1024], P(('section', 'mp'))
- span_mem_grad: float32 [1024, 1024], P('dp', ('section', 'mp'))
- span_dec_grad: float32 [1024, 1024], P('dp', ('section', 'mp'))
- span_bias_grad: float32 [1024], P(('section', 'mp'))
- span_vec_grad: float32 [1024], P(('section', 'mp'))
- out_weight_grad: float32 [2, 1024, 1024], P(None, 'dp', ('section', 'mp'))
- out_bias_grad: float32 [1024], P(('section', 'mp'))
- vocab_weight_grad: float32 [1024, 1000], P(('section', 'mp'))
- vocab_bias_grad: float32 [1000], replicated
The draws below stay inside these ranges and needn't reach their ends.
Inputs may be any that keep to these rules, and one draw needn't show every extreme that they name: `enc_lengths`: each utterance has 1 to 16 valid frames; some utterance has exactly 16. `label_lengths`: each utterance has 1 to 16 counted decoder steps; some utterance has exactly 16.
All inputs are finite; a program needn't handle non-finite values.
Results may differ from the reference program's by a relative error of at most 0.02.
Values may be sent and summed in bfloat16 or wider, within the bound.
No kernel may reach another device: no remote copies, remote signals or barrier semaphores. Data moves between devices by JAX's collectives and lax.ppermute only.
A program may use at most 128 MiB of HBM per device.

```python
import math
import jax
import jax.numpy as jnp
import numpy as np
from jax import lax

D = 1024
E = 1024
P_SIZE = 1024
V = 1000
L = 16
UTT = 256


def tail_lengths(key, frame_limit, slot_count):
    first_key, second_key, place_key = jax.random.split(key, 3)
    first_draw = jax.random.randint(first_key, (slot_count,), 0, frame_limit)
    second_draw = jax.random.randint(second_key, (slot_count,), 0, frame_limit)
    raw_length = 1 + (frame_limit * frame_limit - (frame_limit - first_draw) * (frame_limit - second_draw)) // frame_limit
    longest = jax.random.randint(place_key, (), 0, slot_count)
    return jnp.where(jnp.arange(slot_count) == longest, frame_limit, raw_length).astype(jnp.int32)


def draw_enc_lengths(key, part):
    return tail_lengths(jax.random.fold_in(key, 17), L, UTT)


def draw_label_lengths(key, part):
    return tail_lengths(jax.random.fold_in(key, 29), L, UTT)


def draw_lstm_bias(key, part):
    own_key = jax.random.fold_in(key, 41)
    gate_offsets = jnp.array([1.5, 0.5, 0.0, 1.5], jnp.float32)
    spread = jnp.clip(0.5 * jax.random.normal(own_key, (2, 4, D), jnp.float32), -1.2, 1.2)
    return (gate_offsets[None, :, None] + spread).astype(jnp.bfloat16)


def draw_noise(key, part):
    own_key = jax.random.fold_in(key, 53)
    values = jnp.clip(3.0 + jax.random.normal(own_key, (UTT, L, L), jnp.float32), 0.0, 4.0)
    return values.astype(jnp.float32)


def with_ends(drawn, stream_key, least, largest):
    place = [jax.random.randint(jax.random.fold_in(stream_key, axis), (), 0, length) for axis, length in enumerate(drawn.shape)]
    widest = drawn.shape.index(max(drawn.shape))
    neighbour = place[:widest] + [(place[widest] + 1) % drawn.shape[widest]] + place[widest + 1:]
    return drawn.at[tuple(place)].set(least).at[tuple(neighbour)].set(largest)


def block_scale(key, dims, cuts, low, largest):
    loudness, own = 1.0, jax.random.fold_in(key, 6)
    for axis_at, blocks in cuts:
        draws = jnp.exp(jax.random.uniform(jax.random.fold_in(own, axis_at), (blocks,), jnp.float32, low / len(cuts), largest / len(cuts)))
        loudness = loudness * jnp.repeat(draws, dims[axis_at] // blocks).reshape([-1 if axis == axis_at else 1 for axis in range(len(dims))])
    return loudness


def rank_bounds(number_of, slope):
    weights = [(1 << 20) // math.isqrt(grade ** slope) + 1 for grade in range(1, number_of + 1)]
    scale = 1 + sum(weights) // (1 << 30)
    return np.cumsum(np.array([max(1, weight // scale) for weight in weights]))


def skewed_ids(key, shape, amount, skew):
    table = rank_bounds(amount, skew)
    pick = jax.random.randint(jax.random.fold_in(key, 1), shape, 0, int(table[amount - 1]))
    rank = jnp.searchsorted(jnp.asarray(table, jnp.int32), pick, side="right")
    return jax.random.permutation(jax.random.fold_in(key, 2), amount)[rank].astype(jnp.int32)


def scatter_about(stream_key, extent, scale, reach, pieces=(), kind=jnp.bfloat16):
    values = scale * jax.random.normal(stream_key, extent, jnp.float32)
    if pieces:
        values = values * block_scale(stream_key, extent, pieces, -0.22, 0.18)
    return jnp.clip(values, -reach, reach).astype(kind)


def setup_inputs(seed: int = 0) -> dict:
    key_of = jax.random.split(jax.random.key(seed), 22)
    block_input = scatter_about(key_of[0], (2, UTT, L, D), 1.0, 6.0, ((0, 2), (1, 8)))
    norm_gain = jnp.clip(1.0 + 0.1 * jax.random.normal(key_of[1], (2, D), jnp.float32), 0.5, 1.5)
    lstm_in = scatter_about(key_of[2], (2, D, 4, D), D ** -0.5, 0.1875, ((0, 2), (1, 8), (3, 2)))
    lstm_rec = scatter_about(key_of[3], (2, D, 4, D), (D // 6) ** -0.5, 0.4375, ((0, 2), (1, 8), (3, 2)))
    lstm_bias = draw_lstm_bias(jax.random.fold_in(key_of[21], 71), 0)
    mono_mem = scatter_about(key_of[5], (D, E), D ** -0.5, 0.1875, ((0, 8), (1, 4)))
    mono_dec = scatter_about(key_of[6], (D, E), D ** -0.5, 0.1875, ((0, 8), (1, 4)))
    mono_bias = scatter_about(key_of[7], (E,), 0.5, 3.0, ((0, 4),), jnp.float32)
    mono_vec = scatter_about(key_of[8], (E,), 0.1, 0.6, ((0, 4),), jnp.float32)
    span_mem = scatter_about(key_of[9], (D, E), D ** -0.5, 0.1875, ((0, 8), (1, 4)))
    span_dec = scatter_about(key_of[10], (D, E), D ** -0.5, 0.1875, ((0, 8), (1, 4)))
    span_bias = scatter_about(key_of[11], (E,), 0.5, 3.0, ((0, 4),), jnp.float32)
    span_vec = scatter_about(key_of[12], (E,), 0.1, 0.6, ((0, 4),), jnp.float32)
    out_weight = scatter_about(key_of[13], (2, D, P_SIZE), (2 * D) ** -0.5, 0.125, ((1, 8), (2, 4)))
    out_bias = scatter_about(key_of[14], (P_SIZE,), 0.3, 2.0, ((0, 4),), jnp.float32)
    vocab_weight = scatter_about(key_of[15], (P_SIZE, V), 32 ** -0.5, 1.0, ((0, 4),))
    vocab_bias = scatter_about(key_of[16], (V,), 0.5, 3.0, (), jnp.float32)
    noise = draw_noise(jax.random.fold_in(key_of[21], 71), 0)
    enc_lengths = draw_enc_lengths(jax.random.fold_in(key_of[21], 71), 0)
    label_lengths = draw_label_lengths(jax.random.fold_in(key_of[21], 71), 0)
    labels = with_ends(skewed_ids(key_of[20], (UTT, L), V, 2), jax.random.fold_in(key_of[20], 3), 0, V - 1).astype(jnp.int32)
    return dict(block_input=block_input, norm_gain=norm_gain, lstm_in=lstm_in, lstm_rec=lstm_rec, lstm_bias=lstm_bias, mono_mem=mono_mem, mono_dec=mono_dec, mono_bias=mono_bias, mono_vec=mono_vec, span_mem=span_mem, span_dec=span_dec, span_bias=span_bias, span_vec=span_vec, out_weight=out_weight, out_bias=out_bias, vocab_weight=vocab_weight, vocab_bias=vocab_bias, noise=noise, enc_lengths=enc_lengths, label_lengths=label_lengths, labels=labels)


@jax.custom_vjp
def low(v):
    return lax.optimization_barrier(v.astype(jnp.bfloat16)).astype(jnp.float32)

@jax.custom_vjp
def low_back(v):
    return v

def low_keep(v):
    return (low(v), None)

def low_pass(kept, grad):
    return (grad,)

def back_keep(v):
    return (v, None)

def back_low(kept, grad):
    return (low(grad),)
low.defvjp(low_keep, low_pass)
low_back.defvjp(back_keep, back_low)
highest = lax.Precision.HIGHEST
epsilon = 1e-05
offset = -4.0

def normalize(inputs, gain_row):
    average = lax.optimization_barrier(jnp.mean(inputs, axis=-1, keepdims=True))
    centred = inputs - average
    spread = lax.optimization_barrier(jnp.mean(centred * centred, axis=-1, keepdims=True))
    return centred * lax.rsqrt(spread + epsilon) * gain_row

def gate_split(gate_values):
    return (jax.nn.sigmoid(gate_values[:, 0]), jax.nn.sigmoid(gate_values[:, 1]), jnp.tanh(gate_values[:, 2]), jax.nn.sigmoid(gate_values[:, 3]))

def cell_update(gate_values, cell_state):
    inflow, forget, candidate, outflow = gate_split(gate_values)
    new_cell = forget * cell_state + inflow * candidate
    return (new_cell, outflow * jnp.tanh(new_cell))

def recurrence(inputs, gain_row, weight_input, weight_recur, bias_values):
    normed = low(normalize(inputs, gain_row))
    project = jnp.einsum('bld,dgh->lbgh', normed, weight_input, precision=highest)
    row_count = inputs.shape[0]
    unit_count = weight_recur.shape[2]

    def advance(carried, project_row):
        hidden_state, cell_state = carried
        gate_values = low_back(project_row + jnp.einsum('bd,dgh->bgh', hidden_state, weight_recur, precision=highest) + bias_values)
        new_cell, emitted = cell_update(gate_values, cell_state)
        emitted = low(emitted)
        return ((emitted, new_cell), emitted)
    start_state = (jnp.zeros((row_count, unit_count), jnp.float32), jnp.zeros((row_count, unit_count), jnp.float32))
    _, history = lax.scan(advance, start_state, project)
    return jnp.swapaxes(history, 0, 1)

def pair_energy(queries, keys_all, bias_vec, weight_vec):

    def single(row_pack):
        query_rows, key_rows = row_pack
        squash = jnp.tanh(query_rows[:, None, :] + key_rows[None, :, :] + bias_vec)
        return lax.optimization_barrier(jnp.sum(squash * weight_vec, axis=-1))
    return lax.map(jax.checkpoint(single), (queries, keys_all))

def link_pair(earlier, later):
    return (earlier[0] * later[0], later[0] * earlier[1] + later[1])

def monotonic(probable):
    keep_prob = jnp.concatenate([jnp.ones_like(probable[:, :, :1]), 1.0 - probable[:, :, :-1]], axis=2)
    frame_count = probable.shape[2]
    initial = jnp.broadcast_to((jnp.arange(frame_count) == 0).astype(jnp.float32), probable[:, 0].shape)

    def advance(previous, row_pack):
        keep_row, prob_row = row_pack
        _, queued = lax.associative_scan(link_pair, (keep_row, previous), axis=1)
        attended = prob_row * queued
        return (attended, attended)
    _, history = lax.scan(advance, initial, (jnp.swapaxes(keep_prob, 0, 1), jnp.swapaxes(probable, 0, 1)))
    return jnp.swapaxes(history, 0, 1)

def spanwise(span_energy, alphas, frame_mask):
    masked = jnp.where(frame_mask > 0, span_energy, -1e+30)
    highest_value = lax.optimization_barrier(jnp.max(masked, axis=2, keepdims=True))
    scaled = jnp.where(frame_mask > 0, jnp.exp(span_energy - highest_value), 0.0)
    window_sum = scaled + jnp.pad(scaled[:, :, :-1], ((0, 0), (0, 0), (1, 0)))
    ratio = alphas / jnp.where(frame_mask > 0, window_sum, 1.0)
    return scaled * (ratio + jnp.pad(ratio[:, :, 1:], ((0, 0), (0, 0), (0, 1))))

def attention_weights(mono_energy, span_energy, noise_rows, frame_mask):
    probable = jax.nn.sigmoid(mono_energy + offset + noise_rows) * frame_mask
    alphas = monotonic(probable)
    return spanwise(span_energy, alphas, frame_mask)

def layer_loss(params, inputs_pair, noise_rows, enc_rows, label_len_rows, label_rows):
    norm_gain, lstm_in, lstm_rec, lstm_bias, mono_mem, mono_dec, mono_bias, mono_vec, span_mem, span_dec, span_bias, span_vec, out_weight, out_bias, vocab_weight, vocab_bias = params
    memory = recurrence(inputs_pair[0], norm_gain[0], lstm_in[0], lstm_rec[0], lstm_bias[0])
    decoded = recurrence(inputs_pair[1], norm_gain[1], lstm_in[1], lstm_rec[1], lstm_bias[1])
    positions = jnp.arange(noise_rows.shape[2])
    frame_mask = (positions[None, :] < enc_rows[:, None]).astype(jnp.float32)[:, None, :]
    step_mask = (positions[None, :] < label_len_rows[:, None]).astype(jnp.float32)
    mono_keys = low_back(jnp.einsum('bjd,de->bje', memory, mono_mem, precision=highest))
    mono_query = low_back(jnp.einsum('bid,de->bie', decoded, mono_dec, precision=highest))
    span_keys = low_back(jnp.einsum('bjd,de->bje', memory, span_mem, precision=highest))
    span_query = low_back(jnp.einsum('bid,de->bie', decoded, span_dec, precision=highest))
    mono_energy = pair_energy(mono_query, mono_keys, mono_bias, mono_vec)
    span_energy = pair_energy(span_query, span_keys, span_bias, span_vec)
    beta = attention_weights(mono_energy, span_energy, noise_rows, frame_mask)
    context = low(jnp.einsum('bij,bjd->bid', low(beta), memory, precision=highest))
    pre_out = low_back(jnp.einsum('bid,dp->bip', decoded, out_weight[0], precision=highest) + jnp.einsum('bid,dp->bip', context, out_weight[1], precision=highest) + out_bias)
    emitted = low(jnp.tanh(pre_out))
    logits = low_back(jnp.einsum('bip,pv->biv', emitted, vocab_weight, precision=highest) + vocab_bias)
    normalizer = jax.nn.logsumexp(logits, axis=-1)
    chosen = jnp.take_along_axis(logits, label_rows[:, :, None], axis=2)[:, :, 0]
    return jnp.sum((normalizer - chosen) * step_mask)

def reference(block_input, norm_gain, lstm_in, lstm_rec, lstm_bias, mono_mem, mono_dec, mono_bias, mono_vec, span_mem, span_dec, span_bias, span_vec, out_weight, out_bias, vocab_weight, vocab_bias, noise, enc_lengths, label_lengths, labels):
    params = tuple((array.astype(jnp.float32) for array in (norm_gain, lstm_in, lstm_rec, lstm_bias, mono_mem, mono_dec, mono_bias, mono_vec, span_mem, span_dec, span_bias, span_vec, out_weight, out_bias, vocab_weight, vocab_bias)))
    inputs = block_input.astype(jnp.float32)
    total_rows = noise.shape[0]
    group_rows = math.gcd(total_rows, 64)
    block_count = total_rows // group_rows
    frame_count = inputs.shape[2]
    width = inputs.shape[3]
    split_inputs = jnp.swapaxes(inputs.reshape(2, block_count, group_rows, frame_count, width), 0, 1)

    def regroup(array):
        return array.reshape((block_count, group_rows) + array.shape[1:])

    def accumulate(carried, batch_pack):
        inputs_pair, noise_rows, enc_rows, label_len_rows, label_rows = batch_pack

        def loss_of(param_pack, input_pack):
            return layer_loss(param_pack, input_pack, noise_rows, enc_rows, label_len_rows, label_rows)
        _, pullback = jax.vjp(loss_of, params, inputs_pair)
        grad_params, grad_inputs = pullback(jnp.ones((), jnp.float32))
        return (jax.tree.map(jnp.add, carried, grad_params), grad_inputs)
    zero_params = jax.tree.map(jnp.zeros_like, params)
    summed, input_grads = lax.scan(accumulate, zero_params, (split_inputs, regroup(noise), regroup(enc_lengths), regroup(label_lengths), regroup(labels)))
    input_grad = jnp.swapaxes(input_grads, 0, 1).reshape(2, total_rows, frame_count, width)
    return (input_grad,) + tuple(summed)
```

```python
import jax
import jax.numpy as jnp
from jax import lax
from jax.experimental import pallas as pl
from jax.experimental.pallas import tpu as pltpu
from jax.sharding import PartitionSpec as P

epsilon = 1e-05
offset = -4.0
wide = jnp.float32
low = jnp.bfloat16
in_vmem = pl.BlockSpec(memory_space=pltpu.VMEM)
in_smem = pl.BlockSpec(memory_space=pltpu.SMEM)
in_place = pl.BlockSpec(memory_space=pl.ANY)
core_swap = [(0, 1), (1, 0)]
corner_swap = [(0, 0), (1, 2), (2, 1), (3, 3)]


def normalize(inputs, gain_row):
    average = jnp.mean(inputs, axis=-1, keepdims=True)
    centred = inputs - average
    spread = jnp.mean(centred * centred, axis=-1, keepdims=True)
    return centred * lax.rsqrt(spread + epsilon) * gain_row


def across_cores(array):
    return lax.ppermute(array, "section", core_swap)


def across_chips(array):
    return lax.ppermute(array, "mp", core_swap)


def corners(array):
    return lax.ppermute(array, ("section", "mp"), corner_swap)


class Ring:
    def __init__(self, dp):
        self.dp = dp
        self.outer = dp // 2
        self.small = dp % 2 == 0 and self.outer <= 4
        pairs = [(z, x) for z in range(self.outer) for x in range(2)]
        self.pair = [(2 * z + x, 2 * z + 1 - x) for z, x in pairs]
        self.ring = [(2 * z + x, 2 * ((z + 1) % self.outer) + x) for z, x in pairs]

    def gather(self, shards):
        if not self.small:
            return [lax.all_gather(a, "dp", axis=0, tiled=True) for a in shards]
        place = lax.axis_index("dp")
        z, x = place // 2, place % 2
        held = list(shards)
        got = [[] for _ in shards]
        for k in range(self.outer):
            for i in range(len(shards)):
                got[i].append((k, held[i], lax.ppermute(held[i], "dp", self.pair)))
                if k < self.outer - 1:
                    held[i] = lax.ppermute(held[i], "dp", self.ring)
        whole = []
        for i, shard in enumerate(shards):
            r, c = shard.shape
            full = jnp.zeros((self.dp * r, c), shard.dtype)
            for k, own, other in got[i]:
                at = lax.rem(z - k + self.outer, self.outer)
                full = lax.dynamic_update_slice(full, own, ((at * 2 + x) * r, 0))
                full = lax.dynamic_update_slice(full, other, ((at * 2 + 1 - x) * r, 0))
            whole.append(full)
        return whole

    def scatter(self, totals):
        if not self.small:
            return [
                lax.psum_scatter(g, "dp", scatter_dimension=0, tiled=True).astype(wide)
                for g in totals
            ]
        place = lax.axis_index("dp")
        z, x = place // 2, place % 2
        sums = [None] * len(totals)
        for j in range(1, self.outer + 1):
            for i, g in enumerate(totals):
                r = g.shape[0] // self.dp
                at = lax.rem(z - j + self.outer, self.outer)
                mine = lax.dynamic_slice(g, ((at * 2 + x) * r, 0), (r, g.shape[1]))
                theirs = lax.dynamic_slice(g, ((at * 2 + 1 - x) * r, 0), (r, g.shape[1]))
                total = mine.astype(wide) + lax.ppermute(theirs, "dp", self.pair).astype(wide)
                if sums[i] is not None:
                    total = total + lax.ppermute(sums[i], "dp", self.ring).astype(wide)
                sums[i] = total.astype(low) if j < self.outer else total
        return sums

    def total(self, array):
        if not self.small:
            return lax.psum(array, "dp")
        array = array + lax.ppermute(array, "dp", self.pair)
        step = 1
        while step < self.outer:
            hop = [
                (2 * z + x, 2 * (z ^ step) + x) for z in range(self.outer) for x in range(2)
            ]
            array = array + lax.ppermute(array, "dp", hop)
            step *= 2
        return array


def sigmoid(x):
    return 0.5 * jnp.tanh(0.5 * x) + 0.5


def forward_kernel(
    side, z_own, z_other, w_own, w_other, b_own, b_other,
    quarters, before, gates, cells,
    z, w, b, state, cell, sems,
):
    steps, rows, wide_half = z_own.shape
    unit_half = wide_half // 4
    chunk = min(256, unit_half)
    s = side[0]
    copies = []
    for n, (src_z, src_w, src_b, at) in enumerate(
        ((z_own, w_own, b_own, s), (z_other, w_other, b_other, 1 - s))
    ):
        columns = pl.ds(pl.multiple_of(at * wide_half, wide_half), wide_half)
        copies.append(pltpu.make_async_copy(src_w, w.at[:, columns], sems.at[n]))
        copies.append(pltpu.make_async_copy(src_z, z.at[:, :, columns], sems.at[2 + n]))
        b[:, columns] = src_b[...]
    for copy in copies:
        copy.start()
    state[...] = jnp.zeros_like(state)
    cell[...] = jnp.zeros_like(cell)
    for copy in copies:
        copy.wait()
    eighth = rows // 2

    def advance(t, carried):
        hidden = state[...]
        before[t] = hidden
        for at in range(0, 2 * unit_half, chunk):
            half, inside = at // unit_half, at % unit_half
            acts = []
            for g in range(4):
                cols = pl.ds(half * wide_half + g * unit_half + inside, chunk)
                value = (
                    z[t, :, cols]
                    + jnp.dot(hidden, w[:, cols], preferred_element_type=wide)
                    + b[:, cols]
                )
                value = jnp.tanh(value) if g == 2 else sigmoid(value)
                gates[t, :, cols] = value
                acts.append(value)
            units = pl.ds(at, chunk)
            new_cell = acts[1] * cell[:, units] + acts[0] * acts[2]
            cell[:, units] = new_cell
            cells[t, :, units] = new_cell
            new_hidden = acts[3] * jnp.tanh(new_cell)
            state[:, units] = new_hidden.astype(low)
            quarters[0, t, :, units] = new_hidden[:eighth].astype(low)
            quarters[1, t, :, units] = new_hidden[eighth:].astype(low)
        return carried

    lax.fori_loop(0, steps, advance, 0)


def run_forward(side, z_own, z_other, w_own, w_other, b_own, b_other):
    steps, rows, wide_half = z_own.shape
    units = w_own.shape[0]
    return pl.pallas_call(
        forward_kernel,
        out_shape=(
            jax.ShapeDtypeStruct((2, steps, rows // 2, units), low),
            jax.ShapeDtypeStruct((steps, rows, units), low),
            jax.ShapeDtypeStruct((steps, rows, 2 * wide_half), wide),
            jax.ShapeDtypeStruct((steps, rows, units), wide),
        ),
        in_specs=[in_smem] + [in_place] * 4 + [in_vmem] * 2,
        out_specs=[in_vmem] * 4,
        scratch_shapes=[
            pltpu.VMEM((steps, rows, 2 * wide_half), wide),
            pltpu.VMEM((units, 2 * wide_half), low),
            pltpu.VMEM((1, 2 * wide_half), wide),
            pltpu.VMEM((rows, units), low),
            pltpu.VMEM((rows, units), wide),
            pltpu.SemaphoreType.DMA((4,)),
        ],
        compiler_params=pltpu.CompilerParams(vmem_limit_bytes=56 << 20),
        name="recur_forward",
    )(side, z_own, z_other, w_own, w_other, b_own, b_other)


def backward_kernel(side, outside, gates, cells, t_own, t_other, dz, w, dh, dc, sems):
    steps, rows, wide_full = gates.shape
    wide_half = wide_full // 2
    unit_half = wide_half // 4
    chunk = min(256, unit_half)
    eighth = rows // 2
    s = side[0]
    copies = []
    for n, (src, at) in enumerate(((t_own, s), (t_other, 1 - s))):
        span = pl.ds(pl.multiple_of(at * wide_half, wide_half), wide_half)
        copies.append(pltpu.make_async_copy(src, w.at[span, :], sems.at[n]))
    for copy in copies:
        copy.start()
    dh[...] = jnp.zeros_like(dh)
    dc[...] = jnp.zeros_like(dc)
    for copy in copies:
        copy.wait()

    def retreat(k, carried):
        t = steps - 1 - k
        earlier = jnp.maximum(t - 1, 0)
        live = jnp.where(t > 0, 1.0, 0.0).astype(wide)
        for at in range(0, 2 * unit_half, chunk):
            half, inside = at // unit_half, at % unit_half
            units = pl.ds(at, chunk)
            grad = (
                jnp.concatenate([outside[0, t, :, units], outside[1, t, :, units]], axis=0)
                + dh[:, units]
            )
            i, f, g, o = [
                gates[t, :, pl.ds(half * wide_half + n * unit_half + inside, chunk)]
                for n in range(4)
            ]
            squash = jnp.tanh(cells[t, :, units])
            total = dc[:, units] + grad * o * (1.0 - squash * squash)
            parts = (
                total * g * i * (1.0 - i),
                total * (cells[earlier, :, units] * live) * f * (1.0 - f),
                total * i * (1.0 - g * g),
                grad * squash * o * (1.0 - o),
            )
            for n, part in enumerate(parts):
                dz[half, t, :, pl.ds(n * unit_half + inside, chunk)] = part.astype(low)
            dc[:, units] = total * f
        first, second = dz[0, t], dz[1, t]
        for at in range(0, 2 * unit_half, chunk):
            units = pl.ds(at, chunk)
            dh[:, units] = jnp.dot(
                first, w[:wide_half, units], preferred_element_type=wide
            ) + jnp.dot(second, w[wide_half:, units], preferred_element_type=wide)
        return carried

    lax.fori_loop(0, steps, retreat, 0)


def run_backward(side, outside, gates, cells, t_own, t_other):
    steps, rows, wide_full = gates.shape
    units = cells.shape[2]
    return pl.pallas_call(
        backward_kernel,
        out_shape=jax.ShapeDtypeStruct((2, steps, rows, wide_full // 2), low),
        in_specs=[in_smem] + [in_vmem] * 3 + [in_place] * 2,
        out_specs=in_vmem,
        scratch_shapes=[
            pltpu.VMEM((wide_full, units), low),
            pltpu.VMEM((rows, units), wide),
            pltpu.VMEM((rows, units), wide),
            pltpu.SemaphoreType.DMA((2,)),
        ],
        compiler_params=pltpu.CompilerParams(vmem_limit_bytes=56 << 20),
        name="recur_backward",
    )(side, outside, gates, cells, t_own, t_other)


def dot_nt(a, b):
    return lax.dot_general(a, b, (((1,), (1,)), ((), ())), preferred_element_type=wide)


def dot_tn(a, b):
    return lax.dot_general(a, b, (((0,), (0,)), ((), ())), preferred_element_type=wide)


def attend_kernel(
    memory, decoded, w0, w1, w2, w3, v0, v1, v2, v3, vectors, vocab_bias, noise, lengths,
    labels, counted,
    grad_memory, grad_decoded, pack, seen, sums,
    w, v, sems, mk, sk, mq, sq, mono, span, keep, queue, scaled, ratio, window, mix, pre,
):
    rows, _ = memory.shape
    frames, group, _ = mk.shape
    block = w.shape[2] // 6
    lanes = 128
    chunks = 4 * block // lanes
    copies = [pltpu.make_async_copy(src, w.at[r], sems.at[r]) for r, src in enumerate((w0, w1, w2, w3))]
    copies += [
        pltpu.make_async_copy(src, v.at[r], sems.at[4 + r]) for r, src in enumerate((v0, v1, v2, v3))
    ]
    for copy in copies:
        copy.start()

    def split(value):
        return value.reshape(frames, group, value.shape[-1])

    mem, dec = memory[...], decoded[...]
    for r in range(4):
        copies[r].wait()
        cols = pl.ds(r * block, block)
        keys = jnp.dot(mem, w[r, :, : 2 * block], preferred_element_type=wide)
        queries = jnp.dot(dec, w[r, :, 2 * block : 5 * block], preferred_element_type=wide)
        mk[:, :, cols] = split(keys[:, :block])
        sk[:, :, cols] = split(keys[:, block:])
        mq[:, :, cols] = split(queries[:, :block] + vectors[0:1, cols])
        sq[:, :, cols] = split(queries[:, block : 2 * block] + vectors[2:3, cols])
        pre[:, cols] = queries[:, 2 * block :] + vectors[4:5, cols]

    def lane(c):
        return pl.ds(c * lanes, lanes)

    def spread(row, c):
        return jnp.broadcast_to(vectors[row : row + 1, lane(c)], (group, lanes))

    def energies(queries, keys, vec_row, energy):
        weights = [spread(vec_row, c) for c in range(chunks)]

        def one(i, carried):
            query = [queries[i, :, lane(c)] for c in range(chunks)]
            for j in range(frames):
                total = jnp.tanh(query[0] + keys[j, :, lane(0)]) * weights[0]
                for c in range(1, chunks):
                    total = total + jnp.tanh(query[c] + keys[j, :, lane(c)]) * weights[c]
                energy[i * frames + j] = jnp.broadcast_to(
                    jnp.sum(total, axis=-1, keepdims=True), (group, lanes)
                )
            return carried

        lax.fori_loop(0, frames, one, 0)

    energies(mq, mk, 1, mono)
    energies(sq, sk, 3, span)

    length = lengths[...]
    valid = [(length > j) for j in range(frames)]
    ones = jnp.ones((group, lanes), wide)
    zeros = jnp.zeros((group, lanes), wide)
    live = [jnp.where(valid[j], 1.0, 0.0).astype(wide) for j in range(frames)]
    diagonal = lax.broadcasted_iota(jnp.int32, (group, lanes), 1) - lax.broadcasted_iota(
        jnp.int32, (group, lanes), 0
    )

    def attend(i, previous):
        base = i * frames
        top = jnp.full((group, lanes), -1e30, wide)
        for j in range(frames):
            top = jnp.maximum(top, jnp.where(valid[j], span[base + j], -1e30))
        weight = [jnp.where(valid[j], jnp.exp(span[base + j] - top), 0.0) for j in range(frames)]
        current, ratios = [], []
        queued = previous[0]
        for j in range(frames):
            prob = sigmoid(mono[base + j] + offset + noise[base + j]) * live[j]
            keep[base + j] = prob
            queue[base + j] = queued
            alpha = prob * queued
            current.append(alpha)
            if j + 1 < frames:
                queued = (1.0 - prob) * queued + previous[j + 1]
            both = weight[j] + weight[j - 1] if j else weight[j]
            both = jnp.where(valid[j], both, 1.0)
            window[base + j] = both
            scaled[base + j] = weight[j]
            quotient = alpha / both
            ratio[base + j] = quotient
            ratios.append(quotient)
        row = zeros
        for j in range(frames):
            beta = weight[j] * (ratios[j] + (ratios[j + 1] if j + 1 < frames else zeros))
            row = jnp.where(diagonal == group * j, beta, row)
        mix[i] = row
        return tuple(current)

    lax.fori_loop(0, frames, attend, tuple([ones] + [zeros] * (frames - 1)))

    beta_low = mix[...].reshape(rows, lanes)[:, :rows].astype(low)
    context = jnp.dot(beta_low, mem, preferred_element_type=wide).astype(low)
    seen[0] = context
    for r in range(4):
        cols = pl.ds(r * block, block)
        value = jnp.tanh(
            pre[:, cols] + jnp.dot(context, w[r, :, 5 * block :], preferred_element_type=wide)
        )
        pre[:, cols] = value
        pack[r, :, 5 * block :] = value.astype(low)
    logits = vocab_bias[...]
    for r in range(4):
        copies[4 + r].wait()
        logits = logits + jnp.dot(pack[r, :, 5 * block :], v[r], preferred_element_type=wide)
    shifted = jnp.exp(logits - jnp.max(logits, axis=-1, keepdims=True))
    softmax = shifted / jnp.sum(shifted, axis=-1, keepdims=True)
    onehot = (labels[...] == lax.broadcasted_iota(jnp.int32, softmax.shape, 1)).astype(wide)
    grad_logits = ((softmax - onehot) * counted[...]).astype(low)
    seen[1] = grad_logits
    sums[5:6, :] = jnp.sum(grad_logits.astype(wide), axis=0, keepdims=True)
    sums[6:8, :] = jnp.zeros((2, sums.shape[1]), wide)

    grad_context = jnp.zeros((rows, memory.shape[1]), wide)
    for r in range(4):
        cols = pl.ds(r * block, block)
        value = pre[:, cols]
        grad_pre = (dot_nt(grad_logits, v[r]) * (1.0 - value * value)).astype(low)
        pack[r, :, 4 * block : 5 * block] = grad_pre
        sums[4:5, cols] = jnp.sum(grad_pre.astype(wide), axis=0, keepdims=True)
        grad_context = grad_context + dot_nt(grad_pre, w[r, :, 5 * block :])
    upper = grad_context.astype(low)
    lower = (grad_context - upper.astype(wide)).astype(low)
    grad_memory[...] = dot_tn(beta_low, upper) + dot_tn(beta_low, lower)
    cross = dot_nt(upper, mem) + dot_nt(lower, mem)
    if rows < lanes:
        cross = jnp.concatenate([cross, jnp.zeros((rows, lanes - rows), wide)], axis=1)
    mix[...] = split(cross)

    def unattend(k, later):
        i = frames - 1 - k
        base = i * frames
        cross_row = mix[i]
        grad_beta = [
            jnp.broadcast_to(
                jnp.sum(
                    jnp.where(diagonal == group * j, cross_row, 0.0), axis=-1, keepdims=True
                ),
                (group, lanes),
            )
            for j in range(frames)
        ]
        weight = [scaled[base + j] for j in range(frames)]
        share = [ratio[base + j] for j in range(frames)]
        direct, from_window, grad_weight = [], [], []
        for j in range(frames):
            grad_ratio = grad_beta[j] * weight[j]
            if j:
                grad_ratio = grad_ratio + grad_beta[j - 1] * weight[j - 1]
            pull = grad_ratio / window[base + j]
            direct.append(pull)
            from_window.append(jnp.where(valid[j], -pull * share[j], 0.0))
            grad_weight.append(
                grad_beta[j] * (share[j] + (share[j + 1] if j + 1 < frames else zeros))
            )
        top = jnp.full((group, lanes), -1e30, wide)
        for j in range(frames):
            top = jnp.maximum(top, jnp.where(valid[j], span[base + j], -1e30))
        total, ties, at_top, through = zeros, zeros, [], []
        for j in range(frames):
            pulled = grad_weight[j] + from_window[j]
            if j + 1 < frames:
                pulled = pulled + from_window[j + 1]
            pulled = weight[j] * pulled
            through.append(pulled)
            total = total + pulled
            hit = jnp.where(span[base + j] == top, live[j], 0.0)
            at_top.append(hit)
            ties = ties + hit
        back = total / ties
        for j in range(frames):
            span[base + j] = through[j] - at_top[j] * back
        grad_queue = zeros
        now = [None] * frames
        for j in reversed(range(frames)):
            prob = keep[base + j]
            grad_alpha = direct[j] + later[j]
            mono[base + j] = queue[base + j] * (grad_alpha - grad_queue) * prob * (1.0 - prob)
            grad_queue = prob * grad_alpha + (1.0 - prob) * grad_queue
            now[j] = grad_queue
        return tuple(now)

    lax.fori_loop(0, frames, unattend, tuple([zeros] * frames))

    def energy_back(queries, keys, energy, bias_row, vec_row):
        def one_chunk(c, carried):
            at = pl.ds(pl.multiple_of(c * lanes, lanes), lanes)
            weight = jnp.broadcast_to(vectors[vec_row : vec_row + 1, at], (group, lanes))

            def one(i, carry):
                grad_keys, vec_total, bias_total = carry
                query = queries[i, :, at]
                grad_query = zeros
                new_keys = []
                for j in range(frames):
                    squash = jnp.tanh(query + keys[j, :, at])
                    grad = energy[i * frames + j]
                    scaled_squash = grad * squash
                    vec_total = vec_total + scaled_squash
                    inner = grad - scaled_squash * squash
                    grad_query = grad_query + inner
                    new_keys.append(grad_keys[j] + inner)
                queries[i, :, at] = grad_query * weight
                return (tuple(new_keys), vec_total, bias_total + grad_query)

            grad_keys, vec_total, bias_total = lax.fori_loop(
                0, frames, one, (tuple([zeros] * frames), zeros, zeros)
            )
            for j in range(frames):
                keys[j, :, at] = grad_keys[j] * weight
            sums[bias_row : bias_row + 1, at] = jnp.sum(bias_total * weight, axis=0, keepdims=True)
            sums[vec_row : vec_row + 1, at] = jnp.sum(vec_total, axis=0, keepdims=True)
            return carried

        lax.fori_loop(0, chunks, one_chunk, 0)

    energy_back(mq, mk, mono, 0, 1)
    energy_back(sq, sk, span, 2, 3)

    total_memory = grad_memory[...]
    total_decoded = jnp.zeros_like(total_memory)
    for r in range(4):
        cols = pl.ds(r * block, block)
        for n, source in enumerate((mk, sk, mq, sq)):
            pack[r, :, n * block : (n + 1) * block] = (
                source[:, :, cols].reshape(rows, block).astype(low)
            )
        total_memory = total_memory + dot_nt(pack[r, :, : 2 * block], w[r, :, : 2 * block])
        total_decoded = total_decoded + dot_nt(
            pack[r, :, 2 * block : 5 * block], w[r, :, 2 * block : 5 * block]
        )
    grad_memory[...] = total_memory
    grad_decoded[...] = total_decoded


def run_attend(memory, decoded, weights, vocab, vectors, vocab_bias, noise, lengths, labels, counted, frames):
    rows, width = memory.shape
    group = rows // frames
    full = weights[0].shape[1] // 6 * 4
    vocab_width = vocab[0].shape[1]
    cell = (frames * frames, group, 128)
    return pl.pallas_call(
        attend_kernel,
        out_shape=(
            jax.ShapeDtypeStruct((rows, width), wide),
            jax.ShapeDtypeStruct((rows, width), wide),
            jax.ShapeDtypeStruct((4, rows, full // 4 * 6), low),
            jax.ShapeDtypeStruct((2, rows, vocab_width), low),
            jax.ShapeDtypeStruct((8, full), wide),
        ),
        in_specs=[in_vmem] * 2 + [in_place] * 8 + [in_vmem] * 6,
        out_specs=[in_vmem] * 5,
        scratch_shapes=[
            pltpu.VMEM((4,) + weights[0].shape, low),
            pltpu.VMEM((4,) + vocab[0].shape, low),
            pltpu.SemaphoreType.DMA((8,)),
        ]
        + [pltpu.VMEM((frames, group, full), wide)] * 4
        + [pltpu.VMEM(cell, wide)] * 7
        + [pltpu.VMEM((frames, group, 128), wide), pltpu.VMEM((rows, full), wide)],
        compiler_params=pltpu.CompilerParams(vmem_limit_bytes=56 << 20),
        name="attend",
    )(memory, decoded, *weights, *vocab, vectors, vocab_bias, noise, lengths, labels, counted)


def local(
    dp,
    block_input, norm_gain, lstm_in, lstm_rec, lstm_bias,
    mono_mem, mono_dec, mono_bias, mono_vec, span_mem, span_dec, span_bias, span_vec,
    out_weight, out_bias, vocab_weight, vocab_bias, noise, enc_lengths, label_lengths, labels,
):
    ring = Ring(dp)
    s, y = lax.axis_index("section"), lax.axis_index("mp")
    side = s.reshape(1).astype(jnp.int32)
    _, utts, frames, width = block_input.shape
    half, quarter = utts // 2, utts // 4
    shard_rows, _, unit_half = lstm_in.shape[1:]
    wide_half = 4 * unit_half
    block = mono_mem.shape[1]
    vocab_size = vocab_weight.shape[1]
    vocab_pad = 4 * block

    in_shard = corners(lstm_in[0].reshape(shard_rows, wide_half))
    rec_shard = corners(lstm_rec[0].reshape(shard_rows, wide_half))
    b_own = corners(lstm_bias[0].reshape(1, wide_half)).astype(wide)
    b_other = across_cores(b_own)

    inputs = jnp.swapaxes(block_input[0], 0, 1).astype(wide)
    normed, norm_pullback = jax.vjp(normalize, inputs, norm_gain[0])
    normed_low = normed.astype(low)
    normed_section = jnp.where(s == y, normed_low, across_cores(normed_low))
    normed_own = lax.dynamic_slice_in_dim(normed_section, s * half, half, axis=1)
    normed_other = lax.dynamic_slice_in_dim(normed_section, (1 - s) * half, half, axis=1)
    normed_own = normed_own.reshape(frames * half, width)
    normed_other = normed_other.reshape(frames * half, width)

    shards = jnp.concatenate(
        [mono_mem, span_mem, mono_dec, span_dec, out_weight[0], out_weight[1]], axis=1
    )
    weight_own = lax.all_gather(shards, "dp", axis=0, tiled=True)
    weight_chip = across_chips(weight_own)
    weights = [weight_own, weight_chip, across_cores(weight_own), across_cores(weight_chip)]
    vocab_own = jnp.pad(vocab_weight, ((0, 0), (0, vocab_pad - vocab_size)))
    vocab_chip = across_chips(vocab_own)
    vocab = [vocab_own, vocab_chip, across_cores(vocab_own), across_cores(vocab_chip)]
    vector_own = jnp.stack([mono_bias, mono_vec, span_bias, span_vec, out_bias])
    vector_pair = jnp.concatenate([vector_own, across_chips(vector_own)], axis=1)
    vectors = jnp.concatenate([vector_pair, across_cores(vector_pair)], axis=1)
    vectors = jnp.pad(vectors, ((0, 3), (0, 0)))

    in_own, rec_own = ring.gather([in_shard, rec_shard])
    in_other = across_cores(in_own)
    rec_other = across_cores(rec_own)

    def project(weight):
        value = jnp.dot(normed_own, weight, preferred_element_type=wide)
        return value.reshape(frames, half, wide_half)

    quarters, before, gates, cells = run_forward(
        side, project(in_own), project(in_other), rec_own, rec_other, b_own, b_other
    )

    kept = lax.dynamic_index_in_dim(quarters, y, axis=0, keepdims=False)
    given = lax.dynamic_index_in_dim(quarters, 1 - y, axis=0, keepdims=False)
    taken = across_chips(given)
    rows = frames * quarter
    memory = jnp.where(y == 0, kept, taken).reshape(rows, width)
    decoded = jnp.where(y == 0, taken, kept).reshape(rows, width)

    start = s * half + y * quarter
    noise_part = jnp.transpose(
        lax.dynamic_slice_in_dim(noise, start, quarter, axis=0), (1, 2, 0)
    ).reshape(frames * frames, quarter, 1)
    noise_part = jnp.broadcast_to(noise_part, (frames * frames, quarter, 128))
    length_part = lax.dynamic_slice_in_dim(enc_lengths, start, quarter, axis=0)
    length_part = jnp.broadcast_to(length_part[:, None], (quarter, 128))
    label_part = lax.dynamic_slice_in_dim(labels, start, quarter, axis=0).T.reshape(rows, 1)
    count_part = lax.dynamic_slice_in_dim(label_lengths, start, quarter, axis=0)
    counted = (jnp.arange(frames)[:, None] < count_part[None, :]).astype(wide).reshape(rows, 1)
    bias_row = jnp.pad(vocab_bias, (0, vocab_pad - vocab_size), constant_values=-1e30)[None]

    grad_memory, grad_decoded, pack, seen, sums = run_attend(
        memory, decoded, weights, vocab, vectors, bias_row, noise_part, length_part,
        label_part, counted, frames,
    )

    grad_kept = jnp.where(y == 0, grad_memory, grad_decoded)
    grad_given = jnp.where(y == 0, grad_decoded, grad_memory).astype(low)
    grad_taken = across_chips(grad_given).astype(wide)
    outside = jnp.stack(
        [jnp.where(y == 0, grad_kept, grad_taken), jnp.where(y == 0, grad_taken, grad_kept)]
    ).reshape(2, frames, quarter, width)
    dz = run_backward(side, outside, gates, cells, rec_own.T, rec_other.T)

    dz = dz.reshape(2, frames * half, wide_half)
    dz_kept = lax.dynamic_index_in_dim(dz, s, axis=0, keepdims=False)
    dz_given = lax.dynamic_index_in_dim(dz, 1 - s, axis=0, keepdims=False)
    dz_all = jnp.concatenate([dz_kept, across_cores(dz_given)], axis=0)
    before = before.reshape(frames * half, width)
    before_all = jnp.concatenate([before, across_cores(before)], axis=0)
    normed_all = jnp.concatenate([normed_own, normed_other], axis=0)
    rec_total = dot_tn(before_all, dz_all).astype(low)
    in_total = dot_tn(normed_all, dz_all).astype(low)
    rec_grad, in_grad = ring.scatter([rec_total, in_total])

    grad_part = dot_nt(dz_kept, in_own) + dot_nt(dz_given, in_other)
    grad_part = grad_part.reshape(frames, half, width)
    grad_peer = across_cores(grad_part)
    grad_section = jnp.concatenate(
        [jnp.where(s == 0, grad_part, grad_peer), jnp.where(s == 0, grad_peer, grad_part)], axis=1
    )
    grad_far = lax.ppermute(grad_section, ("section", "mp"), [(0, 1), (3, 2)])
    grad_inputs, grad_gain = norm_pullback(jnp.where(s == y, grad_section, grad_far))

    kept_far = across_chips(kept)
    memory_next = jnp.where(y == 0, given, kept_far).reshape(rows, width)
    decoded_next = jnp.where(y == 0, kept_far, given).reshape(rows, width)
    states = jnp.stack([memory, memory_next, decoded, decoded_next])
    states_core = across_cores(states)

    def gathered(n):
        return jnp.concatenate(
            [states[n], states_core[n], states[n + 1], states_core[n + 1]], axis=0
        )

    memory_all, decoded_all = gathered(0), gathered(2)
    pack_core = across_cores(pack[2:4])
    pack_far = across_chips(jnp.stack([pack[1], pack_core[1]]))
    pack_all = jnp.concatenate([pack[0], pack_core[0], pack_far[0], pack_far[1]], axis=0)
    seen_pair = jnp.concatenate([seen, across_chips(seen)], axis=0)
    seen_core = across_cores(seen_pair)
    seen_all = [
        jnp.concatenate([seen_pair[n], seen_core[n], seen_pair[2 + n], seen_core[2 + n]], axis=0)
        for n in range(2)
    ]
    grads = jnp.concatenate(
        [
            dot_tn(memory_all, pack_all[:, : 2 * block]),
            dot_tn(decoded_all, pack_all[:, 2 * block : 5 * block]),
            dot_tn(seen_all[0], pack_all[:, 4 * block : 5 * block]),
        ],
        axis=1,
    ).astype(low)
    grads = lax.psum_scatter(grads, "dp", scatter_dimension=0, tiled=True).astype(wide)
    vocab_grad = dot_tn(pack_all[:, 5 * block :], seen_all[1])[:, :vocab_size].astype(low)
    vocab_grad = lax.psum(vocab_grad, "dp").astype(wide)

    blocks = sums[:5].reshape(5, 4, block)
    pair = blocks[:, :2] + across_cores(blocks[:, 2:])
    vector_sum = pair[:, 0] + across_chips(pair[:, 1])
    bias_sum = sums[5] + across_cores(sums[5])
    bias_sum = bias_sum + across_chips(bias_sum)
    lstm_bias_sum = jnp.sum(dz_all.astype(wide), axis=0)
    flat = jnp.concatenate(
        [
            vector_sum.reshape(-1),
            bias_sum,
            lstm_bias_sum,
            grad_gain.reshape(-1),
        ]
    )
    flat = jnp.pad(flat, (0, -flat.shape[0] % 1024)).reshape(-1, 1024)
    flat = ring.total(flat).reshape(-1)
    ends = [5 * block, 5 * block + vocab_pad, 5 * block + vocab_pad + wide_half]
    vector_sum = flat[: ends[0]].reshape(5, block)
    bias_sum = flat[ends[0] : ends[0] + vocab_size]
    lstm_bias_sum = corners(flat[ends[1] : ends[2]].reshape(4, unit_half))
    gain_sum = flat[ends[2] : ends[2] + width]

    in_grad = corners(in_grad.astype(low)).astype(wide).reshape(1, shard_rows, 4, unit_half)
    rec_grad = corners(rec_grad.astype(low)).astype(wide).reshape(1, shard_rows, 4, unit_half)
    column = [grads[:, n * block : (n + 1) * block] for n in range(6)]
    return (
        jnp.swapaxes(grad_inputs, 0, 1)[None],
        gain_sum[None],
        in_grad,
        rec_grad,
        lstm_bias_sum[None],
        column[0],
        column[2],
        vector_sum[0],
        vector_sum[1],
        column[1],
        column[3],
        vector_sum[2],
        vector_sum[3],
        jnp.stack([column[4], column[5]]),
        vector_sum[4],
        vocab_grad,
        bias_sum,
    )


def solution(mesh):
    both = ("section", "mp")
    in_specs = (
        P("section", "dp", None, None),
        P("section", None),
        P("section", "dp", None, "mp"),
        P("section", "dp", None, "mp"),
        P("section", None, "mp"),
        P("dp", both),
        P("dp", both),
        P(both),
        P(both),
        P("dp", both),
        P("dp", both),
        P(both),
        P(both),
        P(None, "dp", both),
        P(both),
        P(both, None),
        P(),
        P("dp", None, None),
        P("dp"),
        P("dp"),
        P("dp", None),
    )
    out_specs = (
        P("section", "dp", None, None),
        P("section", None),
        P("section", "dp", None, "mp"),
        P("section", "dp", None, "mp"),
        P("section", None, "mp"),
        P("dp", both),
        P("dp", both),
        P(both),
        P(both),
        P("dp", both),
        P("dp", both),
        P(both),
        P(both),
        P(None, "dp", both),
        P(both),
        P(both, None),
        P(),
    )
    dp = mesh.shape["dp"]

    def step(*arrays):
        return local(dp, *arrays)

    return jax.shard_map(step, mesh=mesh, in_specs=in_specs, out_specs=out_specs, check_vma=False)
```

```python
import functools

import jax
import jax.numpy as jnp
from jax import lax
from jax.experimental import pallas as pl
from jax.experimental.pallas import tpu as pltpu
from jax.sharding import PartitionSpec as P

epsilon = 1e-05
offset = -4.0
wide = jnp.float32
low = jnp.bfloat16
in_vmem = pl.BlockSpec(memory_space=pltpu.VMEM)
in_smem = pl.BlockSpec(memory_space=pltpu.SMEM)
in_place = pl.BlockSpec(memory_space=pl.ANY)
core_swap = [(0, 1), (1, 0)]
corner_swap = [(0, 0), (1, 2), (2, 1), (3, 3)]


def normalize(inputs, gain_row):
    average = jnp.mean(inputs, axis=-1, keepdims=True)
    centred = inputs - average
    spread = jnp.mean(centred * centred, axis=-1, keepdims=True)
    return centred * lax.rsqrt(spread + epsilon) * gain_row


def across_cores(array):
    return lax.ppermute(array, "section", core_swap)


def across_chips(array):
    return lax.ppermute(array, "mp", core_swap)


def corners(array):
    return lax.ppermute(array, ("section", "mp"), corner_swap)


def tie(value, *others):
    return lax.optimization_barrier((value,) + others)[0]


def cut(array, block, rows):
    return lax.dynamic_slice_in_dim(array, block * rows, rows, axis=0)


class Ring:
    def __init__(self, dp):
        self.dp = dp
        self.outer = dp // 2
        self.short = dp % 2 == 0 and self.outer == 4
        pairs = [(z, x) for z in range(self.outer) for x in range(2)]
        self.pair = [(2 * z + x, 2 * z + 1 - x) for z, x in pairs]
        self.ring = [(2 * z + x, 2 * ((z + 1) % self.outer) + x) for z, x in pairs]
        place = lax.axis_index("dp")
        self.z, self.x = place // 2, place % 2

    def across(self, array):
        return lax.ppermute(array, "dp", self.pair)

    def onward(self, array):
        return lax.ppermute(array, "dp", self.ring)

    def back(self, k):
        return lax.rem(self.z - k + self.outer, self.outer)

    def part(self, group, block, rows):
        return jnp.concatenate([cut(a, block, rows) for a in group], axis=1)


def halves(array, height):
    array = array.reshape(height, -1)
    upper = array.astype(low)
    lower = (array - upper.astype(wide)).astype(low)
    return jnp.pad(
        jnp.concatenate([upper, lower], axis=1), ((0, 0), (0, -2 * array.shape[1] % 128))
    )


def joined(array, count):
    return array[:, :count].astype(wide) + array[:, count : 2 * count].astype(wide)


def sigmoid(x):
    return 0.5 * jnp.tanh(0.5 * x) + 0.5


def fetch(blocks, places, side_blocks, target, sems, first=0):
    wide_half = target.shape[1] // 2
    columns = pl.ds(pl.multiple_of(side_blocks * wide_half, wide_half), wide_half)
    copies = []
    for k, block in enumerate(blocks):
        height = block.shape[0]
        span = pl.ds(pl.multiple_of(places[1 + k] * height, height), height)
        copies.append(
            pltpu.make_async_copy(
                block.at[:, :wide_half], target.at[span, columns], sems.at[first + k]
            )
        )
    return copies


def forward_kernel(count, places, normed, b_own, b_other, *refs):
    in_own, in_other, w_own, w_other = [refs[n * count : (n + 1) * count] for n in range(4)]
    quarters, before, gates, cells, wi, w, b, state, cell, sems = refs[4 * count :]
    steps, rows, wide_full = gates.shape
    wide_half = wide_full // 2
    unit_half = wide_half // 4
    chunk = min(256, unit_half)
    s = places[0]
    copies = fetch(in_own, places, s, wi, sems) + fetch(in_other, places, 1 - s, wi, sems, count)
    later = fetch(w_own, places, s, w, sems, 2 * count)
    later += fetch(w_other, places, 1 - s, w, sems, 3 * count)
    for copy in copies + later:
        copy.start()
    for source, at in ((b_own, s), (b_other, 1 - s)):
        b[:, pl.ds(pl.multiple_of(at * wide_half, wide_half), wide_half)] = source[...]
    state[...] = jnp.zeros_like(state)
    cell[...] = jnp.zeros_like(cell)
    for copy in copies:
        copy.wait()

    def project(g, carried):
        cols = pl.ds(pl.multiple_of(g * unit_half, unit_half), unit_half)
        value = jnp.dot(normed[...], wi[:, cols], preferred_element_type=wide) + b[:, cols]
        gates[:, :, cols] = value.reshape(steps, rows, unit_half)
        return carried

    lax.fori_loop(0, 8, project, 0)
    for copy in later:
        copy.wait()
    eighth = rows // 2

    def advance(t, carried):
        hidden = state[...]
        before[t] = hidden
        for at in range(0, 2 * unit_half, chunk):
            half, inside = at // unit_half, at % unit_half
            acts = []
            for g in range(4):
                cols = pl.ds(half * wide_half + g * unit_half + inside, chunk)
                value = gates[t, :, cols] + jnp.dot(
                    hidden, w[:, cols], preferred_element_type=wide
                )
                value = jnp.tanh(value) if g == 2 else sigmoid(value)
                gates[t, :, cols] = value
                acts.append(value)
            units = pl.ds(at, chunk)
            new_cell = acts[1] * cell[:, units] + acts[0] * acts[2]
            cell[:, units] = new_cell
            cells[t, :, units] = new_cell
            new_hidden = acts[3] * jnp.tanh(new_cell)
            state[:, units] = new_hidden.astype(low)
            quarters[0, t, :, units] = new_hidden[:eighth].astype(low)
            quarters[1, t, :, units] = new_hidden[eighth:].astype(low)
        return carried

    lax.fori_loop(0, steps, advance, 0)


def run_forward(places, normed, b_own, b_other, in_own, in_other, w_own, w_other, steps):
    rows = normed.shape[0] // steps
    units = normed.shape[1]
    wide_half = b_own.shape[1]
    count = len(w_own)
    return pl.pallas_call(
        functools.partial(forward_kernel, count),
        out_shape=(
            jax.ShapeDtypeStruct((2, steps, rows // 2, units), low),
            jax.ShapeDtypeStruct((steps, rows, units), low),
            jax.ShapeDtypeStruct((steps, rows, 2 * wide_half), wide),
            jax.ShapeDtypeStruct((steps, rows, units), wide),
        ),
        in_specs=[in_smem] + [in_vmem] * 3 + [in_place] * (4 * count),
        out_specs=[in_vmem] * 4,
        scratch_shapes=[
            pltpu.VMEM((units, 2 * wide_half), low),
            pltpu.VMEM((units, 2 * wide_half), low),
            pltpu.VMEM((1, 2 * wide_half), wide),
            pltpu.VMEM((rows, units), low),
            pltpu.VMEM((rows, units), wide),
            pltpu.SemaphoreType.DMA((4 * count,)),
        ],
        compiler_params=pltpu.CompilerParams(vmem_limit_bytes=56 << 20),
        name="recur_forward",
    )(places, normed, b_own, b_other, *in_own, *in_other, *w_own, *w_other)


def backward_kernel(count, places, outside, gates, cells, *refs):
    w_own, w_other = refs[:count], refs[count : 2 * count]
    dz, stage, w, dh, dc, sems = refs[2 * count :]
    steps, rows, wide_full = gates.shape
    wide_half = wide_full // 2
    unit_half = wide_half // 4
    chunk = min(256, unit_half)
    s = places[0]
    jobs = []
    for n, (sources, at) in enumerate(((w_own, s), (w_other, 1 - s))):
        for k, block in enumerate(sources):
            slot = n * count + k
            copy = pltpu.make_async_copy(
                block.at[:, :wide_half], stage.at[slot], sems.at[slot]
            )
            copy.start()
            jobs.append((copy, slot, at, places[1 + k] * block.shape[0]))
    dh[...] = jnp.zeros_like(dh)
    dc[...] = jnp.zeros_like(dc)
    height = w_own[0].shape[0]
    piece = min(height, 128)
    for copy, slot, at, first in jobs:
        copy.wait()

        def turn(g, carried, slot=slot, at=at, first=first):
            columns = pl.ds(pl.multiple_of(g * unit_half, unit_half), unit_half)
            span = pl.ds(pl.multiple_of(at * wide_half + g * unit_half, unit_half), unit_half)
            for low_row in range(0, height, piece):
                into = pl.ds(pl.multiple_of(first + low_row, piece), piece)
                w[span, into] = stage[slot, low_row : low_row + piece, columns].T
            return carried

        lax.fori_loop(0, 4, turn, 0)

    def retreat(k, carried):
        t = steps - 1 - k
        earlier = jnp.maximum(t - 1, 0)
        live = jnp.where(t > 0, 1.0, 0.0).astype(wide)
        for at in range(0, 2 * unit_half, chunk):
            half, inside = at // unit_half, at % unit_half
            units = pl.ds(at, chunk)
            grad = (
                jnp.concatenate([outside[0, t, :, units], outside[1, t, :, units]], axis=0)
                + dh[:, units]
            )
            i, f, g, o = [
                gates[t, :, pl.ds(half * wide_half + n * unit_half + inside, chunk)]
                for n in range(4)
            ]
            squash = jnp.tanh(cells[t, :, units])
            total = dc[:, units] + grad * o * (1.0 - squash * squash)
            parts = (
                total * g * i * (1.0 - i),
                total * (cells[earlier, :, units] * live) * f * (1.0 - f),
                total * i * (1.0 - g * g),
                grad * squash * o * (1.0 - o),
            )
            for n, part in enumerate(parts):
                dz[half, t, :, pl.ds(n * unit_half + inside, chunk)] = part.astype(low)
            dc[:, units] = total * f
        first, second = dz[0, t], dz[1, t]
        for at in range(0, 2 * unit_half, chunk):
            units = pl.ds(at, chunk)
            dh[:, units] = jnp.dot(
                first, w[:wide_half, units], preferred_element_type=wide
            ) + jnp.dot(second, w[wide_half:, units], preferred_element_type=wide)
        return carried

    lax.fori_loop(0, steps, retreat, 0)


def run_backward(places, outside, gates, cells, w_own, w_other):
    steps, rows, wide_full = gates.shape
    units = cells.shape[2]
    count = len(w_own)
    return pl.pallas_call(
        functools.partial(backward_kernel, count),
        out_shape=jax.ShapeDtypeStruct((2, steps, rows, wide_full // 2), low),
        in_specs=[in_smem] + [in_vmem] * 3 + [in_place] * (2 * count),
        out_specs=in_vmem,
        scratch_shapes=[
            pltpu.VMEM((2 * count, units // count, wide_full // 2), low),
            pltpu.VMEM((wide_full, units), low),
            pltpu.VMEM((rows, units), wide),
            pltpu.VMEM((rows, units), wide),
            pltpu.SemaphoreType.DMA((2 * count,)),
        ],
        compiler_params=pltpu.CompilerParams(vmem_limit_bytes=56 << 20),
        name="recur_backward",
    )(places, outside, gates, cells, *w_own, *w_other)


def input_kernel(count, places, inputs, gain, dz, *refs):
    in_own, in_other = refs[:count], refs[count : 2 * count]
    grad_inputs, grad_gain, wi, sems = refs[2 * count :]
    s = places[0]
    copies = fetch(in_own, places, s, wi, sems) + fetch(in_other, places, 1 - s, wi, sems, count)
    for copy in copies:
        copy.start()
    x = inputs[...].astype(wide)
    centred = x - jnp.mean(x, axis=-1, keepdims=True)
    scale = lax.rsqrt(jnp.mean(centred * centred, axis=-1, keepdims=True) + epsilon)
    shape = centred * scale
    for copy in copies:
        copy.wait()
    wide_half = wi.shape[1] // 2
    grad = dot_nt(dz[0], wi[:, :wide_half]) + dot_nt(dz[1], wi[:, wide_half:])
    grad_gain[...] = jnp.sum(grad * shape, axis=0, keepdims=True)
    pulled = grad * gain[...]
    grad_inputs[...] = scale * (
        pulled
        - jnp.mean(pulled, axis=-1, keepdims=True)
        - shape * jnp.mean(pulled * shape, axis=-1, keepdims=True)
    )


def run_input(places, inputs, gain, dz, in_own, in_other):
    count = len(in_own)
    rows, width = inputs.shape
    return pl.pallas_call(
        functools.partial(input_kernel, count),
        out_shape=(
            jax.ShapeDtypeStruct((rows, width), wide),
            jax.ShapeDtypeStruct((1, width), wide),
        ),
        in_specs=[in_smem] + [in_vmem] * 3 + [in_place] * (2 * count),
        out_specs=[in_vmem] * 2,
        scratch_shapes=[
            pltpu.VMEM((width, 2 * dz.shape[2]), low),
            pltpu.SemaphoreType.DMA((2 * count,)),
        ],
        compiler_params=pltpu.CompilerParams(vmem_limit_bytes=56 << 20),
        name="input_back",
    )(places, inputs, gain, dz, *in_own, *in_other)


def dot_nt(a, b):
    return lax.dot_general(a, b, (((1,), (1,)), ((), ())), preferred_element_type=wide)


def dot_tn(a, b):
    return lax.dot_general(a, b, (((0,), (0,)), ((), ())), preferred_element_type=wide)


def attend_kernel(
    count, places, memory, decoded, vectors, vocab_bias, noise, lengths, labels, counted, *refs
):
    small, vocab = refs[: 4 * count], refs[4 * count : 4 * count + 4]
    (
        grad_memory, grad_decoded, pack, seen, sums,
        w, v, sems, v_sems, mk, sk, mq, sq, mono, span, keep, queue, scaled, ratio, window, mix, pre,
    ) = refs[4 * count + 4 :]
    rows, _ = memory.shape
    frames, group, _ = mk.shape
    block = w.shape[2] // 6
    lanes = 128
    chunks = 4 * block // lanes
    copies = []
    for r in range(4):
        arrived = []
        for k in range(count):
            source = small[r * count + k]
            height = source.shape[0]
            for h in range(source.shape[1] // (6 * block)):
                to = pl.ds(pl.multiple_of(places[1 + len(arrived)] * height, height), height)
                arrived.append(
                    pltpu.make_async_copy(
                        source.at[:, 6 * block * h : 6 * block * (h + 1)],
                        w.at[r, to, :],
                        sems.at[r, len(arrived)],
                    )
                )
        copies.append(arrived)
    vocab_copies = [pltpu.make_async_copy(vocab[r], v.at[r], v_sems.at[r]) for r in range(4)]
    for copy in sum(copies, []) + vocab_copies:
        copy.start()

    def split(value):
        return value.reshape(frames, group, value.shape[-1])

    mem, dec = memory[...], decoded[...]
    for r in range(4):
        for copy in copies[r]:
            copy.wait()
        cols = pl.ds(r * block, block)
        keys = jnp.dot(mem, w[r, :, : 2 * block], preferred_element_type=wide)
        queries = jnp.dot(dec, w[r, :, 2 * block : 5 * block], preferred_element_type=wide)
        mk[:, :, cols] = split(keys[:, :block])
        sk[:, :, cols] = split(keys[:, block:])
        mq[:, :, cols] = split(queries[:, :block] + vectors[0:1, cols])
        sq[:, :, cols] = split(queries[:, block : 2 * block] + vectors[2:3, cols])
        pre[:, cols] = queries[:, 2 * block :] + vectors[4:5, cols]

    def lane(c):
        return pl.ds(c * lanes, lanes)

    def spread(row, c):
        return jnp.broadcast_to(vectors[row : row + 1, lane(c)], (group, lanes))

    def energies(queries, keys, vec_row, energy):
        weights = [spread(vec_row, c) for c in range(chunks)]

        def one(i, carried):
            query = [queries[i, :, lane(c)] for c in range(chunks)]
            for j in range(frames):
                total = jnp.tanh(query[0] + keys[j, :, lane(0)]) * weights[0]
                for c in range(1, chunks):
                    total = total + jnp.tanh(query[c] + keys[j, :, lane(c)]) * weights[c]
                energy[i * frames + j] = jnp.broadcast_to(
                    jnp.sum(total, axis=-1, keepdims=True), (group, lanes)
                )
            return carried

        lax.fori_loop(0, frames, one, 0)

    energies(mq, mk, 1, mono)
    energies(sq, sk, 3, span)

    length = lengths[...]
    valid = [(length > j) for j in range(frames)]
    ones = jnp.ones((group, lanes), wide)
    zeros = jnp.zeros((group, lanes), wide)
    live = [jnp.where(valid[j], 1.0, 0.0).astype(wide) for j in range(frames)]
    diagonal = lax.broadcasted_iota(jnp.int32, (group, lanes), 1) - lax.broadcasted_iota(
        jnp.int32, (group, lanes), 0
    )

    def attend(i, previous):
        base = i * frames
        top = jnp.full((group, lanes), -1e30, wide)
        for j in range(frames):
            top = jnp.maximum(top, jnp.where(valid[j], span[base + j], -1e30))
        weight = [jnp.where(valid[j], jnp.exp(span[base + j] - top), 0.0) for j in range(frames)]
        current, ratios = [], []
        queued = previous[0]
        for j in range(frames):
            prob = sigmoid(mono[base + j] + offset + noise[base + j]) * live[j]
            keep[base + j] = prob
            queue[base + j] = queued
            alpha = prob * queued
            current.append(alpha)
            if j + 1 < frames:
                queued = (1.0 - prob) * queued + previous[j + 1]
            both = weight[j] + weight[j - 1] if j else weight[j]
            both = jnp.where(valid[j], both, 1.0)
            window[base + j] = both
            scaled[base + j] = weight[j]
            quotient = alpha / both
            ratio[base + j] = quotient
            ratios.append(quotient)
        row = zeros
        for j in range(frames):
            beta = weight[j] * (ratios[j] + (ratios[j + 1] if j + 1 < frames else zeros))
            row = jnp.where(diagonal == group * j, beta, row)
        mix[i] = row
        return tuple(current)

    lax.fori_loop(0, frames, attend, tuple([ones] + [zeros] * (frames - 1)))

    beta_low = mix[...].reshape(rows, lanes)[:, :rows].astype(low)
    context = jnp.dot(beta_low, mem, preferred_element_type=wide).astype(low)
    seen[0] = context
    for r in range(4):
        cols = pl.ds(r * block, block)
        value = jnp.tanh(
            pre[:, cols] + jnp.dot(context, w[r, :, 5 * block :], preferred_element_type=wide)
        )
        pre[:, cols] = value
        pack[r, :, 5 * block :] = value.astype(low)
    logits = vocab_bias[...]
    for r in range(4):
        vocab_copies[r].wait()
        logits = logits + jnp.dot(pack[r, :, 5 * block :], v[r], preferred_element_type=wide)
    shifted = jnp.exp(logits - jnp.max(logits, axis=-1, keepdims=True))
    softmax = shifted / jnp.sum(shifted, axis=-1, keepdims=True)
    onehot = (labels[...] == lax.broadcasted_iota(jnp.int32, softmax.shape, 1)).astype(wide)
    grad_logits = ((softmax - onehot) * counted[...]).astype(low)
    seen[1] = grad_logits
    sums[5:6, :] = jnp.sum(grad_logits.astype(wide), axis=0, keepdims=True)
    sums[6:8, :] = jnp.zeros((2, sums.shape[1]), wide)

    grad_context = jnp.zeros((rows, memory.shape[1]), wide)
    for r in range(4):
        cols = pl.ds(r * block, block)
        value = pre[:, cols]
        grad_pre = (dot_nt(grad_logits, v[r]) * (1.0 - value * value)).astype(low)
        pack[r, :, 4 * block : 5 * block] = grad_pre
        sums[4:5, cols] = jnp.sum(grad_pre.astype(wide), axis=0, keepdims=True)
        grad_context = grad_context + dot_nt(grad_pre, w[r, :, 5 * block :])
    upper = grad_context.astype(low)
    lower = (grad_context - upper.astype(wide)).astype(low)
    grad_memory[...] = dot_tn(beta_low, upper) + dot_tn(beta_low, lower)
    cross = dot_nt(upper, mem) + dot_nt(lower, mem)
    if rows < lanes:
        cross = jnp.concatenate([cross, jnp.zeros((rows, lanes - rows), wide)], axis=1)
    mix[...] = split(cross)

    def unattend(k, later):
        i = frames - 1 - k
        base = i * frames
        cross_row = mix[i]
        grad_beta = [
            jnp.broadcast_to(
                jnp.sum(
                    jnp.where(diagonal == group * j, cross_row, 0.0), axis=-1, keepdims=True
                ),
                (group, lanes),
            )
            for j in range(frames)
        ]
        weight = [scaled[base + j] for j in range(frames)]
        share = [ratio[base + j] for j in range(frames)]
        direct, from_window, grad_weight = [], [], []
        for j in range(frames):
            grad_ratio = grad_beta[j] * weight[j]
            if j:
                grad_ratio = grad_ratio + grad_beta[j - 1] * weight[j - 1]
            pull = grad_ratio / window[base + j]
            direct.append(pull)
            from_window.append(jnp.where(valid[j], -pull * share[j], 0.0))
            grad_weight.append(
                grad_beta[j] * (share[j] + (share[j + 1] if j + 1 < frames else zeros))
            )
        top = jnp.full((group, lanes), -1e30, wide)
        for j in range(frames):
            top = jnp.maximum(top, jnp.where(valid[j], span[base + j], -1e30))
        total, ties, at_top, through = zeros, zeros, [], []
        for j in range(frames):
            pulled = grad_weight[j] + from_window[j]
            if j + 1 < frames:
                pulled = pulled + from_window[j + 1]
            pulled = weight[j] * pulled
            through.append(pulled)
            total = total + pulled
            hit = jnp.where(span[base + j] == top, live[j], 0.0)
            at_top.append(hit)
            ties = ties + hit
        back = total / ties
        for j in range(frames):
            span[base + j] = through[j] - at_top[j] * back
        grad_queue = zeros
        now = [None] * frames
        for j in reversed(range(frames)):
            prob = keep[base + j]
            grad_alpha = direct[j] + later[j]
            mono[base + j] = queue[base + j] * (grad_alpha - grad_queue) * prob * (1.0 - prob)
            grad_queue = prob * grad_alpha + (1.0 - prob) * grad_queue
            now[j] = grad_queue
        return tuple(now)

    lax.fori_loop(0, frames, unattend, tuple([zeros] * frames))

    def energy_back(queries, keys, energy, bias_row, vec_row):
        def one_chunk(c, carried):
            at = pl.ds(pl.multiple_of(c * lanes, lanes), lanes)
            weight = jnp.broadcast_to(vectors[vec_row : vec_row + 1, at], (group, lanes))

            def one(i, carry):
                grad_keys, vec_total, bias_total = carry
                query = queries[i, :, at]
                grad_query = zeros
                new_keys = []
                for j in range(frames):
                    squash = jnp.tanh(query + keys[j, :, at])
                    grad = energy[i * frames + j]
                    scaled_squash = grad * squash
                    vec_total = vec_total + scaled_squash
                    inner = grad - scaled_squash * squash
                    grad_query = grad_query + inner
                    new_keys.append(grad_keys[j] + inner)
                queries[i, :, at] = grad_query * weight
                return (tuple(new_keys), vec_total, bias_total + grad_query)

            grad_keys, vec_total, bias_total = lax.fori_loop(
                0, frames, one, (tuple([zeros] * frames), zeros, zeros)
            )
            for j in range(frames):
                keys[j, :, at] = grad_keys[j] * weight
            sums[bias_row : bias_row + 1, at] = jnp.sum(bias_total * weight, axis=0, keepdims=True)
            sums[vec_row : vec_row + 1, at] = jnp.sum(vec_total, axis=0, keepdims=True)
            return carried

        lax.fori_loop(0, chunks, one_chunk, 0)

    energy_back(mq, mk, mono, 0, 1)
    energy_back(sq, sk, span, 2, 3)

    total_memory = grad_memory[...]
    total_decoded = jnp.zeros_like(total_memory)
    for r in range(4):
        cols = pl.ds(r * block, block)
        for n, source in enumerate((mk, sk, mq, sq)):
            pack[r, :, n * block : (n + 1) * block] = (
                source[:, :, cols].reshape(rows, block).astype(low)
            )
        total_memory = total_memory + dot_nt(pack[r, :, : 2 * block], w[r, :, : 2 * block])
        total_decoded = total_decoded + dot_nt(
            pack[r, :, 2 * block : 5 * block], w[r, :, 2 * block : 5 * block]
        )
    grad_memory[...] = total_memory
    grad_decoded[...] = total_decoded


def run_attend(
    places, memory, decoded, smalls, vocab, vectors, vocab_bias, noise, lengths, labels, counted,
    frames,
):
    rows, width = memory.shape
    group = rows // frames
    full = vectors.shape[1]
    vocab_width = vocab[0].shape[1]
    cell = (frames * frames, group, 128)
    count = len(smalls[0])
    return pl.pallas_call(
        functools.partial(attend_kernel, count),
        out_shape=(
            jax.ShapeDtypeStruct((rows, width), wide),
            jax.ShapeDtypeStruct((rows, width), wide),
            jax.ShapeDtypeStruct((4, rows, full // 4 * 6), low),
            jax.ShapeDtypeStruct((2, rows, vocab_width), low),
            jax.ShapeDtypeStruct((8, full), wide),
        ),
        in_specs=[in_smem] + [in_vmem] * 8 + [in_place] * (4 * count + 4),
        out_specs=[in_vmem] * 5,
        scratch_shapes=[
            pltpu.VMEM((4, width, full // 4 * 6), low),
            pltpu.VMEM((4,) + vocab[0].shape, low),
            pltpu.SemaphoreType.DMA((4, places.shape[0] - 1)),
            pltpu.SemaphoreType.DMA((4,)),
        ]
        + [pltpu.VMEM((frames, group, full), wide)] * 4
        + [pltpu.VMEM(cell, wide)] * 7
        + [pltpu.VMEM((frames, group, 128), wide), pltpu.VMEM((rows, full), wide)],
        compiler_params=pltpu.CompilerParams(vmem_limit_bytes=56 << 20),
        name="attend",
    )(
        places, memory, decoded, vectors, vocab_bias, noise, lengths, labels, counted,
        *sum(smalls, []), *vocab,
    )


def local(
    dp,
    block_input, norm_gain, lstm_in, lstm_rec, lstm_bias,
    mono_mem, mono_dec, mono_bias, mono_vec, span_mem, span_dec, span_bias, span_vec,
    out_weight, out_bias, vocab_weight, vocab_bias, noise, enc_lengths, label_lengths, labels,
):
    ring = Ring(dp)
    s, y = lax.axis_index("section"), lax.axis_index("mp")
    _, utts, frames, width = block_input.shape
    half, quarter = utts // 2, utts // 4
    rows = frames * quarter
    shard_rows, _, unit_half = lstm_in.shape[1:]
    wide_half = 4 * unit_half
    block = mono_mem.shape[1]
    vocab_size = vocab_weight.shape[1]
    vocab_pad = 4 * block

    in_shard = corners(lstm_in[0].reshape(shard_rows, wide_half))
    rec_shard = corners(lstm_rec[0].reshape(shard_rows, wide_half))
    b_own = corners(lstm_bias[0].reshape(1, wide_half)).astype(wide)
    b_other = across_cores(b_own)

    def of_section(array):
        return jnp.where(s == y, array, across_cores(array))

    inputs = of_section(jnp.swapaxes(block_input[0], 0, 1))
    gain = of_section(norm_gain[0])
    inputs_own = lax.dynamic_slice_in_dim(inputs, s * half, half, axis=1)
    inputs_other = lax.dynamic_slice_in_dim(inputs, (1 - s) * half, half, axis=1)
    normed_own = normalize(inputs_own.astype(wide), gain)
    normed_own = normed_own.astype(low).reshape(frames * half, width)
    normed_other = normalize(inputs_other.astype(wide), gain)
    normed_other = normed_other.astype(low).reshape(frames * half, width)

    start = s * half + y * quarter
    noise_part = jnp.transpose(
        lax.dynamic_slice_in_dim(noise, start, quarter, axis=0), (1, 2, 0)
    ).reshape(frames * frames, quarter, 1)
    noise_part = jnp.broadcast_to(noise_part, (frames * frames, quarter, 128))
    length_part = lax.dynamic_slice_in_dim(enc_lengths, start, quarter, axis=0)
    length_part = jnp.broadcast_to(length_part[:, None], (quarter, 128))
    label_part = lax.dynamic_slice_in_dim(labels, start, quarter, axis=0).T.reshape(rows, 1)
    count_part = lax.dynamic_slice_in_dim(label_lengths, start, quarter, axis=0)
    counted = (jnp.arange(frames)[:, None] < count_part[None, :]).astype(wide).reshape(rows, 1)
    bias_row = jnp.pad(vocab_bias, (0, vocab_pad - vocab_size), constant_values=-1e30)[None]

    vector_own = jnp.stack([mono_bias, mono_vec, span_bias, span_vec, out_bias])
    vector_pair = jnp.concatenate([vector_own, across_chips(vector_own)], axis=1)
    vectors = jnp.concatenate([vector_pair, across_cores(vector_pair)], axis=1)
    vectors = jnp.pad(vectors, ((0, 3), (0, 0)))
    vocab_own = jnp.pad(vocab_weight, ((0, 0), (0, vocab_pad - vocab_size)))
    ready = (noise_part, length_part, label_part, counted, bias_row, normed_own, normed_other)
    places, in_own, rec_own, small_own, small_chip = [], [], [], [], []
    small = jnp.concatenate(
        [mono_mem, span_mem, mono_dec, span_dec, out_weight[0], out_weight[1]], axis=1
    )
    if ring.short:
        small_far, small_next = ring.across(small), ring.onward(small)
        in_shard, rec_shard, b_own, small_far, small_next = lax.optimization_barrier(
            (in_shard, rec_shard, b_own, small_far, small_next)
        )
        vocab_chip = across_chips(tie(vocab_own, in_shard))
        small_own.append(jnp.concatenate([small, small_far], axis=1))
        first = jnp.concatenate([in_shard, small_next], axis=1)
        second = rec_shard
        places = [ring.back(k // 2) * 2 + (ring.x if k % 2 == 0 else 1 - ring.x) for k in range(8)]
        in_other, rec_other, small_core = [], [], []
        earlier = ()
        for k in range(ring.outer):
            if k:
                first = tie(first, *earlier, *ready)
                ready = ()
            earlier = (second,)
            if k == 1:
                earlier += (vocab_chip, vectors, b_other)
            if k == 2:
                earlier += (vocab[2], vocab[3])
            in_other += [across_cores(part) for part in in_own[len(in_other) :]]
            rec_other += [across_cores(part) for part in rec_own[len(rec_other) :]]
            small_core += [across_cores(small_own[-1])]
            small_chip += [across_chips(small_own[-1])]
            if k:
                earlier += (*in_other[-2:], *rec_other[-2:], small_core[-1], small_chip[-2])
            if k == 1:
                vocab = [vocab_own, vocab_chip, across_cores(vocab_own), across_cores(vocab_chip)]
            far, far_rec = ring.across(first), ring.across(second)
            in_own += [first, far]
            rec_own += [second, far_rec]
            earlier += (far, far_rec)
            if k < ring.outer - 1:
                small_own.append(
                    jnp.concatenate([first[:, wide_half:], far[:, wide_half:]], axis=1)
                )
                first = ring.onward(first if k < ring.outer - 2 else first[:, :wide_half])
                second = ring.onward(second)
        in_other += [across_cores(part) for part in in_own[len(in_other) :]]
        rec_other += [across_cores(part) for part in rec_own[len(rec_other) :]]
    else:
        vocab_chip = across_chips(vocab_own)
        small, in_block, rec_block = [
            lax.all_gather(a, "dp", axis=0, tiled=True) for a in (small, in_shard, rec_shard)
        ]
        places, in_own, rec_own = [jnp.int32(0)], [in_block], [rec_block]
        small_own, small_chip = [small], [across_chips(small)]
        vocab = [vocab_own, vocab_chip, across_cores(vocab_own), across_cores(vocab_chip)]
        in_other, rec_other = [across_cores(in_block)], [across_cores(rec_block)]
        small_core = [across_cores(small)]
    places = jnp.stack([s] + places).astype(jnp.int32)
    places = tie(places, vectors, *vocab, *ready, *small_chip[:-1], *small_core)

    quarters, before, gates, cells = run_forward(
        places, normed_own, b_own, b_other, in_own, in_other, rec_own, rec_other, frames
    )

    kept = lax.dynamic_index_in_dim(quarters, y, axis=0, keepdims=False)
    given = lax.dynamic_index_in_dim(quarters, 1 - y, axis=0, keepdims=False)
    taken = across_chips(given)
    memory = jnp.where(y == 0, kept, taken).reshape(rows, width)
    decoded = jnp.where(y == 0, taken, kept).reshape(rows, width)
    small_both = [across_cores(part) for part in small_chip]
    smalls = [small_own, small_chip, small_core, small_both]
    grad_memory, grad_decoded, pack, seen, sums = run_attend(
        places, memory, decoded, smalls, vocab, vectors, bias_row, noise_part, length_part,
        label_part, counted, frames,
    )
    kept_far = across_chips(tie(kept, taken))
    before = before.reshape(frames * half, width)
    before_peer = across_cores(tie(before, taken))

    grad_kept = jnp.where(y == 0, grad_memory, grad_decoded)
    grad_given = jnp.where(y == 0, grad_decoded, grad_memory).astype(low)
    grad_taken = across_chips(grad_given)
    outside = jnp.stack(
        [jnp.where(y == 0, grad_kept, grad_taken), jnp.where(y == 0, grad_taken, grad_kept)]
    ).reshape(2, frames, quarter, width)
    pack_core = across_cores(pack[2:4])
    pack_out = jnp.stack([pack[1], pack_core[1]])
    memory_next = jnp.where(y == 0, given, kept_far).reshape(rows, width)
    decoded_next = jnp.where(y == 0, kept_far, given).reshape(rows, width)
    states = jnp.stack([memory, memory_next, decoded, decoded_next])
    states_core = across_cores(states)
    blocks = sums[:5].reshape(5, 4, block)
    vector_pair = blocks[:, :2] + across_cores(blocks[:, 2:])
    bias_pair = sums[5] + across_cores(sums[5])
    vector_out = jnp.concatenate([vector_pair[:, 1].reshape(-1), bias_pair])
    places_back, pack_out, vector_out, states_core = lax.optimization_barrier(
        (places, pack_out, vector_out, states_core, outside, before_peer)
    )[:4]
    dz = run_backward(places_back, outside, gates, cells, rec_own, rec_other)

    dz = dz.reshape(2, frames * half, wide_half)
    dz_kept = lax.dynamic_index_in_dim(dz, s, axis=0, keepdims=False)
    dz_given = lax.dynamic_index_in_dim(dz, 1 - s, axis=0, keepdims=False)
    dz_all = jnp.concatenate([dz_kept, across_cores(dz_given)], axis=0)
    before_all = jnp.concatenate([before, before_peer], axis=0)
    normed_all = jnp.concatenate([normed_own, normed_other], axis=0)
    rec_total = dot_tn(before_all, dz_all).astype(low)
    in_total = dot_tn(normed_all, dz_all).astype(low)

    pack_far = across_chips(pack_out)
    seen_far = across_chips(tie(seen, pack_out))
    vector_far = across_chips(vector_out)
    seen_pair = jnp.concatenate([seen, seen_far], axis=0)
    seen_core = across_cores(seen_pair)

    def gathered(n):
        return jnp.concatenate(
            [states[n], states_core[n], states[n + 1], states_core[n + 1]], axis=0
        )

    memory_all, decoded_all = gathered(0), gathered(2)
    pack_all = jnp.concatenate([pack[0], pack_core[0], pack_far[0], pack_far[1]], axis=0)
    seen_all = [
        jnp.concatenate([seen_pair[n], seen_core[n], seen_pair[2 + n], seen_core[2 + n]], axis=0)
        for n in range(2)
    ]
    energy_total = [
        dot_tn(memory_all, pack_all[:, : 2 * block]).astype(low),
        dot_tn(decoded_all, pack_all[:, 2 * block : 4 * block]).astype(low),
    ]
    grad_pre = pack_all[:, 4 * block : 5 * block]
    output_total = [
        dot_tn(decoded_all, grad_pre).astype(low),
        dot_tn(seen_all[0], grad_pre).astype(low),
        dot_tn(seen_all[1], pack_all[:, 5 * block :]).astype(low),
    ]

    def input_back(dz):
        grad_inputs, grad_gain = run_input(
            places, inputs_own.reshape(frames * half, width), gain[None], dz, in_own, in_other
        )
        grad_inputs = jnp.swapaxes(grad_inputs.reshape(frames, half, width), 0, 1)
        grad_peer = across_cores(grad_inputs)
        section = jnp.concatenate(
            [
                jnp.where(s == 0, grad_inputs, grad_peer),
                jnp.where(s == 0, grad_peer, grad_inputs),
            ],
            axis=0,
        )
        far = lax.ppermute(section, ("section", "mp"), [(0, 1), (3, 2)])
        grad_gain = grad_gain.reshape(width)
        gain_sum = grad_gain + across_cores(grad_gain)
        flat = jnp.concatenate(
            [
                vector_pair[:, 0].reshape(-1) + vector_far[: 5 * block],
                bias_pair + vector_far[5 * block :],
                jnp.sum(dz_all.astype(wide), axis=0),
                gain_sum,
            ]
        )
        return section, far, jnp.pad(flat, (0, -flat.shape[0] % (2 * shard_rows)))

    if ring.short:
        r = shard_rows
        back, x, onward, across = ring.back, ring.x, ring.onward, ring.across
        chains = [[rec_total], [in_total], energy_total]
        sums_so_far = [None] * 3
        arrived, passed = {}, {}
        held = flat_sum = None
        for k in range(1, 5):
            for n, group in enumerate(chains):
                theirs = ring.part(group, back(k) * 2 + 1 - x, r)
                if k > 2:
                    theirs = tie(theirs, passed[n, k - 2], arrived[n, k - 1], passed[3, k - 2])
                if k == 4:
                    theirs = tie(theirs, grad_far)
                arrived[n, k] = across(theirs)
                total = ring.part(group, back(k) * 2 + x, r).astype(wide)
                total = total + arrived[n, k].astype(wide)
                if k > 1:
                    total = total + passed[n, k - 1].astype(wide)
                sums_so_far[n] = total
                if k < 4:
                    passed[n, k] = onward(total.astype(low))
            if k == 1:
                grad_section, grad_far, flat = input_back(tie(dz, arrived[0, 1]))
                flat_sum = flat
                flat_width = flat.shape[0] // (2 * r)
                held = jnp.concatenate(
                    [ring.part(output_total, back(1), 2 * r), halves(flat, 2 * r)], axis=1
                )
            if k < 4:
                passed[3, k] = onward(held)
                ours = ring.part(output_total, back(k + 1), 2 * r).astype(wide)
                columns = ours.shape[1]
                ours = (ours + passed[3, k][:, :columns].astype(wide)).astype(low)
                flat_sum = flat_sum + joined(passed[3, k][:, columns:], flat_width).reshape(-1)
                held = jnp.concatenate([ours, passed[3, k][:, columns:]], axis=1)
        ours = held[:, :columns]
        message = jnp.concatenate(
            [cut(ours, 1 - x, r), halves(flat_sum, 2 * r).reshape(r, -1)], axis=1
        )
        message = across(tie(message, arrived[2, 3]))
        output_grad = cut(ours, x, r).astype(wide) + message[:, :columns].astype(wide)
        flat = flat_sum + joined(
            message[:, columns:].reshape(2 * r, -1), flat_width
        ).reshape(-1)
        shard = output_grad[:, 2 * block :].astype(low)
        held = jnp.concatenate([shard, across(shard)], axis=1)
        vocab_grad = jnp.zeros((vocab_pad, block), low)
        for k in range(4):
            for n, at in enumerate((x, 1 - x)):
                vocab_grad = lax.dynamic_update_slice(
                    vocab_grad, held[:, n * block : (n + 1) * block], ((back(k) * 2 + at) * r, 0)
                )
            if k < 3:
                held = onward(held)
        rec_grad, in_grad, energy_grad = sums_so_far
    else:
        grad_section, grad_far, flat = input_back(dz)

        def scatter(total):
            return lax.psum_scatter(total, "dp", scatter_dimension=0, tiled=True).astype(wide)

        rec_grad, in_grad = scatter(rec_total), scatter(in_total)
        energy_grad = jnp.concatenate([scatter(a) for a in energy_total], axis=1)
        output_grad = jnp.concatenate([scatter(a) for a in output_total], axis=1)
        flat = lax.psum(flat, "dp")
        vocab_grad = lax.all_gather(
            output_grad[:, 2 * block :].astype(low), "dp", axis=0, tiled=True
        )

    input_grad = jnp.where(s == y, grad_section, grad_far)
    vocab_grad = vocab_grad.T[:, :vocab_size].astype(wide)
    ends = [5 * block, 5 * block + vocab_pad, 5 * block + vocab_pad + wide_half + width]
    vector_sum = flat[: ends[0]].reshape(5, block)
    bias_sum = flat[ends[0] : ends[0] + vocab_size]
    moved = halves(flat[ends[1] : ends[2]], shard_rows)
    moved = corners(jnp.concatenate([rec_grad.astype(low), moved], axis=1))
    rec_grad = moved[:, :wide_half].astype(wide).reshape(1, shard_rows, 4, unit_half)
    moved = joined(moved[:, wide_half:], (ends[2] - ends[1]) // shard_rows).reshape(-1)
    lstm_bias_sum = moved[:wide_half].reshape(1, 4, unit_half)
    gain_sum = moved[wide_half:][None]
    in_grad = corners(in_grad.astype(low)).astype(wide).reshape(1, shard_rows, 4, unit_half)
    mono_mem_grad, span_mem_grad, mono_dec_grad, span_dec_grad = [
        energy_grad[:, n * block : (n + 1) * block] for n in range(4)
    ]
    return (
        input_grad[None],
        gain_sum,
        in_grad,
        rec_grad,
        lstm_bias_sum,
        mono_mem_grad,
        mono_dec_grad,
        vector_sum[0],
        vector_sum[1],
        span_mem_grad,
        span_dec_grad,
        vector_sum[2],
        vector_sum[3],
        jnp.stack([output_grad[:, :block], output_grad[:, block : 2 * block]]),
        vector_sum[4],
        vocab_grad,
        bias_sum,
    )


def solution(mesh):
    both = ("section", "mp")
    in_specs = (
        P("section", "dp", None, None),
        P("section", None),
        P("section", "dp", None, "mp"),
        P("section", "dp", None, "mp"),
        P("section", None, "mp"),
        P("dp", both),
        P("dp", both),
        P(both),
        P(both),
        P("dp", both),
        P("dp", both),
        P(both),
        P(both),
        P(None, "dp", both),
        P(both),
        P(both, None),
        P(),
        P("dp", None, None),
        P("dp"),
        P("dp"),
        P("dp", None),
    )
    out_specs = (
        P("section", "dp", None, None),
        P("section", None),
        P("section", "dp", None, "mp"),
        P("section", "dp", None, "mp"),
        P("section", None, "mp"),
        P("dp", both),
        P("dp", both),
        P(both),
        P(both),
        P("dp", both),
        P("dp", both),
        P(both),
        P(both),
        P(None, "dp", both),
        P(both),
        P(both, None),
        P(),
    )
    dp = mesh.shape["dp"]

    def step(*arrays):
        return local(dp, *arrays)

    return jax.shard_map(step, mesh=mesh, in_specs=in_specs, out_specs=out_specs, check_vma=False)
```

```python
import functools

import jax
import jax.numpy as jnp
from jax import lax
from jax.experimental import pallas as pl
from jax.experimental.pallas import tpu as pltpu
from jax.sharding import PartitionSpec as P

epsilon = 1e-05
offset = -4.0
wide = jnp.float32
low = jnp.bfloat16
in_vmem = pl.BlockSpec(memory_space=pltpu.VMEM)
in_smem = pl.BlockSpec(memory_space=pltpu.SMEM)
in_place = pl.BlockSpec(memory_space=pl.ANY)
core_swap = [(0, 1), (1, 0)]
corner_swap = [(0, 0), (1, 2), (2, 1), (3, 3)]


def normalize(inputs, gain_row):
    average = jnp.mean(inputs, axis=-1, keepdims=True)
    centred = inputs - average
    spread = jnp.mean(centred * centred, axis=-1, keepdims=True)
    return centred * lax.rsqrt(spread + epsilon) * gain_row


def across_cores(array):
    return lax.ppermute(array, "section", core_swap)


def across_chips(array):
    return lax.ppermute(array, "mp", core_swap)


def corners(array):
    return lax.ppermute(array, ("section", "mp"), corner_swap)


def tie(value, *others):
    return lax.optimization_barrier((value,) + others)[0]


def cut(array, block, rows):
    return lax.dynamic_slice_in_dim(array, block * rows, rows, axis=0)


class Flow:
    def __init__(self):
        self.landed = ()

    def step(self, *jobs, also=()):
        operands = tuple(operand for _, operand in jobs)
        operands = lax.optimization_barrier(operands + self.landed + tuple(also))[: len(jobs)]
        results = [send(operand) for (send, _), operand in zip(jobs, operands)]
        self.landed = tuple(results)
        return results


class Ring:
    def __init__(self, dp):
        self.dp = dp
        self.outer = dp // 2
        self.short = dp % 2 == 0 and self.outer == 4
        pairs = [(z, x) for z in range(self.outer) for x in range(2)]
        self.pair = [(2 * z + x, 2 * z + 1 - x) for z, x in pairs]
        self.ring = [(2 * z + x, 2 * ((z + 1) % self.outer) + x) for z, x in pairs]
        self.turn = [(b, a) for a, b in self.ring]
        place = lax.axis_index("dp")
        self.z, self.x = place // 2, place % 2

    def across(self, array):
        return lax.ppermute(array, "dp", self.pair)

    def onward(self, array):
        return lax.ppermute(array, "dp", self.ring)

    def astern(self, array):
        return lax.ppermute(array, "dp", self.turn)

    def back(self, k):
        return lax.rem(self.z - k + self.outer, self.outer)

    def part(self, group, block, rows):
        return jnp.concatenate([cut(a, block, rows) for a in group], axis=1)


def halves(array, height):
    array = array.reshape(height, -1)
    upper = array.astype(low)
    lower = (array - upper.astype(wide)).astype(low)
    return jnp.pad(
        jnp.concatenate([upper, lower], axis=1), ((0, 0), (0, -2 * array.shape[1] % 128))
    )


def joined(array, count):
    return array[:, :count].astype(wide) + array[:, count : 2 * count].astype(wide)


def sigmoid(x):
    return 0.5 * jnp.tanh(0.5 * x) + 0.5


def fetch(blocks, places, side_blocks, target, sems, first=0, column=0):
    wide_half = target.shape[1] // 2
    columns = pl.ds(pl.multiple_of(side_blocks * wide_half, wide_half), wide_half)
    copies = []
    for k, block in enumerate(blocks):
        height = block.shape[0]
        span = pl.ds(pl.multiple_of(places[1 + k] * height, height), height)
        copies.append(
            pltpu.make_async_copy(
                block.at[:, column : column + wide_half],
                target.at[span, columns],
                sems.at[first + k],
            )
        )
    return copies


def forward_kernel(count, column, places, normed, b_own, b_other, *refs):
    in_own, in_other, w_own, w_other = [refs[n * count : (n + 1) * count] for n in range(4)]
    quarters, before, gates, cells, wi, w, b, state, cell, sems = refs[4 * count :]
    steps, rows, wide_full = gates.shape
    wide_half = wide_full // 2
    unit_half = wide_half // 4
    chunk = min(256, unit_half)
    s = places[0]
    copies = fetch(in_own, places, s, wi, sems) + fetch(in_other, places, 1 - s, wi, sems, count)
    later = fetch(w_own, places, s, w, sems, 2 * count, column)
    later += fetch(w_other, places, 1 - s, w, sems, 3 * count, column)
    for copy in copies + later:
        copy.start()
    for source, at in ((b_own, s), (b_other, 1 - s)):
        b[:, pl.ds(pl.multiple_of(at * wide_half, wide_half), wide_half)] = source[...]
    state[...] = jnp.zeros_like(state)
    cell[...] = jnp.zeros_like(cell)
    for copy in copies:
        copy.wait()

    def project(g, carried):
        cols = pl.ds(pl.multiple_of(g * unit_half, unit_half), unit_half)
        value = jnp.dot(normed[...], wi[:, cols], preferred_element_type=wide) + b[:, cols]
        gates[:, :, cols] = value.reshape(steps, rows, unit_half)
        return carried

    lax.fori_loop(0, 8, project, 0)
    for copy in later:
        copy.wait()
    eighth = rows // 2

    def advance(t, carried):
        hidden = state[...]
        before[t] = hidden
        for at in range(0, 2 * unit_half, chunk):
            half, inside = at // unit_half, at % unit_half
            acts = []
            for g in range(4):
                cols = pl.ds(half * wide_half + g * unit_half + inside, chunk)
                value = gates[t, :, cols] + jnp.dot(
                    hidden, w[:, cols], preferred_element_type=wide
                )
                value = jnp.tanh(value) if g == 2 else sigmoid(value)
                gates[t, :, cols] = value
                acts.append(value)
            units = pl.ds(at, chunk)
            new_cell = acts[1] * cell[:, units] + acts[0] * acts[2]
            cell[:, units] = new_cell
            cells[t, :, units] = new_cell
            new_hidden = acts[3] * jnp.tanh(new_cell)
            state[:, units] = new_hidden.astype(low)
            quarters[0, t, :, units] = new_hidden[:eighth].astype(low)
            quarters[1, t, :, units] = new_hidden[eighth:].astype(low)
        return carried

    lax.fori_loop(0, steps, advance, 0)


def run_forward(places, normed, b_own, b_other, in_own, in_other, w_own, w_other, steps, column):
    rows = normed.shape[0] // steps
    units = normed.shape[1]
    wide_half = b_own.shape[1]
    count = len(w_own)
    return pl.pallas_call(
        functools.partial(forward_kernel, count, column),
        out_shape=(
            jax.ShapeDtypeStruct((2, steps, rows // 2, units), low),
            jax.ShapeDtypeStruct((steps, rows, units), low),
            jax.ShapeDtypeStruct((steps, rows, 2 * wide_half), wide),
            jax.ShapeDtypeStruct((steps, rows, units), wide),
        ),
        in_specs=[in_smem] + [in_vmem] * 3 + [in_place] * (4 * count),
        out_specs=[in_vmem] * 4,
        scratch_shapes=[
            pltpu.VMEM((units, 2 * wide_half), low),
            pltpu.VMEM((units, 2 * wide_half), low),
            pltpu.VMEM((1, 2 * wide_half), wide),
            pltpu.VMEM((rows, units), low),
            pltpu.VMEM((rows, units), wide),
            pltpu.SemaphoreType.DMA((4 * count,)),
        ],
        compiler_params=pltpu.CompilerParams(vmem_limit_bytes=56 << 20),
        name="recur_forward",
    )(places, normed, b_own, b_other, *in_own, *in_other, *w_own, *w_other)


def backward_steps(first, last, outside, gates, cells, dz, w, dh, dc):
    _, rows, wide_full = gates.shape
    wide_half = wide_full // 2
    unit_half = wide_half // 4
    chunk = min(256, unit_half)

    def retreat(k, carried):
        t = first - 1 - k
        earlier = jnp.maximum(t - 1, 0)
        live = jnp.where(t > 0, 1.0, 0.0).astype(wide)
        for at in range(0, 2 * unit_half, chunk):
            half, inside = at // unit_half, at % unit_half
            units = pl.ds(at, chunk)
            grad = (
                jnp.concatenate([outside[0, t, :, units], outside[1, t, :, units]], axis=0)
                + dh[:, units]
            )
            i, f, g, o = [
                gates[t, :, pl.ds(half * wide_half + n * unit_half + inside, chunk)]
                for n in range(4)
            ]
            squash = jnp.tanh(cells[t, :, units])
            total = dc[:, units] + grad * o * (1.0 - squash * squash)
            parts = (
                total * g * i * (1.0 - i),
                total * (cells[earlier, :, units] * live) * f * (1.0 - f),
                total * i * (1.0 - g * g),
                grad * squash * o * (1.0 - o),
            )
            for n, part in enumerate(parts):
                dz[half, t - last, :, pl.ds(n * unit_half + inside, chunk)] = part.astype(low)
            dc[:, units] = total * f
        upper, lower = dz[0, t - last], dz[1, t - last]
        for at in range(0, 2 * unit_half, chunk):
            units = pl.ds(at, chunk)
            dh[:, units] = jnp.dot(
                upper, w[:wide_half, units], preferred_element_type=wide
            ) + jnp.dot(lower, w[wide_half:, units], preferred_element_type=wide)
        return carried

    lax.fori_loop(0, first - last, retreat, 0)


def late_kernel(count, column, middle, places, outside, gates, cells, *refs):
    w_own, w_other = refs[:count], refs[count : 2 * count]
    dz, turned, dh, dc, stage, w, sems, out_sem = refs[2 * count :]
    steps, _, wide_full = gates.shape
    wide_half = wide_full // 2
    unit_half = wide_half // 4
    s = places[0]
    jobs = []
    for n, (sources, at) in enumerate(((w_own, s), (w_other, 1 - s))):
        for k, block in enumerate(sources):
            slot = n * count + k
            copy = pltpu.make_async_copy(
                block.at[:, column : column + wide_half], stage.at[slot], sems.at[slot]
            )
            copy.start()
            jobs.append((copy, slot, at, places[1 + k] * block.shape[0]))
    dh[...] = jnp.zeros_like(dh)
    dc[...] = jnp.zeros_like(dc)
    height = w_own[0].shape[0]
    piece = min(height, 128)
    for copy, slot, at, first in jobs:
        copy.wait()

        def turn(g, carried, slot=slot, at=at, first=first):
            columns = pl.ds(pl.multiple_of(g * unit_half, unit_half), unit_half)
            span = pl.ds(pl.multiple_of(at * wide_half + g * unit_half, unit_half), unit_half)
            for low_row in range(0, height, piece):
                into = pl.ds(pl.multiple_of(first + low_row, piece), piece)
                w[span, into] = stage[slot, low_row : low_row + piece, columns].T
            return carried

        lax.fori_loop(0, 4, turn, 0)
    save = pltpu.make_async_copy(w, turned, out_sem)
    save.start()
    backward_steps(steps, middle, outside, gates, cells, dz, w, dh, dc)
    save.wait()


def early_kernel(middle, outside, gates, cells, dh_in, dc_in, turned, dz, w, dh, dc, sem):
    load = pltpu.make_async_copy(turned, w, sem)
    load.start()
    dh[...] = dh_in[...]
    dc[...] = dc_in[...]
    load.wait()
    backward_steps(middle, 0, outside, gates, cells, dz, w, dh, dc)


def run_late(places, outside, gates, cells, w_own, w_other, column, middle):
    steps, rows, wide_full = gates.shape
    units = cells.shape[2]
    count = len(w_own)
    return pl.pallas_call(
        functools.partial(late_kernel, count, column, middle),
        out_shape=(
            jax.ShapeDtypeStruct((2, steps - middle, rows, wide_full // 2), low),
            jax.ShapeDtypeStruct((wide_full, units), low),
            jax.ShapeDtypeStruct((rows, units), wide),
            jax.ShapeDtypeStruct((rows, units), wide),
        ),
        in_specs=[in_smem] + [in_vmem] * 3 + [in_place] * (2 * count),
        out_specs=[in_vmem, in_place, in_vmem, in_vmem],
        scratch_shapes=[
            pltpu.VMEM((2 * count, units // count, wide_full // 2), low),
            pltpu.VMEM((wide_full, units), low),
            pltpu.SemaphoreType.DMA((2 * count,)),
            pltpu.SemaphoreType.DMA,
        ],
        compiler_params=pltpu.CompilerParams(vmem_limit_bytes=56 << 20),
        name="recur_backward_late",
    )(places, outside, gates, cells, *w_own, *w_other)


def run_early(outside, gates, cells, dh, dc, turned, middle):
    steps, rows, wide_full = gates.shape
    units = cells.shape[2]
    return pl.pallas_call(
        functools.partial(early_kernel, middle),
        out_shape=jax.ShapeDtypeStruct((2, middle, rows, wide_full // 2), low),
        in_specs=[in_vmem] * 5 + [in_place],
        out_specs=in_vmem,
        scratch_shapes=[
            pltpu.VMEM((wide_full, units), low),
            pltpu.VMEM((rows, units), wide),
            pltpu.VMEM((rows, units), wide),
            pltpu.SemaphoreType.DMA,
        ],
        compiler_params=pltpu.CompilerParams(vmem_limit_bytes=56 << 20),
        name="recur_backward_early",
    )(outside, gates, cells, dh, dc, turned)


def input_kernel(count, places, inputs, gain, dz, dz_given, *refs):
    in_own, in_other = refs[:count], refs[count : 2 * count]
    grad_inputs, grad_gain, wi, sems = refs[2 * count :]
    s = places[0]
    copies = fetch(in_own, places, s, wi, sems) + fetch(in_other, places, 1 - s, wi, sems, count)
    for copy in copies:
        copy.start()
    x = inputs[...].astype(wide)
    centred = x - jnp.mean(x, axis=-1, keepdims=True)
    scale = lax.rsqrt(jnp.mean(centred * centred, axis=-1, keepdims=True) + epsilon)
    shape = centred * scale
    for copy in copies:
        copy.wait()
    wide_half = wi.shape[1] // 2
    own = pl.ds(pl.multiple_of(s * wide_half, wide_half), wide_half)
    other = pl.ds(pl.multiple_of((1 - s) * wide_half, wide_half), wide_half)
    grad = dot_nt(dz[...], wi[:, own]) + dot_nt(dz_given[...], wi[:, other])
    grad_gain[...] = jnp.sum(grad * shape, axis=0, keepdims=True)
    pulled = grad * gain[...]
    grad_inputs[...] = scale * (
        pulled
        - jnp.mean(pulled, axis=-1, keepdims=True)
        - shape * jnp.mean(pulled * shape, axis=-1, keepdims=True)
    )


def run_input(places, inputs, gain, dz, dz_given, in_own, in_other):
    count = len(in_own)
    rows, width = inputs.shape
    return pl.pallas_call(
        functools.partial(input_kernel, count),
        out_shape=(
            jax.ShapeDtypeStruct((rows, width), wide),
            jax.ShapeDtypeStruct((1, width), wide),
        ),
        in_specs=[in_smem] + [in_vmem] * 4 + [in_place] * (2 * count),
        out_specs=[in_vmem] * 2,
        scratch_shapes=[
            pltpu.VMEM((width, 2 * dz.shape[1]), low),
            pltpu.SemaphoreType.DMA((2 * count,)),
        ],
        compiler_params=pltpu.CompilerParams(vmem_limit_bytes=56 << 20),
        name="input_back",
    )(places, inputs, gain, dz, dz_given, *in_own, *in_other)


def dot_nt(a, b):
    return lax.dot_general(a, b, (((1,), (1,)), ((), ())), preferred_element_type=wide)


def dot_tn(a, b):
    return lax.dot_general(a, b, (((0,), (0,)), ((), ())), preferred_element_type=wide)


def attend_kernel(
    count, places, memory, decoded, vectors, vocab_bias, noise, lengths, labels, counted, *refs
):
    small, vocab = refs[: 4 * count], refs[4 * count : 4 * count + 4]
    (
        grad_memory, grad_decoded, pack, seen, sums,
        w, v, sems, v_sems, mk, sk, mq, sq, mono, span, keep, queue, scaled, ratio, window, mix, pre,
    ) = refs[4 * count + 4 :]
    rows, _ = memory.shape
    frames, group, _ = mk.shape
    block = w.shape[2] // 6
    lanes = 128
    chunks = 4 * block // lanes
    copies = []
    for r in range(4):
        arrived = []
        for k in range(count):
            source = small[r * count + k]
            height = source.shape[0]
            for h in range(source.shape[1] // (6 * block)):
                to = pl.ds(pl.multiple_of(places[1 + len(arrived)] * height, height), height)
                arrived.append(
                    pltpu.make_async_copy(
                        source.at[:, 6 * block * h : 6 * block * (h + 1)],
                        w.at[r, to, :],
                        sems.at[r, len(arrived)],
                    )
                )
        copies.append(arrived)
    vocab_copies = [pltpu.make_async_copy(vocab[r], v.at[r], v_sems.at[r]) for r in range(4)]
    for copy in sum(copies, []) + vocab_copies:
        copy.start()

    def split(value):
        return value.reshape(frames, group, value.shape[-1])

    mem, dec = memory[...], decoded[...]
    for r in range(4):
        for copy in copies[r]:
            copy.wait()
        cols = pl.ds(r * block, block)
        keys = jnp.dot(mem, w[r, :, : 2 * block], preferred_element_type=wide)
        queries = jnp.dot(dec, w[r, :, 2 * block : 5 * block], preferred_element_type=wide)
        mk[:, :, cols] = split(keys[:, :block])
        sk[:, :, cols] = split(keys[:, block:])
        mq[:, :, cols] = split(queries[:, :block] + vectors[0:1, cols])
        sq[:, :, cols] = split(queries[:, block : 2 * block] + vectors[2:3, cols])
        pre[:, cols] = queries[:, 2 * block :] + vectors[4:5, cols]

    def lane(c):
        return pl.ds(c * lanes, lanes)

    def spread(row, c):
        return jnp.broadcast_to(vectors[row : row + 1, lane(c)], (group, lanes))

    def energies(queries, keys, vec_row, energy):
        weights = [spread(vec_row, c) for c in range(chunks)]

        def one(i, carried):
            query = [queries[i, :, lane(c)] for c in range(chunks)]
            for j in range(frames):
                total = jnp.tanh(query[0] + keys[j, :, lane(0)]) * weights[0]
                for c in range(1, chunks):
                    total = total + jnp.tanh(query[c] + keys[j, :, lane(c)]) * weights[c]
                energy[i * frames + j] = jnp.broadcast_to(
                    jnp.sum(total, axis=-1, keepdims=True), (group, lanes)
                )
            return carried

        lax.fori_loop(0, frames, one, 0)

    energies(mq, mk, 1, mono)
    energies(sq, sk, 3, span)

    length = lengths[...]
    valid = [(length > j) for j in range(frames)]
    ones = jnp.ones((group, lanes), wide)
    zeros = jnp.zeros((group, lanes), wide)
    live = [jnp.where(valid[j], 1.0, 0.0).astype(wide) for j in range(frames)]
    diagonal = lax.broadcasted_iota(jnp.int32, (group, lanes), 1) - lax.broadcasted_iota(
        jnp.int32, (group, lanes), 0
    )

    def attend(i, previous):
        base = i * frames
        top = jnp.full((group, lanes), -1e30, wide)
        for j in range(frames):
            top = jnp.maximum(top, jnp.where(valid[j], span[base + j], -1e30))
        weight = [jnp.where(valid[j], jnp.exp(span[base + j] - top), 0.0) for j in range(frames)]
        current, ratios = [], []
        queued = previous[0]
        for j in range(frames):
            prob = sigmoid(mono[base + j] + offset + noise[base + j]) * live[j]
            keep[base + j] = prob
            queue[base + j] = queued
            alpha = prob * queued
            current.append(alpha)
            if j + 1 < frames:
                queued = (1.0 - prob) * queued + previous[j + 1]
            both = weight[j] + weight[j - 1] if j else weight[j]
            both = jnp.where(valid[j], both, 1.0)
            window[base + j] = both
            scaled[base + j] = weight[j]
            quotient = alpha / both
            ratio[base + j] = quotient
            ratios.append(quotient)
        row = zeros
        for j in range(frames):
            beta = weight[j] * (ratios[j] + (ratios[j + 1] if j + 1 < frames else zeros))
            row = jnp.where(diagonal == group * j, beta, row)
        mix[i] = row
        return tuple(current)

    lax.fori_loop(0, frames, attend, tuple([ones] + [zeros] * (frames - 1)))

    beta_low = mix[...].reshape(rows, lanes)[:, :rows].astype(low)
    context = jnp.dot(beta_low, mem, preferred_element_type=wide).astype(low)
    seen[0] = context
    for r in range(4):
        cols = pl.ds(r * block, block)
        value = jnp.tanh(
            pre[:, cols] + jnp.dot(context, w[r, :, 5 * block :], preferred_element_type=wide)
        )
        pre[:, cols] = value
        pack[r, :, 5 * block :] = value.astype(low)
    logits = vocab_bias[...]
    for r in range(4):
        vocab_copies[r].wait()
        logits = logits + jnp.dot(pack[r, :, 5 * block :], v[r], preferred_element_type=wide)
    shifted = jnp.exp(logits - jnp.max(logits, axis=-1, keepdims=True))
    softmax = shifted / jnp.sum(shifted, axis=-1, keepdims=True)
    onehot = (labels[...] == lax.broadcasted_iota(jnp.int32, softmax.shape, 1)).astype(wide)
    grad_logits = ((softmax - onehot) * counted[...]).astype(low)
    seen[1] = grad_logits
    sums[5:6, :] = jnp.sum(grad_logits.astype(wide), axis=0, keepdims=True)
    sums[6:8, :] = jnp.zeros((2, sums.shape[1]), wide)

    grad_context = jnp.zeros((rows, memory.shape[1]), wide)
    for r in range(4):
        cols = pl.ds(r * block, block)
        value = pre[:, cols]
        grad_pre = (dot_nt(grad_logits, v[r]) * (1.0 - value * value)).astype(low)
        pack[r, :, 4 * block : 5 * block] = grad_pre
        sums[4:5, cols] = jnp.sum(grad_pre.astype(wide), axis=0, keepdims=True)
        grad_context = grad_context + dot_nt(grad_pre, w[r, :, 5 * block :])
    upper = grad_context.astype(low)
    lower = (grad_context - upper.astype(wide)).astype(low)
    grad_memory[...] = dot_tn(beta_low, upper) + dot_tn(beta_low, lower)
    cross = dot_nt(upper, mem) + dot_nt(lower, mem)
    if rows < lanes:
        cross = jnp.concatenate([cross, jnp.zeros((rows, lanes - rows), wide)], axis=1)
    mix[...] = split(cross)

    def unattend(k, later):
        i = frames - 1 - k
        base = i * frames
        cross_row = mix[i]
        grad_beta = [
            jnp.broadcast_to(
                jnp.sum(
                    jnp.where(diagonal == group * j, cross_row, 0.0), axis=-1, keepdims=True
                ),
                (group, lanes),
            )
            for j in range(frames)
        ]
        weight = [scaled[base + j] for j in range(frames)]
        share = [ratio[base + j] for j in range(frames)]
        direct, from_window, grad_weight = [], [], []
        for j in range(frames):
            grad_ratio = grad_beta[j] * weight[j]
            if j:
                grad_ratio = grad_ratio + grad_beta[j - 1] * weight[j - 1]
            pull = grad_ratio / window[base + j]
            direct.append(pull)
            from_window.append(jnp.where(valid[j], -pull * share[j], 0.0))
            grad_weight.append(
                grad_beta[j] * (share[j] + (share[j + 1] if j + 1 < frames else zeros))
            )
        top = jnp.full((group, lanes), -1e30, wide)
        for j in range(frames):
            top = jnp.maximum(top, jnp.where(valid[j], span[base + j], -1e30))
        total, ties, at_top, through = zeros, zeros, [], []
        for j in range(frames):
            pulled = grad_weight[j] + from_window[j]
            if j + 1 < frames:
                pulled = pulled + from_window[j + 1]
            pulled = weight[j] * pulled
            through.append(pulled)
            total = total + pulled
            hit = jnp.where(span[base + j] == top, live[j], 0.0)
            at_top.append(hit)
            ties = ties + hit
        back = total / ties
        for j in range(frames):
            span[base + j] = through[j] - at_top[j] * back
        grad_queue = zeros
        now = [None] * frames
        for j in reversed(range(frames)):
            prob = keep[base + j]
            grad_alpha = direct[j] + later[j]
            mono[base + j] = queue[base + j] * (grad_alpha - grad_queue) * prob * (1.0 - prob)
            grad_queue = prob * grad_alpha + (1.0 - prob) * grad_queue
            now[j] = grad_queue
        return tuple(now)

    lax.fori_loop(0, frames, unattend, tuple([zeros] * frames))

    def energy_back(queries, keys, energy, bias_row, vec_row):
        def one_chunk(c, carried):
            at = pl.ds(pl.multiple_of(c * lanes, lanes), lanes)
            weight = jnp.broadcast_to(vectors[vec_row : vec_row + 1, at], (group, lanes))

            def one(i, carry):
                grad_keys, vec_total, bias_total = carry
                query = queries[i, :, at]
                grad_query = zeros
                new_keys = []
                for j in range(frames):
                    squash = jnp.tanh(query + keys[j, :, at])
                    grad = energy[i * frames + j]
                    scaled_squash = grad * squash
                    vec_total = vec_total + scaled_squash
                    inner = grad - scaled_squash * squash
                    grad_query = grad_query + inner
                    new_keys.append(grad_keys[j] + inner)
                queries[i, :, at] = grad_query * weight
                return (tuple(new_keys), vec_total, bias_total + grad_query)

            grad_keys, vec_total, bias_total = lax.fori_loop(
                0, frames, one, (tuple([zeros] * frames), zeros, zeros)
            )
            for j in range(frames):
                keys[j, :, at] = grad_keys[j] * weight
            sums[bias_row : bias_row + 1, at] = jnp.sum(bias_total * weight, axis=0, keepdims=True)
            sums[vec_row : vec_row + 1, at] = jnp.sum(vec_total, axis=0, keepdims=True)
            return carried

        lax.fori_loop(0, chunks, one_chunk, 0)

    energy_back(mq, mk, mono, 0, 1)
    energy_back(sq, sk, span, 2, 3)

    total_memory = grad_memory[...]
    total_decoded = jnp.zeros_like(total_memory)
    for r in range(4):
        cols = pl.ds(r * block, block)
        for n, source in enumerate((mk, sk, mq, sq)):
            pack[r, :, n * block : (n + 1) * block] = (
                source[:, :, cols].reshape(rows, block).astype(low)
            )
        total_memory = total_memory + dot_nt(pack[r, :, : 2 * block], w[r, :, : 2 * block])
        total_decoded = total_decoded + dot_nt(
            pack[r, :, 2 * block : 5 * block], w[r, :, 2 * block : 5 * block]
        )
    grad_memory[...] = total_memory
    grad_decoded[...] = total_decoded


def run_attend(
    places, memory, decoded, smalls, vocab, vectors, vocab_bias, noise, lengths, labels, counted,
    frames,
):
    rows, width = memory.shape
    group = rows // frames
    full = vectors.shape[1]
    vocab_width = vocab[0].shape[1]
    cell = (frames * frames, group, 128)
    count = len(smalls[0])
    return pl.pallas_call(
        functools.partial(attend_kernel, count),
        out_shape=(
            jax.ShapeDtypeStruct((rows, width), wide),
            jax.ShapeDtypeStruct((rows, width), wide),
            jax.ShapeDtypeStruct((4, rows, full // 4 * 6), low),
            jax.ShapeDtypeStruct((2, rows, vocab_width), low),
            jax.ShapeDtypeStruct((8, full), wide),
        ),
        in_specs=[in_smem] + [in_vmem] * 8 + [in_place] * (4 * count + 4),
        out_specs=[in_vmem] * 5,
        scratch_shapes=[
            pltpu.VMEM((4, width, full // 4 * 6), low),
            pltpu.VMEM((4,) + vocab[0].shape, low),
            pltpu.SemaphoreType.DMA((4, places.shape[0] - 1)),
            pltpu.SemaphoreType.DMA((4,)),
        ]
        + [pltpu.VMEM((frames, group, full), wide)] * 4
        + [pltpu.VMEM(cell, wide)] * 7
        + [pltpu.VMEM((frames, group, 128), wide), pltpu.VMEM((rows, full), wide)],
        compiler_params=pltpu.CompilerParams(vmem_limit_bytes=56 << 20),
        name="attend",
    )(
        places, memory, decoded, vectors, vocab_bias, noise, lengths, labels, counted,
        *sum(smalls, []), *vocab,
    )


def local(
    dp,
    block_input, norm_gain, lstm_in, lstm_rec, lstm_bias,
    mono_mem, mono_dec, mono_bias, mono_vec, span_mem, span_dec, span_bias, span_vec,
    out_weight, out_bias, vocab_weight, vocab_bias, noise, enc_lengths, label_lengths, labels,
):
    ring = Ring(dp)
    s, y = lax.axis_index("section"), lax.axis_index("mp")
    _, utts, frames, width = block_input.shape
    half, quarter = utts // 2, utts // 4
    rows = frames * quarter
    shard_rows, _, unit_half = lstm_in.shape[1:]
    wide_half = 4 * unit_half
    block = mono_mem.shape[1]
    vocab_size = vocab_weight.shape[1]
    vocab_pad = 4 * block

    in_shard = lstm_in[0].reshape(shard_rows, wide_half)
    rec_shard = lstm_rec[0].reshape(shard_rows, wide_half)
    bias_shard = lstm_bias[0].reshape(1, wide_half)

    def of_section(array):
        return jnp.where(s == y, array, across_cores(array))

    inputs = of_section(jnp.swapaxes(block_input[0], 0, 1))
    gain = of_section(norm_gain[0])
    inputs_own = lax.dynamic_slice_in_dim(inputs, s * half, half, axis=1)
    inputs_other = lax.dynamic_slice_in_dim(inputs, (1 - s) * half, half, axis=1)
    normed_own = normalize(inputs_own.astype(wide), gain)
    normed_own = normed_own.astype(low).reshape(frames * half, width)
    normed_other = normalize(inputs_other.astype(wide), gain)
    normed_other = normed_other.astype(low).reshape(frames * half, width)

    start = s * half + y * quarter
    noise_part = jnp.transpose(
        lax.dynamic_slice_in_dim(noise, start, quarter, axis=0), (1, 2, 0)
    ).reshape(frames * frames, quarter, 1)
    noise_part = jnp.broadcast_to(noise_part, (frames * frames, quarter, 128))
    length_part = lax.dynamic_slice_in_dim(enc_lengths, start, quarter, axis=0)
    length_part = jnp.broadcast_to(length_part[:, None], (quarter, 128))
    label_part = lax.dynamic_slice_in_dim(labels, start, quarter, axis=0).T.reshape(rows, 1)
    count_part = lax.dynamic_slice_in_dim(label_lengths, start, quarter, axis=0)
    counted = (jnp.arange(frames)[:, None] < count_part[None, :]).astype(wide).reshape(rows, 1)
    bias_row = jnp.pad(vocab_bias, (0, vocab_pad - vocab_size), constant_values=-1e30)[None]

    vector_own = jnp.stack([mono_bias, mono_vec, span_bias, span_vec, out_bias])
    vocab_own = jnp.pad(vocab_weight, ((0, 0), (0, vocab_pad - vocab_size)))
    ready = (noise_part, length_part, label_part, counted, bias_row, normed_own, normed_other)
    places, in_own, rec_own, small_own, small_chip = [], [], [], [], []
    small = jnp.concatenate(
        [mono_mem, span_mem, mono_dec, span_dec, out_weight[0], out_weight[1]], axis=1
    )
    if ring.short:
        flow, across, onward = Flow(), ring.across, ring.onward
        both = 2 * wide_half
        corner = jnp.pad(bias_shard.reshape(shard_rows, -1), ((0, 0), (0, 128 - 16)))
        corner = jnp.concatenate([in_shard, rec_shard, corner], axis=1)
        corner, vector_pair, small_far, small_next = flow.step(
            (corners, corner), (across_chips, vector_own), (across, small), (onward, small)
        )
        b_own = corner[:, both : both + 16].astype(wide).reshape(1, wide_half)
        vector_pair = jnp.concatenate([vector_own, vector_pair], axis=1)
        small_own = [jnp.concatenate([small, small_far], axis=1)]
        small_chip, small_core = [], []
        held = jnp.concatenate([corner[:, :both], small_next], axis=1)
        near, far, near_core, far_core = [], [], [], []
        for k in range(ring.outer):
            near.append(held)
            jobs = [(across, held), (across_chips, small_own[k])]
            if k < ring.outer - 1:
                jobs.append((onward, held[:, :both] if k == ring.outer - 2 else held))
            if k == 0:
                jobs.append((across_chips, vocab_own))
            results = flow.step(*jobs, also=ready if k == 1 else ())
            far.append(results[0])
            small_chip.append(results[1])
            if k == 0:
                vocab_chip = results[3]
            if k < ring.outer - 1:
                small_own.append(jnp.concatenate([held[:, both:], far[k][:, both:]], axis=1))
                held = results[2]
        for a, b in zip(near, far):
            near_core.append(across_cores(a))
            far_core.append(across_cores(b))
        small_core = [across_cores(a) for a in small_own]
        b_other = across_cores(b_own)
        vocab = [vocab_own, vocab_chip, across_cores(vocab_own), across_cores(vocab_chip)]
        vector_core = across_cores(vector_pair)
        in_own = [a for pair in zip(near, far) for a in pair]
        in_other = [a for pair in zip(near_core, far_core) for a in pair]
        rec_own, rec_other, rec_column = in_own, in_other, wide_half
        for k in range(ring.outer):
            places += [ring.back(k) * 2 + ring.x, ring.back(k) * 2 + 1 - ring.x]
    else:
        vocab_chip = across_chips(vocab_own)
        small, in_block, rec_block = [
            lax.all_gather(a, "dp", axis=0, tiled=True)
            for a in (small, corners(in_shard), corners(rec_shard))
        ]
        places, in_own, rec_own = [jnp.int32(0)], [in_block], [rec_block]
        small_own, small_chip = [small], [across_chips(small)]
        vocab = [vocab_own, vocab_chip, across_cores(vocab_own), across_cores(vocab_chip)]
        in_other, rec_other, rec_column = [across_cores(in_block)], [across_cores(rec_block)], 0
        small_core = [across_cores(small)]
        b_own = corners(bias_shard).astype(wide)
        b_other = across_cores(b_own)
        vector_pair = across_chips(vector_own)
        vector_pair = jnp.concatenate([vector_own, vector_pair], axis=1)
        vector_core = across_cores(vector_pair)
    vectors = jnp.concatenate([vector_pair, vector_core], axis=1)
    vectors = jnp.pad(vectors, ((0, 3), (0, 0)))
    places = jnp.stack([s] + places).astype(jnp.int32)
    places = tie(places, vectors, *vocab, *ready, *small_chip[:-1], *small_core)

    quarters, before, gates, cells = run_forward(
        places, normed_own, b_own, b_other, in_own, in_other, rec_own, rec_other, frames,
        rec_column,
    )

    kept = lax.dynamic_index_in_dim(quarters, y, axis=0, keepdims=False)
    given = lax.dynamic_index_in_dim(quarters, 1 - y, axis=0, keepdims=False)
    taken = across_chips(given)
    memory = jnp.where(y == 0, kept, taken).reshape(rows, width)
    decoded = jnp.where(y == 0, taken, kept).reshape(rows, width)
    small_chip[-1] = tie(small_chip[-1], kept)
    small_both = [across_cores(part) for part in small_chip]
    smalls = [small_own, small_chip, small_core, small_both]
    grad_memory, grad_decoded, pack, seen, sums = run_attend(
        places, memory, decoded, smalls, vocab, vectors, bias_row, noise_part, length_part,
        label_part, counted, frames,
    )
    kept_far = across_chips(tie(kept, taken))
    before = before.reshape(frames * half, width)
    before_peer = across_cores(tie(before, taken))

    grad_kept = jnp.where(y == 0, grad_memory, grad_decoded)
    grad_given = jnp.where(y == 0, grad_decoded, grad_memory).astype(low)
    grad_taken = across_chips(grad_given)
    outside = jnp.stack(
        [jnp.where(y == 0, grad_kept, grad_taken), jnp.where(y == 0, grad_taken, grad_kept)]
    ).reshape(2, frames, quarter, width)
    pack_core = across_cores(pack[2:4])
    pack_out = jnp.stack([pack[1], pack_core[1]])
    memory_next = jnp.where(y == 0, given, kept_far).reshape(rows, width)
    decoded_next = jnp.where(y == 0, kept_far, given).reshape(rows, width)
    states = jnp.stack([memory, memory_next, decoded, decoded_next])
    states_core = across_cores(states)
    blocks = sums[:5].reshape(5, 4, block)
    vector_pair = blocks[:, :2] + across_cores(blocks[:, 2:])
    bias_pair = sums[5] + across_cores(sums[5])
    vector_out = jnp.concatenate([vector_pair[:, 1].reshape(-1), bias_pair])
    vector_count = vector_out.shape[0] // (2 * rows)
    places_back, pack_out, states_core = lax.optimization_barrier(
        (places, pack_out, states_core, outside, before_peer)
    )[:3]
    middle = frames * 3 // 8
    dz_late, turned, dh, dc = run_late(
        places_back, outside, gates, cells, rec_own, rec_other, rec_column, middle
    )
    pack_far = across_chips(pack_out)
    seen_out = jnp.concatenate(
        [seen, halves(vector_out, 2 * rows).reshape(2, rows, -1)], axis=2
    )
    seen_far = across_chips(tie(seen_out, pack_out))
    pack_all = jnp.concatenate([pack[0], pack_core[0], pack_far[0], pack_far[1]], axis=0)
    memory_all, decoded_all = [
        jnp.concatenate([states[n], states_core[n], states[n + 1], states_core[n + 1]], axis=0)
        for n in (0, 2)
    ]
    energy_total = [
        dot_tn(memory_all, pack_all[:, : 2 * block]).astype(low),
        dot_tn(decoded_all, pack_all[:, 2 * block : 4 * block]).astype(low),
    ]
    grad_pre = pack_all[:, 4 * block : 5 * block]
    decoded_total = dot_tn(decoded_all, grad_pre).astype(low)
    dh, *energy_total, decoded_total = lax.optimization_barrier((dh, *energy_total, decoded_total))
    dz_early = run_early(outside, gates, cells, dh, dc, turned, middle)

    def rows_of(part, at):
        part = lax.dynamic_index_in_dim(part, at, axis=0, keepdims=False)
        return part.reshape(-1, wide_half)

    dz_kept = jnp.concatenate([rows_of(dz_early, s), rows_of(dz_late, s)], axis=0)
    dz_given = jnp.concatenate([rows_of(dz_early, 1 - s), rows_of(dz_late, 1 - s)], axis=0)
    dz_all = jnp.concatenate([dz_kept, across_cores(dz_given)], axis=0)
    before_all = jnp.concatenate([before, before_peer], axis=0)
    normed_all = jnp.concatenate([normed_own, normed_other], axis=0)
    rec_total = dot_tn(before_all, dz_all).astype(low)
    in_total = dot_tn(normed_all, dz_all).astype(low)

    vector_far = joined(seen_far[:, :, seen.shape[2] :].reshape(2 * rows, -1), vector_count)
    vector_far = vector_far.reshape(-1)
    seen_far = seen_far[:, :, : seen.shape[2]]
    seen_pair = jnp.concatenate([seen, seen_far], axis=0)
    seen_core = across_cores(seen_pair)

    seen_all = [
        jnp.concatenate([seen_pair[n], seen_core[n], seen_pair[2 + n], seen_core[2 + n]], axis=0)
        for n in range(2)
    ]
    output_total = [
        decoded_total,
        dot_tn(seen_all[0], grad_pre).astype(low),
        dot_tn(seen_all[1], pack_all[:, 5 * block :]).astype(low),
    ]

    def to_other_chip(section):
        return lax.ppermute(section, ("section", "mp"), [(0, 1), (3, 2)])

    def input_back(dz_kept):
        grad_inputs, grad_gain = run_input(
            places, inputs_own.reshape(frames * half, width), gain[None], dz_kept, dz_given,
            in_own, in_other,
        )
        grad_inputs = jnp.swapaxes(grad_inputs.reshape(frames, half, width), 0, 1)
        grad_peer = across_cores(grad_inputs)
        section = jnp.concatenate(
            [
                jnp.where(s == 0, grad_inputs, grad_peer),
                jnp.where(s == 0, grad_peer, grad_inputs),
            ],
            axis=0,
        )
        grad_gain = grad_gain.reshape(width)
        gain_sum = grad_gain + across_cores(grad_gain)
        flat = jnp.concatenate(
            [
                vector_pair[:, 0].reshape(-1) + vector_far[: 5 * block],
                bias_pair + vector_far[5 * block :],
                jnp.sum(dz_all.astype(wide), axis=0),
                gain_sum,
            ]
        )
        return section, jnp.pad(flat, (0, -flat.shape[0] % (2 * shard_rows)))

    if ring.short:
        r, x = shard_rows, ring.x
        columns = 3 * block
        flow, across, onward = Flow(), ring.across, ring.onward
        chain = [rec_total, in_total] + energy_total

        def theirs(k):
            return ring.part(chain, ring.back(k) * 2 + 1 - x, r)

        def total(k, arrived, passed):
            value = ring.part(chain, ring.back(k) * 2 + x, r).astype(wide)
            value = value + arrived.astype(wide)
            return value if passed is None else value + passed.astype(wide)

        def output_part(k):
            return ring.part(output_total, ring.back(k), 2 * r)

        def output_sum(k, arrived):
            return output_part(k).astype(wide) + arrived.astype(wide)

        arrived, out = flow.step((across, theirs(1)), (onward, output_part(1)))
        grad_section, flat = input_back(tie(dz_kept, arrived))
        out = onward(output_sum(2, out).astype(low))
        value = total(1, arrived, None).astype(low)
        passed, arrived, out, grad_far = flow.step(
            (onward, value), (across, theirs(2)), (onward, output_sum(3, out).astype(low)),
            (to_other_chip, grad_section), also=(out,),
        )
        out = output_sum(4, out)
        value = total(2, arrived, passed).astype(low)
        passed, arrived, out_far = flow.step(
            (onward, value), (across, theirs(3)), (across, cut(out, 1 - x, r).astype(low))
        )
        output_grad = cut(out, x, r) + out_far.astype(wide)
        flat_width = flat.shape[0] // r
        shard = jnp.concatenate(
            [output_grad[:, 2 * block :].astype(low), halves(flat, r)], axis=1
        )
        value = total(3, arrived, passed).astype(low)
        passed, arrived, shard_far = flow.step(
            (onward, value), (across, theirs(4)), (across, shard)
        )
        flat = flat + joined(shard_far[:, block:], flat_width).reshape(-1)
        shard = jnp.concatenate([shard[:, :block], shard_far[:, :block], halves(flat, r)], axis=1)
        chain_grad = total(4, arrived, passed)
        moved = chain_grad[:, : 2 * wide_half].astype(low)
        moved, next_one, next_three = flow.step(
            (corners, moved), (onward, shard), (ring.astern, shard)
        )
        shards = {0: shard, 1: next_one, 3: next_three, 2: onward(next_one)}
        vocab_grad = jnp.zeros((vocab_pad, block), low)
        flat = 0.0
        for k, held in shards.items():
            flat = flat + joined(held[:, 2 * block :], flat_width).reshape(-1)
            for n, at in enumerate((x, 1 - x)):
                vocab_grad = lax.dynamic_update_slice(
                    vocab_grad,
                    held[:, n * block : (n + 1) * block],
                    ((ring.back(k) * 2 + at) * r, 0),
                )
        energy_grad = chain_grad[:, 2 * wide_half :]
    else:
        grad_section, flat = input_back(dz_kept)
        grad_far = to_other_chip(grad_section)

        def scatter(total):
            return lax.psum_scatter(total, "dp", scatter_dimension=0, tiled=True).astype(wide)

        moved = jnp.concatenate([scatter(rec_total), scatter(in_total)], axis=1)
        moved = corners(moved.astype(low))
        energy_grad = jnp.concatenate([scatter(a) for a in energy_total], axis=1)
        output_grad = jnp.concatenate([scatter(a) for a in output_total], axis=1)
        flat = lax.psum(flat, "dp")
        vocab_grad = lax.all_gather(
            output_grad[:, 2 * block :].astype(low), "dp", axis=0, tiled=True
        )

    input_grad = jnp.where(s == y, grad_section, grad_far)
    vocab_grad = vocab_grad.T[:, :vocab_size].astype(wide)
    ends = [5 * block, 5 * block + vocab_pad, 5 * block + vocab_pad + wide_half + width]
    vector_sum = flat[: ends[0]].reshape(5, block)
    bias_sum = flat[ends[0] : ends[0] + vocab_size]
    sides = corners(flat[ends[1] : ends[2]])
    lstm_bias_sum = sides[:wide_half].reshape(1, 4, unit_half)
    gain_sum = sides[wide_half:][None]
    rec_grad = moved[:, :wide_half].astype(wide).reshape(1, shard_rows, 4, unit_half)
    in_grad = moved[:, wide_half:].astype(wide).reshape(1, shard_rows, 4, unit_half)
    mono_mem_grad, span_mem_grad, mono_dec_grad, span_dec_grad = [
        energy_grad[:, n * block : (n + 1) * block] for n in range(4)
    ]
    return (
        input_grad[None],
        gain_sum,
        in_grad,
        rec_grad,
        lstm_bias_sum,
        mono_mem_grad,
        mono_dec_grad,
        vector_sum[0],
        vector_sum[1],
        span_mem_grad,
        span_dec_grad,
        vector_sum[2],
        vector_sum[3],
        jnp.stack([output_grad[:, :block], output_grad[:, block : 2 * block]]),
        vector_sum[4],
        vocab_grad,
        bias_sum,
    )


def solution(mesh):
    both = ("section", "mp")
    in_specs = (
        P("section", "dp", None, None),
        P("section", None),
        P("section", "dp", None, "mp"),
        P("section", "dp", None, "mp"),
        P("section", None, "mp"),
        P("dp", both),
        P("dp", both),
        P(both),
        P(both),
        P("dp", both),
        P("dp", both),
        P(both),
        P(both),
        P(None, "dp", both),
        P(both),
        P(both, None),
        P(),
        P("dp", None, None),
        P("dp"),
        P("dp"),
        P("dp", None),
    )
    out_specs = (
        P("section", "dp", None, None),
        P("section", None),
        P("section", "dp", None, "mp"),
        P("section", "dp", None, "mp"),
        P("section", None, "mp"),
        P("dp", both),
        P("dp", both),
        P(both),
        P(both),
        P("dp", both),
        P("dp", both),
        P(both),
        P(both),
        P(None, "dp", both),
        P(both),
        P(both, None),
        P(),
    )
    dp = mesh.shape["dp"]

    def step(*arrays):
        return local(dp, *arrays)

    return jax.shard_map(step, mesh=mesh, in_specs=in_specs, out_specs=out_specs, check_vma=False)
```

```python
import functools

import jax
import jax.numpy as jnp
from jax import lax
from jax.experimental import pallas as pl
from jax.experimental.pallas import tpu as pltpu
from jax.sharding import PartitionSpec as P

epsilon = 1e-05
offset = -4.0
wide = jnp.float32
low = jnp.bfloat16
in_vmem = pl.BlockSpec(memory_space=pltpu.VMEM)
in_smem = pl.BlockSpec(memory_space=pltpu.SMEM)
in_place = pl.BlockSpec(memory_space=pl.ANY)
core_swap = [(0, 1), (1, 0)]
corner_swap = [(0, 0), (1, 2), (2, 1), (3, 3)]


def normalize(inputs, gain_row):
    average = jnp.mean(inputs, axis=-1, keepdims=True)
    centred = inputs - average
    spread = jnp.mean(centred * centred, axis=-1, keepdims=True)
    return centred * lax.rsqrt(spread + epsilon) * gain_row


def across_cores(array):
    return lax.ppermute(array, "section", core_swap)


def across_chips(array):
    return lax.ppermute(array, "mp", core_swap)


def corners(array):
    return lax.ppermute(array, ("section", "mp"), corner_swap)


def tie(value, *others):
    return lax.optimization_barrier((value,) + others)[0]


def cut(array, block, rows):
    return lax.dynamic_slice_in_dim(array, block * rows, rows, axis=0)


class Flow:
    def __init__(self):
        self.landed = ()

    def step(self, *jobs, also=()):
        operands = tuple(operand for _, operand in jobs)
        operands = lax.optimization_barrier(operands + self.landed + tuple(also))[: len(jobs)]
        results = [send(operand) for (send, _), operand in zip(jobs, operands)]
        self.landed = tuple(results)
        return results


class Ring:
    def __init__(self, dp):
        self.dp = dp
        self.outer = dp // 2
        self.short = dp % 2 == 0 and self.outer == 4
        pairs = [(z, x) for z in range(self.outer) for x in range(2)]
        self.pair = [(2 * z + x, 2 * z + 1 - x) for z, x in pairs]
        self.ring = [(2 * z + x, 2 * ((z + 1) % self.outer) + x) for z, x in pairs]
        self.turn = [(b, a) for a, b in self.ring]
        place = lax.axis_index("dp")
        self.z, self.x = place // 2, place % 2

    def across(self, array):
        return lax.ppermute(array, "dp", self.pair)

    def onward(self, array):
        return lax.ppermute(array, "dp", self.ring)

    def astern(self, array):
        return lax.ppermute(array, "dp", self.turn)

    def back(self, k):
        return lax.rem(self.z - k + self.outer, self.outer)

    def part(self, group, block, rows):
        return jnp.concatenate([cut(a, block, rows) for a in group], axis=1)


def halves(array, height):
    array = array.reshape(height, -1)
    upper = array.astype(low)
    lower = (array - upper.astype(wide)).astype(low)
    return jnp.pad(
        jnp.concatenate([upper, lower], axis=1), ((0, 0), (0, -2 * array.shape[1] % 128))
    )


def joined(array, count):
    return array[:, :count].astype(wide) + array[:, count : 2 * count].astype(wide)


def sigmoid(x):
    return 0.5 * jnp.tanh(0.5 * x) + 0.5


def fetch(blocks, places, side_blocks, target, sems, first=0, column=0):
    wide_half = target.shape[1] // 2
    columns = pl.ds(pl.multiple_of(side_blocks * wide_half, wide_half), wide_half)
    copies = []
    for k, block in enumerate(blocks):
        height = block.shape[0]
        span = pl.ds(pl.multiple_of(places[2 + k] * height, height), height)
        copies.append(
            pltpu.make_async_copy(
                block.at[:, column : column + wide_half],
                target.at[span, columns],
                sems.at[first + k],
            )
        )
    return copies


def forward_kernel(count, column, places, normed, b_own, b_other, *refs):
    in_own, in_other, w_own, w_other = [refs[n * count : (n + 1) * count] for n in range(4)]
    kept, given, before, gates, cells, wi, w, b, state, cell, sems = refs[4 * count :]
    steps, rows, wide_full = gates.shape
    wide_half = wide_full // 2
    unit_half = wide_half // 4
    chunk = min(256, unit_half)
    s = places[0]
    copies = fetch(in_own, places, s, wi, sems) + fetch(in_other, places, 1 - s, wi, sems, count)
    later = fetch(w_own, places, s, w, sems, 2 * count, column)
    later += fetch(w_other, places, 1 - s, w, sems, 3 * count, column)
    for copy in copies + later:
        copy.start()
    for source, at in ((b_own, s), (b_other, 1 - s)):
        b[:, pl.ds(pl.multiple_of(at * wide_half, wide_half), wide_half)] = source[...]
    state[...] = jnp.zeros_like(state)
    cell[...] = jnp.zeros_like(cell)
    for copy in copies:
        copy.wait()

    def project(g, carried):
        cols = pl.ds(pl.multiple_of(g * unit_half, unit_half), unit_half)
        value = jnp.dot(normed[...], wi[:, cols], preferred_element_type=wide) + b[:, cols]
        gates[:, :, cols] = value.reshape(steps, rows, unit_half)
        return carried

    lax.fori_loop(0, 8, project, 0)
    for copy in later:
        copy.wait()
    eighth = rows // 2
    first_chip = places[1] == 0

    def advance(t, carried):
        hidden = state[...]
        before[t] = hidden
        for at in range(0, 2 * unit_half, chunk):
            half, inside = at // unit_half, at % unit_half
            acts = []
            for g in range(4):
                cols = pl.ds(half * wide_half + g * unit_half + inside, chunk)
                value = gates[t, :, cols] + jnp.dot(
                    hidden, w[:, cols], preferred_element_type=wide
                )
                value = jnp.tanh(value) if g == 2 else sigmoid(value)
                gates[t, :, cols] = value
                acts.append(value)
            units = pl.ds(at, chunk)
            new_cell = acts[1] * cell[:, units] + acts[0] * acts[2]
            cell[:, units] = new_cell
            cells[t, :, units] = new_cell
            new_hidden = acts[3] * jnp.tanh(new_cell)
            state[:, units] = new_hidden.astype(low)
            upper, lower = new_hidden[:eighth], new_hidden[eighth:]
            kept[t, :, units] = jnp.where(first_chip, upper, lower).astype(low)
            given[t, :, units] = jnp.where(first_chip, lower, upper).astype(low)
        return carried

    lax.fori_loop(0, steps, advance, 0)


def run_forward(places, normed, b_own, b_other, in_own, in_other, w_own, w_other, steps, column):
    rows = normed.shape[0] // steps
    units = normed.shape[1]
    wide_half = b_own.shape[1]
    count = len(w_own)
    return pl.pallas_call(
        functools.partial(forward_kernel, count, column),
        out_shape=(
            jax.ShapeDtypeStruct((steps, rows // 2, units), low),
            jax.ShapeDtypeStruct((steps, rows // 2, units), low),
            jax.ShapeDtypeStruct((steps, rows, units), low),
            jax.ShapeDtypeStruct((steps, rows, 2 * wide_half), wide),
            jax.ShapeDtypeStruct((steps, rows, units), wide),
        ),
        in_specs=[in_smem] + [in_vmem] * 3 + [in_place] * (4 * count),
        out_specs=[in_vmem] * 5,
        scratch_shapes=[
            pltpu.VMEM((units, 2 * wide_half), low),
            pltpu.VMEM((units, 2 * wide_half), low),
            pltpu.VMEM((1, 2 * wide_half), wide),
            pltpu.VMEM((rows, units), low),
            pltpu.VMEM((rows, units), wide),
            pltpu.SemaphoreType.DMA((4 * count,)),
        ],
        compiler_params=pltpu.CompilerParams(vmem_limit_bytes=56 << 20),
        name="recur_forward",
    )(places, normed, b_own, b_other, *in_own, *in_other, *w_own, *w_other)


def backward_kernel(count, column, places, kept, taken, gates, cells, *refs):
    w_own, w_other = refs[:count], refs[count : 2 * count]
    dz, stage, w, dh, dc, sems = refs[2 * count :]
    steps, rows, wide_full = gates.shape
    wide_half = wide_full // 2
    unit_half = wide_half // 4
    chunk = min(256, unit_half)
    s = places[0]
    first_chip = places[1] == 0
    jobs = []
    for n, (sources, at) in enumerate(((w_own, s), (w_other, 1 - s))):
        for k, block in enumerate(sources):
            slot = n * count + k
            copy = pltpu.make_async_copy(
                block.at[:, column : column + wide_half], stage.at[slot], sems.at[slot]
            )
            copy.start()
            jobs.append((copy, slot, at, places[2 + k] * block.shape[0]))
    dh[...] = jnp.zeros_like(dh)
    dc[...] = jnp.zeros_like(dc)
    height = w_own[0].shape[0]
    piece = min(height, 128)
    for copy, slot, at, first in jobs:
        copy.wait()

        def turn(g, carried, slot=slot, at=at, first=first):
            columns = pl.ds(pl.multiple_of(g * unit_half, unit_half), unit_half)
            span = pl.ds(pl.multiple_of(at * wide_half + g * unit_half, unit_half), unit_half)
            for low_row in range(0, height, piece):
                into = pl.ds(pl.multiple_of(first + low_row, piece), piece)
                w[span, into] = stage[slot, low_row : low_row + piece, columns].T
            return carried

        lax.fori_loop(0, 4, turn, 0)

    place_of = (s, 1 - s)

    def retreat(k, carried):
        t = steps - 1 - k
        earlier = jnp.maximum(t - 1, 0)
        live = jnp.where(t > 0, 1.0, 0.0).astype(wide)
        for at in range(0, 2 * unit_half, chunk):
            half, inside = at // unit_half, at % unit_half
            units = pl.ds(at, chunk)
            ours, theirs = kept[t, :, units], taken[t, :, units].astype(wide)
            grad = dh[:, units] + jnp.concatenate(
                [jnp.where(first_chip, ours, theirs), jnp.where(first_chip, theirs, ours)], axis=0
            )
            i, f, g, o = [
                gates[t, :, pl.ds(half * wide_half + n * unit_half + inside, chunk)]
                for n in range(4)
            ]
            squash = jnp.tanh(cells[t, :, units])
            total = dc[:, units] + grad * o * (1.0 - squash * squash)
            parts = (
                total * g * i * (1.0 - i),
                total * (cells[earlier, :, units] * live) * f * (1.0 - f),
                total * i * (1.0 - g * g),
                grad * squash * o * (1.0 - o),
            )
            for n, part in enumerate(parts):
                dz[place_of[half], t, :, pl.ds(n * unit_half + inside, chunk)] = part.astype(low)
            dc[:, units] = total * f
        upper, lower = dz[place_of[0], t], dz[place_of[1], t]
        for at in range(0, 2 * unit_half, chunk):
            units = pl.ds(at, chunk)
            dh[:, units] = jnp.dot(
                upper, w[:wide_half, units], preferred_element_type=wide
            ) + jnp.dot(lower, w[wide_half:, units], preferred_element_type=wide)
        return carried

    lax.fori_loop(0, steps, retreat, 0)


def run_backward(places, kept, taken, gates, cells, w_own, w_other, column):
    steps, rows, wide_full = gates.shape
    units = cells.shape[2]
    count = len(w_own)
    return pl.pallas_call(
        functools.partial(backward_kernel, count, column),
        out_shape=jax.ShapeDtypeStruct((2, steps, rows, wide_full // 2), low),
        in_specs=[in_smem] + [in_vmem] * 4 + [in_place] * (2 * count),
        out_specs=in_vmem,
        scratch_shapes=[
            pltpu.VMEM((2 * count, units // count, wide_full // 2), low),
            pltpu.VMEM((wide_full, units), low),
            pltpu.VMEM((rows, units), wide),
            pltpu.VMEM((rows, units), wide),
            pltpu.SemaphoreType.DMA((2 * count,)),
        ],
        compiler_params=pltpu.CompilerParams(vmem_limit_bytes=56 << 20),
        name="recur_backward",
    )(places, kept, taken, gates, cells, *w_own, *w_other)


def input_kernel(count, places, inputs, gain, dz, dz_given, *refs):
    in_own, in_other = refs[:count], refs[count : 2 * count]
    grad_inputs, grad_gain, wi, sems = refs[2 * count :]
    s = places[0]
    copies = fetch(in_own, places, s, wi, sems) + fetch(in_other, places, 1 - s, wi, sems, count)
    for copy in copies:
        copy.start()
    x = inputs[...].astype(wide)
    centred = x - jnp.mean(x, axis=-1, keepdims=True)
    scale = lax.rsqrt(jnp.mean(centred * centred, axis=-1, keepdims=True) + epsilon)
    shape = centred * scale
    for copy in copies:
        copy.wait()
    wide_half = wi.shape[1] // 2
    own = pl.ds(pl.multiple_of(s * wide_half, wide_half), wide_half)
    other = pl.ds(pl.multiple_of((1 - s) * wide_half, wide_half), wide_half)
    grad = dot_nt(dz[...], wi[:, own]) + dot_nt(dz_given[...], wi[:, other])
    grad_gain[...] = jnp.sum(grad * shape, axis=0, keepdims=True)
    pulled = grad * gain[...]
    grad_inputs[...] = scale * (
        pulled
        - jnp.mean(pulled, axis=-1, keepdims=True)
        - shape * jnp.mean(pulled * shape, axis=-1, keepdims=True)
    )


def run_input(places, inputs, gain, dz, dz_given, in_own, in_other):
    count = len(in_own)
    rows, width = inputs.shape
    return pl.pallas_call(
        functools.partial(input_kernel, count),
        out_shape=(
            jax.ShapeDtypeStruct((rows, width), wide),
            jax.ShapeDtypeStruct((1, width), wide),
        ),
        in_specs=[in_smem] + [in_vmem] * 4 + [in_place] * (2 * count),
        out_specs=[in_vmem] * 2,
        scratch_shapes=[
            pltpu.VMEM((width, 2 * dz.shape[1]), low),
            pltpu.SemaphoreType.DMA((2 * count,)),
        ],
        compiler_params=pltpu.CompilerParams(vmem_limit_bytes=56 << 20),
        name="input_back",
    )(places, inputs, gain, dz, dz_given, *in_own, *in_other)


def dot_nt(a, b):
    return lax.dot_general(a, b, (((1,), (1,)), ((), ())), preferred_element_type=wide)


def dot_tn(a, b):
    return lax.dot_general(a, b, (((0,), (0,)), ((), ())), preferred_element_type=wide)


def attend_kernel(
    count, places, kept, taken, vectors, vocab_bias, noise, lengths, labels, counted, *refs
):
    small, vocab = refs[: 4 * count], refs[4 * count : 4 * count + 4]
    (
        grad_own, grad_given, pack, seen, sums,
        memory, decoded, grad_memory, w, v, sems, v_sems, mk, sk, mq, sq, mono, span, keep, queue, scaled, ratio, window, mix, pre,
    ) = refs[4 * count + 4 :]
    rows, _ = kept.shape
    frames, group, _ = mk.shape
    block = w.shape[2] // 6
    lanes = 128
    chunks = 4 * block // lanes
    copies = []
    for r in range(4):
        arrived = []
        for k in range(count):
            source = small[r * count + k]
            height = source.shape[0]
            for h in range(source.shape[1] // (6 * block)):
                to = pl.ds(pl.multiple_of(places[2 + len(arrived)] * height, height), height)
                arrived.append(
                    pltpu.make_async_copy(
                        source.at[:, 6 * block * h : 6 * block * (h + 1)],
                        w.at[r, to, :],
                        sems.at[r, len(arrived)],
                    )
                )
        copies.append(arrived)
    vocab_copies = [pltpu.make_async_copy(vocab[r], v.at[r], v_sems.at[r]) for r in range(4)]
    for copy in sum(copies, []) + vocab_copies:
        copy.start()

    first_chip = places[1] == 0

    @pl.when(first_chip)
    def _():
        memory[...] = kept[...]
        decoded[...] = taken[...]

    @pl.when(jnp.logical_not(first_chip))
    def _():
        memory[...] = taken[...]
        decoded[...] = kept[...]

    def split(value):
        return value.reshape(frames, group, value.shape[-1])

    mem, dec = memory[...], decoded[...]
    for r in range(4):
        for copy in copies[r]:
            copy.wait()
        cols = pl.ds(r * block, block)
        keys = jnp.dot(mem, w[r, :, : 2 * block], preferred_element_type=wide)
        queries = jnp.dot(dec, w[r, :, 2 * block : 5 * block], preferred_element_type=wide)
        mk[:, :, cols] = split(keys[:, :block])
        sk[:, :, cols] = split(keys[:, block:])
        mq[:, :, cols] = split(queries[:, :block] + vectors[0:1, cols])
        sq[:, :, cols] = split(queries[:, block : 2 * block] + vectors[2:3, cols])
        pre[:, cols] = queries[:, 2 * block :] + vectors[4:5, cols]

    def lane(c):
        return pl.ds(c * lanes, lanes)

    def spread(row, c):
        return jnp.broadcast_to(vectors[row : row + 1, lane(c)], (group, lanes))

    def energies(queries, keys, vec_row, energy):
        weights = [spread(vec_row, c) for c in range(chunks)]

        def one(i, carried):
            query = [queries[i, :, lane(c)] for c in range(chunks)]
            for j in range(frames):
                total = jnp.tanh(query[0] + keys[j, :, lane(0)]) * weights[0]
                for c in range(1, chunks):
                    total = total + jnp.tanh(query[c] + keys[j, :, lane(c)]) * weights[c]
                energy[i * frames + j] = jnp.broadcast_to(
                    jnp.sum(total, axis=-1, keepdims=True), (group, lanes)
                )
            return carried

        lax.fori_loop(0, frames, one, 0)

    energies(mq, mk, 1, mono)
    energies(sq, sk, 3, span)

    length = lengths[...]
    valid = [(length > j) for j in range(frames)]
    ones = jnp.ones((group, lanes), wide)
    zeros = jnp.zeros((group, lanes), wide)
    live = [jnp.where(valid[j], 1.0, 0.0).astype(wide) for j in range(frames)]
    diagonal = lax.broadcasted_iota(jnp.int32, (group, lanes), 1) - lax.broadcasted_iota(
        jnp.int32, (group, lanes), 0
    )

    def attend(i, previous):
        base = i * frames
        top = jnp.full((group, lanes), -1e30, wide)
        for j in range(frames):
            top = jnp.maximum(top, jnp.where(valid[j], span[base + j], -1e30))
        weight = [jnp.where(valid[j], jnp.exp(span[base + j] - top), 0.0) for j in range(frames)]
        current, ratios = [], []
        queued = previous[0]
        for j in range(frames):
            prob = sigmoid(mono[base + j] + offset + noise[base + j]) * live[j]
            keep[base + j] = prob
            queue[base + j] = queued
            alpha = prob * queued
            current.append(alpha)
            if j + 1 < frames:
                queued = (1.0 - prob) * queued + previous[j + 1]
            both = weight[j] + weight[j - 1] if j else weight[j]
            both = jnp.where(valid[j], both, 1.0)
            window[base + j] = both
            scaled[base + j] = weight[j]
            quotient = alpha / both
            ratio[base + j] = quotient
            ratios.append(quotient)
        row = zeros
        for j in range(frames):
            beta = weight[j] * (ratios[j] + (ratios[j + 1] if j + 1 < frames else zeros))
            row = jnp.where(diagonal == group * j, beta, row)
        mix[i] = row
        return tuple(current)

    lax.fori_loop(0, frames, attend, tuple([ones] + [zeros] * (frames - 1)))

    beta_low = mix[...].reshape(rows, lanes)[:, :rows].astype(low)
    context = jnp.dot(beta_low, mem, preferred_element_type=wide).astype(low)
    seen[0] = context
    for r in range(4):
        cols = pl.ds(r * block, block)
        value = jnp.tanh(
            pre[:, cols] + jnp.dot(context, w[r, :, 5 * block :], preferred_element_type=wide)
        )
        pre[:, cols] = value
        pack[r, :, 5 * block :] = value.astype(low)
    logits = vocab_bias[...]
    for r in range(4):
        vocab_copies[r].wait()
        logits = logits + jnp.dot(pack[r, :, 5 * block :], v[r], preferred_element_type=wide)
    shifted = jnp.exp(logits - jnp.max(logits, axis=-1, keepdims=True))
    softmax = shifted / jnp.sum(shifted, axis=-1, keepdims=True)
    onehot = (labels[...] == lax.broadcasted_iota(jnp.int32, softmax.shape, 1)).astype(wide)
    grad_logits = ((softmax - onehot) * counted[...]).astype(low)
    seen[1] = grad_logits
    sums[5:6, :] = jnp.sum(grad_logits.astype(wide), axis=0, keepdims=True)
    sums[6:8, :] = jnp.zeros((2, sums.shape[1]), wide)

    grad_context = jnp.zeros((rows, memory.shape[1]), wide)
    for r in range(4):
        cols = pl.ds(r * block, block)
        value = pre[:, cols]
        grad_pre = (dot_nt(grad_logits, v[r]) * (1.0 - value * value)).astype(low)
        pack[r, :, 4 * block : 5 * block] = grad_pre
        sums[4:5, cols] = jnp.sum(grad_pre.astype(wide), axis=0, keepdims=True)
        grad_context = grad_context + dot_nt(grad_pre, w[r, :, 5 * block :])
    upper = grad_context.astype(low)
    lower = (grad_context - upper.astype(wide)).astype(low)
    grad_memory[...] = dot_tn(beta_low, upper) + dot_tn(beta_low, lower)
    cross = dot_nt(upper, mem) + dot_nt(lower, mem)
    if rows < lanes:
        cross = jnp.concatenate([cross, jnp.zeros((rows, lanes - rows), wide)], axis=1)
    mix[...] = split(cross)

    def unattend(k, later):
        i = frames - 1 - k
        base = i * frames
        cross_row = mix[i]
        grad_beta = [
            jnp.broadcast_to(
                jnp.sum(
                    jnp.where(diagonal == group * j, cross_row, 0.0), axis=-1, keepdims=True
                ),
                (group, lanes),
            )
            for j in range(frames)
        ]
        weight = [scaled[base + j] for j in range(frames)]
        share = [ratio[base + j] for j in range(frames)]
        direct, from_window, grad_weight = [], [], []
        for j in range(frames):
            grad_ratio = grad_beta[j] * weight[j]
            if j:
                grad_ratio = grad_ratio + grad_beta[j - 1] * weight[j - 1]
            pull = grad_ratio / window[base + j]
            direct.append(pull)
            from_window.append(jnp.where(valid[j], -pull * share[j], 0.0))
            grad_weight.append(
                grad_beta[j] * (share[j] + (share[j + 1] if j + 1 < frames else zeros))
            )
        top = jnp.full((group, lanes), -1e30, wide)
        for j in range(frames):
            top = jnp.maximum(top, jnp.where(valid[j], span[base + j], -1e30))
        total, ties, at_top, through = zeros, zeros, [], []
        for j in range(frames):
            pulled = grad_weight[j] + from_window[j]
            if j + 1 < frames:
                pulled = pulled + from_window[j + 1]
            pulled = weight[j] * pulled
            through.append(pulled)
            total = total + pulled
            hit = jnp.where(span[base + j] == top, live[j], 0.0)
            at_top.append(hit)
            ties = ties + hit
        back = total / ties
        for j in range(frames):
            span[base + j] = through[j] - at_top[j] * back
        grad_queue = zeros
        now = [None] * frames
        for j in reversed(range(frames)):
            prob = keep[base + j]
            grad_alpha = direct[j] + later[j]
            mono[base + j] = queue[base + j] * (grad_alpha - grad_queue) * prob * (1.0 - prob)
            grad_queue = prob * grad_alpha + (1.0 - prob) * grad_queue
            now[j] = grad_queue
        return tuple(now)

    lax.fori_loop(0, frames, unattend, tuple([zeros] * frames))

    def energy_back(queries, keys, energy, bias_row, vec_row):
        def one_chunk(c, carried):
            at = pl.ds(pl.multiple_of(c * lanes, lanes), lanes)
            weight = jnp.broadcast_to(vectors[vec_row : vec_row + 1, at], (group, lanes))

            def one(i, carry):
                grad_keys, vec_total, bias_total = carry
                query = queries[i, :, at]
                grad_query = zeros
                new_keys = []
                for j in range(frames):
                    squash = jnp.tanh(query + keys[j, :, at])
                    grad = energy[i * frames + j]
                    scaled_squash = grad * squash
                    vec_total = vec_total + scaled_squash
                    inner = grad - scaled_squash * squash
                    grad_query = grad_query + inner
                    new_keys.append(grad_keys[j] + inner)
                queries[i, :, at] = grad_query * weight
                return (tuple(new_keys), vec_total, bias_total + grad_query)

            grad_keys, vec_total, bias_total = lax.fori_loop(
                0, frames, one, (tuple([zeros] * frames), zeros, zeros)
            )
            for j in range(frames):
                keys[j, :, at] = grad_keys[j] * weight
            sums[bias_row : bias_row + 1, at] = jnp.sum(bias_total * weight, axis=0, keepdims=True)
            sums[vec_row : vec_row + 1, at] = jnp.sum(vec_total, axis=0, keepdims=True)
            return carried

        lax.fori_loop(0, chunks, one_chunk, 0)

    energy_back(mq, mk, mono, 0, 1)
    energy_back(sq, sk, span, 2, 3)

    total_memory = grad_memory[...]
    total_decoded = jnp.zeros_like(total_memory)
    for r in range(4):
        cols = pl.ds(r * block, block)
        for n, source in enumerate((mk, sk, mq, sq)):
            pack[r, :, n * block : (n + 1) * block] = (
                source[:, :, cols].reshape(rows, block).astype(low)
            )
        total_memory = total_memory + dot_nt(pack[r, :, : 2 * block], w[r, :, : 2 * block])
        total_decoded = total_decoded + dot_nt(
            pack[r, :, 2 * block : 5 * block], w[r, :, 2 * block : 5 * block]
        )
    grad_own[...] = jnp.where(first_chip, total_memory, total_decoded)
    grad_given[...] = jnp.where(first_chip, total_decoded, total_memory).astype(low)


def run_attend(
    places, kept, taken, smalls, vocab, vectors, vocab_bias, noise, lengths, labels, counted,
    frames,
):
    rows, width = kept.shape
    group = rows // frames
    full = vectors.shape[1]
    vocab_width = vocab[0].shape[1]
    cell = (frames * frames, group, 128)
    count = len(smalls[0])
    return pl.pallas_call(
        functools.partial(attend_kernel, count),
        out_shape=(
            jax.ShapeDtypeStruct((rows, width), wide),
            jax.ShapeDtypeStruct((rows, width), low),
            jax.ShapeDtypeStruct((4, rows, full // 4 * 6), low),
            jax.ShapeDtypeStruct((2, rows, vocab_width), low),
            jax.ShapeDtypeStruct((8, full), wide),
        ),
        in_specs=[in_smem] + [in_vmem] * 8 + [in_place] * (4 * count + 4),
        out_specs=[in_vmem] * 5,
        scratch_shapes=[
            pltpu.VMEM((rows, width), low),
            pltpu.VMEM((rows, width), low),
            pltpu.VMEM((rows, width), wide),
            pltpu.VMEM((4, width, full // 4 * 6), low),
            pltpu.VMEM((4,) + vocab[0].shape, low),
            pltpu.SemaphoreType.DMA((4, places.shape[0] - 2)),
            pltpu.SemaphoreType.DMA((4,)),
        ]
        + [pltpu.VMEM((frames, group, full), wide)] * 4
        + [pltpu.VMEM(cell, wide)] * 7
        + [pltpu.VMEM((frames, group, 128), wide), pltpu.VMEM((rows, full), wide)],
        compiler_params=pltpu.CompilerParams(vmem_limit_bytes=56 << 20),
        name="attend",
    )(
        places, kept, taken, vectors, vocab_bias, noise, lengths, labels, counted,
        *sum(smalls, []), *vocab,
    )


def local(
    dp,
    block_input, norm_gain, lstm_in, lstm_rec, lstm_bias,
    mono_mem, mono_dec, mono_bias, mono_vec, span_mem, span_dec, span_bias, span_vec,
    out_weight, out_bias, vocab_weight, vocab_bias, noise, enc_lengths, label_lengths, labels,
):
    ring = Ring(dp)
    s, y = lax.axis_index("section"), lax.axis_index("mp")
    _, utts, frames, width = block_input.shape
    half, quarter = utts // 2, utts // 4
    rows = frames * quarter
    shard_rows, _, unit_half = lstm_in.shape[1:]
    wide_half = 4 * unit_half
    block = mono_mem.shape[1]
    vocab_size = vocab_weight.shape[1]
    vocab_pad = 4 * block

    in_shard = lstm_in[0].reshape(shard_rows, wide_half)
    rec_shard = lstm_rec[0].reshape(shard_rows, wide_half)
    bias_shard = lstm_bias[0].reshape(1, wide_half)

    def of_section(array):
        return jnp.where(s == y, array, across_cores(array))

    inputs = of_section(jnp.swapaxes(block_input[0], 0, 1))
    gain = of_section(norm_gain[0])
    inputs_own = lax.dynamic_slice_in_dim(inputs, s * half, half, axis=1)
    inputs_other = lax.dynamic_slice_in_dim(inputs, (1 - s) * half, half, axis=1)
    normed_own = normalize(inputs_own.astype(wide), gain)
    normed_own = normed_own.astype(low).reshape(frames * half, width)
    normed_other = normalize(inputs_other.astype(wide), gain)
    normed_other = normed_other.astype(low).reshape(frames * half, width)

    start = s * half + y * quarter
    noise_part = jnp.transpose(
        lax.dynamic_slice_in_dim(noise, start, quarter, axis=0), (1, 2, 0)
    ).reshape(frames * frames, quarter, 1)
    noise_part = jnp.broadcast_to(noise_part, (frames * frames, quarter, 128))
    length_part = lax.dynamic_slice_in_dim(enc_lengths, start, quarter, axis=0)
    length_part = jnp.broadcast_to(length_part[:, None], (quarter, 128))
    label_part = lax.dynamic_slice_in_dim(labels, start, quarter, axis=0).T.reshape(rows, 1)
    count_part = lax.dynamic_slice_in_dim(label_lengths, start, quarter, axis=0)
    counted = (jnp.arange(frames)[:, None] < count_part[None, :]).astype(wide).reshape(rows, 1)
    bias_row = jnp.pad(vocab_bias, (0, vocab_pad - vocab_size), constant_values=-1e30)[None]

    vector_own = jnp.stack([mono_bias, mono_vec, span_bias, span_vec, out_bias])
    vocab_own = jnp.pad(vocab_weight, ((0, 0), (0, vocab_pad - vocab_size)))
    ready = (noise_part, length_part, label_part, counted, bias_row, normed_own, normed_other)
    places, in_own, rec_own, small_own, small_chip = [], [], [], [], []
    small = jnp.concatenate(
        [
            tie(mono_mem, in_shard, rec_shard), span_mem, mono_dec, span_dec,
            out_weight[0], out_weight[1],
        ],
        axis=1,
    )
    if ring.short:
        flow, across, onward = Flow(), ring.across, ring.onward
        both = 2 * wide_half
        corner_in, corner_rec, b_own = flow.step(
            (corners, in_shard), (corners, rec_shard), (corners, bias_shard)
        )
        small_far, small_next = across(small), onward(small)
        flow.landed += (small_far, small_next)
        b_own = b_own.astype(wide)
        small_own = [jnp.concatenate([small, small_far], axis=1)]
        small_chip, small_core = [], []
        held = jnp.concatenate([corner_in, corner_rec, small_next], axis=1)
        near, far, near_core, far_core = [], [], [], []
        for k in range(ring.outer):
            near.append(held)
            jobs = [(across, held), (across_chips, small_own[k])]
            if k < ring.outer - 1:
                jobs.append((onward, held[:, :both] if k == ring.outer - 2 else held))
            if k == 0:
                jobs += [(across_chips, vocab_own), (across_chips, vector_own)]
            results = flow.step(*jobs, also=ready if k == 1 else ())
            far.append(results[0])
            small_chip.append(results[1])
            if k == 0:
                vocab_chip, vector_pair = results[3:]
                vector_pair = jnp.concatenate([vector_own, vector_pair], axis=1)
            if k < ring.outer - 1:
                small_own.append(jnp.concatenate([held[:, both:], far[k][:, both:]], axis=1))
                held = results[2]
        for a, b in zip(near, far):
            near_core.append(across_cores(a))
            far_core.append(across_cores(b))
        small_core = [across_cores(a) for a in small_own]
        b_last, vocab_last, chip_last, vector_last = lax.optimization_barrier(
            (b_own, vocab_own, vocab_chip, vector_pair, held)
        )[:4]
        b_other = across_cores(b_last)
        vocab = [vocab_own, vocab_chip, across_cores(vocab_last), across_cores(chip_last)]
        vector_core = across_cores(vector_last)
        in_own = [a for pair in zip(near, far) for a in pair]
        in_other = [a for pair in zip(near_core, far_core) for a in pair]
        rec_own, rec_other, rec_column = in_own, in_other, wide_half
        for k in range(ring.outer):
            places += [ring.back(k) * 2 + ring.x, ring.back(k) * 2 + 1 - ring.x]
    else:
        vocab_chip = across_chips(vocab_own)
        small, in_block, rec_block = [
            lax.all_gather(a, "dp", axis=0, tiled=True)
            for a in (small, corners(in_shard), corners(rec_shard))
        ]
        places, in_own, rec_own = [jnp.int32(0)], [in_block], [rec_block]
        small_own, small_chip = [small], [across_chips(small)]
        vocab = [vocab_own, vocab_chip, across_cores(vocab_own), across_cores(vocab_chip)]
        in_other, rec_other, rec_column = [across_cores(in_block)], [across_cores(rec_block)], 0
        small_core = [across_cores(small)]
        b_own = corners(bias_shard).astype(wide)
        b_other = across_cores(b_own)
        vector_pair = across_chips(vector_own)
        vector_pair = jnp.concatenate([vector_own, vector_pair], axis=1)
        vector_core = across_cores(vector_pair)
    vectors = jnp.concatenate([vector_pair, vector_core], axis=1)
    vectors = jnp.pad(vectors, ((0, 3), (0, 0)))
    places = jnp.stack([s, y] + places).astype(jnp.int32)
    places = tie(places, vectors, *vocab, *ready, *small_chip[:-1], *small_core)

    kept, given, before, gates, cells = run_forward(
        places, normed_own, b_own, b_other, in_own, in_other, rec_own, rec_other, frames,
        rec_column,
    )

    kept, given = kept.reshape(rows, width), given.reshape(rows, width)
    taken = across_chips(given)
    small_chip[-1] = tie(small_chip[-1], kept)
    small_both = [across_cores(part) for part in small_chip]
    smalls = [small_own, small_chip, small_core, small_both]
    grad_own, grad_given, pack, seen, sums = run_attend(
        places, kept, taken, smalls, vocab, vectors, bias_row, noise_part, length_part,
        label_part, counted, frames,
    )
    grad_taken = across_chips(grad_given)
    pack_core = across_cores(pack[2:4])
    pack_out = jnp.stack([pack[1], pack_core[1]])
    blocks = sums[:5].reshape(5, 4, block)
    vector_pair = blocks[:, :2] + across_cores(blocks[:, 2:])
    bias_pair = sums[5] + across_cores(sums[5])
    vector_out = jnp.concatenate([vector_pair[:, 1].reshape(-1), bias_pair])
    vector_count = vector_out.shape[0] // (3 * rows)
    seen_out = jnp.concatenate(
        [
            jnp.concatenate([seen, kept[None]], axis=0),
            halves(vector_out, 3 * rows).reshape(3, rows, -1),
        ],
        axis=2,
    )
    before = before.reshape(frames * half, width)
    before_peer = across_cores(tie(before, taken))
    states = jnp.stack([kept, taken])
    states_core = across_cores(tie(states, grad_given))
    places_back, pack_out, seen_out = lax.optimization_barrier(
        (places, pack_out, seen_out, grad_taken, before_peer, states_core)
    )[:3]
    dz = run_backward(
        places_back, grad_own.reshape(frames, quarter, width),
        grad_taken.reshape(frames, quarter, width), gates, cells, rec_own, rec_other, rec_column,
    )
    pack_far = across_chips(pack_out)
    seen_far = across_chips(tie(seen_out, pack_out))

    dz = dz.reshape(2, frames * half, wide_half)
    dz_kept, dz_given, pack_far, seen_far = lax.optimization_barrier(
        (dz[0], dz[1], pack_far, seen_far)
    )
    dz_all = jnp.concatenate([dz_kept, across_cores(dz_given)], axis=0)
    before_all = jnp.concatenate([before, before_peer], axis=0)
    normed_all = jnp.concatenate([normed_own, normed_other], axis=0)
    rec_total = dot_tn(before_all, dz_all).astype(low)
    in_total = dot_tn(normed_all, dz_all).astype(low)

    vector_far = joined(seen_far[:, :, width:].reshape(3 * rows, -1), vector_count).reshape(-1)
    chip_rows = jnp.concatenate(
        [seen, seen_far[:2, :, :width], jnp.stack([given, seen_far[2, :, :width]])], axis=0
    )
    core_rows = across_cores(chip_rows)
    section_all = jnp.concatenate([kept, states_core[0], chip_rows[4], core_rows[4]], axis=0)
    other_all = jnp.concatenate([taken, states_core[1], chip_rows[5], core_rows[5]], axis=0)
    memory_all = jnp.where(y == 0, section_all, other_all)
    decoded_all = jnp.where(y == 0, other_all, section_all)
    seen_all = [
        jnp.concatenate([chip_rows[n], core_rows[n], chip_rows[2 + n], core_rows[2 + n]], axis=0)
        for n in range(2)
    ]
    pack_all = jnp.concatenate([pack[0], pack_core[0], pack_far[0], pack_far[1]], axis=0)
    if ring.short:
        first_rec, first_in = [
            cut(a, ring.back(1) * 2 + 1 - ring.x, shard_rows) for a in (rec_total, in_total)
        ]
        pack_all = tie(pack_all, first_rec, first_in)
    energy_total = [
        dot_tn(memory_all, pack_all[:, : 2 * block]).astype(low),
        dot_tn(decoded_all, pack_all[:, 2 * block : 4 * block]).astype(low),
    ]
    grad_pre = pack_all[:, 4 * block : 5 * block]
    output_total = [
        dot_tn(decoded_all, grad_pre).astype(low),
        dot_tn(seen_all[0], grad_pre).astype(low),
        dot_tn(seen_all[1], pack_all[:, 5 * block :]).astype(low),
    ]

    sides_at = 5 * block + vocab_pad

    def to_other_chip(section):
        return lax.ppermute(section, ("section", "mp"), [(0, 1), (3, 2)])

    def input_back(dz_kept):
        grad_inputs, grad_gain = run_input(
            places, inputs_own.reshape(frames * half, width), gain[None], dz_kept, dz_given,
            in_own, in_other,
        )
        grad_inputs = jnp.swapaxes(grad_inputs.reshape(frames, half, width), 0, 1)
        grad_peer = across_cores(grad_inputs)
        section = jnp.concatenate(
            [
                jnp.where(s == 0, grad_inputs, grad_peer),
                jnp.where(s == 0, grad_peer, grad_inputs),
            ],
            axis=0,
        )
        grad_gain = grad_gain.reshape(width)
        gain_sum = grad_gain + across_cores(grad_gain)
        flat = jnp.concatenate(
            [
                vector_pair[:, 0].reshape(-1) + vector_far[: 5 * block],
                bias_pair + vector_far[5 * block :],
                jnp.sum(dz_all.astype(wide), axis=0),
                gain_sum,
            ]
        )
        return section, jnp.pad(flat, (0, -flat.shape[0] % (2 * shard_rows)))

    if ring.short:
        r, x = shard_rows, ring.x
        both, width_out = 2 * wide_half, 2 * block
        flow, across, onward = Flow(), ring.across, ring.onward
        chain = [rec_total, in_total] + energy_total

        def theirs(group, k):
            return ring.part(group, ring.back(k) * 2 + 1 - x, r)

        def total(k, arrived, passed):
            value = ring.part(chain, ring.back(k) * 2 + x, r).astype(wide)
            value = value + arrived.astype(wide)
            return value if passed is None else value + passed.astype(wide)

        def cornered(hop):
            index = lambda at, place, chip: (at * ring.dp + place) * 2 + chip
            pairs = [
                (index(p, a, q), index(q, b, p)) for a, b in hop for p in range(2) for q in range(2)
            ]
            return lambda array: lax.ppermute(array, ("section", "dp", "mp"), pairs)

        def output_part(k):
            return ring.part(output_total, ring.back(k), 2 * r)

        arrived = [across(a) for a in (first_rec, first_in, theirs(energy_total, 1))]
        out_two, out_before = onward(output_part(2)), ring.astern(output_part(1))
        grad_section, flat = input_back(tie(dz_kept, first_in, *output_total))
        flat_width = flat.shape[0] // r
        out_one = output_part(3).astype(wide) + out_two.astype(wide)
        out_one = onward(out_one.astype(low))
        flat_far = across(tie(halves(flat, r), out_two, out_before))
        arrived = jnp.concatenate(arrived, axis=1)
        flow.landed = (arrived, out_one, flat_far)
        value = total(1, arrived, None).astype(low)
        out = output_part(4).astype(wide) + out_before.astype(wide) + out_one.astype(wide)
        vocab_rows = out[:, width_out:].astype(low)
        message = jnp.concatenate(
            [cut(out, 1 - x, r)[:, :width_out].astype(low), vocab_rows[:r], vocab_rows[r:]], axis=1
        )
        passed, arrived, out_far, grad_far = flow.step(
            (onward, value), (across, theirs(chain, 2)), (across, message),
            (to_other_chip, grad_section),
        )
        output_grad = cut(out, x, r)[:, :width_out] + out_far[:, :width_out].astype(wide)
        flat = flat + joined(flat_far, flat_width).reshape(-1)
        shard = jnp.concatenate([out[:r, width_out:], out[r:, width_out:]], axis=1)
        shard = (shard + out_far[:, width_out:].astype(wide)).astype(low)
        shard = jnp.concatenate([shard, halves(flat, r)], axis=1)
        value = total(2, arrived, passed).astype(low)
        mine = ring.part([rec_total, in_total], ring.back(4) * 2 + x, r)
        passed, arrived, next_one, next_three, mine = flow.step(
            (onward, value), (across, theirs(chain, 3)), (onward, shard), (ring.astern, shard),
            (corners, mine),
        )
        shards = {0: shard, 1: next_one, 3: next_three, 2: onward(next_one)}
        flat = sum(joined(a[:, 2 * block :], flat_width).reshape(-1) for a in shards.values())
        value = total(3, arrived, passed).astype(low)
        passed, arrived, energy_passed, energy_arrived = flow.step(
            (cornered(ring.ring), value[:, :both]),
            (cornered(ring.pair), theirs([rec_total, in_total], 4)),
            (onward, value[:, both:]), (across, theirs(energy_total, 4)),
        )
        sides = corners(flat[sides_at : sides_at + wide_half + width])
        moved = mine.astype(wide) + arrived.astype(wide) + passed.astype(wide)
        energy_grad = ring.part(energy_total, ring.back(4) * 2 + x, r).astype(wide)
        energy_grad = energy_grad + energy_arrived.astype(wide) + energy_passed.astype(wide)
        vocab_grad = jnp.zeros((vocab_pad, block), low)
        for k, held in shards.items():
            held = jnp.concatenate([held[:, :block], held[:, block : 2 * block]], axis=0)
            vocab_grad = lax.dynamic_update_slice(vocab_grad, held, (ring.back(k) * 2 * r, 0))
    else:
        grad_section, flat = input_back(dz_kept)
        grad_far = to_other_chip(grad_section)

        def scatter(total):
            return lax.psum_scatter(total, "dp", scatter_dimension=0, tiled=True).astype(wide)

        moved = jnp.concatenate([scatter(rec_total), scatter(in_total)], axis=1)
        moved = corners(moved.astype(low)).astype(wide)
        energy_grad = jnp.concatenate([scatter(a) for a in energy_total], axis=1)
        output_grad = jnp.concatenate([scatter(a) for a in output_total], axis=1)
        flat = lax.psum(flat, "dp")
        sides = corners(flat[sides_at : sides_at + wide_half + width])
        vocab_grad = lax.all_gather(
            output_grad[:, 2 * block :].astype(low), "dp", axis=0, tiled=True
        )

    input_grad = jnp.where(s == y, grad_section, grad_far)
    vocab_grad = vocab_grad.T[:, :vocab_size].astype(wide)
    vector_sum = flat[: 5 * block].reshape(5, block)
    bias_sum = flat[5 * block : 5 * block + vocab_size]
    lstm_bias_sum = sides[:wide_half].reshape(1, 4, unit_half)
    gain_sum = sides[wide_half:][None]
    rec_grad = moved[:, :wide_half].reshape(1, shard_rows, 4, unit_half)
    in_grad = moved[:, wide_half:].reshape(1, shard_rows, 4, unit_half)
    mono_mem_grad, span_mem_grad, mono_dec_grad, span_dec_grad = [
        energy_grad[:, n * block : (n + 1) * block] for n in range(4)
    ]
    return (
        input_grad[None],
        gain_sum,
        in_grad,
        rec_grad,
        lstm_bias_sum,
        mono_mem_grad,
        mono_dec_grad,
        vector_sum[0],
        vector_sum[1],
        span_mem_grad,
        span_dec_grad,
        vector_sum[2],
        vector_sum[3],
        jnp.stack([output_grad[:, :block], output_grad[:, block : 2 * block]]),
        vector_sum[4],
        vocab_grad,
        bias_sum,
    )


def solution(mesh):
    both = ("section", "mp")
    in_specs = (
        P("section", "dp", None, None),
        P("section", None),
        P("section", "dp", None, "mp"),
        P("section", "dp", None, "mp"),
        P("section", None, "mp"),
        P("dp", both),
        P("dp", both),
        P(both),
        P(both),
        P("dp", both),
        P("dp", both),
        P(both),
        P(both),
        P(None, "dp", both),
        P(both),
        P(both, None),
        P(),
        P("dp", None, None),
        P("dp"),
        P("dp"),
        P("dp", None),
    )
    out_specs = (
        P("section", "dp", None, None),
        P("section", None),
        P("section", "dp", None, "mp"),
        P("section", "dp", None, "mp"),
        P("section", None, "mp"),
        P("dp", both),
        P("dp", both),
        P(both),
        P(both),
        P("dp", both),
        P("dp", both),
        P(both),
        P(both),
        P(None, "dp", both),
        P(both),
        P(both, None),
        P(),
    )
    dp = mesh.shape["dp"]

    def step(*arrays):
        return local(dp, *arrays)

    return jax.shard_map(step, mesh=mesh, in_specs=in_specs, out_specs=out_specs, check_vma=False)
```

```python
import functools

import jax
import jax.numpy as jnp
from jax import lax
from jax.experimental import pallas as pl
from jax.experimental.pallas import tpu as pltpu
from jax.sharding import PartitionSpec as P

epsilon = 1e-05
offset = -4.0
wide = jnp.float32
low = jnp.bfloat16
in_vmem = pl.BlockSpec(memory_space=pltpu.VMEM)
in_smem = pl.BlockSpec(memory_space=pltpu.SMEM)
in_place = pl.BlockSpec(memory_space=pl.ANY)
core_swap = [(0, 1), (1, 0)]
corner_swap = [(0, 0), (1, 2), (2, 1), (3, 3)]


def normalize(inputs, gain_row):
    average = jnp.mean(inputs, axis=-1, keepdims=True)
    centred = inputs - average
    spread = jnp.mean(centred * centred, axis=-1, keepdims=True)
    return centred * lax.rsqrt(spread + epsilon) * gain_row


def across_cores(array):
    return lax.ppermute(array, "section", core_swap)


def across_chips(array):
    return lax.ppermute(array, "mp", core_swap)


def corners(array):
    return lax.ppermute(array, ("section", "mp"), corner_swap)


def tie(value, *others):
    return lax.optimization_barrier((value,) + others)[0]


def cut(array, block, rows):
    return lax.dynamic_slice_in_dim(array, block * rows, rows, axis=0)


class Flow:
    def __init__(self):
        self.landed = ()

    def step(self, *jobs, also=()):
        operands = tuple(operand for _, operand in jobs)
        operands = lax.optimization_barrier(operands + self.landed + tuple(also))[: len(jobs)]
        results = [send(operand) for (send, _), operand in zip(jobs, operands)]
        self.landed = tuple(results)
        return results


class Ring:
    def __init__(self, dp):
        self.dp = dp
        self.outer = dp // 2
        self.short = dp % 2 == 0 and self.outer == 4
        pairs = [(z, x) for z in range(self.outer) for x in range(2)]
        self.pair = [(2 * z + x, 2 * z + 1 - x) for z, x in pairs]
        self.ring = [(2 * z + x, 2 * ((z + 1) % self.outer) + x) for z, x in pairs]
        self.turn = [(b, a) for a, b in self.ring]
        place = lax.axis_index("dp")
        self.z, self.x = place // 2, place % 2

    def across(self, array):
        return lax.ppermute(array, "dp", self.pair)

    def onward(self, array):
        return lax.ppermute(array, "dp", self.ring)

    def astern(self, array):
        return lax.ppermute(array, "dp", self.turn)

    def back(self, k):
        return lax.rem(self.z - k + self.outer, self.outer)


def halves(array, height):
    array = array.reshape(height, -1)
    upper = array.astype(low)
    lower = (array - upper.astype(wide)).astype(low)
    return jnp.pad(
        jnp.concatenate([upper, lower], axis=1), ((0, 0), (0, -2 * array.shape[1] % 128))
    )


def joined(array, count):
    return array[:, :count].astype(wide) + array[:, count : 2 * count].astype(wide)


def sigmoid(x):
    return 0.5 * jnp.tanh(0.5 * x) + 0.5


def fetch(blocks, places, side_blocks, target, sems, first=0, column=0):
    wide_half = target.shape[1] // 2
    columns = pl.ds(pl.multiple_of(side_blocks * wide_half, wide_half), wide_half)
    copies = []
    for k, block in enumerate(blocks):
        height = block.shape[0]
        span = pl.ds(pl.multiple_of(places[2 + k] * height, height), height)
        copies.append(
            pltpu.make_async_copy(
                block.at[:, column : column + wide_half],
                target.at[span, columns],
                sems.at[first + k],
            )
        )
    return copies


def forward_kernel(count, column, places, normed, b_own, b_other, *refs):
    in_own, in_other, w_own, w_other = [refs[n * count : (n + 1) * count] for n in range(4)]
    kept, given, before, gates, cells, wi, w, b, state, cell, sems = refs[4 * count :]
    steps, rows, wide_full = gates.shape
    wide_half = wide_full // 2
    unit_half = wide_half // 4
    chunk = min(256, unit_half)
    s = places[0]
    copies = fetch(in_own, places, s, wi, sems) + fetch(in_other, places, 1 - s, wi, sems, count)
    later = fetch(w_own, places, s, w, sems, 2 * count, column)
    later += fetch(w_other, places, 1 - s, w, sems, 3 * count, column)
    for copy in copies + later:
        copy.start()
    for source, at in ((b_own, s), (b_other, 1 - s)):
        b[:, pl.ds(pl.multiple_of(at * wide_half, wide_half), wide_half)] = source[...]
    state[...] = jnp.zeros_like(state)
    cell[...] = jnp.zeros_like(cell)
    for copy in copies:
        copy.wait()

    def project(g, carried):
        cols = pl.ds(pl.multiple_of(g * unit_half, unit_half), unit_half)
        value = jnp.dot(normed[...], wi[:, cols], preferred_element_type=wide) + b[:, cols]
        gates[:, :, cols] = value.reshape(steps, rows, unit_half)
        return carried

    lax.fori_loop(0, 8, project, 0)
    for copy in later:
        copy.wait()
    eighth = rows // 2
    first_chip = places[1] == 0

    def advance(t, carried):
        hidden = state[...]
        before[t] = hidden
        for at in range(0, 2 * unit_half, chunk):
            half, inside = at // unit_half, at % unit_half
            acts = []
            for g in range(4):
                cols = pl.ds(half * wide_half + g * unit_half + inside, chunk)
                value = gates[t, :, cols] + jnp.dot(
                    hidden, w[:, cols], preferred_element_type=wide
                )
                value = jnp.tanh(value) if g == 2 else sigmoid(value)
                gates[t, :, cols] = value
                acts.append(value)
            units = pl.ds(at, chunk)
            new_cell = acts[1] * cell[:, units] + acts[0] * acts[2]
            cell[:, units] = new_cell
            cells[t, :, units] = new_cell
            new_hidden = acts[3] * jnp.tanh(new_cell)
            state[:, units] = new_hidden.astype(low)
            upper, lower = new_hidden[:eighth], new_hidden[eighth:]
            kept[t, :, units] = jnp.where(first_chip, upper, lower).astype(low)
            given[t, :, units] = jnp.where(first_chip, lower, upper).astype(low)
        return carried

    lax.fori_loop(0, steps, advance, 0)


def run_forward(places, normed, b_own, b_other, in_own, in_other, w_own, w_other, steps, column):
    rows = normed.shape[0] // steps
    units = normed.shape[1]
    wide_half = b_own.shape[1]
    count = len(w_own)
    return pl.pallas_call(
        functools.partial(forward_kernel, count, column),
        out_shape=(
            jax.ShapeDtypeStruct((steps, rows // 2, units), low),
            jax.ShapeDtypeStruct((steps, rows // 2, units), low),
            jax.ShapeDtypeStruct((steps, rows, units), low),
            jax.ShapeDtypeStruct((steps, rows, 2 * wide_half), wide),
            jax.ShapeDtypeStruct((steps, rows, units), wide),
        ),
        in_specs=[in_smem] + [in_vmem] * 3 + [in_place] * (4 * count),
        out_specs=[in_vmem] * 5,
        scratch_shapes=[
            pltpu.VMEM((units, 2 * wide_half), low),
            pltpu.VMEM((units, 2 * wide_half), low),
            pltpu.VMEM((1, 2 * wide_half), wide),
            pltpu.VMEM((rows, units), low),
            pltpu.VMEM((rows, units), wide),
            pltpu.SemaphoreType.DMA((4 * count,)),
        ],
        compiler_params=pltpu.CompilerParams(vmem_limit_bytes=56 << 20),
        name="recur_forward",
    )(places, normed, b_own, b_other, *in_own, *in_other, *w_own, *w_other)


def backward_kernel(count, column, places, kept, taken, gates, cells, *refs):
    w_own, w_other = refs[:count], refs[count : 2 * count]
    dz, stage, w, dh, dc, sems = refs[2 * count :]
    steps, rows, wide_full = gates.shape
    wide_half = wide_full // 2
    unit_half = wide_half // 4
    chunk = min(256, unit_half)
    s = places[0]
    first_chip = places[1] == 0
    jobs = []
    for n, (sources, at) in enumerate(((w_own, s), (w_other, 1 - s))):
        for k, block in enumerate(sources):
            slot = n * count + k
            copy = pltpu.make_async_copy(
                block.at[:, column : column + wide_half], stage.at[slot], sems.at[slot]
            )
            copy.start()
            jobs.append((copy, slot, at, places[2 + k] * block.shape[0]))
    dh[...] = jnp.zeros_like(dh)
    dc[...] = jnp.zeros_like(dc)
    height = w_own[0].shape[0]
    piece = min(height, 128)
    for copy, slot, at, first in jobs:
        copy.wait()

        def turn(g, carried, slot=slot, at=at, first=first):
            columns = pl.ds(pl.multiple_of(g * unit_half, unit_half), unit_half)
            span = pl.ds(pl.multiple_of(at * wide_half + g * unit_half, unit_half), unit_half)
            for low_row in range(0, height, piece):
                into = pl.ds(pl.multiple_of(first + low_row, piece), piece)
                w[span, into] = stage[slot, low_row : low_row + piece, columns].T
            return carried

        lax.fori_loop(0, 4, turn, 0)

    place_of = (s, 1 - s)

    def retreat(k, carried):
        t = steps - 1 - k
        earlier = jnp.maximum(t - 1, 0)
        live = jnp.where(t > 0, 1.0, 0.0).astype(wide)
        for at in range(0, 2 * unit_half, chunk):
            half, inside = at // unit_half, at % unit_half
            units = pl.ds(at, chunk)
            ours, theirs = kept[t, :, units], taken[t, :, units].astype(wide)
            grad = dh[:, units] + jnp.concatenate(
                [jnp.where(first_chip, ours, theirs), jnp.where(first_chip, theirs, ours)], axis=0
            )
            i, f, g, o = [
                gates[t, :, pl.ds(half * wide_half + n * unit_half + inside, chunk)]
                for n in range(4)
            ]
            squash = jnp.tanh(cells[t, :, units])
            total = dc[:, units] + grad * o * (1.0 - squash * squash)
            parts = (
                total * g * i * (1.0 - i),
                total * (cells[earlier, :, units] * live) * f * (1.0 - f),
                total * i * (1.0 - g * g),
                grad * squash * o * (1.0 - o),
            )
            for n, part in enumerate(parts):
                dz[place_of[half], t, :, pl.ds(n * unit_half + inside, chunk)] = part.astype(low)
            dc[:, units] = total * f
        upper, lower = dz[place_of[0], t], dz[place_of[1], t]
        for at in range(0, 2 * unit_half, chunk):
            units = pl.ds(at, chunk)
            dh[:, units] = jnp.dot(
                upper, w[:wide_half, units], preferred_element_type=wide
            ) + jnp.dot(lower, w[wide_half:, units], preferred_element_type=wide)
        return carried

    lax.fori_loop(0, steps, retreat, 0)


def run_backward(places, kept, taken, gates, cells, w_own, w_other, column):
    steps, rows, wide_full = gates.shape
    units = cells.shape[2]
    count = len(w_own)
    return pl.pallas_call(
        functools.partial(backward_kernel, count, column),
        out_shape=jax.ShapeDtypeStruct((2, steps, rows, wide_full // 2), low),
        in_specs=[in_smem] + [in_vmem] * 4 + [in_place] * (2 * count),
        out_specs=in_vmem,
        scratch_shapes=[
            pltpu.VMEM((2 * count, units // count, wide_full // 2), low),
            pltpu.VMEM((wide_full, units), low),
            pltpu.VMEM((rows, units), wide),
            pltpu.VMEM((rows, units), wide),
            pltpu.SemaphoreType.DMA((2 * count,)),
        ],
        compiler_params=pltpu.CompilerParams(vmem_limit_bytes=56 << 20),
        name="recur_backward",
    )(places, kept, taken, gates, cells, *w_own, *w_other)


def input_kernel(count, places, inputs, gain, dz, *refs):
    in_own, in_other = refs[:count], refs[count : 2 * count]
    grad_inputs, grad_gain, wi, sems = refs[2 * count :]
    s = places[0]
    copies = fetch(in_own, places, s, wi, sems) + fetch(in_other, places, 1 - s, wi, sems, count)
    for copy in copies:
        copy.start()
    x = inputs[...].astype(wide)
    centred = x - jnp.mean(x, axis=-1, keepdims=True)
    scale = lax.rsqrt(jnp.mean(centred * centred, axis=-1, keepdims=True) + epsilon)
    shape = centred * scale
    for copy in copies:
        copy.wait()
    wide_half = wi.shape[1] // 2
    own = pl.ds(pl.multiple_of(s * wide_half, wide_half), wide_half)
    other = pl.ds(pl.multiple_of((1 - s) * wide_half, wide_half), wide_half)
    grad = dot_nt(dz[0], wi[:, own]) + dot_nt(dz[1], wi[:, other])
    grad_gain[...] = jnp.sum(grad * shape, axis=0, keepdims=True)
    pulled = grad * gain[...]
    grad_inputs[...] = scale * (
        pulled
        - jnp.mean(pulled, axis=-1, keepdims=True)
        - shape * jnp.mean(pulled * shape, axis=-1, keepdims=True)
    )


def run_input(places, inputs, gain, dz, in_own, in_other):
    count = len(in_own)
    rows, width = inputs.shape
    return pl.pallas_call(
        functools.partial(input_kernel, count),
        out_shape=(
            jax.ShapeDtypeStruct((rows, width), wide),
            jax.ShapeDtypeStruct((1, width), wide),
        ),
        in_specs=[in_smem] + [in_vmem] * 3 + [in_place] * (2 * count),
        out_specs=[in_vmem] * 2,
        scratch_shapes=[
            pltpu.VMEM((width, 2 * dz.shape[2]), low),
            pltpu.SemaphoreType.DMA((2 * count,)),
        ],
        compiler_params=pltpu.CompilerParams(vmem_limit_bytes=56 << 20),
        name="input_back",
    )(places, inputs, gain, dz, *in_own, *in_other)


def dot_nt(a, b):
    return lax.dot_general(a, b, (((1,), (1,)), ((), ())), preferred_element_type=wide)


def dot_tn(a, b):
    return lax.dot_general(a, b, (((0,), (0,)), ((), ())), preferred_element_type=wide)


def attend_kernel(
    count, places, kept, taken, vectors, vocab_bias, noise, lengths, labels, counted, *refs
):
    small, vocab = refs[: 4 * count], refs[4 * count : 4 * count + 4]
    (
        grad_own, grad_given, pack_me, pack_chip, pack_cores, seen, near, far,
        memory, decoded, grad_memory, pack, sums, w, v, sems, v_sems, mk, sk, mq, sq, mono, span, keep, queue, scaled, ratio, window, mix, pre,
    ) = refs[4 * count + 4 :]
    rows, _ = kept.shape
    frames, group, _ = mk.shape
    block = w.shape[2] // 6
    lanes = 128
    chunks = 4 * block // lanes
    copies = []
    for r in range(4):
        arrived = []
        for k in range(count):
            source = small[r * count + k]
            height = source.shape[0]
            for h in range(source.shape[1] // (6 * block)):
                to = pl.ds(pl.multiple_of(places[2 + len(arrived)] * height, height), height)
                arrived.append(
                    pltpu.make_async_copy(
                        source.at[:, 6 * block * h : 6 * block * (h + 1)],
                        w.at[r, to, :],
                        sems.at[r, len(arrived)],
                    )
                )
        copies.append(arrived)
    vocab_copies = [pltpu.make_async_copy(vocab[r], v.at[r], v_sems.at[r]) for r in range(4)]
    for copy in sum(copies, []) + vocab_copies:
        copy.start()

    first_chip = places[1] == 0

    @pl.when(first_chip)
    def _():
        memory[...] = kept[...]
        decoded[...] = taken[...]

    @pl.when(jnp.logical_not(first_chip))
    def _():
        memory[...] = taken[...]
        decoded[...] = kept[...]

    def split(value):
        return value.reshape(frames, group, value.shape[-1])

    mem, dec = memory[...], decoded[...]
    for r in range(4):
        for copy in copies[r]:
            copy.wait()
        cols = pl.ds(r * block, block)
        keys = jnp.dot(mem, w[r, :, : 2 * block], preferred_element_type=wide)
        queries = jnp.dot(dec, w[r, :, 2 * block : 5 * block], preferred_element_type=wide)
        mk[:, :, cols] = split(keys[:, :block])
        sk[:, :, cols] = split(keys[:, block:])
        mq[:, :, cols] = split(queries[:, :block] + vectors[0:1, cols])
        sq[:, :, cols] = split(queries[:, block : 2 * block] + vectors[2:3, cols])
        pre[:, cols] = queries[:, 2 * block :] + vectors[4:5, cols]

    def lane(c):
        return pl.ds(c * lanes, lanes)

    def spread(row, c):
        return jnp.broadcast_to(vectors[row : row + 1, lane(c)], (group, lanes))

    def energies(queries, keys, vec_row, energy):
        weights = [spread(vec_row, c) for c in range(chunks)]

        def one(i, carried):
            query = [queries[i, :, lane(c)] for c in range(chunks)]
            for j in range(frames):
                total = jnp.tanh(query[0] + keys[j, :, lane(0)]) * weights[0]
                for c in range(1, chunks):
                    total = total + jnp.tanh(query[c] + keys[j, :, lane(c)]) * weights[c]
                energy[i * frames + j] = jnp.broadcast_to(
                    jnp.sum(total, axis=-1, keepdims=True), (group, lanes)
                )
            return carried

        lax.fori_loop(0, frames, one, 0)

    energies(mq, mk, 1, mono)
    energies(sq, sk, 3, span)

    length = lengths[...]
    valid = [(length > j) for j in range(frames)]
    ones = jnp.ones((group, lanes), wide)
    zeros = jnp.zeros((group, lanes), wide)
    live = [jnp.where(valid[j], 1.0, 0.0).astype(wide) for j in range(frames)]
    diagonal = lax.broadcasted_iota(jnp.int32, (group, lanes), 1) - lax.broadcasted_iota(
        jnp.int32, (group, lanes), 0
    )

    def attend(i, previous):
        base = i * frames
        top = jnp.full((group, lanes), -1e30, wide)
        for j in range(frames):
            top = jnp.maximum(top, jnp.where(valid[j], span[base + j], -1e30))
        weight = [jnp.where(valid[j], jnp.exp(span[base + j] - top), 0.0) for j in range(frames)]
        current, ratios = [], []
        queued = previous[0]
        for j in range(frames):
            prob = sigmoid(mono[base + j] + offset + noise[base + j]) * live[j]
            keep[base + j] = prob
            queue[base + j] = queued
            alpha = prob * queued
            current.append(alpha)
            if j + 1 < frames:
                queued = (1.0 - prob) * queued + previous[j + 1]
            both = weight[j] + weight[j - 1] if j else weight[j]
            both = jnp.where(valid[j], both, 1.0)
            window[base + j] = both
            scaled[base + j] = weight[j]
            quotient = alpha / both
            ratio[base + j] = quotient
            ratios.append(quotient)
        row = zeros
        for j in range(frames):
            beta = weight[j] * (ratios[j] + (ratios[j + 1] if j + 1 < frames else zeros))
            row = jnp.where(diagonal == group * j, beta, row)
        mix[i] = row
        return tuple(current)

    lax.fori_loop(0, frames, attend, tuple([ones] + [zeros] * (frames - 1)))

    beta_low = mix[...].reshape(rows, lanes)[:, :rows].astype(low)
    context = jnp.dot(beta_low, mem, preferred_element_type=wide).astype(low)
    seen[0] = context
    for r in range(4):
        cols = pl.ds(r * block, block)
        value = jnp.tanh(
            pre[:, cols] + jnp.dot(context, w[r, :, 5 * block :], preferred_element_type=wide)
        )
        pre[:, cols] = value
        pack[r, :, 5 * block :] = value.astype(low)
    logits = vocab_bias[...]
    for r in range(4):
        vocab_copies[r].wait()
        logits = logits + jnp.dot(pack[r, :, 5 * block :], v[r], preferred_element_type=wide)
    shifted = jnp.exp(logits - jnp.max(logits, axis=-1, keepdims=True))
    softmax = shifted / jnp.sum(shifted, axis=-1, keepdims=True)
    onehot = (labels[...] == lax.broadcasted_iota(jnp.int32, softmax.shape, 1)).astype(wide)
    grad_logits = ((softmax - onehot) * counted[...]).astype(low)
    seen[1] = grad_logits
    sums[5:6, :] = jnp.sum(grad_logits.astype(wide), axis=0, keepdims=True)
    sums[6:8, :] = jnp.zeros((2, sums.shape[1]), wide)

    grad_context = jnp.zeros((rows, memory.shape[1]), wide)
    for r in range(4):
        cols = pl.ds(r * block, block)
        value = pre[:, cols]
        grad_pre = (dot_nt(grad_logits, v[r]) * (1.0 - value * value)).astype(low)
        pack[r, :, 4 * block : 5 * block] = grad_pre
        sums[4:5, cols] = jnp.sum(grad_pre.astype(wide), axis=0, keepdims=True)
        grad_context = grad_context + dot_nt(grad_pre, w[r, :, 5 * block :])
    upper = grad_context.astype(low)
    lower = (grad_context - upper.astype(wide)).astype(low)
    grad_memory[...] = dot_tn(beta_low, upper) + dot_tn(beta_low, lower)
    cross = dot_nt(upper, mem) + dot_nt(lower, mem)
    if rows < lanes:
        cross = jnp.concatenate([cross, jnp.zeros((rows, lanes - rows), wide)], axis=1)
    mix[...] = split(cross)

    def unattend(k, later):
        i = frames - 1 - k
        base = i * frames
        cross_row = mix[i]
        grad_beta = [
            jnp.broadcast_to(
                jnp.sum(
                    jnp.where(diagonal == group * j, cross_row, 0.0), axis=-1, keepdims=True
                ),
                (group, lanes),
            )
            for j in range(frames)
        ]
        weight = [scaled[base + j] for j in range(frames)]
        share = [ratio[base + j] for j in range(frames)]
        direct, from_window, grad_weight = [], [], []
        for j in range(frames):
            grad_ratio = grad_beta[j] * weight[j]
            if j:
                grad_ratio = grad_ratio + grad_beta[j - 1] * weight[j - 1]
            pull = grad_ratio / window[base + j]
            direct.append(pull)
            from_window.append(jnp.where(valid[j], -pull * share[j], 0.0))
            grad_weight.append(
                grad_beta[j] * (share[j] + (share[j + 1] if j + 1 < frames else zeros))
            )
        top = jnp.full((group, lanes), -1e30, wide)
        for j in range(frames):
            top = jnp.maximum(top, jnp.where(valid[j], span[base + j], -1e30))
        total, ties, at_top, through = zeros, zeros, [], []
        for j in range(frames):
            pulled = grad_weight[j] + from_window[j]
            if j + 1 < frames:
                pulled = pulled + from_window[j + 1]
            pulled = weight[j] * pulled
            through.append(pulled)
            total = total + pulled
            hit = jnp.where(span[base + j] == top, live[j], 0.0)
            at_top.append(hit)
            ties = ties + hit
        back = total / ties
        for j in range(frames):
            span[base + j] = through[j] - at_top[j] * back
        grad_queue = zeros
        now = [None] * frames
        for j in reversed(range(frames)):
            prob = keep[base + j]
            grad_alpha = direct[j] + later[j]
            mono[base + j] = queue[base + j] * (grad_alpha - grad_queue) * prob * (1.0 - prob)
            grad_queue = prob * grad_alpha + (1.0 - prob) * grad_queue
            now[j] = grad_queue
        return tuple(now)

    lax.fori_loop(0, frames, unattend, tuple([zeros] * frames))

    def energy_back(queries, keys, energy, bias_row, vec_row):
        def one_chunk(c, carried):
            at = pl.ds(pl.multiple_of(c * lanes, lanes), lanes)
            weight = jnp.broadcast_to(vectors[vec_row : vec_row + 1, at], (group, lanes))

            def one(i, carry):
                grad_keys, vec_total, bias_total = carry
                query = queries[i, :, at]
                grad_query = zeros
                new_keys = []
                for j in range(frames):
                    squash = jnp.tanh(query + keys[j, :, at])
                    grad = energy[i * frames + j]
                    scaled_squash = grad * squash
                    vec_total = vec_total + scaled_squash
                    inner = grad - scaled_squash * squash
                    grad_query = grad_query + inner
                    new_keys.append(grad_keys[j] + inner)
                queries[i, :, at] = grad_query * weight
                return (tuple(new_keys), vec_total, bias_total + grad_query)

            grad_keys, vec_total, bias_total = lax.fori_loop(
                0, frames, one, (tuple([zeros] * frames), zeros, zeros)
            )
            for j in range(frames):
                keys[j, :, at] = grad_keys[j] * weight
            sums[bias_row : bias_row + 1, at] = jnp.sum(bias_total * weight, axis=0, keepdims=True)
            sums[vec_row : vec_row + 1, at] = jnp.sum(vec_total, axis=0, keepdims=True)
            return carried

        lax.fori_loop(0, chunks, one_chunk, 0)

    energy_back(mq, mk, mono, 0, 1)
    energy_back(sq, sk, span, 2, 3)

    total_memory = grad_memory[...]
    total_decoded = jnp.zeros_like(total_memory)
    for r in range(4):
        cols = pl.ds(r * block, block)
        for n, source in enumerate((mk, sk, mq, sq)):
            pack[r, :, n * block : (n + 1) * block] = (
                source[:, :, cols].reshape(rows, block).astype(low)
            )
        total_memory = total_memory + dot_nt(pack[r, :, : 2 * block], w[r, :, : 2 * block])
        total_decoded = total_decoded + dot_nt(
            pack[r, :, 2 * block : 5 * block], w[r, :, 2 * block : 5 * block]
        )
    pack_me[...] = pack[0]
    pack_chip[...] = pack[1]
    pack_cores[...] = pack[2:4]
    middle = 2 * block
    near[...] = sums[:, :middle]
    far[:8, :] = sums[:, middle:]
    far[8:9, :] = sums[5:6, :middle]
    far[9:10, :] = sums[5:6, middle:]
    far[10:, :] = jnp.zeros((6, middle), wide)
    grad_own[...] = jnp.where(first_chip, total_memory, total_decoded)
    grad_given[...] = jnp.where(first_chip, total_decoded, total_memory).astype(low)


def run_attend(
    places, kept, taken, smalls, vocab, vectors, vocab_bias, noise, lengths, labels, counted,
    frames,
):
    rows, width = kept.shape
    group = rows // frames
    full = vectors.shape[1]
    vocab_width = vocab[0].shape[1]
    cell = (frames * frames, group, 128)
    count = len(smalls[0])
    return pl.pallas_call(
        functools.partial(attend_kernel, count),
        out_shape=(
            jax.ShapeDtypeStruct((rows, width), wide),
            jax.ShapeDtypeStruct((rows, width), low),
            jax.ShapeDtypeStruct((rows, full // 4 * 6), low),
            jax.ShapeDtypeStruct((rows, full // 4 * 6), low),
            jax.ShapeDtypeStruct((2, rows, full // 4 * 6), low),
            jax.ShapeDtypeStruct((2, rows, vocab_width), low),
            jax.ShapeDtypeStruct((8, full // 2), wide),
            jax.ShapeDtypeStruct((16, full // 2), wide),
        ),
        in_specs=[in_smem] + [in_vmem] * 8 + [in_place] * (4 * count + 4),
        out_specs=[in_vmem] * 8,
        scratch_shapes=[
            pltpu.VMEM((rows, width), low),
            pltpu.VMEM((rows, width), low),
            pltpu.VMEM((rows, width), wide),
            pltpu.VMEM((4, rows, full // 4 * 6), low),
            pltpu.VMEM((8, full), wide),
            pltpu.VMEM((4, width, full // 4 * 6), low),
            pltpu.VMEM((4,) + vocab[0].shape, low),
            pltpu.SemaphoreType.DMA((4, places.shape[0] - 2)),
            pltpu.SemaphoreType.DMA((4,)),
        ]
        + [pltpu.VMEM((frames, group, full), wide)] * 4
        + [pltpu.VMEM(cell, wide)] * 7
        + [pltpu.VMEM((frames, group, 128), wide), pltpu.VMEM((rows, full), wide)],
        compiler_params=pltpu.CompilerParams(vmem_limit_bytes=56 << 20),
        name="attend",
    )(
        places, kept, taken, vectors, vocab_bias, noise, lengths, labels, counted,
        *sum(smalls, []), *vocab,
    )


def gradient_kernel(
    order, before, before_peer, normed, normed_peer, dz, dz_peer, states_own, states_core,
    seen, seen_core, far, far_core, pack_me, pack_core, pack_far, *refs
):
    outputs, paired = refs[:8], refs[8:12]
    a_rec, a_in, a_dz, states, a_context, a_grads, a_pack, block, paired_block, sems, out_sems = (
        refs[12:]
    )
    y = order[0]
    height = block.shape[1]
    wide_half = a_dz.shape[1]
    part = a_pack.shape[1] // 6
    width = a_rec.shape[1]
    jobs = []
    for sources, target in (
        ((dz.at[0], dz_peer), a_dz),
        ((before, before_peer), a_rec),
        ((normed, normed_peer), a_in),
        (
            (states_own.at[0], states_core.at[0], states_own.at[2], states_core.at[2]),
            states.at[y],
        ),
        (
            (
                states_own.at[1], states_core.at[1],
                far.at[2, :, :width], far_core.at[2, :, :width],
            ),
            states.at[1 - y],
        ),
        ((pack_me, pack_core.at[0], pack_far.at[0], pack_far.at[1]), a_pack),
        ((seen.at[0], seen_core.at[0], far.at[0, :, :width], far_core.at[0, :, :width]), a_context),
        ((seen.at[1], seen_core.at[1], far.at[1, :, :width], far_core.at[1, :, :width]), a_grads),
    ):
        rows = target.shape[0] // len(sources)
        for r, source in enumerate(sources):
            jobs.append(
                pltpu.make_async_copy(
                    source, target.at[r * rows : (r + 1) * rows, :], sems.at[len(jobs)]
                )
            )
    for job in jobs:
        job.start()
    for job in jobs:
        job.wait()

    def one(n, carried):
        cols = pl.ds(pl.multiple_of(order[1 + n] * height, height), height)
        both = jnp.concatenate([a_rec[:, cols], a_in[:, cols]], axis=1)
        for at in range(0, wide_half, 1024):
            value = dot_tn(both, a_dz[:, at : at + 1024]).astype(low)
            block[n, :, at : at + 1024] = value[:height]
            block[n, :, wide_half + at : wide_half + at + 1024] = value[height:]
        for m in range(2):
            to = 2 * wide_half + 2 * m * part
            block[n, :, to : to + 2 * part] = dot_tn(
                states[m, :, cols], a_pack[:, 2 * m * part : 2 * (m + 1) * part]
            ).astype(low)
        for m, output in enumerate(outputs):

            @pl.when(n == m)
            def _(m=m, output=output):
                pltpu.make_async_copy(block.at[m], output, out_sems.at[m]).start()

        return carried

    lax.fori_loop(0, 8, one, 0)

    def pair(n, carried):
        cols = pl.ds(pl.multiple_of(order[9 + n] * 2 * height, 2 * height), 2 * height)
        grad_pre = a_pack[:, 4 * part : 5 * part]
        for m, (a, b) in enumerate(
            (
                (states[1, :, cols], grad_pre),
                (a_context[:, cols], grad_pre),
                (a_grads[:, cols], a_pack[:, 5 * part :]),
            )
        ):
            paired_block[n, :, m * part : (m + 1) * part] = dot_tn(a, b).astype(low)
        return carried

    lax.fori_loop(0, 4, pair, 0)
    for m, output in enumerate(paired):
        pltpu.make_async_copy(paired_block.at[m], output, out_sems.at[8 + m]).start()
    for m, output in enumerate(outputs):
        pltpu.make_async_copy(block.at[m], output, out_sems.at[m]).wait()
    for m, output in enumerate(paired):
        pltpu.make_async_copy(paired_block.at[m], output, out_sems.at[8 + m]).wait()


def run_gradients(order, *arrays):
    rows, width = arrays[0].shape
    wide_half = arrays[5].shape[1]
    part = arrays[12].shape[1] // 6
    columns = 2 * wide_half + 4 * part
    height = width // 8
    deep = 2 * rows
    return pl.pallas_call(
        gradient_kernel,
        out_shape=tuple(
            [jax.ShapeDtypeStruct((height, columns), low)] * 8
            + [jax.ShapeDtypeStruct((2 * height, 3 * part), low)] * 4
        ),
        in_specs=[in_smem] + [in_place] * 15,
        out_specs=[in_place] * 12,
        scratch_shapes=[
            pltpu.VMEM((deep, width), low),
            pltpu.VMEM((deep, width), low),
            pltpu.VMEM((deep, wide_half), low),
            pltpu.VMEM((2, deep, width), low),
            pltpu.VMEM((deep, width), low),
            pltpu.VMEM((deep, width), low),
            pltpu.VMEM((deep, 6 * part), low),
            pltpu.VMEM((8, height, columns), low),
            pltpu.VMEM((4, 2 * height, 3 * part), low),
            pltpu.SemaphoreType.DMA((26,)),
            pltpu.SemaphoreType.DMA((12,)),
        ],
        compiler_params=pltpu.CompilerParams(vmem_limit_bytes=56 << 20),
        name="weight_gradients",
    )(order, *arrays)


def local(
    dp,
    block_input, norm_gain, lstm_in, lstm_rec, lstm_bias,
    mono_mem, mono_dec, mono_bias, mono_vec, span_mem, span_dec, span_bias, span_vec,
    out_weight, out_bias, vocab_weight, vocab_bias, noise, enc_lengths, label_lengths, labels,
):
    ring = Ring(dp)
    s, y = lax.axis_index("section"), lax.axis_index("mp")
    _, utts, frames, width = block_input.shape
    half, quarter = utts // 2, utts // 4
    rows = frames * quarter
    shard_rows, _, unit_half = lstm_in.shape[1:]
    wide_half = 4 * unit_half
    block = mono_mem.shape[1]
    vocab_size = vocab_weight.shape[1]
    vocab_pad = 4 * block

    in_shard = lstm_in[0].reshape(shard_rows, wide_half)
    rec_shard = lstm_rec[0].reshape(shard_rows, wide_half)
    bias_shard = lstm_bias[0].reshape(1, wide_half)

    def of_section(array):
        return jnp.where(s == y, array, across_cores(array))

    inputs = of_section(jnp.swapaxes(block_input[0], 0, 1))
    gain = of_section(norm_gain[0])
    inputs_own = lax.dynamic_slice_in_dim(inputs, s * half, half, axis=1)
    inputs_other = lax.dynamic_slice_in_dim(inputs, (1 - s) * half, half, axis=1)
    normed_own = normalize(inputs_own.astype(wide), gain)
    normed_own = normed_own.astype(low).reshape(frames * half, width)
    normed_other = normalize(inputs_other.astype(wide), gain)
    normed_other = normed_other.astype(low).reshape(frames * half, width)

    start = s * half + y * quarter
    noise_part = jnp.transpose(
        lax.dynamic_slice_in_dim(noise, start, quarter, axis=0), (1, 2, 0)
    ).reshape(frames * frames, quarter, 1)
    noise_part = jnp.broadcast_to(noise_part, (frames * frames, quarter, 128))
    length_part = lax.dynamic_slice_in_dim(enc_lengths, start, quarter, axis=0)
    length_part = jnp.broadcast_to(length_part[:, None], (quarter, 128))
    label_part = lax.dynamic_slice_in_dim(labels, start, quarter, axis=0).T.reshape(rows, 1)
    count_part = lax.dynamic_slice_in_dim(label_lengths, start, quarter, axis=0)
    counted = (jnp.arange(frames)[:, None] < count_part[None, :]).astype(wide).reshape(rows, 1)
    bias_row = jnp.pad(vocab_bias, (0, vocab_pad - vocab_size), constant_values=-1e30)[None]

    vector_own = jnp.stack([mono_bias, mono_vec, span_bias, span_vec, out_bias])
    vocab_own = jnp.pad(vocab_weight, ((0, 0), (0, vocab_pad - vocab_size)))
    ready = (noise_part, length_part, label_part, counted, bias_row, normed_own, normed_other)
    places, in_own, rec_own, small_own, small_chip = [], [], [], [], []
    small = jnp.concatenate(
        [
            tie(mono_mem, in_shard, rec_shard), span_mem, mono_dec, span_dec,
            out_weight[0], out_weight[1],
        ],
        axis=1,
    )
    if ring.short:
        flow, across, onward = Flow(), ring.across, ring.onward
        both = 2 * wide_half
        corner_in, corner_rec, b_own = flow.step(
            (corners, in_shard), (corners, rec_shard), (corners, bias_shard)
        )
        small_far, small_next = across(small), onward(small)
        flow.landed += (small_far, small_next)
        b_own = b_own.astype(wide)
        small_own = [jnp.concatenate([small, small_far], axis=1)]
        small_chip, small_core = [], []
        held = jnp.concatenate([corner_in, corner_rec, small_next], axis=1)
        near, far, near_core, far_core = [], [], [], []
        for k in range(ring.outer):
            near.append(held)
            jobs = [(across, held), (across_chips, small_own[k])]
            if k < ring.outer - 1:
                jobs.append((onward, held[:, :both] if k == ring.outer - 2 else held))
            if k == 0:
                jobs += [(across_chips, vocab_own), (across_chips, vector_own)]
            results = flow.step(*jobs, also=ready if k == 1 else ())
            far.append(results[0])
            small_chip.append(results[1])
            if k == 0:
                vocab_chip, vector_pair = results[3:]
                vector_pair = jnp.concatenate([vector_own, vector_pair], axis=1)
            if k < ring.outer - 1:
                small_own.append(jnp.concatenate([held[:, both:], far[k][:, both:]], axis=1))
                held = results[2]
        for a, b in zip(near, far):
            near_core.append(across_cores(a))
            far_core.append(across_cores(b))
        small_core = [across_cores(a) for a in small_own]
        b_last, vocab_last, chip_last, vector_last = lax.optimization_barrier(
            (b_own, vocab_own, vocab_chip, vector_pair, held)
        )[:4]
        b_other = across_cores(b_last)
        vocab = [vocab_own, vocab_chip, across_cores(vocab_last), across_cores(chip_last)]
        vector_core = across_cores(vector_last)
        in_own = [a for pair in zip(near, far) for a in pair]
        in_other = [a for pair in zip(near_core, far_core) for a in pair]
        rec_own, rec_other, rec_column = in_own, in_other, wide_half
        for k in range(ring.outer):
            places += [ring.back(k) * 2 + ring.x, ring.back(k) * 2 + 1 - ring.x]
    else:
        vocab_chip = across_chips(vocab_own)
        small, in_block, rec_block = [
            lax.all_gather(a, "dp", axis=0, tiled=True)
            for a in (small, corners(in_shard), corners(rec_shard))
        ]
        places, in_own, rec_own = [jnp.int32(0)], [in_block], [rec_block]
        small_own, small_chip = [small], [across_chips(small)]
        vocab = [vocab_own, vocab_chip, across_cores(vocab_own), across_cores(vocab_chip)]
        in_other, rec_other, rec_column = [across_cores(in_block)], [across_cores(rec_block)], 0
        small_core = [across_cores(small)]
        b_own = corners(bias_shard).astype(wide)
        b_other = across_cores(b_own)
        vector_pair = across_chips(vector_own)
        vector_pair = jnp.concatenate([vector_own, vector_pair], axis=1)
        vector_core = across_cores(vector_pair)
    vectors = jnp.concatenate([vector_pair, vector_core], axis=1)
    vectors = jnp.pad(vectors, ((0, 3), (0, 0)))
    places = jnp.stack([s, y] + places).astype(jnp.int32)
    places = tie(places, vectors, *vocab, *ready, *small_chip[:-1], *small_core)

    kept, given, before, gates, cells = run_forward(
        places, normed_own, b_own, b_other, in_own, in_other, rec_own, rec_other, frames,
        rec_column,
    )

    kept, given = kept.reshape(rows, width), given.reshape(rows, width)
    taken = across_chips(given)
    small_chip[-1] = tie(small_chip[-1], kept)
    small_both = [across_cores(part) for part in small_chip]
    smalls = [small_own, small_chip, small_core, small_both]
    grad_own, grad_given, pack_me, pack_chip, pack_cores, seen, near, far = run_attend(
        places, kept, taken, smalls, vocab, vectors, bias_row, noise_part, length_part,
        label_part, counted, frames,
    )
    grad_taken = across_chips(grad_given)
    pack_core = across_cores(pack_cores)
    pack_out = jnp.stack([pack_chip, pack_core[1]])
    far_peer = across_cores(far)
    vector_pair = (near[:5] + far_peer[:5]).reshape(5, 2, block)
    bias_pair = (far[8:10] + far_peer[8:10]).reshape(-1)
    vector_out = jnp.concatenate([vector_pair[:, 1].reshape(-1), bias_pair])
    vector_count = vector_out.shape[0] // (3 * rows)
    seen_out = jnp.concatenate(
        [
            jnp.concatenate([seen, kept[None]], axis=0),
            halves(vector_out, 3 * rows).reshape(3, rows, -1),
        ],
        axis=2,
    )
    before = before.reshape(frames * half, width)
    before_peer = across_cores(tie(before, taken))
    states = jnp.stack([tie(kept, grad_given), taken, given])
    states_core, seen_core = across_cores(states), across_cores(seen)
    places_back, pack_out, seen_out = lax.optimization_barrier(
        (places, pack_out, seen_out, grad_taken, before_peer, states_core, seen_core)
    )[:3]
    dz = run_backward(
        places_back, grad_own.reshape(frames, quarter, width),
        grad_taken.reshape(frames, quarter, width), gates, cells, rec_own, rec_other, rec_column,
    )
    pack_far = across_chips(pack_out)
    seen_far = across_chips(tie(seen_out, pack_out))

    dz = dz.reshape(2, frames * half, wide_half)
    dz, pack_far, seen_far = lax.optimization_barrier((dz, pack_far, seen_far))
    dz_peer = across_cores(dz[1])
    grad_inputs, grad_gain = run_input(
        places, inputs_own.reshape(frames * half, width), gain[None], dz, in_own, in_other
    )
    grad_gain = grad_gain.reshape(width)
    z, x = ring.z, ring.x
    if ring.short:
        steps_back = [ring.back(k) for k in range(1, 5)]
        order = [at * 2 + 1 - x for at in steps_back] + [at * 2 + x for at in steps_back]
        order = [y] + order + steps_back
    else:
        order = [y] + [jnp.int32(k) for k in [*range(8), *range(4)]]
    totals = run_gradients(
        tie(jnp.stack(order).astype(jnp.int32), grad_gain), before, before_peer, normed_own, normed_other, dz,
        dz_peer, states, states_core, seen, seen_core, seen_far, across_cores(seen_far),
        pack_me, pack_core, pack_far,
    )
    grad_inputs = jnp.swapaxes(grad_inputs.reshape(frames, half, width), 0, 1)
    vector_far = joined(seen_far[:, :, width:].reshape(3 * rows, -1), vector_count).reshape(-1)

    sides_at = 5 * block + vocab_pad
    grad_peer = across_cores(grad_inputs)
    grad_section = jnp.concatenate(
        [
            jnp.where(s == 0, grad_inputs, grad_peer),
            jnp.where(s == 0, grad_peer, grad_inputs),
        ],
        axis=0,
    )
    gain_sum = grad_gain + across_cores(grad_gain)
    flat = jnp.concatenate(
        [
            vector_pair[:, 0].reshape(-1) + vector_far[: 5 * block],
            bias_pair + vector_far[5 * block :],
            jnp.sum(dz[0].astype(wide), axis=0) + jnp.sum(dz_peer.astype(wide), axis=0),
            gain_sum,
        ]
    )
    flat = jnp.pad(flat, (0, -flat.shape[0] % (8 * shard_rows)))

    def to_other_chip(section):
        return lax.ppermute(section, ("section", "mp"), [(0, 1), (3, 2)])

    if ring.short:
        r = shard_rows
        both, width_out = 2 * wide_half, 2 * block
        flow, across, onward = Flow(), ring.across, ring.onward
        theirs, mine, outputs = totals[:4], totals[4:8], totals[8:]

        def total(k, arrived, passed):
            value = mine[k - 1].astype(wide) + arrived.astype(wide)
            return value if passed is None else value + passed.astype(wide)

        def cornered(hop):
            index = lambda at, place, chip: (at * ring.dp + place) * 2 + chip
            pairs = [
                (index(p, a, q), index(q, b, p)) for a, b in hop for p in range(2) for q in range(2)
            ]
            return lambda array: lax.ppermute(array, ("section", "dp", "mp"), pairs)

        arrived, out_two, out_before = flow.step(
            (across, theirs[0]), (onward, outputs[1]), (ring.astern, outputs[0])
        )
        grad_far = to_other_chip(grad_section)
        flat = flat.reshape(8, -1)
        flat = flat + across(flat)
        flow.landed = (arrived,)
        value = total(1, arrived, None).astype(low)
        out = (outputs[2].astype(wide) + out_two.astype(wide)).astype(low)
        passed, arrived, out_one = flow.step((onward, value), (across, theirs[1]), (onward, out))
        flat_one, flat_three = onward(flat), ring.astern(flat)
        out = outputs[3].astype(wide) + out_before.astype(wide) + out_one.astype(wide)
        vocab_rows = out[:, width_out:].astype(low)
        message = jnp.concatenate(
            [cut(out, 1 - x, r)[:, :width_out].astype(low), vocab_rows[:r], vocab_rows[r:]], axis=1
        )
        value = total(2, arrived, passed).astype(low)
        passed, arrived, out_far, kept_rows = flow.step(
            (onward, value), (across, theirs[2]), (across, message), (corners, mine[3][:, :both]),
            also=(flat_one, flat_three),
        )
        flat = flat + flat_one + flat_three + onward(flat_one)
        output_grad = cut(out, x, r)[:, :width_out] + out_far[:, :width_out].astype(wide)
        shard = jnp.concatenate([out[:r, width_out:], out[r:, width_out:]], axis=1)
        shard = (shard + out_far[:, width_out:].astype(wide)).astype(low)
        value = total(3, arrived, passed).astype(low)
        passed, arrived, energy_passed, energy_arrived, next_three = flow.step(
            (cornered(ring.ring), value[:, :both]), (cornered(ring.pair), theirs[3][:, :both]),
            (onward, jnp.concatenate([value[:, both:], shard], axis=1)),
            (across, theirs[3][:, both:]), (ring.astern, shard),
            also=(grad_far, flat),
        )
        flat = flat.reshape(-1)
        sides = corners(tie(flat[sides_at : sides_at + wide_half + width], value))
        next_one, energy_passed = energy_passed[:, 4 * block :], energy_passed[:, : 4 * block]
        shards = {0: shard, 1: next_one, 3: next_three, 2: onward(next_one)}
        moved = kept_rows.astype(wide) + arrived.astype(wide) + passed.astype(wide)
        energy_grad = mine[3][:, both:].astype(wide) + energy_arrived.astype(wide)
        energy_grad = energy_grad + energy_passed.astype(wide)
        vocab_grad = jnp.zeros((vocab_pad, block), low)
        for k, held in shards.items():
            held = jnp.concatenate([held[:, :block], held[:, block : 2 * block]], axis=0)
            vocab_grad = lax.dynamic_update_slice(vocab_grad, held, (ring.back(k) * 2 * r, 0))
    else:
        grad_far = to_other_chip(grad_section)

        def scatter(parts):
            total = jnp.concatenate(parts, axis=0)
            return lax.psum_scatter(total, "dp", scatter_dimension=0, tiled=True).astype(wide)

        moved, output_grad = scatter(totals[:8]), scatter(totals[8:])
        moved, energy_grad = moved[:, : 2 * wide_half], moved[:, 2 * wide_half :]
        moved = corners(moved.astype(low)).astype(wide)
        flat = lax.psum(flat, "dp")
        sides = corners(flat[sides_at : sides_at + wide_half + width])
        vocab_grad = lax.all_gather(
            output_grad[:, 2 * block :].astype(low), "dp", axis=0, tiled=True
        )

    input_grad = jnp.where(s == y, grad_section, grad_far)
    vocab_grad = vocab_grad.T[:, :vocab_size].astype(wide)
    vector_sum = flat[: 5 * block].reshape(5, block)
    bias_sum = flat[5 * block : 5 * block + vocab_size]
    lstm_bias_sum = sides[:wide_half].reshape(1, 4, unit_half)
    gain_sum = sides[wide_half:][None]
    rec_grad = moved[:, :wide_half].reshape(1, shard_rows, 4, unit_half)
    in_grad = moved[:, wide_half:].reshape(1, shard_rows, 4, unit_half)
    mono_mem_grad, span_mem_grad, mono_dec_grad, span_dec_grad = [
        energy_grad[:, n * block : (n + 1) * block] for n in range(4)
    ]
    return (
        input_grad[None],
        gain_sum,
        in_grad,
        rec_grad,
        lstm_bias_sum,
        mono_mem_grad,
        mono_dec_grad,
        vector_sum[0],
        vector_sum[1],
        span_mem_grad,
        span_dec_grad,
        vector_sum[2],
        vector_sum[3],
        jnp.stack([output_grad[:, :block], output_grad[:, block : 2 * block]]),
        vector_sum[4],
        vocab_grad,
        bias_sum,
    )


def solution(mesh):
    both = ("section", "mp")
    in_specs = (
        P("section", "dp", None, None),
        P("section", None),
        P("section", "dp", None, "mp"),
        P("section", "dp", None, "mp"),
        P("section", None, "mp"),
        P("dp", both),
        P("dp", both),
        P(both),
        P(both),
        P("dp", both),
        P("dp", both),
        P(both),
        P(both),
        P(None, "dp", both),
        P(both),
        P(both, None),
        P(),
        P("dp", None, None),
        P("dp"),
        P("dp"),
        P("dp", None),
    )
    out_specs = (
        P("section", "dp", None, None),
        P("section", None),
        P("section", "dp", None, "mp"),
        P("section", "dp", None, "mp"),
        P("section", None, "mp"),
        P("dp", both),
        P("dp", both),
        P(both),
        P(both),
        P("dp", both),
        P("dp", both),
        P(both),
        P(both),
        P(None, "dp", both),
        P(both),
        P(both, None),
        P(),
    )
    dp = mesh.shape["dp"]

    def step(*arrays):
        return local(dp, *arrays)

    return jax.shard_map(step, mesh=mesh, in_specs=in_specs, out_specs=out_specs, check_vma=False)
```

```python
import functools

import jax
import jax.numpy as jnp
from jax import lax
from jax.experimental import pallas as pl
from jax.experimental.pallas import tpu as pltpu
from jax.sharding import PartitionSpec as P

epsilon = 1e-05
offset = -4.0
wide = jnp.float32
low = jnp.bfloat16
in_vmem = pl.BlockSpec(memory_space=pltpu.VMEM)
in_smem = pl.BlockSpec(memory_space=pltpu.SMEM)
in_place = pl.BlockSpec(memory_space=pl.ANY)
core_swap = [(0, 1), (1, 0)]
corner_swap = [(0, 0), (1, 2), (2, 1), (3, 3)]


def normalize(inputs, gain_row):
    average = jnp.mean(inputs, axis=-1, keepdims=True)
    centred = inputs - average
    spread = jnp.mean(centred * centred, axis=-1, keepdims=True)
    return centred * lax.rsqrt(spread + epsilon) * gain_row


def across_cores(array):
    return lax.ppermute(array, "section", core_swap)


def across_chips(array):
    return lax.ppermute(array, "mp", core_swap)


def corners(array):
    return lax.ppermute(array, ("section", "mp"), corner_swap)


def tie(value, *others):
    return lax.optimization_barrier((value,) + others)[0]


def cut(array, block, rows):
    return lax.dynamic_slice_in_dim(array, block * rows, rows, axis=0)


class Flow:
    def __init__(self):
        self.landed = ()

    def step(self, *jobs, also=()):
        operands = tuple(operand for _, operand in jobs)
        operands = lax.optimization_barrier(operands + self.landed + tuple(also))[: len(jobs)]
        results = [send(operand) for (send, _), operand in zip(jobs, operands)]
        self.landed = tuple(results)
        return results


class Ring:
    def __init__(self, dp):
        self.dp = dp
        self.outer = dp // 2
        self.short = dp % 2 == 0 and self.outer == 4
        pairs = [(z, x) for z in range(self.outer) for x in range(2)]
        self.pair = [(2 * z + x, 2 * z + 1 - x) for z, x in pairs]
        self.ring = [(2 * z + x, 2 * ((z + 1) % self.outer) + x) for z, x in pairs]
        self.turn = [(b, a) for a, b in self.ring]
        place = lax.axis_index("dp")
        self.z, self.x = place // 2, place % 2

    def across(self, array):
        return lax.ppermute(array, "dp", self.pair)

    def onward(self, array):
        return lax.ppermute(array, "dp", self.ring)

    def astern(self, array):
        return lax.ppermute(array, "dp", self.turn)

    def back(self, k):
        return lax.rem(self.z - k + self.outer, self.outer)


def halves(array, height):
    array = array.reshape(height, -1)
    upper = array.astype(low)
    lower = (array - upper.astype(wide)).astype(low)
    return jnp.pad(
        jnp.concatenate([upper, lower], axis=1), ((0, 0), (0, -2 * array.shape[1] % 128))
    )


def joined(array, count):
    return array[:, :count].astype(wide) + array[:, count : 2 * count].astype(wide)


def sigmoid(x):
    return 0.5 * jnp.tanh(0.5 * x) + 0.5


def fetch(blocks, places, side_blocks, target, sems, first=0, column=0):
    wide_half = target.shape[1] // 2
    columns = pl.ds(pl.multiple_of(side_blocks * wide_half, wide_half), wide_half)
    copies = []
    for k, block in enumerate(blocks):
        height = block.shape[0]
        span = pl.ds(pl.multiple_of(places[2 + k] * height, height), height)
        copies.append(
            pltpu.make_async_copy(
                block.at[:, column : column + wide_half],
                target.at[span, columns],
                sems.at[first + k],
            )
        )
    return copies


def forward_kernel(count, column, places, normed, b_own, b_other, *refs):
    in_own, in_other, w_own, w_other = [refs[n * count : (n + 1) * count] for n in range(4)]
    kept, given, before, gates, cells, wi, w, b, state, cell, sems = refs[4 * count :]
    steps, rows, wide_full = gates.shape
    wide_half = wide_full // 2
    unit_half = wide_half // 4
    chunk = min(256, unit_half)
    s = places[0]
    copies = fetch(in_own, places, s, wi, sems) + fetch(in_other, places, 1 - s, wi, sems, count)
    later = fetch(w_own, places, s, w, sems, 2 * count, column)
    later += fetch(w_other, places, 1 - s, w, sems, 3 * count, column)
    for copy in copies + later:
        copy.start()
    for source, at in ((b_own, s), (b_other, 1 - s)):
        b[:, pl.ds(pl.multiple_of(at * wide_half, wide_half), wide_half)] = source[...]
    state[...] = jnp.zeros_like(state)
    cell[...] = jnp.zeros_like(cell)
    for copy in copies:
        copy.wait()

    def project(g, carried):
        cols = pl.ds(pl.multiple_of(g * unit_half, unit_half), unit_half)
        value = jnp.dot(normed[...], wi[:, cols], preferred_element_type=wide) + b[:, cols]
        gates[:, :, cols] = value.reshape(steps, rows, unit_half)
        return carried

    lax.fori_loop(0, 8, project, 0)
    for copy in later:
        copy.wait()
    eighth = rows // 2
    first_chip = places[1] == 0

    def advance(t, carried):
        hidden = state[...]
        before[t] = hidden
        for at in range(0, 2 * unit_half, chunk):
            half, inside = at // unit_half, at % unit_half
            acts = []
            for g in range(4):
                cols = pl.ds(half * wide_half + g * unit_half + inside, chunk)
                value = gates[t, :, cols] + jnp.dot(
                    hidden, w[:, cols], preferred_element_type=wide
                )
                value = jnp.tanh(value) if g == 2 else sigmoid(value)
                gates[t, :, cols] = value
                acts.append(value)
            units = pl.ds(at, chunk)
            new_cell = acts[1] * cell[:, units] + acts[0] * acts[2]
            cell[:, units] = new_cell
            cells[t, :, units] = new_cell
            new_hidden = acts[3] * jnp.tanh(new_cell)
            state[:, units] = new_hidden.astype(low)
            upper, lower = new_hidden[:eighth], new_hidden[eighth:]
            kept[t, :, units] = jnp.where(first_chip, upper, lower).astype(low)
            given[t, :, units] = jnp.where(first_chip, lower, upper).astype(low)
        return carried

    lax.fori_loop(0, steps, advance, 0)


def run_forward(places, normed, b_own, b_other, in_own, in_other, w_own, w_other, steps, column):
    rows = normed.shape[0] // steps
    units = normed.shape[1]
    wide_half = b_own.shape[1]
    count = len(w_own)
    return pl.pallas_call(
        functools.partial(forward_kernel, count, column),
        out_shape=(
            jax.ShapeDtypeStruct((steps, rows // 2, units), low),
            jax.ShapeDtypeStruct((steps, rows // 2, units), low),
            jax.ShapeDtypeStruct((steps, rows, units), low),
            jax.ShapeDtypeStruct((steps, rows, 2 * wide_half), wide),
            jax.ShapeDtypeStruct((steps, rows, units), wide),
        ),
        in_specs=[in_smem] + [in_vmem] * 3 + [in_place] * (4 * count),
        out_specs=[in_vmem] * 5,
        scratch_shapes=[
            pltpu.VMEM((units, 2 * wide_half), low),
            pltpu.VMEM((units, 2 * wide_half), low),
            pltpu.VMEM((1, 2 * wide_half), wide),
            pltpu.VMEM((rows, units), low),
            pltpu.VMEM((rows, units), wide),
            pltpu.SemaphoreType.DMA((4 * count,)),
        ],
        compiler_params=pltpu.CompilerParams(vmem_limit_bytes=56 << 20),
        name="recur_forward",
    )(places, normed, b_own, b_other, *in_own, *in_other, *w_own, *w_other)


def backward_kernel(count, column, places, kept, taken, gates, cells, *refs):
    w_own, w_other = refs[:count], refs[count : 2 * count]
    dz, stage, w, dh, dc, sems = refs[2 * count :]
    steps, rows, wide_full = gates.shape
    wide_half = wide_full // 2
    unit_half = wide_half // 4
    chunk = min(256, unit_half)
    s = places[0]
    first_chip = places[1] == 0
    jobs = []
    for n, (sources, at) in enumerate(((w_own, s), (w_other, 1 - s))):
        for k, block in enumerate(sources):
            slot = n * count + k
            copy = pltpu.make_async_copy(
                block.at[:, column : column + wide_half], stage.at[slot], sems.at[slot]
            )
            copy.start()
            jobs.append((copy, slot, at, places[2 + k] * block.shape[0]))
    dh[...] = jnp.zeros_like(dh)
    dc[...] = jnp.zeros_like(dc)
    height = w_own[0].shape[0]
    piece = min(height, 128)
    for copy, slot, at, first in jobs:
        copy.wait()

        def turn(g, carried, slot=slot, at=at, first=first):
            columns = pl.ds(pl.multiple_of(g * unit_half, unit_half), unit_half)
            span = pl.ds(pl.multiple_of(at * wide_half + g * unit_half, unit_half), unit_half)
            for low_row in range(0, height, piece):
                into = pl.ds(pl.multiple_of(first + low_row, piece), piece)
                w[span, into] = stage[slot, low_row : low_row + piece, columns].T
            return carried

        lax.fori_loop(0, 4, turn, 0)

    place_of = (s, 1 - s)

    def retreat(k, carried):
        t = steps - 1 - k
        earlier = jnp.maximum(t - 1, 0)
        live = jnp.where(t > 0, 1.0, 0.0).astype(wide)
        for at in range(0, 2 * unit_half, chunk):
            half, inside = at // unit_half, at % unit_half
            units = pl.ds(at, chunk)
            ours, theirs = kept[t, :, units], taken[t, :, units].astype(wide)
            grad = dh[:, units] + jnp.concatenate(
                [jnp.where(first_chip, ours, theirs), jnp.where(first_chip, theirs, ours)], axis=0
            )
            i, f, g, o = [
                gates[t, :, pl.ds(half * wide_half + n * unit_half + inside, chunk)]
                for n in range(4)
            ]
            squash = jnp.tanh(cells[t, :, units])
            total = dc[:, units] + grad * o * (1.0 - squash * squash)
            parts = (
                total * g * i * (1.0 - i),
                total * (cells[earlier, :, units] * live) * f * (1.0 - f),
                total * i * (1.0 - g * g),
                grad * squash * o * (1.0 - o),
            )
            for n, part in enumerate(parts):
                dz[place_of[half], t, :, pl.ds(n * unit_half + inside, chunk)] = part.astype(low)
            dc[:, units] = total * f
        upper, lower = dz[place_of[0], t], dz[place_of[1], t]
        for at in range(0, 2 * unit_half, chunk):
            units = pl.ds(at, chunk)
            dh[:, units] = jnp.dot(
                upper, w[:wide_half, units], preferred_element_type=wide
            ) + jnp.dot(lower, w[wide_half:, units], preferred_element_type=wide)
        return carried

    lax.fori_loop(0, steps, retreat, 0)


def run_backward(places, kept, taken, gates, cells, w_own, w_other, column):
    steps, rows, wide_full = gates.shape
    units = cells.shape[2]
    count = len(w_own)
    return pl.pallas_call(
        functools.partial(backward_kernel, count, column),
        out_shape=jax.ShapeDtypeStruct((2, steps, rows, wide_full // 2), low),
        in_specs=[in_smem] + [in_vmem] * 4 + [in_place] * (2 * count),
        out_specs=in_vmem,
        scratch_shapes=[
            pltpu.VMEM((2 * count, units // count, wide_full // 2), low),
            pltpu.VMEM((wide_full, units), low),
            pltpu.VMEM((rows, units), wide),
            pltpu.VMEM((rows, units), wide),
            pltpu.SemaphoreType.DMA((2 * count,)),
        ],
        compiler_params=pltpu.CompilerParams(vmem_limit_bytes=56 << 20),
        name="recur_backward",
    )(places, kept, taken, gates, cells, *w_own, *w_other)


def input_kernel(count, places, inputs, gain, dz, *refs):
    in_own, in_other = refs[:count], refs[count : 2 * count]
    grad_inputs, grad_gain, wi, sems = refs[2 * count :]
    s = places[0]
    copies = fetch(in_own, places, s, wi, sems) + fetch(in_other, places, 1 - s, wi, sems, count)
    for copy in copies:
        copy.start()
    x = inputs[...].astype(wide)
    centred = x - jnp.mean(x, axis=-1, keepdims=True)
    scale = lax.rsqrt(jnp.mean(centred * centred, axis=-1, keepdims=True) + epsilon)
    shape = centred * scale
    for copy in copies:
        copy.wait()
    wide_half = wi.shape[1] // 2
    own = pl.ds(pl.multiple_of(s * wide_half, wide_half), wide_half)
    other = pl.ds(pl.multiple_of((1 - s) * wide_half, wide_half), wide_half)
    grad = dot_nt(dz[0], wi[:, own]) + dot_nt(dz[1], wi[:, other])
    grad_gain[...] = jnp.sum(grad * shape, axis=0, keepdims=True)
    pulled = grad * gain[...]
    grad_inputs[...] = scale * (
        pulled
        - jnp.mean(pulled, axis=-1, keepdims=True)
        - shape * jnp.mean(pulled * shape, axis=-1, keepdims=True)
    )


def run_input(places, inputs, gain, dz, in_own, in_other):
    count = len(in_own)
    rows, width = inputs.shape
    return pl.pallas_call(
        functools.partial(input_kernel, count),
        out_shape=(
            jax.ShapeDtypeStruct((rows, width), wide),
            jax.ShapeDtypeStruct((1, width), wide),
        ),
        in_specs=[in_smem] + [in_vmem] * 3 + [in_place] * (2 * count),
        out_specs=[in_vmem] * 2,
        scratch_shapes=[
            pltpu.VMEM((width, 2 * dz.shape[2]), low),
            pltpu.SemaphoreType.DMA((2 * count,)),
        ],
        compiler_params=pltpu.CompilerParams(vmem_limit_bytes=56 << 20),
        name="input_back",
    )(places, inputs, gain, dz, *in_own, *in_other)


def dot_nt(a, b):
    return lax.dot_general(a, b, (((1,), (1,)), ((), ())), preferred_element_type=wide)


def dot_tn(a, b):
    return lax.dot_general(a, b, (((0,), (0,)), ((), ())), preferred_element_type=wide)


def attend_kernel(
    count, places, kept, taken, vectors, vocab_bias, noise, lengths, labels, counted, *refs
):
    small, vocab = refs[: 4 * count], refs[4 * count : 4 * count + 4]
    (
        grad_own, grad_given, pack_me, pack_chip, pack_cores, seen, near, far,
        memory, decoded, grad_memory, pack, sums, w, v, sems, v_sems, mk, sk, mq, sq, mono, span, keep, queue, scaled, ratio, window, mix, pre,
        mono_squash, span_squash,
    ) = refs[4 * count + 4 :]
    rows, _ = kept.shape
    frames, group, _ = mk.shape
    block = w.shape[2] // 6
    lanes = 128
    chunks = 4 * block // lanes
    copies = []
    for r in range(4):
        arrived = []
        for k in range(count):
            source = small[r * count + k]
            height = source.shape[0]
            for h in range(source.shape[1] // (6 * block)):
                to = pl.ds(pl.multiple_of(places[2 + len(arrived)] * height, height), height)
                arrived.append(
                    pltpu.make_async_copy(
                        source.at[:, 6 * block * h : 6 * block * (h + 1)],
                        w.at[r, to, :],
                        sems.at[r, len(arrived)],
                    )
                )
        copies.append(arrived)
    vocab_copies = [pltpu.make_async_copy(vocab[r], v.at[r], v_sems.at[r]) for r in range(4)]
    for copy in sum(copies, []) + vocab_copies:
        copy.start()

    first_chip = places[1] == 0

    @pl.when(first_chip)
    def _():
        memory[...] = kept[...]
        decoded[...] = taken[...]

    @pl.when(jnp.logical_not(first_chip))
    def _():
        memory[...] = taken[...]
        decoded[...] = kept[...]

    def split(value):
        return value.reshape(frames, group, value.shape[-1])

    mem, dec = memory[...], decoded[...]
    for r in range(4):
        for copy in copies[r]:
            copy.wait()
        cols = pl.ds(r * block, block)
        keys = jnp.dot(mem, w[r, :, : 2 * block], preferred_element_type=wide)
        queries = jnp.dot(dec, w[r, :, 2 * block : 5 * block], preferred_element_type=wide)
        mk[:, :, cols] = split(keys[:, :block])
        sk[:, :, cols] = split(keys[:, block:])
        mq[:, :, cols] = split(queries[:, :block] + vectors[0:1, cols])
        sq[:, :, cols] = split(queries[:, block : 2 * block] + vectors[2:3, cols])
        pre[:, cols] = queries[:, 2 * block :] + vectors[4:5, cols]

    def lane(c):
        return pl.ds(c * lanes, lanes)

    def spread(row, c):
        return jnp.broadcast_to(vectors[row : row + 1, lane(c)], (group, lanes))

    def energies(queries, keys, vec_row, energy, kept_squash):
        weights = [spread(vec_row, c) for c in range(chunks)]

        def one(i, carried):
            query = [queries[i, :, lane(c)] for c in range(chunks)]
            for j in range(frames):
                total = None
                for c in range(chunks):
                    squash = jnp.tanh(query[c] + keys[j, :, lane(c)])
                    kept_squash[i * frames + j, :, lane(c)] = squash
                    part = squash * weights[c]
                    total = part if total is None else total + part
                energy[i * frames + j] = jnp.broadcast_to(
                    jnp.sum(total, axis=-1, keepdims=True), (group, lanes)
                )
            return carried

        lax.fori_loop(0, frames, one, 0)

    energies(mq, mk, 1, mono, mono_squash)
    energies(sq, sk, 3, span, span_squash)

    length = lengths[...]
    valid = [(length > j) for j in range(frames)]
    ones = jnp.ones((group, lanes), wide)
    zeros = jnp.zeros((group, lanes), wide)
    live = [jnp.where(valid[j], 1.0, 0.0).astype(wide) for j in range(frames)]
    diagonal = lax.broadcasted_iota(jnp.int32, (group, lanes), 1) - lax.broadcasted_iota(
        jnp.int32, (group, lanes), 0
    )

    def attend(i, previous):
        base = i * frames
        top = jnp.full((group, lanes), -1e30, wide)
        for j in range(frames):
            top = jnp.maximum(top, jnp.where(valid[j], span[base + j], -1e30))
        weight = [jnp.where(valid[j], jnp.exp(span[base + j] - top), 0.0) for j in range(frames)]
        current, ratios = [], []
        queued = previous[0]
        for j in range(frames):
            prob = sigmoid(mono[base + j] + offset + noise[base + j]) * live[j]
            keep[base + j] = prob
            queue[base + j] = queued
            alpha = prob * queued
            current.append(alpha)
            if j + 1 < frames:
                queued = (1.0 - prob) * queued + previous[j + 1]
            both = weight[j] + weight[j - 1] if j else weight[j]
            both = jnp.where(valid[j], both, 1.0)
            window[base + j] = both
            scaled[base + j] = weight[j]
            quotient = alpha / both
            ratio[base + j] = quotient
            ratios.append(quotient)
        row = zeros
        for j in range(frames):
            beta = weight[j] * (ratios[j] + (ratios[j + 1] if j + 1 < frames else zeros))
            row = jnp.where(diagonal == group * j, beta, row)
        mix[i] = row
        return tuple(current)

    lax.fori_loop(0, frames, attend, tuple([ones] + [zeros] * (frames - 1)))

    beta_low = mix[...].reshape(rows, lanes)[:, :rows].astype(low)
    context = jnp.dot(beta_low, mem, preferred_element_type=wide).astype(low)
    seen[0] = context
    for r in range(4):
        cols = pl.ds(r * block, block)
        value = jnp.tanh(
            pre[:, cols] + jnp.dot(context, w[r, :, 5 * block :], preferred_element_type=wide)
        )
        pre[:, cols] = value
        pack[r, :, 5 * block :] = value.astype(low)
    logits = vocab_bias[...]
    for r in range(4):
        vocab_copies[r].wait()
        logits = logits + jnp.dot(pack[r, :, 5 * block :], v[r], preferred_element_type=wide)
    shifted = jnp.exp(logits - jnp.max(logits, axis=-1, keepdims=True))
    softmax = shifted / jnp.sum(shifted, axis=-1, keepdims=True)
    onehot = (labels[...] == lax.broadcasted_iota(jnp.int32, softmax.shape, 1)).astype(wide)
    grad_logits = ((softmax - onehot) * counted[...]).astype(low)
    seen[1] = grad_logits
    sums[5:6, :] = jnp.sum(grad_logits.astype(wide), axis=0, keepdims=True)
    sums[6:8, :] = jnp.zeros((2, sums.shape[1]), wide)

    grad_context = jnp.zeros((rows, memory.shape[1]), wide)
    for r in range(4):
        cols = pl.ds(r * block, block)
        value = pre[:, cols]
        grad_pre = (dot_nt(grad_logits, v[r]) * (1.0 - value * value)).astype(low)
        pack[r, :, 4 * block : 5 * block] = grad_pre
        sums[4:5, cols] = jnp.sum(grad_pre.astype(wide), axis=0, keepdims=True)
        grad_context = grad_context + dot_nt(grad_pre, w[r, :, 5 * block :])
    upper = grad_context.astype(low)
    lower = (grad_context - upper.astype(wide)).astype(low)
    grad_memory[...] = dot_tn(beta_low, upper) + dot_tn(beta_low, lower)
    cross = dot_nt(upper, mem) + dot_nt(lower, mem)
    if rows < lanes:
        cross = jnp.concatenate([cross, jnp.zeros((rows, lanes - rows), wide)], axis=1)
    mix[...] = split(cross)

    def unattend(k, later):
        i = frames - 1 - k
        base = i * frames
        cross_row = mix[i]
        grad_beta = [
            jnp.broadcast_to(
                jnp.sum(
                    jnp.where(diagonal == group * j, cross_row, 0.0), axis=-1, keepdims=True
                ),
                (group, lanes),
            )
            for j in range(frames)
        ]
        weight = [scaled[base + j] for j in range(frames)]
        share = [ratio[base + j] for j in range(frames)]
        direct, from_window, grad_weight = [], [], []
        for j in range(frames):
            grad_ratio = grad_beta[j] * weight[j]
            if j:
                grad_ratio = grad_ratio + grad_beta[j - 1] * weight[j - 1]
            pull = grad_ratio / window[base + j]
            direct.append(pull)
            from_window.append(jnp.where(valid[j], -pull * share[j], 0.0))
            grad_weight.append(
                grad_beta[j] * (share[j] + (share[j + 1] if j + 1 < frames else zeros))
            )
        top = jnp.full((group, lanes), -1e30, wide)
        for j in range(frames):
            top = jnp.maximum(top, jnp.where(valid[j], span[base + j], -1e30))
        total, ties, at_top, through = zeros, zeros, [], []
        for j in range(frames):
            pulled = grad_weight[j] + from_window[j]
            if j + 1 < frames:
                pulled = pulled + from_window[j + 1]
            pulled = weight[j] * pulled
            through.append(pulled)
            total = total + pulled
            hit = jnp.where(span[base + j] == top, live[j], 0.0)
            at_top.append(hit)
            ties = ties + hit
        back = total / ties
        for j in range(frames):
            span[base + j] = through[j] - at_top[j] * back
        grad_queue = zeros
        now = [None] * frames
        for j in reversed(range(frames)):
            prob = keep[base + j]
            grad_alpha = direct[j] + later[j]
            mono[base + j] = queue[base + j] * (grad_alpha - grad_queue) * prob * (1.0 - prob)
            grad_queue = prob * grad_alpha + (1.0 - prob) * grad_queue
            now[j] = grad_queue
        return tuple(now)

    lax.fori_loop(0, frames, unattend, tuple([zeros] * frames))

    def energy_back(queries, keys, energy, kept_squash, bias_row, vec_row):
        def one_chunk(c, carried):
            at = pl.ds(pl.multiple_of(c * lanes, lanes), lanes)
            weight = jnp.broadcast_to(vectors[vec_row : vec_row + 1, at], (group, lanes))

            def one(i, carry):
                grad_keys, vec_total, bias_total = carry
                grad_query = zeros
                new_keys = []
                for j in range(frames):
                    squash = kept_squash[i * frames + j, :, at]
                    grad = energy[i * frames + j]
                    scaled_squash = grad * squash
                    vec_total = vec_total + scaled_squash
                    inner = grad - scaled_squash * squash
                    grad_query = grad_query + inner
                    new_keys.append(grad_keys[j] + inner)
                queries[i, :, at] = grad_query * weight
                return (tuple(new_keys), vec_total, bias_total + grad_query)

            grad_keys, vec_total, bias_total = lax.fori_loop(
                0, frames, one, (tuple([zeros] * frames), zeros, zeros)
            )
            for j in range(frames):
                keys[j, :, at] = grad_keys[j] * weight
            sums[bias_row : bias_row + 1, at] = jnp.sum(bias_total * weight, axis=0, keepdims=True)
            sums[vec_row : vec_row + 1, at] = jnp.sum(vec_total, axis=0, keepdims=True)
            return carried

        lax.fori_loop(0, chunks, one_chunk, 0)

    energy_back(mq, mk, mono, mono_squash, 0, 1)
    energy_back(sq, sk, span, span_squash, 2, 3)

    total_memory = grad_memory[...]
    total_decoded = jnp.zeros_like(total_memory)
    for r in range(4):
        cols = pl.ds(r * block, block)
        for n, source in enumerate((mk, sk, mq, sq)):
            pack[r, :, n * block : (n + 1) * block] = (
                source[:, :, cols].reshape(rows, block).astype(low)
            )
        total_memory = total_memory + dot_nt(pack[r, :, : 2 * block], w[r, :, : 2 * block])
        total_decoded = total_decoded + dot_nt(
            pack[r, :, 2 * block : 5 * block], w[r, :, 2 * block : 5 * block]
        )
    pack_me[...] = pack[0]
    pack_chip[...] = pack[1]
    pack_cores[...] = pack[2:4]
    middle = 2 * block
    near[...] = sums[:, :middle]
    far[:8, :] = sums[:, middle:]
    far[8:9, :] = sums[5:6, :middle]
    far[9:10, :] = sums[5:6, middle:]
    far[10:, :] = jnp.zeros((6, middle), wide)
    grad_own[...] = jnp.where(first_chip, total_memory, total_decoded)
    grad_given[...] = jnp.where(first_chip, total_decoded, total_memory).astype(low)


def run_attend(
    places, kept, taken, smalls, vocab, vectors, vocab_bias, noise, lengths, labels, counted,
    frames,
):
    rows, width = kept.shape
    group = rows // frames
    full = vectors.shape[1]
    vocab_width = vocab[0].shape[1]
    cell = (frames * frames, group, 128)
    count = len(smalls[0])
    return pl.pallas_call(
        functools.partial(attend_kernel, count),
        out_shape=(
            jax.ShapeDtypeStruct((rows, width), wide),
            jax.ShapeDtypeStruct((rows, width), low),
            jax.ShapeDtypeStruct((rows, full // 4 * 6), low),
            jax.ShapeDtypeStruct((rows, full // 4 * 6), low),
            jax.ShapeDtypeStruct((2, rows, full // 4 * 6), low),
            jax.ShapeDtypeStruct((2, rows, vocab_width), low),
            jax.ShapeDtypeStruct((8, full // 2), wide),
            jax.ShapeDtypeStruct((16, full // 2), wide),
        ),
        in_specs=[in_smem] + [in_vmem] * 8 + [in_place] * (4 * count + 4),
        out_specs=[in_vmem] * 8,
        scratch_shapes=[
            pltpu.VMEM((rows, width), low),
            pltpu.VMEM((rows, width), low),
            pltpu.VMEM((rows, width), wide),
            pltpu.VMEM((4, rows, full // 4 * 6), low),
            pltpu.VMEM((8, full), wide),
            pltpu.VMEM((4, width, full // 4 * 6), low),
            pltpu.VMEM((4,) + vocab[0].shape, low),
            pltpu.SemaphoreType.DMA((4, places.shape[0] - 2)),
            pltpu.SemaphoreType.DMA((4,)),
        ]
        + [pltpu.VMEM((frames, group, full), wide)] * 4
        + [pltpu.VMEM(cell, wide)] * 7
        + [pltpu.VMEM((frames, group, 128), wide), pltpu.VMEM((rows, full), wide)]
        + [pltpu.VMEM((frames * frames, group, full), wide)] * 2,
        compiler_params=pltpu.CompilerParams(vmem_limit_bytes=56 << 20),
        name="attend",
    )(
        places, kept, taken, vectors, vocab_bias, noise, lengths, labels, counted,
        *sum(smalls, []), *vocab,
    )


def gradient_kernel(
    order, before, before_peer, normed, normed_peer, dz, dz_peer, states_own, states_core,
    seen, seen_core, far, far_core, pack_me, pack_core, pack_far, *refs
):
    outputs, paired = refs[:8], refs[8:12]
    a_rec, a_in, a_dz, states, a_context, a_grads, a_pack, block, paired_block, sems, out_sems = (
        refs[12:]
    )
    y = order[0]
    height = block.shape[1]
    wide_half = a_dz.shape[1]
    part = a_pack.shape[1] // 6
    width = a_rec.shape[1]
    jobs = []
    for sources, target in (
        ((dz.at[0], dz_peer), a_dz),
        ((before, before_peer), a_rec),
        ((normed, normed_peer), a_in),
        (
            (states_own.at[0], states_core.at[0], states_own.at[2], states_core.at[2]),
            states.at[y],
        ),
        (
            (
                states_own.at[1], states_core.at[1],
                states_own.at[3], states_core.at[3],
            ),
            states.at[1 - y],
        ),
        ((pack_me, pack_core.at[0], pack_far.at[0], pack_far.at[1]), a_pack),
        ((seen.at[0], seen_core.at[0], far.at[0, :, :width], far_core.at[0, :, :width]), a_context),
        ((seen.at[1], seen_core.at[1], far.at[1, :, :width], far_core.at[1, :, :width]), a_grads),
    ):
        rows = target.shape[0] // len(sources)
        for r, source in enumerate(sources):
            jobs.append(
                pltpu.make_async_copy(
                    source, target.at[r * rows : (r + 1) * rows, :], sems.at[len(jobs)]
                )
            )
    for job in jobs:
        job.start()
    for job in jobs[:6]:
        job.wait()
    both = 2 * wide_half

    def one(n, carried):
        cols = pl.ds(pl.multiple_of(order[1 + n] * height, height), height)
        pair = jnp.concatenate([a_rec[:, cols], a_in[:, cols]], axis=1)
        for at in range(0, wide_half, 1024):
            value = dot_tn(pair, a_dz[:, at : at + 1024]).astype(low)
            block[n, :, at : at + 1024] = value[:height]
            block[n, :, wide_half + at : wide_half + at + 1024] = value[height:]
        for m, output in enumerate(outputs):

            @pl.when(n == m)
            def _(m=m, output=output):
                pltpu.make_async_copy(
                    block.at[m, :, :both], output.at[:, :both], out_sems.at[m]
                ).start()

        return carried

    lax.fori_loop(0, 8, one, 0)
    for job in jobs[6:]:
        job.wait()

    def two(n, carried):
        cols = pl.ds(pl.multiple_of(order[1 + n] * height, height), height)
        for m in range(2):
            to = both + 2 * m * part
            block[n, :, to : to + 2 * part] = dot_tn(
                states[m, :, cols], a_pack[:, 2 * m * part : 2 * (m + 1) * part]
            ).astype(low)
        for m, output in enumerate(outputs):

            @pl.when(n == m)
            def _(m=m, output=output):
                pltpu.make_async_copy(
                    block.at[m, :, both:], output.at[:, both:], out_sems.at[12 + m]
                ).start()

        return carried

    lax.fori_loop(0, 8, two, 0)

    def pair(n, carried):
        cols = pl.ds(pl.multiple_of(order[9 + n] * 2 * height, 2 * height), 2 * height)
        grad_pre = a_pack[:, 4 * part : 5 * part]
        for m, (a, b) in enumerate(
            (
                (states[1, :, cols], grad_pre),
                (a_context[:, cols], grad_pre),
                (a_grads[:, cols], a_pack[:, 5 * part :]),
            )
        ):
            paired_block[n, :, m * part : (m + 1) * part] = dot_tn(a, b).astype(low)
        return carried

    lax.fori_loop(0, 4, pair, 0)
    for m, output in enumerate(paired):
        pltpu.make_async_copy(paired_block.at[m], output, out_sems.at[8 + m]).start()
    for m, output in enumerate(outputs):
        pltpu.make_async_copy(
            block.at[m, :, :both], output.at[:, :both], out_sems.at[m]
        ).wait()
        pltpu.make_async_copy(
            block.at[m, :, both:], output.at[:, both:], out_sems.at[12 + m]
        ).wait()
    for m, output in enumerate(paired):
        pltpu.make_async_copy(paired_block.at[m], output, out_sems.at[8 + m]).wait()


def run_gradients(order, *arrays):
    rows, width = arrays[0].shape
    wide_half = arrays[5].shape[1]
    part = arrays[12].shape[1] // 6
    columns = 2 * wide_half + 4 * part
    height = width // 8
    deep = 2 * rows
    return pl.pallas_call(
        gradient_kernel,
        out_shape=tuple(
            [jax.ShapeDtypeStruct((height, columns), low)] * 8
            + [jax.ShapeDtypeStruct((2 * height, 3 * part), low)] * 4
        ),
        in_specs=[in_smem] + [in_place] * 15,
        out_specs=[in_place] * 12,
        scratch_shapes=[
            pltpu.VMEM((deep, width), low),
            pltpu.VMEM((deep, width), low),
            pltpu.VMEM((deep, wide_half), low),
            pltpu.VMEM((2, deep, width), low),
            pltpu.VMEM((deep, width), low),
            pltpu.VMEM((deep, width), low),
            pltpu.VMEM((deep, 6 * part), low),
            pltpu.VMEM((8, height, columns), low),
            pltpu.VMEM((4, 2 * height, 3 * part), low),
            pltpu.SemaphoreType.DMA((26,)),
            pltpu.SemaphoreType.DMA((20,)),
        ],
        compiler_params=pltpu.CompilerParams(vmem_limit_bytes=56 << 20),
        name="weight_gradients",
    )(order, *arrays)


def local(
    dp,
    block_input, norm_gain, lstm_in, lstm_rec, lstm_bias,
    mono_mem, mono_dec, mono_bias, mono_vec, span_mem, span_dec, span_bias, span_vec,
    out_weight, out_bias, vocab_weight, vocab_bias, noise, enc_lengths, label_lengths, labels,
):
    ring = Ring(dp)
    s, y = lax.axis_index("section"), lax.axis_index("mp")
    _, utts, frames, width = block_input.shape
    half, quarter = utts // 2, utts // 4
    rows = frames * quarter
    shard_rows, _, unit_half = lstm_in.shape[1:]
    wide_half = 4 * unit_half
    block = mono_mem.shape[1]
    vocab_size = vocab_weight.shape[1]
    vocab_pad = 4 * block

    in_shard = lstm_in[0].reshape(shard_rows, wide_half)
    rec_shard = lstm_rec[0].reshape(shard_rows, wide_half)
    bias_shard = lstm_bias[0].reshape(1, wide_half)

    def of_section(array):
        return jnp.where(s == y, array, across_cores(array))

    inputs = of_section(jnp.swapaxes(block_input[0], 0, 1))
    gain = of_section(norm_gain[0])
    inputs_own = lax.dynamic_slice_in_dim(inputs, s * half, half, axis=1)
    inputs_other = lax.dynamic_slice_in_dim(inputs, (1 - s) * half, half, axis=1)
    normed_own = normalize(inputs_own.astype(wide), gain)
    normed_own = normed_own.astype(low).reshape(frames * half, width)
    normed_other = normalize(inputs_other.astype(wide), gain)
    normed_other = normed_other.astype(low).reshape(frames * half, width)

    start = s * half + y * quarter
    noise_part = jnp.transpose(
        lax.dynamic_slice_in_dim(noise, start, quarter, axis=0), (1, 2, 0)
    ).reshape(frames * frames, quarter, 1)
    noise_part = jnp.broadcast_to(noise_part, (frames * frames, quarter, 128))
    length_part = lax.dynamic_slice_in_dim(enc_lengths, start, quarter, axis=0)
    length_part = jnp.broadcast_to(length_part[:, None], (quarter, 128))
    label_part = lax.dynamic_slice_in_dim(labels, start, quarter, axis=0).T.reshape(rows, 1)
    count_part = lax.dynamic_slice_in_dim(label_lengths, start, quarter, axis=0)
    counted = (jnp.arange(frames)[:, None] < count_part[None, :]).astype(wide).reshape(rows, 1)
    bias_row = jnp.pad(vocab_bias, (0, vocab_pad - vocab_size), constant_values=-1e30)[None]

    vector_own = jnp.stack([mono_bias, mono_vec, span_bias, span_vec, out_bias])
    vocab_own = jnp.pad(vocab_weight, ((0, 0), (0, vocab_pad - vocab_size)))
    ready = (noise_part, length_part, label_part, counted, bias_row, normed_own, normed_other)
    places, in_own, rec_own, small_own, small_chip = [], [], [], [], []
    small = jnp.concatenate(
        [
            mono_mem, span_mem, mono_dec, span_dec,
            out_weight[0], out_weight[1],
        ],
        axis=1,
    )
    if ring.short:
        flow, across, onward = Flow(), ring.across, ring.onward
        both = 2 * wide_half
        for k in range(ring.outer):
            places += [ring.back(k) * 2 + ring.x, ring.back(k) * 2 + 1 - ring.x]
        places = jnp.stack([s, y] + places).astype(jnp.int32)
        corner = jnp.concatenate([in_shard, rec_shard], axis=1)
        small = jnp.concatenate(
            [
                tie(mono_mem, corner), span_mem, mono_dec, span_dec, out_weight[0], out_weight[1]
            ],
            axis=1,
        )
        corner, small_far, small_next = corners(corner), across(small), onward(small)
        flow.landed = (corner, small_far, small_next)
        small_own = [jnp.concatenate([small, small_far], axis=1)]
        small_chip, small_core = [], []
        held = jnp.concatenate([corner, small_next], axis=1)
        near, far, near_core, far_core = [], [], [], []
        for k in range(ring.outer):
            near.append(held)
            jobs = [(across, held), (across_chips, small_own[k])]
            if k < ring.outer - 1:
                jobs.append((onward, held[:, :both] if k == ring.outer - 2 else held))
            if k == 0:
                jobs += [(across_chips, vocab_own), (corners, bias_shard)]
            if k == 1:
                jobs.append((across_chips, vector_own))
            also = ready if k == 1 else ()
            if k == ring.outer - 1:
                vectors = jnp.concatenate([vector_pair, across_cores(vector_pair)], axis=1)
                vectors = jnp.pad(vectors, ((0, 3), (0, 0)))
                also = (vectors, places)
            results = flow.step(*jobs, also=also)
            far.append(results[0])
            small_chip.append(results[1])
            if k == 0:
                vocab_chip, b_own = results[3], results[4].astype(wide)
            if k == 1:
                vector_pair = jnp.concatenate([vector_own, results[3]], axis=1)
            if k < ring.outer - 1:
                small_own.append(jnp.concatenate([held[:, both:], far[k][:, both:]], axis=1))
                held = results[2]
        for a, b in zip(near, far):
            near_core.append(across_cores(a))
            far_core.append(across_cores(b))
        small_core = [across_cores(a) for a in small_own]
        b_last, vocab_last, chip_last = lax.optimization_barrier(
            (b_own, vocab_own, vocab_chip, held)
        )[:3]
        b_other = across_cores(b_last)
        vocab = [vocab_own, vocab_chip, across_cores(vocab_last), across_cores(chip_last)]
        in_own = [a for pair in zip(near, far) for a in pair]
        in_other = [a for pair in zip(near_core, far_core) for a in pair]
        rec_own, rec_other, rec_column = in_own, in_other, wide_half
    else:
        vocab_chip = across_chips(vocab_own)
        small, in_block, rec_block = [
            lax.all_gather(a, "dp", axis=0, tiled=True)
            for a in (small, corners(in_shard), corners(rec_shard))
        ]
        places, in_own, rec_own = [jnp.int32(0)], [in_block], [rec_block]
        small_own, small_chip = [small], [across_chips(small)]
        vocab = [vocab_own, vocab_chip, across_cores(vocab_own), across_cores(vocab_chip)]
        in_other, rec_other, rec_column = [across_cores(in_block)], [across_cores(rec_block)], 0
        small_core = [across_cores(small)]
        b_own = corners(bias_shard).astype(wide)
        b_other = across_cores(b_own)
        vector_pair = across_chips(vector_own)
        vector_pair = jnp.concatenate([vector_own, vector_pair], axis=1)
        vectors = jnp.concatenate([vector_pair, across_cores(vector_pair)], axis=1)
        vectors = jnp.pad(vectors, ((0, 3), (0, 0)))
        places = jnp.stack([s, y] + places).astype(jnp.int32)
    places = tie(places, vectors, *vocab, *ready, *small_chip[:-1], *small_core)

    kept, given, before, gates, cells = run_forward(
        places, normed_own, b_own, b_other, in_own, in_other, rec_own, rec_other, frames,
        rec_column,
    )

    kept, given = kept.reshape(rows, width), given.reshape(rows, width)
    taken = across_chips(given)
    small_chip[-1] = tie(small_chip[-1], kept)
    small_both = [across_cores(part) for part in small_chip]
    smalls = [small_own, small_chip, small_core, small_both]
    grad_own, grad_given, pack_me, pack_chip, pack_cores, seen, near, far = run_attend(
        places, kept, taken, smalls, vocab, vectors, bias_row, noise_part, length_part,
        label_part, counted, frames,
    )
    grad_given, kept_far = lax.optimization_barrier((grad_given, across_chips(tie(kept, taken))))
    grad_taken = across_chips(grad_given)
    pack_core = across_cores(pack_cores)
    pack_out = jnp.stack([pack_chip, pack_core[1]])
    far_peer = across_cores(far)
    vector_pair = (near[:5] + far_peer[:5]).reshape(5, 2, block)
    bias_pair = (far[8:10] + far_peer[8:10]).reshape(-1)
    vector_out = jnp.concatenate([vector_pair[:, 1].reshape(-1), bias_pair])
    vector_count = vector_out.shape[0] // (2 * rows)
    seen_out = jnp.concatenate(
        [seen, halves(vector_out, 2 * rows).reshape(2, rows, -1)], axis=2
    )
    before = before.reshape(frames * half, width)
    before_peer = across_cores(tie(before, taken))
    states = jnp.stack([tie(kept, grad_given), taken, given, kept_far])
    states_core, seen_core = across_cores(states), across_cores(seen)
    places_back, pack_out, seen_out = lax.optimization_barrier(
        (places, pack_out, seen_out, grad_taken, before_peer, states_core, seen_core)
    )[:3]
    dz = run_backward(
        places_back, grad_own.reshape(frames, quarter, width),
        grad_taken.reshape(frames, quarter, width), gates, cells, rec_own, rec_other, rec_column,
    )
    pack_far = across_chips(pack_out)
    seen_far = across_chips(tie(seen_out, pack_out))

    dz = dz.reshape(2, frames * half, wide_half)
    dz, pack_far, seen_far = lax.optimization_barrier((dz, pack_far, seen_far))
    dz_peer = across_cores(dz[1])
    grad_inputs, grad_gain = run_input(
        places, inputs_own.reshape(frames * half, width), gain[None], dz, in_own, in_other
    )
    grad_gain = grad_gain.reshape(width)
    z, x = ring.z, ring.x
    if ring.short:
        steps_back = [ring.back(k) for k in range(1, 5)]
        order = [at * 2 + 1 - x for at in steps_back] + [at * 2 + x for at in steps_back]
        order = [y] + order + steps_back
    else:
        order = [y] + [jnp.int32(k) for k in [*range(8), *range(4)]]
    totals = run_gradients(
        tie(jnp.stack(order).astype(jnp.int32), grad_gain), before, before_peer, normed_own, normed_other, dz,
        dz_peer, states, states_core, seen, seen_core, seen_far, across_cores(seen_far),
        pack_me, pack_core, pack_far,
    )
    grad_inputs = jnp.swapaxes(grad_inputs.reshape(frames, half, width), 0, 1)
    vector_far = joined(seen_far[:, :, width:].reshape(2 * rows, -1), vector_count).reshape(-1)

    sides_at = 5 * block + vocab_pad
    grad_peer = across_cores(grad_inputs)
    grad_section = jnp.concatenate(
        [
            jnp.where(s == 0, grad_inputs, grad_peer),
            jnp.where(s == 0, grad_peer, grad_inputs),
        ],
        axis=0,
    )
    gain_sum = grad_gain + across_cores(grad_gain)
    flat = jnp.concatenate(
        [
            vector_pair[:, 0].reshape(-1) + vector_far[: 5 * block],
            bias_pair + vector_far[5 * block :],
            jnp.sum(dz[0].astype(wide), axis=0) + jnp.sum(dz_peer.astype(wide), axis=0),
            gain_sum,
        ]
    )
    flat = jnp.pad(flat, (0, -flat.shape[0] % (8 * shard_rows)))

    def to_other_chip(section):
        return lax.ppermute(section, ("section", "mp"), [(0, 1), (3, 2)])

    if ring.short:
        r = shard_rows
        both, width_out = 2 * wide_half, 2 * block
        flow, across, onward = Flow(), ring.across, ring.onward
        theirs, mine, outputs = totals[:4], totals[4:8], totals[8:]

        def total(k, arrived, passed):
            value = mine[k - 1].astype(wide) + arrived.astype(wide)
            return value if passed is None else value + passed.astype(wide)

        def cornered(hop):
            index = lambda at, place, chip: (at * ring.dp + place) * 2 + chip
            pairs = [
                (index(p, a, q), index(q, b, p)) for a, b in hop for p in range(2) for q in range(2)
            ]
            return lambda array: lax.ppermute(array, ("section", "dp", "mp"), pairs)

        arrived, out_two, out_before = flow.step(
            (across, theirs[0]), (onward, outputs[1]), (ring.astern, outputs[0])
        )
        grad_far = to_other_chip(grad_section)
        flat = flat.reshape(8, -1)
        flat = flat + across(flat)
        flow.landed = (arrived,)
        value = total(1, arrived, None).astype(low)
        out = (outputs[2].astype(wide) + out_two.astype(wide)).astype(low)
        passed, arrived, out_one = flow.step((onward, value), (across, theirs[1]), (onward, out))
        flat_one, flat_three = onward(flat), ring.astern(flat)
        out = outputs[3].astype(wide) + out_before.astype(wide) + out_one.astype(wide)
        vocab_rows = out[:, width_out:].astype(low)
        message = jnp.concatenate(
            [cut(out, 1 - x, r)[:, :width_out].astype(low), vocab_rows[:r], vocab_rows[r:]], axis=1
        )
        value = total(2, arrived, passed).astype(low)
        passed, arrived, out_far, kept_rows = flow.step(
            (onward, value), (across, theirs[2]), (across, message), (corners, mine[3][:, :both]),
            also=(flat_one, flat_three),
        )
        flat = flat + flat_one + flat_three + onward(flat_one)
        output_grad = cut(out, x, r)[:, :width_out] + out_far[:, :width_out].astype(wide)
        shard = jnp.concatenate([out[:r, width_out:], out[r:, width_out:]], axis=1)
        shard = (shard + out_far[:, width_out:].astype(wide)).astype(low)
        value = total(3, arrived, passed).astype(low)
        passed, arrived, energy_passed, energy_arrived, next_three = flow.step(
            (cornered(ring.ring), value[:, :both]), (cornered(ring.pair), theirs[3][:, :both]),
            (onward, jnp.concatenate([value[:, both:], shard], axis=1)),
            (across, theirs[3][:, both:]), (ring.astern, shard),
            also=(grad_far, flat),
        )
        flat = flat.reshape(-1)
        sides = corners(tie(flat[sides_at : sides_at + wide_half + width], value))
        next_one, energy_passed = energy_passed[:, 4 * block :], energy_passed[:, : 4 * block]
        shards = {0: shard, 1: next_one, 3: next_three, 2: onward(next_one)}
        moved = kept_rows.astype(wide) + arrived.astype(wide) + passed.astype(wide)
        energy_grad = mine[3][:, both:].astype(wide) + energy_arrived.astype(wide)
        energy_grad = energy_grad + energy_passed.astype(wide)
        vocab_grad = jnp.zeros((vocab_pad, block), low)
        for k, held in shards.items():
            held = jnp.concatenate([held[:, :block], held[:, block : 2 * block]], axis=0)
            vocab_grad = lax.dynamic_update_slice(vocab_grad, held, (ring.back(k) * 2 * r, 0))
    else:
        grad_far = to_other_chip(grad_section)

        def scatter(parts):
            total = jnp.concatenate(parts, axis=0)
            return lax.psum_scatter(total, "dp", scatter_dimension=0, tiled=True).astype(wide)

        moved, output_grad = scatter(totals[:8]), scatter(totals[8:])
        moved, energy_grad = moved[:, : 2 * wide_half], moved[:, 2 * wide_half :]
        moved = corners(moved.astype(low)).astype(wide)
        flat = lax.psum(flat, "dp")
        sides = corners(flat[sides_at : sides_at + wide_half + width])
        vocab_grad = lax.all_gather(
            output_grad[:, 2 * block :].astype(low), "dp", axis=0, tiled=True
        )

    input_grad = jnp.where(s == y, grad_section, grad_far)
    vocab_grad = vocab_grad.T[:, :vocab_size].astype(wide)
    vector_sum = flat[: 5 * block].reshape(5, block)
    bias_sum = flat[5 * block : 5 * block + vocab_size]
    lstm_bias_sum = sides[:wide_half].reshape(1, 4, unit_half)
    gain_sum = sides[wide_half:][None]
    rec_grad = moved[:, :wide_half].reshape(1, shard_rows, 4, unit_half)
    in_grad = moved[:, wide_half:].reshape(1, shard_rows, 4, unit_half)
    mono_mem_grad, span_mem_grad, mono_dec_grad, span_dec_grad = [
        energy_grad[:, n * block : (n + 1) * block] for n in range(4)
    ]
    return (
        input_grad[None],
        gain_sum,
        in_grad,
        rec_grad,
        lstm_bias_sum,
        mono_mem_grad,
        mono_dec_grad,
        vector_sum[0],
        vector_sum[1],
        span_mem_grad,
        span_dec_grad,
        vector_sum[2],
        vector_sum[3],
        jnp.stack([output_grad[:, :block], output_grad[:, block : 2 * block]]),
        vector_sum[4],
        vocab_grad,
        bias_sum,
    )


def solution(mesh):
    both = ("section", "mp")
    in_specs = (
        P("section", "dp", None, None),
        P("section", None),
        P("section", "dp", None, "mp"),
        P("section", "dp", None, "mp"),
        P("section", None, "mp"),
        P("dp", both),
        P("dp", both),
        P(both),
        P(both),
        P("dp", both),
        P("dp", both),
        P(both),
        P(both),
        P(None, "dp", both),
        P(both),
        P(both, None),
        P(),
        P("dp", None, None),
        P("dp"),
        P("dp"),
        P("dp", None),
    )
    out_specs = (
        P("section", "dp", None, None),
        P("section", None),
        P("section", "dp", None, "mp"),
        P("section", "dp", None, "mp"),
        P("section", None, "mp"),
        P("dp", both),
        P("dp", both),
        P(both),
        P(both),
        P("dp", both),
        P("dp", both),
        P(both),
        P(both),
        P(None, "dp", both),
        P(both),
        P(both, None),
        P(),
    )
    dp = mesh.shape["dp"]

    def step(*arrays):
        return local(dp, *arrays)

    return jax.shard_map(step, mesh=mesh, in_specs=in_specs, out_specs=out_specs, check_vma=False)
```

```python
import functools

import jax
import jax.numpy as jnp
from jax import lax
from jax.experimental import pallas as pl
from jax.experimental.pallas import tpu as pltpu
from jax.sharding import PartitionSpec as P

epsilon = 1e-05
offset = -4.0
wide = jnp.float32
low = jnp.bfloat16
in_vmem = pl.BlockSpec(memory_space=pltpu.VMEM)
in_smem = pl.BlockSpec(memory_space=pltpu.SMEM)
in_place = pl.BlockSpec(memory_space=pl.ANY)
core_swap = [(0, 1), (1, 0)]
corner_swap = [(0, 0), (1, 2), (2, 1), (3, 3)]


def normalize(inputs, gain_row):
    average = jnp.mean(inputs, axis=-1, keepdims=True)
    centred = inputs - average
    spread = jnp.mean(centred * centred, axis=-1, keepdims=True)
    return centred * lax.rsqrt(spread + epsilon) * gain_row


def across_cores(array):
    return lax.ppermute(array, "section", core_swap)


def across_chips(array):
    return lax.ppermute(array, "mp", core_swap)


def corners(array):
    return lax.ppermute(array, ("section", "mp"), corner_swap)


def tie(value, *others):
    return lax.optimization_barrier((value,) + others)[0]


def cut(array, block, rows):
    return lax.dynamic_slice_in_dim(array, block * rows, rows, axis=0)


class Flow:
    def __init__(self):
        self.landed = ()

    def step(self, *jobs, also=()):
        operands = tuple(operand for _, operand in jobs)
        operands = lax.optimization_barrier(operands + self.landed + tuple(also))[: len(jobs)]
        results = [send(operand) for (send, _), operand in zip(jobs, operands)]
        self.landed = tuple(results)
        return results


class Ring:
    def __init__(self, dp):
        self.dp = dp
        self.outer = dp // 2
        self.short = dp % 2 == 0 and self.outer == 4
        pairs = [(z, x) for z in range(self.outer) for x in range(2)]
        self.pair = [(2 * z + x, 2 * z + 1 - x) for z, x in pairs]
        self.ring = [(2 * z + x, 2 * ((z + 1) % self.outer) + x) for z, x in pairs]
        self.turn = [(b, a) for a, b in self.ring]
        place = lax.axis_index("dp")
        self.z, self.x = place // 2, place % 2

    def across(self, array):
        return lax.ppermute(array, "dp", self.pair)

    def onward(self, array):
        return lax.ppermute(array, "dp", self.ring)

    def astern(self, array):
        return lax.ppermute(array, "dp", self.turn)

    def back(self, k):
        return lax.rem(self.z - k + self.outer, self.outer)


def halves(array, height):
    array = array.reshape(height, -1)
    upper = array.astype(low)
    lower = (array - upper.astype(wide)).astype(low)
    return jnp.pad(
        jnp.concatenate([upper, lower], axis=1), ((0, 0), (0, -2 * array.shape[1] % 128))
    )


def joined(array, count):
    return array[:, :count].astype(wide) + array[:, count : 2 * count].astype(wide)


def sigmoid(x):
    return 0.5 * jnp.tanh(0.5 * x) + 0.5


def fetch(blocks, places, side_blocks, target, sems, first=0, column=0):
    wide_half = target.shape[1] // 2
    columns = pl.ds(pl.multiple_of(side_blocks * wide_half, wide_half), wide_half)
    copies = []
    for k, block in enumerate(blocks):
        height = block.shape[0]
        span = pl.ds(pl.multiple_of(places[2 + k] * height, height), height)
        copies.append(
            pltpu.make_async_copy(
                block.at[:, column : column + wide_half],
                target.at[span, columns],
                sems.at[first + k],
            )
        )
    return copies


def forward_kernel(count, column, places, normed, b_own, b_other, *refs):
    in_own, in_other, w_own, w_other = [refs[n * count : (n + 1) * count] for n in range(4)]
    kept, given, before, gates, cells, wi, w, b, state, cell, sems = refs[4 * count :]
    steps, rows, wide_full = gates.shape
    wide_half = wide_full // 2
    unit_half = wide_half // 4
    chunk = min(256, unit_half)
    s = places[0]
    copies = fetch(in_own, places, s, wi, sems) + fetch(in_other, places, 1 - s, wi, sems, count)
    later = fetch(w_own, places, s, w, sems, 2 * count, column)
    later += fetch(w_other, places, 1 - s, w, sems, 3 * count, column)
    for copy in copies + later:
        copy.start()
    for source, at in ((b_own, s), (b_other, 1 - s)):
        b[:, pl.ds(pl.multiple_of(at * wide_half, wide_half), wide_half)] = source[...]
    state[...] = jnp.zeros_like(state)
    cell[...] = jnp.zeros_like(cell)
    for copy in copies:
        copy.wait()

    def project(g, carried):
        cols = pl.ds(pl.multiple_of(g * unit_half, unit_half), unit_half)
        value = jnp.dot(normed[...], wi[:, cols], preferred_element_type=wide) + b[:, cols]
        gates[:, :, cols] = value.reshape(steps, rows, unit_half)
        return carried

    lax.fori_loop(0, 8, project, 0)
    for copy in later:
        copy.wait()
    eighth = rows // 2
    first_chip = places[1] == 0

    def advance(t, carried):
        hidden = state[...]
        before[t] = hidden
        for at in range(0, 2 * unit_half, chunk):
            half, inside = at // unit_half, at % unit_half
            acts = []
            for g in range(4):
                cols = pl.ds(half * wide_half + g * unit_half + inside, chunk)
                value = gates[t, :, cols] + jnp.dot(
                    hidden, w[:, cols], preferred_element_type=wide
                )
                value = jnp.tanh(value) if g == 2 else sigmoid(value)
                gates[t, :, cols] = value
                acts.append(value)
            units = pl.ds(at, chunk)
            new_cell = acts[1] * cell[:, units] + acts[0] * acts[2]
            cell[:, units] = new_cell
            cells[t, :, units] = new_cell
            new_hidden = acts[3] * jnp.tanh(new_cell)
            state[:, units] = new_hidden.astype(low)
            upper, lower = new_hidden[:eighth], new_hidden[eighth:]
            kept[t, :, units] = jnp.where(first_chip, upper, lower).astype(low)
            given[t, :, units] = jnp.where(first_chip, lower, upper).astype(low)
        return carried

    lax.fori_loop(0, steps, advance, 0)


def run_forward(places, normed, b_own, b_other, in_own, in_other, w_own, w_other, steps, column):
    rows = normed.shape[0] // steps
    units = normed.shape[1]
    wide_half = b_own.shape[1]
    count = len(w_own)
    return pl.pallas_call(
        functools.partial(forward_kernel, count, column),
        out_shape=(
            jax.ShapeDtypeStruct((steps, rows // 2, units), low),
            jax.ShapeDtypeStruct((steps, rows // 2, units), low),
            jax.ShapeDtypeStruct((steps, rows, units), low),
            jax.ShapeDtypeStruct((steps, rows, 2 * wide_half), wide),
            jax.ShapeDtypeStruct((steps, rows, units), wide),
        ),
        in_specs=[in_smem] + [in_vmem] * 3 + [in_place] * (4 * count),
        out_specs=[in_vmem] * 5,
        scratch_shapes=[
            pltpu.VMEM((units, 2 * wide_half), low),
            pltpu.VMEM((units, 2 * wide_half), low),
            pltpu.VMEM((1, 2 * wide_half), wide),
            pltpu.VMEM((rows, units), low),
            pltpu.VMEM((rows, units), wide),
            pltpu.SemaphoreType.DMA((4 * count,)),
        ],
        compiler_params=pltpu.CompilerParams(vmem_limit_bytes=56 << 20),
        name="recur_forward",
    )(places, normed, b_own, b_other, *in_own, *in_other, *w_own, *w_other)


def backward_kernel(count, column, places, kept, taken, gates, cells, *refs):
    w_own, w_other = refs[:count], refs[count : 2 * count]
    dz, stage, w, dh, dc, sems = refs[2 * count :]
    steps, rows, wide_full = gates.shape
    wide_half = wide_full // 2
    unit_half = wide_half // 4
    chunk = min(256, unit_half)
    s = places[0]
    first_chip = places[1] == 0
    jobs = []
    for n, (sources, at) in enumerate(((w_own, s), (w_other, 1 - s))):
        for k, block in enumerate(sources):
            slot = n * count + k
            copy = pltpu.make_async_copy(
                block.at[:, column : column + wide_half], stage.at[slot], sems.at[slot]
            )
            copy.start()
            jobs.append((copy, slot, at, places[2 + k] * block.shape[0]))
    dh[...] = jnp.zeros_like(dh)
    dc[...] = jnp.zeros_like(dc)
    height = w_own[0].shape[0]
    piece = min(height, 128)
    for copy, slot, at, first in jobs:
        copy.wait()

        def turn(g, carried, slot=slot, at=at, first=first):
            columns = pl.ds(pl.multiple_of(g * unit_half, unit_half), unit_half)
            span = pl.ds(pl.multiple_of(at * wide_half + g * unit_half, unit_half), unit_half)
            for low_row in range(0, height, piece):
                into = pl.ds(pl.multiple_of(first + low_row, piece), piece)
                w[span, into] = stage[slot, low_row : low_row + piece, columns].T
            return carried

        lax.fori_loop(0, 4, turn, 0)

    place_of = (s, 1 - s)

    def retreat(k, carried):
        t = steps - 1 - k
        earlier = jnp.maximum(t - 1, 0)
        live = jnp.where(t > 0, 1.0, 0.0).astype(wide)
        for at in range(0, 2 * unit_half, chunk):
            half, inside = at // unit_half, at % unit_half
            units = pl.ds(at, chunk)
            ours, theirs = kept[t, :, units], taken[t, :, units].astype(wide)
            grad = dh[:, units] + jnp.concatenate(
                [jnp.where(first_chip, ours, theirs), jnp.where(first_chip, theirs, ours)], axis=0
            )
            i, f, g, o = [
                gates[t, :, pl.ds(half * wide_half + n * unit_half + inside, chunk)]
                for n in range(4)
            ]
            squash = jnp.tanh(cells[t, :, units])
            total = dc[:, units] + grad * o * (1.0 - squash * squash)
            parts = (
                total * g * i * (1.0 - i),
                total * (cells[earlier, :, units] * live) * f * (1.0 - f),
                total * i * (1.0 - g * g),
                grad * squash * o * (1.0 - o),
            )
            for n, part in enumerate(parts):
                dz[place_of[half], t, :, pl.ds(n * unit_half + inside, chunk)] = part.astype(low)
            dc[:, units] = total * f
        upper, lower = dz[place_of[0], t], dz[place_of[1], t]
        for at in range(0, 2 * unit_half, chunk):
            units = pl.ds(at, chunk)
            dh[:, units] = jnp.dot(
                upper, w[:wide_half, units], preferred_element_type=wide
            ) + jnp.dot(lower, w[wide_half:, units], preferred_element_type=wide)
        return carried

    lax.fori_loop(0, steps, retreat, 0)


def run_backward(places, kept, taken, gates, cells, w_own, w_other, column):
    steps, rows, wide_full = gates.shape
    units = cells.shape[2]
    count = len(w_own)
    return pl.pallas_call(
        functools.partial(backward_kernel, count, column),
        out_shape=jax.ShapeDtypeStruct((2, steps, rows, wide_full // 2), low),
        in_specs=[in_smem] + [in_vmem] * 4 + [in_place] * (2 * count),
        out_specs=in_vmem,
        scratch_shapes=[
            pltpu.VMEM((2 * count, units // count, wide_full // 2), low),
            pltpu.VMEM((wide_full, units), low),
            pltpu.VMEM((rows, units), wide),
            pltpu.VMEM((rows, units), wide),
            pltpu.SemaphoreType.DMA((2 * count,)),
        ],
        compiler_params=pltpu.CompilerParams(vmem_limit_bytes=56 << 20),
        name="recur_backward",
    )(places, kept, taken, gates, cells, *w_own, *w_other)


def input_kernel(count, places, inputs, gain, dz, *refs):
    in_own, in_other = refs[:count], refs[count : 2 * count]
    grad_inputs, grad_gain, wi, sems = refs[2 * count :]
    s = places[0]
    copies = fetch(in_own, places, s, wi, sems) + fetch(in_other, places, 1 - s, wi, sems, count)
    for copy in copies:
        copy.start()
    x = inputs[...].astype(wide)
    centred = x - jnp.mean(x, axis=-1, keepdims=True)
    scale = lax.rsqrt(jnp.mean(centred * centred, axis=-1, keepdims=True) + epsilon)
    shape = centred * scale
    for copy in copies:
        copy.wait()
    wide_half = wi.shape[1] // 2
    own = pl.ds(pl.multiple_of(s * wide_half, wide_half), wide_half)
    other = pl.ds(pl.multiple_of((1 - s) * wide_half, wide_half), wide_half)
    grad = dot_nt(dz[0], wi[:, own]) + dot_nt(dz[1], wi[:, other])
    grad_gain[...] = jnp.sum(grad * shape, axis=0, keepdims=True)
    pulled = grad * gain[...]
    grad_inputs[...] = scale * (
        pulled
        - jnp.mean(pulled, axis=-1, keepdims=True)
        - shape * jnp.mean(pulled * shape, axis=-1, keepdims=True)
    )


def run_input(places, inputs, gain, dz, in_own, in_other):
    count = len(in_own)
    rows, width = inputs.shape
    return pl.pallas_call(
        functools.partial(input_kernel, count),
        out_shape=(
            jax.ShapeDtypeStruct((rows, width), wide),
            jax.ShapeDtypeStruct((1, width), wide),
        ),
        in_specs=[in_smem] + [in_vmem] * 3 + [in_place] * (2 * count),
        out_specs=[in_vmem] * 2,
        scratch_shapes=[
            pltpu.VMEM((width, 2 * dz.shape[2]), low),
            pltpu.SemaphoreType.DMA((2 * count,)),
        ],
        compiler_params=pltpu.CompilerParams(vmem_limit_bytes=56 << 20),
        name="input_back",
    )(places, inputs, gain, dz, *in_own, *in_other)


def dot_nt(a, b):
    return lax.dot_general(a, b, (((1,), (1,)), ((), ())), preferred_element_type=wide)


def dot_tn(a, b):
    return lax.dot_general(a, b, (((0,), (0,)), ((), ())), preferred_element_type=wide)


def attend_kernel(
    count, places, kept, taken, vectors, vocab_bias, noise, lengths, labels, counted, *refs
):
    small, vocab = refs[: 4 * count], refs[4 * count : 4 * count + 4]
    (
        grad_own, grad_given, pack_me, pack_chip, pack_cores, seen, near, far,
        memory, decoded, grad_memory, pack, sums, w, v, sems, v_sems, mk, sk, mq, sq, mono, span, keep, queue, scaled, ratio, window, mix, pre,
        mono_squash, span_squash,
    ) = refs[4 * count + 4 :]
    rows, _ = kept.shape
    frames, group, _ = mk.shape
    block = w.shape[2] // 6
    lanes = 128
    chunks = 4 * block // lanes
    copies = []
    for r in range(4):
        arrived = []
        for k in range(count):
            source = small[r * count + k]
            height = source.shape[0]
            for h in range(source.shape[1] // (6 * block)):
                to = pl.ds(pl.multiple_of(places[2 + len(arrived)] * height, height), height)
                arrived.append(
                    pltpu.make_async_copy(
                        source.at[:, 6 * block * h : 6 * block * (h + 1)],
                        w.at[r, to, :],
                        sems.at[r, len(arrived)],
                    )
                )
        copies.append(arrived)
    vocab_copies = [pltpu.make_async_copy(vocab[r], v.at[r], v_sems.at[r]) for r in range(4)]
    for copy in sum(copies, []) + vocab_copies:
        copy.start()

    first_chip = places[1] == 0

    @pl.when(first_chip)
    def _():
        memory[...] = kept[...]
        decoded[...] = taken[...]

    @pl.when(jnp.logical_not(first_chip))
    def _():
        memory[...] = taken[...]
        decoded[...] = kept[...]

    def split(value):
        return value.reshape(frames, group, value.shape[-1])

    mem, dec = memory[...], decoded[...]
    for r in range(4):
        for copy in copies[r]:
            copy.wait()
        cols = pl.ds(r * block, block)
        keys = jnp.dot(mem, w[r, :, : 2 * block], preferred_element_type=wide)
        queries = jnp.dot(dec, w[r, :, 2 * block : 5 * block], preferred_element_type=wide)
        mk[:, :, cols] = split(keys[:, :block])
        sk[:, :, cols] = split(keys[:, block:])
        mq[:, :, cols] = split(queries[:, :block] + vectors[0:1, cols])
        sq[:, :, cols] = split(queries[:, block : 2 * block] + vectors[2:3, cols])
        pre[:, cols] = queries[:, 2 * block :] + vectors[4:5, cols]

    def lane(c):
        return pl.ds(c * lanes, lanes)

    def spread(row, c):
        return jnp.broadcast_to(vectors[row : row + 1, lane(c)], (group, lanes))

    def energies(queries, keys, vec_row, energy, kept_squash):
        weights = [spread(vec_row, c) for c in range(chunks)]

        def one(i, carried):
            query = [queries[i, :, lane(c)] for c in range(chunks)]
            for j in range(frames):
                total = None
                for c in range(chunks):
                    squash = jnp.tanh(query[c] + keys[j, :, lane(c)])
                    kept_squash[i * frames + j, :, lane(c)] = squash
                    part = squash * weights[c]
                    total = part if total is None else total + part
                energy[i * frames + j] = jnp.broadcast_to(
                    jnp.sum(total, axis=-1, keepdims=True), (group, lanes)
                )
            return carried

        lax.fori_loop(0, frames, one, 0)

    energies(mq, mk, 1, mono, mono_squash)
    energies(sq, sk, 3, span, span_squash)

    length = lengths[...]
    valid = [(length > j) for j in range(frames)]
    ones = jnp.ones((group, lanes), wide)
    zeros = jnp.zeros((group, lanes), wide)
    live = [jnp.where(valid[j], 1.0, 0.0).astype(wide) for j in range(frames)]
    diagonal = lax.broadcasted_iota(jnp.int32, (group, lanes), 1) - lax.broadcasted_iota(
        jnp.int32, (group, lanes), 0
    )

    def attend(i, previous):
        base = i * frames
        top = jnp.full((group, lanes), -1e30, wide)
        for j in range(frames):
            top = jnp.maximum(top, jnp.where(valid[j], span[base + j], -1e30))
        weight = [jnp.where(valid[j], jnp.exp(span[base + j] - top), 0.0) for j in range(frames)]
        current, ratios = [], []
        queued = previous[0]
        for j in range(frames):
            prob = sigmoid(mono[base + j] + offset + noise[base + j]) * live[j]
            keep[base + j] = prob
            queue[base + j] = queued
            alpha = prob * queued
            current.append(alpha)
            if j + 1 < frames:
                queued = (1.0 - prob) * queued + previous[j + 1]
            both = weight[j] + weight[j - 1] if j else weight[j]
            both = jnp.where(valid[j], both, 1.0)
            window[base + j] = both
            scaled[base + j] = weight[j]
            quotient = alpha / both
            ratio[base + j] = quotient
            ratios.append(quotient)
        row = zeros
        for j in range(frames):
            beta = weight[j] * (ratios[j] + (ratios[j + 1] if j + 1 < frames else zeros))
            row = jnp.where(diagonal == group * j, beta, row)
        mix[i] = row
        return tuple(current)

    lax.fori_loop(0, frames, attend, tuple([ones] + [zeros] * (frames - 1)))

    beta_low = mix[...].reshape(rows, lanes)[:, :rows].astype(low)
    context = jnp.dot(beta_low, mem, preferred_element_type=wide).astype(low)
    seen[0] = context
    for r in range(4):
        cols = pl.ds(r * block, block)
        value = jnp.tanh(
            pre[:, cols] + jnp.dot(context, w[r, :, 5 * block :], preferred_element_type=wide)
        )
        pre[:, cols] = value
        pack[r, :, 5 * block :] = value.astype(low)
    logits = vocab_bias[...]
    for r in range(4):
        vocab_copies[r].wait()
        logits = logits + jnp.dot(pack[r, :, 5 * block :], v[r], preferred_element_type=wide)
    shifted = jnp.exp(logits - jnp.max(logits, axis=-1, keepdims=True))
    softmax = shifted / jnp.sum(shifted, axis=-1, keepdims=True)
    onehot = (labels[...] == lax.broadcasted_iota(jnp.int32, softmax.shape, 1)).astype(wide)
    grad_logits = ((softmax - onehot) * counted[...]).astype(low)
    seen[1] = grad_logits
    sums[5:6, :] = jnp.sum(grad_logits.astype(wide), axis=0, keepdims=True)
    sums[6:8, :] = jnp.zeros((2, sums.shape[1]), wide)

    grad_context = jnp.zeros((rows, memory.shape[1]), wide)
    for r in range(4):
        cols = pl.ds(r * block, block)
        value = pre[:, cols]
        grad_pre = (dot_nt(grad_logits, v[r]) * (1.0 - value * value)).astype(low)
        pack[r, :, 4 * block : 5 * block] = grad_pre
        sums[4:5, cols] = jnp.sum(grad_pre.astype(wide), axis=0, keepdims=True)
        grad_context = grad_context + dot_nt(grad_pre, w[r, :, 5 * block :])
    upper = grad_context.astype(low)
    lower = (grad_context - upper.astype(wide)).astype(low)
    grad_memory[...] = dot_tn(beta_low, upper) + dot_tn(beta_low, lower)
    cross = dot_nt(upper, mem) + dot_nt(lower, mem)
    if rows < lanes:
        cross = jnp.concatenate([cross, jnp.zeros((rows, lanes - rows), wide)], axis=1)
    mix[...] = split(cross)

    def unattend(k, later):
        i = frames - 1 - k
        base = i * frames
        cross_row = mix[i]
        grad_beta = [
            jnp.broadcast_to(
                jnp.sum(
                    jnp.where(diagonal == group * j, cross_row, 0.0), axis=-1, keepdims=True
                ),
                (group, lanes),
            )
            for j in range(frames)
        ]
        weight = [scaled[base + j] for j in range(frames)]
        share = [ratio[base + j] for j in range(frames)]
        direct, from_window, grad_weight = [], [], []
        for j in range(frames):
            grad_ratio = grad_beta[j] * weight[j]
            if j:
                grad_ratio = grad_ratio + grad_beta[j - 1] * weight[j - 1]
            pull = grad_ratio / window[base + j]
            direct.append(pull)
            from_window.append(jnp.where(valid[j], -pull * share[j], 0.0))
            grad_weight.append(
                grad_beta[j] * (share[j] + (share[j + 1] if j + 1 < frames else zeros))
            )
        top = jnp.full((group, lanes), -1e30, wide)
        for j in range(frames):
            top = jnp.maximum(top, jnp.where(valid[j], span[base + j], -1e30))
        total, ties, at_top, through = zeros, zeros, [], []
        for j in range(frames):
            pulled = grad_weight[j] + from_window[j]
            if j + 1 < frames:
                pulled = pulled + from_window[j + 1]
            pulled = weight[j] * pulled
            through.append(pulled)
            total = total + pulled
            hit = jnp.where(span[base + j] == top, live[j], 0.0)
            at_top.append(hit)
            ties = ties + hit
        back = total / ties
        for j in range(frames):
            span[base + j] = through[j] - at_top[j] * back
        grad_queue = zeros
        now = [None] * frames
        for j in reversed(range(frames)):
            prob = keep[base + j]
            grad_alpha = direct[j] + later[j]
            mono[base + j] = queue[base + j] * (grad_alpha - grad_queue) * prob * (1.0 - prob)
            grad_queue = prob * grad_alpha + (1.0 - prob) * grad_queue
            now[j] = grad_queue
        return tuple(now)

    lax.fori_loop(0, frames, unattend, tuple([zeros] * frames))

    def energy_back(queries, keys, energy, kept_squash, bias_row, vec_row):
        def one_chunk(c, carried):
            at = pl.ds(pl.multiple_of(c * lanes, lanes), lanes)
            weight = jnp.broadcast_to(vectors[vec_row : vec_row + 1, at], (group, lanes))

            def one(i, carry):
                grad_keys, vec_total, bias_total = carry
                grad_query = zeros
                new_keys = []
                for j in range(frames):
                    squash = kept_squash[i * frames + j, :, at]
                    grad = energy[i * frames + j]
                    scaled_squash = grad * squash
                    vec_total = vec_total + scaled_squash
                    inner = grad - scaled_squash * squash
                    grad_query = grad_query + inner
                    new_keys.append(grad_keys[j] + inner)
                queries[i, :, at] = grad_query * weight
                return (tuple(new_keys), vec_total, bias_total + grad_query)

            grad_keys, vec_total, bias_total = lax.fori_loop(
                0, frames, one, (tuple([zeros] * frames), zeros, zeros)
            )
            for j in range(frames):
                keys[j, :, at] = grad_keys[j] * weight
            sums[bias_row : bias_row + 1, at] = jnp.sum(bias_total * weight, axis=0, keepdims=True)
            sums[vec_row : vec_row + 1, at] = jnp.sum(vec_total, axis=0, keepdims=True)
            return carried

        lax.fori_loop(0, chunks, one_chunk, 0)

    energy_back(mq, mk, mono, mono_squash, 0, 1)
    energy_back(sq, sk, span, span_squash, 2, 3)

    total_memory = grad_memory[...]
    total_decoded = jnp.zeros_like(total_memory)
    for r in range(4):
        cols = pl.ds(r * block, block)
        for n, source in enumerate((mk, sk, mq, sq)):
            pack[r, :, n * block : (n + 1) * block] = (
                source[:, :, cols].reshape(rows, block).astype(low)
            )
        total_memory = total_memory + dot_nt(pack[r, :, : 2 * block], w[r, :, : 2 * block])
        total_decoded = total_decoded + dot_nt(
            pack[r, :, 2 * block : 5 * block], w[r, :, 2 * block : 5 * block]
        )
    pack_me[...] = pack[0]
    pack_chip[...] = pack[1]
    pack_cores[...] = pack[2:4]
    middle = 2 * block
    near[...] = sums[:, :middle]
    far[:8, :] = sums[:, middle:]
    far[8:9, :] = sums[5:6, :middle]
    far[9:10, :] = sums[5:6, middle:]
    far[10:, :] = jnp.zeros((6, middle), wide)
    grad_own[...] = jnp.where(first_chip, total_memory, total_decoded)
    grad_given[...] = jnp.where(first_chip, total_decoded, total_memory).astype(low)


def run_attend(
    places, kept, taken, smalls, vocab, vectors, vocab_bias, noise, lengths, labels, counted,
    frames,
):
    rows, width = kept.shape
    group = rows // frames
    full = vectors.shape[1]
    vocab_width = vocab[0].shape[1]
    cell = (frames * frames, group, 128)
    count = len(smalls[0])
    return pl.pallas_call(
        functools.partial(attend_kernel, count),
        out_shape=(
            jax.ShapeDtypeStruct((rows, width), wide),
            jax.ShapeDtypeStruct((rows, width), low),
            jax.ShapeDtypeStruct((rows, full // 4 * 6), low),
            jax.ShapeDtypeStruct((rows, full // 4 * 6), low),
            jax.ShapeDtypeStruct((2, rows, full // 4 * 6), low),
            jax.ShapeDtypeStruct((2, rows, vocab_width), low),
            jax.ShapeDtypeStruct((8, full // 2), wide),
            jax.ShapeDtypeStruct((16, full // 2), wide),
        ),
        in_specs=[in_smem] + [in_vmem] * 8 + [in_place] * (4 * count + 4),
        out_specs=[in_vmem] * 8,
        scratch_shapes=[
            pltpu.VMEM((rows, width), low),
            pltpu.VMEM((rows, width), low),
            pltpu.VMEM((rows, width), wide),
            pltpu.VMEM((4, rows, full // 4 * 6), low),
            pltpu.VMEM((8, full), wide),
            pltpu.VMEM((4, width, full // 4 * 6), low),
            pltpu.VMEM((4,) + vocab[0].shape, low),
            pltpu.SemaphoreType.DMA((4, places.shape[0] - 2)),
            pltpu.SemaphoreType.DMA((4,)),
        ]
        + [pltpu.VMEM((frames, group, full), wide)] * 4
        + [pltpu.VMEM(cell, wide)] * 7
        + [pltpu.VMEM((frames, group, 128), wide), pltpu.VMEM((rows, full), wide)]
        + [pltpu.VMEM((frames * frames, group, full), wide)] * 2,
        compiler_params=pltpu.CompilerParams(vmem_limit_bytes=56 << 20),
        name="attend",
    )(
        places, kept, taken, vectors, vocab_bias, noise, lengths, labels, counted,
        *sum(smalls, []), *vocab,
    )


def gradient_kernel(
    order, before, before_peer, normed, normed_peer, dz, dz_peer, states_own, states_core,
    seen, seen_core, far, far_core, pack_me, pack_core, pack_far, *refs
):
    outputs, paired = refs[:8], refs[8:12]
    a_rec, a_in, a_dz, states, a_context, a_grads, a_pack, block, paired_block, sems, out_sems = (
        refs[12:]
    )
    y = order[0]
    height = block.shape[1]
    wide_half = a_dz.shape[1]
    part = a_pack.shape[1] // 6
    width = a_rec.shape[1]
    jobs = []
    for sources, target in (
        ((dz.at[0], dz_peer), a_dz),
        ((before, before_peer), a_rec),
        ((normed, normed_peer), a_in),
        (
            (states_own.at[0], states_core.at[0], states_own.at[2], states_core.at[2]),
            states.at[y],
        ),
        (
            (
                states_own.at[1], states_core.at[1],
                states_own.at[3], states_core.at[3],
            ),
            states.at[1 - y],
        ),
        ((pack_me, pack_core.at[0], pack_far.at[0], pack_far.at[1]), a_pack),
        ((seen.at[0], seen_core.at[0], far.at[0, :, :width], far_core.at[0, :, :width]), a_context),
        ((seen.at[1], seen_core.at[1], far.at[1, :, :width], far_core.at[1, :, :width]), a_grads),
    ):
        rows = target.shape[0] // len(sources)
        for r, source in enumerate(sources):
            jobs.append(
                pltpu.make_async_copy(
                    source, target.at[r * rows : (r + 1) * rows, :], sems.at[len(jobs)]
                )
            )
    for job in jobs:
        job.start()
    for job in jobs[:6]:
        job.wait()
    both = 2 * wide_half

    def one(n, carried):
        cols = pl.ds(pl.multiple_of(order[1 + n] * height, height), height)
        pair = jnp.concatenate([a_rec[:, cols], a_in[:, cols]], axis=1)
        for at in range(0, wide_half, 1024):
            value = dot_tn(pair, a_dz[:, at : at + 1024]).astype(low)
            block[n, :, at : at + 1024] = value[:height]
            block[n, :, wide_half + at : wide_half + at + 1024] = value[height:]
        for m, output in enumerate(outputs):

            @pl.when(n == m)
            def _(m=m, output=output):
                pltpu.make_async_copy(
                    block.at[m, :, :both], output.at[:, :both], out_sems.at[m]
                ).start()

        return carried

    lax.fori_loop(0, 8, one, 0)
    for job in jobs[6:]:
        job.wait()

    def two(n, carried):
        cols = pl.ds(pl.multiple_of(order[1 + n] * height, height), height)
        for m in range(2):
            to = both + 2 * m * part
            block[n, :, to : to + 2 * part] = dot_tn(
                states[m, :, cols], a_pack[:, 2 * m * part : 2 * (m + 1) * part]
            ).astype(low)
        for m, output in enumerate(outputs):

            @pl.when(n == m)
            def _(m=m, output=output):
                pltpu.make_async_copy(
                    block.at[m, :, both:], output.at[:, both:], out_sems.at[12 + m]
                ).start()

        return carried

    lax.fori_loop(0, 8, two, 0)

    def pair(n, carried):
        cols = pl.ds(pl.multiple_of(order[9 + n] * 2 * height, 2 * height), 2 * height)
        grad_pre = a_pack[:, 4 * part : 5 * part]
        for m, (a, b) in enumerate(
            (
                (states[1, :, cols], grad_pre),
                (a_context[:, cols], grad_pre),
                (a_grads[:, cols], a_pack[:, 5 * part :]),
            )
        ):
            paired_block[n, :, m * part : (m + 1) * part] = dot_tn(a, b).astype(low)
        return carried

    lax.fori_loop(0, 4, pair, 0)
    for m, output in enumerate(paired):
        pltpu.make_async_copy(paired_block.at[m], output, out_sems.at[8 + m]).start()
    for m, output in enumerate(outputs):
        pltpu.make_async_copy(
            block.at[m, :, :both], output.at[:, :both], out_sems.at[m]
        ).wait()
        pltpu.make_async_copy(
            block.at[m, :, both:], output.at[:, both:], out_sems.at[12 + m]
        ).wait()
    for m, output in enumerate(paired):
        pltpu.make_async_copy(paired_block.at[m], output, out_sems.at[8 + m]).wait()


def run_gradients(order, *arrays):
    rows, width = arrays[0].shape
    wide_half = arrays[5].shape[1]
    part = arrays[12].shape[1] // 6
    columns = 2 * wide_half + 4 * part
    height = width // 8
    deep = 2 * rows
    return pl.pallas_call(
        gradient_kernel,
        out_shape=tuple(
            [jax.ShapeDtypeStruct((height, columns), low)] * 8
            + [jax.ShapeDtypeStruct((2 * height, 3 * part), low)] * 4
        ),
        in_specs=[in_smem] + [in_place] * 15,
        out_specs=[in_place] * 12,
        scratch_shapes=[
            pltpu.VMEM((deep, width), low),
            pltpu.VMEM((deep, width), low),
            pltpu.VMEM((deep, wide_half), low),
            pltpu.VMEM((2, deep, width), low),
            pltpu.VMEM((deep, width), low),
            pltpu.VMEM((deep, width), low),
            pltpu.VMEM((deep, 6 * part), low),
            pltpu.VMEM((8, height, columns), low),
            pltpu.VMEM((4, 2 * height, 3 * part), low),
            pltpu.SemaphoreType.DMA((26,)),
            pltpu.SemaphoreType.DMA((20,)),
        ],
        compiler_params=pltpu.CompilerParams(vmem_limit_bytes=56 << 20),
        name="weight_gradients",
    )(order, *arrays)


def local(
    dp,
    block_input, norm_gain, lstm_in, lstm_rec, lstm_bias,
    mono_mem, mono_dec, mono_bias, mono_vec, span_mem, span_dec, span_bias, span_vec,
    out_weight, out_bias, vocab_weight, vocab_bias, noise, enc_lengths, label_lengths, labels,
):
    ring = Ring(dp)
    s, y = lax.axis_index("section"), lax.axis_index("mp")
    _, utts, frames, width = block_input.shape
    half, quarter = utts // 2, utts // 4
    rows = frames * quarter
    shard_rows, _, unit_half = lstm_in.shape[1:]
    wide_half = 4 * unit_half
    block = mono_mem.shape[1]
    vocab_size = vocab_weight.shape[1]
    vocab_pad = 4 * block

    in_shard = lstm_in[0].reshape(shard_rows, wide_half)
    rec_shard = lstm_rec[0].reshape(shard_rows, wide_half)
    bias_shard = lstm_bias[0].reshape(1, wide_half)

    def of_section(array):
        return jnp.where(s == y, array, across_cores(array))

    inputs = of_section(jnp.swapaxes(block_input[0], 0, 1))
    gain = of_section(norm_gain[0])
    inputs_own = lax.dynamic_slice_in_dim(inputs, s * half, half, axis=1)
    inputs_other = lax.dynamic_slice_in_dim(inputs, (1 - s) * half, half, axis=1)
    normed_own = normalize(inputs_own.astype(wide), gain)
    normed_own = normed_own.astype(low).reshape(frames * half, width)
    normed_other = normalize(inputs_other.astype(wide), gain)
    normed_other = normed_other.astype(low).reshape(frames * half, width)

    start = s * half + y * quarter
    noise_part = jnp.transpose(
        lax.dynamic_slice_in_dim(noise, start, quarter, axis=0), (1, 2, 0)
    ).reshape(frames * frames, quarter, 1)
    noise_part = jnp.broadcast_to(noise_part, (frames * frames, quarter, 128))
    length_part = lax.dynamic_slice_in_dim(enc_lengths, start, quarter, axis=0)
    length_part = jnp.broadcast_to(length_part[:, None], (quarter, 128))
    label_part = lax.dynamic_slice_in_dim(labels, start, quarter, axis=0).T.reshape(rows, 1)
    count_part = lax.dynamic_slice_in_dim(label_lengths, start, quarter, axis=0)
    counted = (jnp.arange(frames)[:, None] < count_part[None, :]).astype(wide).reshape(rows, 1)
    bias_row = jnp.pad(vocab_bias, (0, vocab_pad - vocab_size), constant_values=-1e30)[None]

    vector_own = jnp.stack([mono_bias, mono_vec, span_bias, span_vec, out_bias])
    vocab_own = jnp.pad(vocab_weight, ((0, 0), (0, vocab_pad - vocab_size)))
    ready = (noise_part, length_part, label_part, counted, bias_row, normed_own, normed_other)
    places, in_own, rec_own, small_own, small_chip = [], [], [], [], []
    small = jnp.concatenate(
        [
            mono_mem, span_mem, mono_dec, span_dec,
            out_weight[0], out_weight[1],
        ],
        axis=1,
    )
    if ring.short:
        flow, across, onward = Flow(), ring.across, ring.onward
        both = 2 * wide_half
        for k in range(ring.outer):
            places += [ring.back(k) * 2 + ring.x, ring.back(k) * 2 + 1 - ring.x]
        places = jnp.stack([s, y] + places).astype(jnp.int32)
        corner = jnp.concatenate([in_shard, rec_shard], axis=1)
        small = jnp.concatenate(
            [
                tie(mono_mem, corner), span_mem, mono_dec, span_dec, out_weight[0], out_weight[1]
            ],
            axis=1,
        )
        corner, small_far, small_next = corners(corner), across(small), onward(small)
        flow.landed = (corner, small_far, small_next)
        small_own = [jnp.concatenate([small, small_far], axis=1)]
        small_chip, small_core = [], []
        held = jnp.concatenate([corner, small_next], axis=1)
        near, far, near_core, far_core = [], [], [], []
        for k in range(ring.outer):
            near.append(held)
            jobs = [(across, held), (across_chips, small_own[k])]
            if k < ring.outer - 1:
                jobs.append((onward, held[:, :both] if k == ring.outer - 2 else held))
            if k == 0:
                jobs += [(across_chips, vocab_own), (corners, bias_shard)]
            if k == 1:
                jobs.append((across_chips, vector_own))
            also = ready if k == 1 else ()
            if k == ring.outer - 1:
                vectors = jnp.concatenate([vector_pair, across_cores(vector_pair)], axis=1)
                vectors = jnp.pad(vectors, ((0, 3), (0, 0)))
                also = (vectors, places)
            results = flow.step(*jobs, also=also)
            far.append(results[0])
            small_chip.append(results[1])
            if k == 0:
                vocab_chip, b_own = results[3], results[4].astype(wide)
            if k == 1:
                vector_pair = jnp.concatenate([vector_own, results[3]], axis=1)
            if k < ring.outer - 1:
                small_own.append(jnp.concatenate([held[:, both:], far[k][:, both:]], axis=1))
                held = results[2]
        for a, b in zip(near, far):
            near_core.append(across_cores(a))
            far_core.append(across_cores(b))
        small_core = [across_cores(a) for a in small_own]
        b_last, vocab_last, chip_last = lax.optimization_barrier(
            (b_own, vocab_own, vocab_chip, held)
        )[:3]
        b_other = across_cores(b_last)
        vocab = [vocab_own, vocab_chip, across_cores(vocab_last), across_cores(chip_last)]
        in_own = [a for pair in zip(near, far) for a in pair]
        in_other = [a for pair in zip(near_core, far_core) for a in pair]
        rec_own, rec_other, rec_column = in_own, in_other, wide_half
    else:
        vocab_chip = across_chips(vocab_own)
        small, in_block, rec_block = [
            lax.all_gather(a, "dp", axis=0, tiled=True)
            for a in (small, corners(in_shard), corners(rec_shard))
        ]
        places, in_own, rec_own = [jnp.int32(0)], [in_block], [rec_block]
        small_own, small_chip = [small], [across_chips(small)]
        vocab = [vocab_own, vocab_chip, across_cores(vocab_own), across_cores(vocab_chip)]
        in_other, rec_other, rec_column = [across_cores(in_block)], [across_cores(rec_block)], 0
        small_core = [across_cores(small)]
        b_own = corners(bias_shard).astype(wide)
        b_other = across_cores(b_own)
        vector_pair = across_chips(vector_own)
        vector_pair = jnp.concatenate([vector_own, vector_pair], axis=1)
        vectors = jnp.concatenate([vector_pair, across_cores(vector_pair)], axis=1)
        vectors = jnp.pad(vectors, ((0, 3), (0, 0)))
        places = jnp.stack([s, y] + places).astype(jnp.int32)
    places = tie(places, vectors, *vocab, *ready, *small_chip[:-1], *small_core)

    kept, given, before, gates, cells = run_forward(
        places, normed_own, b_own, b_other, in_own, in_other, rec_own, rec_other, frames,
        rec_column,
    )

    kept, given = kept.reshape(rows, width), given.reshape(rows, width)
    taken = across_chips(given)
    small_chip[-1] = tie(small_chip[-1], kept)
    small_both = [across_cores(part) for part in small_chip]
    smalls = [small_own, small_chip, small_core, small_both]
    grad_own, grad_given, pack_me, pack_chip, pack_cores, seen, near, far = run_attend(
        places, kept, taken, smalls, vocab, vectors, bias_row, noise_part, length_part,
        label_part, counted, frames,
    )
    grad_given, kept_far = lax.optimization_barrier((grad_given, across_chips(tie(kept, taken))))
    grad_taken = across_chips(grad_given)
    pack_core = across_cores(pack_cores)
    pack_out = jnp.stack([pack_chip, pack_core[1]])
    far_peer = across_cores(far)
    vector_pair = (near[:5] + far_peer[:5]).reshape(5, 2, block)
    bias_pair = (far[8:10] + far_peer[8:10]).reshape(-1)
    vector_out = jnp.concatenate([vector_pair[:, 1].reshape(-1), bias_pair])
    vector_count = vector_out.shape[0] // (2 * rows)
    seen_out = jnp.concatenate(
        [seen, halves(vector_out, 2 * rows).reshape(2, rows, -1)], axis=2
    )
    before = before.reshape(frames * half, width)
    before_peer = across_cores(tie(before, taken))
    states = jnp.stack([tie(kept, grad_given), taken, given, kept_far])
    states_core, seen_core = across_cores(states), across_cores(seen)
    places_back, pack_out, seen_out = lax.optimization_barrier(
        (places, pack_out, seen_out, grad_taken, before_peer, states_core, seen_core)
    )[:3]
    dz = run_backward(
        places_back, grad_own.reshape(frames, quarter, width),
        grad_taken.reshape(frames, quarter, width), gates, cells, rec_own, rec_other, rec_column,
    )
    pack_far = across_chips(pack_out)
    seen_far = across_chips(tie(seen_out, pack_out))

    dz = dz.reshape(2, frames * half, wide_half)
    dz, pack_far, seen_far = lax.optimization_barrier((dz, pack_far, seen_far))
    dz_peer = across_cores(dz[1])
    grad_inputs, grad_gain = run_input(
        places, inputs_own.reshape(frames * half, width), gain[None], dz, in_own, in_other
    )
    grad_gain = grad_gain.reshape(width)
    z, x = ring.z, ring.x
    if ring.short:
        steps_back = [ring.back(k) for k in range(1, 5)]
        order = [at * 2 + 1 - x for at in steps_back] + [at * 2 + x for at in steps_back]
        order = [y] + order + steps_back
    else:
        order = [y] + [jnp.int32(k) for k in [*range(8), *range(4)]]
    totals = run_gradients(
        tie(jnp.stack(order).astype(jnp.int32), grad_gain), before, before_peer, normed_own, normed_other, dz,
        dz_peer, states, states_core, seen, seen_core, seen_far, across_cores(seen_far),
        pack_me, pack_core, pack_far,
    )
    grad_inputs = jnp.swapaxes(grad_inputs.reshape(frames, half, width), 0, 1)
    vector_far = joined(seen_far[:, :, width:].reshape(2 * rows, -1), vector_count).reshape(-1)

    sides_at = 5 * block + vocab_pad
    grad_peer = across_cores(grad_inputs)
    grad_section = jnp.concatenate(
        [
            jnp.where(s == 0, grad_inputs, grad_peer),
            jnp.where(s == 0, grad_peer, grad_inputs),
        ],
        axis=0,
    )
    gain_sum = grad_gain + across_cores(grad_gain)
    flat = jnp.concatenate(
        [
            vector_pair[:, 0].reshape(-1) + vector_far[: 5 * block],
            bias_pair + vector_far[5 * block :],
            jnp.sum(dz[0].astype(wide), axis=0) + jnp.sum(dz_peer.astype(wide), axis=0),
            gain_sum,
        ]
    )
    flat = jnp.pad(flat, (0, -flat.shape[0] % (8 * shard_rows)))

    def to_other_chip(section):
        return lax.ppermute(section, ("section", "mp"), [(0, 1), (3, 2)])

    if ring.short:
        r = shard_rows
        both, width_out = 2 * wide_half, 2 * block
        flow, across, onward = Flow(), ring.across, ring.onward
        theirs, mine, outputs = totals[:4], totals[4:8], totals[8:]

        def total(k, arrived, passed):
            value = mine[k - 1].astype(wide) + arrived.astype(wide)
            return value if passed is None else value + passed.astype(wide)

        def cornered(hop):
            index = lambda at, place, chip: (at * ring.dp + place) * 2 + chip
            pairs = [
                (index(p, a, q), index(q, b, p)) for a, b in hop for p in range(2) for q in range(2)
            ]
            return lambda array: lax.ppermute(array, ("section", "dp", "mp"), pairs)

        arrived, out_two, out_before = flow.step(
            (across, theirs[0]), (onward, outputs[1]), (ring.astern, outputs[0])
        )
        out_one = onward(
            tie((outputs[2].astype(wide) + out_two.astype(wide)).astype(low), arrived)
        )
        grad_far = to_other_chip(grad_section)
        flat = flat.reshape(8, -1)
        flat = (flat + across(flat)).reshape(-1)
        flat_width = flat.shape[0] // r
        flow.landed = (arrived,)
        value = total(1, arrived, None).astype(low)
        passed, arrived = flow.step((onward, value), (across, theirs[1]))
        out = outputs[3].astype(wide) + out_before.astype(wide) + out_one.astype(wide)
        vocab_rows = out[:, width_out:].astype(low)
        message = jnp.concatenate(
            [cut(out, 1 - x, r)[:, :width_out].astype(low), vocab_rows[:r], vocab_rows[r:]], axis=1
        )
        out_far = across(message)
        kept_rows = corners(tie(mine[3][:, :both], out_one))
        output_grad = cut(out, x, r)[:, :width_out] + out_far[:, :width_out].astype(wide)
        shard = jnp.concatenate([out[:r, width_out:], out[r:, width_out:]], axis=1)
        shard = (shard + out_far[:, width_out:].astype(wide)).astype(low)
        shard = jnp.concatenate([shard, halves(flat, r)], axis=1)
        value = total(2, arrived, passed).astype(low)
        passed, arrived = flow.step((onward, value), (across, theirs[2]), also=(grad_far,))
        next_one, next_three = onward(shard), ring.astern(shard)
        value = total(3, arrived, passed).astype(low)
        passed, arrived, energy_passed, energy_arrived = flow.step(
            (cornered(ring.ring), value[:, :both]), (cornered(ring.pair), theirs[3][:, :both]),
            (onward, value[:, both:]), (across, theirs[3][:, both:]),
            also=(kept_rows, next_one, next_three),
        )
        shards = {0: shard, 1: next_one, 3: next_three, 2: onward(next_one)}
        flat = sum(joined(a[:, 2 * block :], flat_width).reshape(-1) for a in shards.values())
        sides = corners(flat[sides_at : sides_at + wide_half + width])
        moved = kept_rows.astype(wide) + arrived.astype(wide) + passed.astype(wide)
        energy_grad = mine[3][:, both:].astype(wide) + energy_arrived.astype(wide)
        energy_grad = energy_grad + energy_passed.astype(wide)
        vocab_grad = jnp.zeros((vocab_pad, block), low)
        for k, held in shards.items():
            held = jnp.concatenate([held[:, :block], held[:, block : 2 * block]], axis=0)
            vocab_grad = lax.dynamic_update_slice(vocab_grad, held, (ring.back(k) * 2 * r, 0))
    else:
        grad_far = to_other_chip(grad_section)

        def scatter(parts):
            total = jnp.concatenate(parts, axis=0)
            return lax.psum_scatter(total, "dp", scatter_dimension=0, tiled=True).astype(wide)

        moved, output_grad = scatter(totals[:8]), scatter(totals[8:])
        moved, energy_grad = moved[:, : 2 * wide_half], moved[:, 2 * wide_half :]
        moved = corners(moved.astype(low)).astype(wide)
        flat = lax.psum(flat, "dp")
        sides = corners(flat[sides_at : sides_at + wide_half + width])
        vocab_grad = lax.all_gather(
            output_grad[:, 2 * block :].astype(low), "dp", axis=0, tiled=True
        )

    input_grad = jnp.where(s == y, grad_section, grad_far)
    vocab_grad = vocab_grad.T[:, :vocab_size].astype(wide)
    vector_sum = flat[: 5 * block].reshape(5, block)
    bias_sum = flat[5 * block : 5 * block + vocab_size]
    lstm_bias_sum = sides[:wide_half].reshape(1, 4, unit_half)
    gain_sum = sides[wide_half:][None]
    rec_grad = moved[:, :wide_half].reshape(1, shard_rows, 4, unit_half)
    in_grad = moved[:, wide_half:].reshape(1, shard_rows, 4, unit_half)
    mono_mem_grad, span_mem_grad, mono_dec_grad, span_dec_grad = [
        energy_grad[:, n * block : (n + 1) * block] for n in range(4)
    ]
    return (
        input_grad[None],
        gain_sum,
        in_grad,
        rec_grad,
        lstm_bias_sum,
        mono_mem_grad,
        mono_dec_grad,
        vector_sum[0],
        vector_sum[1],
        span_mem_grad,
        span_dec_grad,
        vector_sum[2],
        vector_sum[3],
        jnp.stack([output_grad[:, :block], output_grad[:, block : 2 * block]]),
        vector_sum[4],
        vocab_grad,
        bias_sum,
    )


def solution(mesh):
    both = ("section", "mp")
    in_specs = (
        P("section", "dp", None, None),
        P("section", None),
        P("section", "dp", None, "mp"),
        P("section", "dp", None, "mp"),
        P("section", None, "mp"),
        P("dp", both),
        P("dp", both),
        P(both),
        P(both),
        P("dp", both),
        P("dp", both),
        P(both),
        P(both),
        P(None, "dp", both),
        P(both),
        P(both, None),
        P(),
        P("dp", None, None),
        P("dp"),
        P("dp"),
        P("dp", None),
    )
    out_specs = (
        P("section", "dp", None, None),
        P("section", None),
        P("section", "dp", None, "mp"),
        P("section", "dp", None, "mp"),
        P("section", None, "mp"),
        P("dp", both),
        P("dp", both),
        P(both),
        P(both),
        P("dp", both),
        P("dp", both),
        P(both),
        P(both),
        P(None, "dp", both),
        P(both),
        P(both, None),
        P(),
    )
    dp = mesh.shape["dp"]

    def step(*arrays):
        return local(dp, *arrays)

    return jax.shard_map(step, mesh=mesh, in_specs=in_specs, out_specs=out_specs, check_vma=False)
```

```python
import functools

import jax
import jax.numpy as jnp
from jax import lax
from jax.experimental import pallas as pl
from jax.experimental.pallas import tpu as pltpu
from jax.sharding import PartitionSpec as P

epsilon = 1e-05
offset = -4.0
wide = jnp.float32
low = jnp.bfloat16
in_vmem = pl.BlockSpec(memory_space=pltpu.VMEM)
in_smem = pl.BlockSpec(memory_space=pltpu.SMEM)
in_place = pl.BlockSpec(memory_space=pl.ANY)
core_swap = [(0, 1), (1, 0)]
corner_swap = [(0, 0), (1, 2), (2, 1), (3, 3)]


def normalize(inputs, gain_row):
    average = jnp.mean(inputs, axis=-1, keepdims=True)
    centred = inputs - average
    spread = jnp.mean(centred * centred, axis=-1, keepdims=True)
    return centred * lax.rsqrt(spread + epsilon) * gain_row


def across_cores(array):
    return lax.ppermute(array, "section", core_swap)


def across_chips(array):
    return lax.ppermute(array, "mp", core_swap)


def corners(array):
    return lax.ppermute(array, ("section", "mp"), corner_swap)


def tie(value, *others):
    return lax.optimization_barrier((value,) + others)[0]


def cut(array, block, rows):
    return lax.dynamic_slice_in_dim(array, block * rows, rows, axis=0)


class Flow:
    def __init__(self):
        self.landed = ()

    def step(self, *jobs, also=()):
        operands = tuple(operand for _, operand in jobs)
        operands = lax.optimization_barrier(operands + self.landed + tuple(also))[: len(jobs)]
        results = [send(operand) for (send, _), operand in zip(jobs, operands)]
        self.landed = tuple(results)
        return results


class Ring:
    def __init__(self, dp):
        self.dp = dp
        self.outer = dp // 2
        self.short = dp % 2 == 0 and self.outer == 4
        pairs = [(z, x) for z in range(self.outer) for x in range(2)]
        self.pair = [(2 * z + x, 2 * z + 1 - x) for z, x in pairs]
        self.ring = [(2 * z + x, 2 * ((z + 1) % self.outer) + x) for z, x in pairs]
        self.turn = [(b, a) for a, b in self.ring]
        place = lax.axis_index("dp")
        self.z, self.x = place // 2, place % 2

    def across(self, array):
        return lax.ppermute(array, "dp", self.pair)

    def onward(self, array):
        return lax.ppermute(array, "dp", self.ring)

    def astern(self, array):
        return lax.ppermute(array, "dp", self.turn)

    def back(self, k):
        return lax.rem(self.z - k + self.outer, self.outer)


def halves(array, height):
    array = array.reshape(height, -1)
    upper = array.astype(low)
    lower = (array - upper.astype(wide)).astype(low)
    return jnp.pad(
        jnp.concatenate([upper, lower], axis=1), ((0, 0), (0, -2 * array.shape[1] % 128))
    )


def joined(array, count):
    return array[:, :count].astype(wide) + array[:, count : 2 * count].astype(wide)


def sigmoid(x):
    return 0.5 * jnp.tanh(0.5 * x) + 0.5


def fetch(blocks, places, side_blocks, target, sems, first=0, column=0):
    wide_half = target.shape[1] // 2
    columns = pl.ds(pl.multiple_of(side_blocks * wide_half, wide_half), wide_half)
    copies = []
    for k, block in enumerate(blocks):
        height = block.shape[0]
        span = pl.ds(pl.multiple_of(places[2 + k] * height, height), height)
        copies.append(
            pltpu.make_async_copy(
                block.at[:, column : column + wide_half],
                target.at[span, columns],
                sems.at[first + k],
            )
        )
    return copies


def forward_kernel(count, column, places, normed, b_own, b_other, *refs):
    in_own, in_other, w_own, w_other = [refs[n * count : (n + 1) * count] for n in range(4)]
    kept, given, before, gates, cells, wi, w, b, state, cell, sems = refs[4 * count :]
    steps, rows, wide_full = gates.shape
    wide_half = wide_full // 2
    unit_half = wide_half // 4
    chunk = min(256, unit_half)
    s = places[0]
    copies = fetch(in_own, places, s, wi, sems) + fetch(in_other, places, 1 - s, wi, sems, count)
    later = fetch(w_own, places, s, w, sems, 2 * count, column)
    later += fetch(w_other, places, 1 - s, w, sems, 3 * count, column)
    for copy in copies + later:
        copy.start()
    for source, at in ((b_own, s), (b_other, 1 - s)):
        b[:, pl.ds(pl.multiple_of(at * wide_half, wide_half), wide_half)] = source[...]
    state[...] = jnp.zeros_like(state)
    cell[...] = jnp.zeros_like(cell)
    for copy in copies:
        copy.wait()

    def project(g, carried):
        cols = pl.ds(pl.multiple_of(g * unit_half, unit_half), unit_half)
        value = jnp.dot(normed[...], wi[:, cols], preferred_element_type=wide) + b[:, cols]
        gates[:, :, cols] = value.reshape(steps, rows, unit_half)
        return carried

    lax.fori_loop(0, 8, project, 0)
    for copy in later:
        copy.wait()
    eighth = rows // 2
    first_chip = places[1] == 0

    def advance(t, carried):
        hidden = state[...]
        before[t] = hidden
        for at in range(0, 2 * unit_half, chunk):
            half, inside = at // unit_half, at % unit_half
            acts = []
            for g in range(4):
                cols = pl.ds(half * wide_half + g * unit_half + inside, chunk)
                value = gates[t, :, cols] + jnp.dot(
                    hidden, w[:, cols], preferred_element_type=wide
                )
                value = jnp.tanh(value) if g == 2 else sigmoid(value)
                gates[t, :, cols] = value
                acts.append(value)
            units = pl.ds(at, chunk)
            new_cell = acts[1] * cell[:, units] + acts[0] * acts[2]
            cell[:, units] = new_cell
            cells[t, :, units] = new_cell
            new_hidden = acts[3] * jnp.tanh(new_cell)
            state[:, units] = new_hidden.astype(low)
            upper, lower = new_hidden[:eighth], new_hidden[eighth:]
            kept[t, :, units] = jnp.where(first_chip, upper, lower).astype(low)
            given[t, :, units] = jnp.where(first_chip, lower, upper).astype(low)
        return carried

    lax.fori_loop(0, steps, advance, 0)


def run_forward(places, normed, b_own, b_other, in_own, in_other, w_own, w_other, steps, column):
    rows = normed.shape[0] // steps
    units = normed.shape[1]
    wide_half = b_own.shape[1]
    count = len(w_own)
    return pl.pallas_call(
        functools.partial(forward_kernel, count, column),
        out_shape=(
            jax.ShapeDtypeStruct((steps, rows // 2, units), low),
            jax.ShapeDtypeStruct((steps, rows // 2, units), low),
            jax.ShapeDtypeStruct((steps, rows, units), low),
            jax.ShapeDtypeStruct((steps, rows, 2 * wide_half), wide),
            jax.ShapeDtypeStruct((steps, rows, units), wide),
        ),
        in_specs=[in_smem] + [in_vmem] * 3 + [in_place] * (4 * count),
        out_specs=[in_vmem] * 5,
        scratch_shapes=[
            pltpu.VMEM((units, 2 * wide_half), low),
            pltpu.VMEM((units, 2 * wide_half), low),
            pltpu.VMEM((1, 2 * wide_half), wide),
            pltpu.VMEM((rows, units), low),
            pltpu.VMEM((rows, units), wide),
            pltpu.SemaphoreType.DMA((4 * count,)),
        ],
        compiler_params=pltpu.CompilerParams(vmem_limit_bytes=56 << 20),
        name="recur_forward",
    )(places, normed, b_own, b_other, *in_own, *in_other, *w_own, *w_other)


def backward_kernel(count, column, places, kept, taken, gates, cells, *refs):
    w_own, w_other = refs[:count], refs[count : 2 * count]
    dz_own, dz_other, dz, stage, w, dh, dc, sems = refs[2 * count :]
    steps, rows, wide_full = gates.shape
    wide_half = wide_full // 2
    unit_half = wide_half // 4
    chunk = min(256, unit_half)
    s = places[0]
    first_chip = places[1] == 0
    jobs = []
    for n, (sources, at) in enumerate(((w_own, s), (w_other, 1 - s))):
        for k, block in enumerate(sources):
            slot = n * count + k
            copy = pltpu.make_async_copy(
                block.at[:, column : column + wide_half], stage.at[slot], sems.at[slot]
            )
            copy.start()
            jobs.append((copy, slot, at, places[2 + k] * block.shape[0]))
    dh[...] = jnp.zeros_like(dh)
    dc[...] = jnp.zeros_like(dc)
    height = w_own[0].shape[0]
    piece = min(height, 128)
    for copy, slot, at, first in jobs:
        copy.wait()

        def turn(g, carried, slot=slot, at=at, first=first):
            columns = pl.ds(pl.multiple_of(g * unit_half, unit_half), unit_half)
            span = pl.ds(pl.multiple_of(at * wide_half + g * unit_half, unit_half), unit_half)
            for low_row in range(0, height, piece):
                into = pl.ds(pl.multiple_of(first + low_row, piece), piece)
                w[span, into] = stage[slot, low_row : low_row + piece, columns].T
            return carried

        lax.fori_loop(0, 4, turn, 0)

    def retreat(k, carried):
        t = steps - 1 - k
        earlier = jnp.maximum(t - 1, 0)
        live = jnp.where(t > 0, 1.0, 0.0).astype(wide)
        for at in range(0, 2 * unit_half, chunk):
            half, inside = at // unit_half, at % unit_half
            units = pl.ds(at, chunk)
            ours, theirs = kept[t, :, units], taken[t, :, units].astype(wide)
            grad = dh[:, units] + jnp.concatenate(
                [jnp.where(first_chip, ours, theirs), jnp.where(first_chip, theirs, ours)], axis=0
            )
            i, f, g, o = [
                gates[t, :, pl.ds(half * wide_half + n * unit_half + inside, chunk)]
                for n in range(4)
            ]
            squash = jnp.tanh(cells[t, :, units])
            total = dc[:, units] + grad * o * (1.0 - squash * squash)
            parts = (
                total * g * i * (1.0 - i),
                total * (cells[earlier, :, units] * live) * f * (1.0 - f),
                total * i * (1.0 - g * g),
                grad * squash * o * (1.0 - o),
            )
            for n, part in enumerate(parts):
                dz[half, :, pl.ds(n * unit_half + inside, chunk)] = part.astype(low)
            dc[:, units] = total * f
        dz_own[t] = dz[s]
        dz_other[t] = dz[1 - s]
        upper, lower = dz[0], dz[1]
        for at in range(0, 2 * unit_half, chunk):
            units = pl.ds(at, chunk)
            dh[:, units] = jnp.dot(
                upper, w[:wide_half, units], preferred_element_type=wide
            ) + jnp.dot(lower, w[wide_half:, units], preferred_element_type=wide)
        return carried

    lax.fori_loop(0, steps, retreat, 0)


def run_backward(places, kept, taken, gates, cells, w_own, w_other, column):
    steps, rows, wide_full = gates.shape
    units = cells.shape[2]
    count = len(w_own)
    return pl.pallas_call(
        functools.partial(backward_kernel, count, column),
        out_shape=(jax.ShapeDtypeStruct((steps, rows, wide_full // 2), low),) * 2,
        in_specs=[in_smem] + [in_vmem] * 4 + [in_place] * (2 * count),
        out_specs=[in_vmem] * 2,
        scratch_shapes=[
            pltpu.VMEM((2, rows, wide_full // 2), low),
            pltpu.VMEM((2 * count, units // count, wide_full // 2), low),
            pltpu.VMEM((wide_full, units), low),
            pltpu.VMEM((rows, units), wide),
            pltpu.VMEM((rows, units), wide),
            pltpu.SemaphoreType.DMA((2 * count,)),
        ],
        compiler_params=pltpu.CompilerParams(vmem_limit_bytes=56 << 20),
        name="recur_backward",
    )(places, kept, taken, gates, cells, *w_own, *w_other)


def input_kernel(count, places, inputs, gain, dz, dz_given, *refs):
    in_own, in_other = refs[:count], refs[count : 2 * count]
    grad_inputs, grad_gain, wi, sems = refs[2 * count :]
    s = places[0]
    copies = fetch(in_own, places, s, wi, sems) + fetch(in_other, places, 1 - s, wi, sems, count)
    for copy in copies:
        copy.start()
    x = inputs[...].astype(wide)
    centred = x - jnp.mean(x, axis=-1, keepdims=True)
    scale = lax.rsqrt(jnp.mean(centred * centred, axis=-1, keepdims=True) + epsilon)
    shape = centred * scale
    for copy in copies:
        copy.wait()
    wide_half = wi.shape[1] // 2
    own = pl.ds(pl.multiple_of(s * wide_half, wide_half), wide_half)
    other = pl.ds(pl.multiple_of((1 - s) * wide_half, wide_half), wide_half)
    grad = dot_nt(dz[...], wi[:, own]) + dot_nt(dz_given[...], wi[:, other])
    grad_gain[...] = jnp.sum(grad * shape, axis=0, keepdims=True)
    pulled = grad * gain[...]
    grad_inputs[...] = scale * (
        pulled
        - jnp.mean(pulled, axis=-1, keepdims=True)
        - shape * jnp.mean(pulled * shape, axis=-1, keepdims=True)
    )


def run_input(places, inputs, gain, dz, dz_given, in_own, in_other):
    count = len(in_own)
    rows, width = inputs.shape
    return pl.pallas_call(
        functools.partial(input_kernel, count),
        out_shape=(
            jax.ShapeDtypeStruct((rows, width), wide),
            jax.ShapeDtypeStruct((1, width), wide),
        ),
        in_specs=[in_smem] + [in_vmem] * 4 + [in_place] * (2 * count),
        out_specs=[in_vmem] * 2,
        scratch_shapes=[
            pltpu.VMEM((width, 2 * dz.shape[1]), low),
            pltpu.SemaphoreType.DMA((2 * count,)),
        ],
        compiler_params=pltpu.CompilerParams(vmem_limit_bytes=56 << 20),
        name="input_back",
    )(places, inputs, gain, dz, dz_given, *in_own, *in_other)


def dot_nt(a, b):
    return lax.dot_general(a, b, (((1,), (1,)), ((), ())), preferred_element_type=wide)


def dot_tn(a, b):
    return lax.dot_general(a, b, (((0,), (0,)), ((), ())), preferred_element_type=wide)


def attend_kernel(
    count, places, kept, taken, vectors, vocab_bias, noise, lengths, labels, counted, *refs
):
    small, vocab = refs[: 4 * count], refs[4 * count : 4 * count + 4]
    (
        grad_own, grad_given, pack_me, pack_chip, pack_cores, seen, near, far,
        memory, decoded, grad_memory, pack, sums, w, v, sems, v_sems, mk, sk, mq, sq, mono, span, keep, queue, scaled, ratio, window, mix, pre,
        mono_squash, span_squash,
    ) = refs[4 * count + 4 :]
    rows, _ = kept.shape
    frames, group, _ = mk.shape
    block = w.shape[2] // 6
    lanes = 128
    chunks = 4 * block // lanes
    copies = []
    for r in range(4):
        arrived = []
        for k in range(count):
            source = small[r * count + k]
            height = source.shape[0]
            for h in range(source.shape[1] // (6 * block)):
                to = pl.ds(pl.multiple_of(places[2 + len(arrived)] * height, height), height)
                arrived.append(
                    pltpu.make_async_copy(
                        source.at[:, 6 * block * h : 6 * block * (h + 1)],
                        w.at[r, to, :],
                        sems.at[r, len(arrived)],
                    )
                )
        copies.append(arrived)
    vocab_copies = [pltpu.make_async_copy(vocab[r], v.at[r], v_sems.at[r]) for r in range(4)]
    for copy in sum(copies, []) + vocab_copies:
        copy.start()

    first_chip = places[1] == 0

    @pl.when(first_chip)
    def _():
        memory[...] = kept[...]
        decoded[...] = taken[...]

    @pl.when(jnp.logical_not(first_chip))
    def _():
        memory[...] = taken[...]
        decoded[...] = kept[...]

    def split(value):
        return value.reshape(frames, group, value.shape[-1])

    mem, dec = memory[...], decoded[...]

    def lane(c):
        return pl.ds(c * lanes, lanes)

    def spread(row, c):
        return jnp.broadcast_to(vectors[row : row + 1, lane(c)], (group, lanes))

    def energies(queries, keys, vec_row, energy, kept_squash, r):
        mine = range(r * chunks // 4, (r + 1) * chunks // 4)
        weights = {c: spread(vec_row, c) for c in mine}

        def one(i, carried):
            query = {c: queries[i, :, lane(c)] for c in mine}
            for j in range(frames):
                total = None if r == 0 else energy[i * frames + j]
                for c in mine:
                    squash = jnp.tanh(query[c] + keys[j, :, lane(c)])
                    kept_squash[i * frames + j, :, lane(c)] = squash
                    part = squash * weights[c]
                    total = part if total is None else total + part
                if r == 3:
                    total = jnp.broadcast_to(
                        jnp.sum(total, axis=-1, keepdims=True), (group, lanes)
                    )
                energy[i * frames + j] = total
            return carried

        lax.fori_loop(0, frames, one, 0)

    for r in range(4):
        for copy in copies[r]:
            copy.wait()
        cols = pl.ds(r * block, block)
        keys = jnp.dot(mem, w[r, :, : 2 * block], preferred_element_type=wide)
        queries = jnp.dot(dec, w[r, :, 2 * block : 5 * block], preferred_element_type=wide)
        mk[:, :, cols] = split(keys[:, :block])
        sk[:, :, cols] = split(keys[:, block:])
        mq[:, :, cols] = split(queries[:, :block] + vectors[0:1, cols])
        sq[:, :, cols] = split(queries[:, block : 2 * block] + vectors[2:3, cols])
        pre[:, cols] = queries[:, 2 * block :] + vectors[4:5, cols]
        energies(mq, mk, 1, mono, mono_squash, r)
        energies(sq, sk, 3, span, span_squash, r)

    length = lengths[...]
    valid = [(length > j) for j in range(frames)]
    ones = jnp.ones((group, lanes), wide)
    zeros = jnp.zeros((group, lanes), wide)
    live = [jnp.where(valid[j], 1.0, 0.0).astype(wide) for j in range(frames)]
    diagonal = lax.broadcasted_iota(jnp.int32, (group, lanes), 1) - lax.broadcasted_iota(
        jnp.int32, (group, lanes), 0
    )

    def attend(i, previous):
        base = i * frames
        top = jnp.full((group, lanes), -1e30, wide)
        for j in range(frames):
            top = jnp.maximum(top, jnp.where(valid[j], span[base + j], -1e30))
        weight = [jnp.where(valid[j], jnp.exp(span[base + j] - top), 0.0) for j in range(frames)]
        current, ratios = [], []
        queued = previous[0]
        for j in range(frames):
            prob = sigmoid(mono[base + j] + offset + noise[base + j]) * live[j]
            keep[base + j] = prob
            queue[base + j] = queued
            alpha = prob * queued
            current.append(alpha)
            if j + 1 < frames:
                queued = (1.0 - prob) * queued + previous[j + 1]
            both = weight[j] + weight[j - 1] if j else weight[j]
            both = jnp.where(valid[j], both, 1.0)
            window[base + j] = both
            scaled[base + j] = weight[j]
            quotient = alpha / both
            ratio[base + j] = quotient
            ratios.append(quotient)
        row = zeros
        for j in range(frames):
            beta = weight[j] * (ratios[j] + (ratios[j + 1] if j + 1 < frames else zeros))
            row = jnp.where(diagonal == group * j, beta, row)
        mix[i] = row
        return tuple(current)

    lax.fori_loop(0, frames, attend, tuple([ones] + [zeros] * (frames - 1)))

    beta_low = mix[...].reshape(rows, lanes)[:, :rows].astype(low)
    context = jnp.dot(beta_low, mem, preferred_element_type=wide).astype(low)
    seen[0] = context
    for r in range(4):
        cols = pl.ds(r * block, block)
        value = jnp.tanh(
            pre[:, cols] + jnp.dot(context, w[r, :, 5 * block :], preferred_element_type=wide)
        )
        pre[:, cols] = value
        pack[r, :, 5 * block :] = value.astype(low)
    logits = vocab_bias[...]
    for r in range(4):
        vocab_copies[r].wait()
        logits = logits + jnp.dot(pack[r, :, 5 * block :], v[r], preferred_element_type=wide)
    shifted = jnp.exp(logits - jnp.max(logits, axis=-1, keepdims=True))
    softmax = shifted / jnp.sum(shifted, axis=-1, keepdims=True)
    onehot = (labels[...] == lax.broadcasted_iota(jnp.int32, softmax.shape, 1)).astype(wide)
    grad_logits = ((softmax - onehot) * counted[...]).astype(low)
    seen[1] = grad_logits
    sums[5:6, :] = jnp.sum(grad_logits.astype(wide), axis=0, keepdims=True)
    sums[6:8, :] = jnp.zeros((2, sums.shape[1]), wide)

    grad_context = jnp.zeros((rows, memory.shape[1]), wide)
    for r in range(4):
        cols = pl.ds(r * block, block)
        value = pre[:, cols]
        grad_pre = (dot_nt(grad_logits, v[r]) * (1.0 - value * value)).astype(low)
        pack[r, :, 4 * block : 5 * block] = grad_pre
        sums[4:5, cols] = jnp.sum(grad_pre.astype(wide), axis=0, keepdims=True)
        grad_context = grad_context + dot_nt(grad_pre, w[r, :, 5 * block :])
    upper = grad_context.astype(low)
    lower = (grad_context - upper.astype(wide)).astype(low)
    grad_memory[...] = dot_tn(beta_low, upper) + dot_tn(beta_low, lower)
    cross = dot_nt(upper, mem) + dot_nt(lower, mem)
    if rows < lanes:
        cross = jnp.concatenate([cross, jnp.zeros((rows, lanes - rows), wide)], axis=1)
    mix[...] = split(cross)

    def unattend(k, later):
        i = frames - 1 - k
        base = i * frames
        cross_row = mix[i]
        grad_beta = [
            jnp.broadcast_to(
                jnp.sum(
                    jnp.where(diagonal == group * j, cross_row, 0.0), axis=-1, keepdims=True
                ),
                (group, lanes),
            )
            for j in range(frames)
        ]
        weight = [scaled[base + j] for j in range(frames)]
        share = [ratio[base + j] for j in range(frames)]
        direct, from_window, grad_weight = [], [], []
        for j in range(frames):
            grad_ratio = grad_beta[j] * weight[j]
            if j:
                grad_ratio = grad_ratio + grad_beta[j - 1] * weight[j - 1]
            pull = grad_ratio / window[base + j]
            direct.append(pull)
            from_window.append(jnp.where(valid[j], -pull * share[j], 0.0))
            grad_weight.append(
                grad_beta[j] * (share[j] + (share[j + 1] if j + 1 < frames else zeros))
            )
        top = jnp.full((group, lanes), -1e30, wide)
        for j in range(frames):
            top = jnp.maximum(top, jnp.where(valid[j], span[base + j], -1e30))
        total, ties, at_top, through = zeros, zeros, [], []
        for j in range(frames):
            pulled = grad_weight[j] + from_window[j]
            if j + 1 < frames:
                pulled = pulled + from_window[j + 1]
            pulled = weight[j] * pulled
            through.append(pulled)
            total = total + pulled
            hit = jnp.where(span[base + j] == top, live[j], 0.0)
            at_top.append(hit)
            ties = ties + hit
        back = total / ties
        for j in range(frames):
            span[base + j] = through[j] - at_top[j] * back
        grad_queue = zeros
        now = [None] * frames
        for j in reversed(range(frames)):
            prob = keep[base + j]
            grad_alpha = direct[j] + later[j]
            mono[base + j] = queue[base + j] * (grad_alpha - grad_queue) * prob * (1.0 - prob)
            grad_queue = prob * grad_alpha + (1.0 - prob) * grad_queue
            now[j] = grad_queue
        return tuple(now)

    lax.fori_loop(0, frames, unattend, tuple([zeros] * frames))

    def energy_back(queries, keys, energy, kept_squash, bias_row, vec_row):
        def one_chunk(c, carried):
            at = pl.ds(pl.multiple_of(c * lanes, lanes), lanes)
            weight = jnp.broadcast_to(vectors[vec_row : vec_row + 1, at], (group, lanes))

            def one(i, carry):
                grad_keys, vec_total, bias_total = carry
                grad_query = zeros
                new_keys = []
                for j in range(frames):
                    squash = kept_squash[i * frames + j, :, at]
                    grad = energy[i * frames + j]
                    scaled_squash = grad * squash
                    vec_total = vec_total + scaled_squash
                    inner = grad - scaled_squash * squash
                    grad_query = grad_query + inner
                    new_keys.append(grad_keys[j] + inner)
                queries[i, :, at] = grad_query * weight
                return (tuple(new_keys), vec_total, bias_total + grad_query)

            grad_keys, vec_total, bias_total = lax.fori_loop(
                0, frames, one, (tuple([zeros] * frames), zeros, zeros)
            )
            for j in range(frames):
                keys[j, :, at] = grad_keys[j] * weight
            sums[bias_row : bias_row + 1, at] = jnp.sum(bias_total * weight, axis=0, keepdims=True)
            sums[vec_row : vec_row + 1, at] = jnp.sum(vec_total, axis=0, keepdims=True)
            return carried

        lax.fori_loop(0, chunks, one_chunk, 0)

    energy_back(mq, mk, mono, mono_squash, 0, 1)
    energy_back(sq, sk, span, span_squash, 2, 3)

    total_memory = grad_memory[...]
    total_decoded = jnp.zeros_like(total_memory)
    for r in range(4):
        cols = pl.ds(r * block, block)
        for n, source in enumerate((mk, sk, mq, sq)):
            pack[r, :, n * block : (n + 1) * block] = (
                source[:, :, cols].reshape(rows, block).astype(low)
            )
        total_memory = total_memory + dot_nt(pack[r, :, : 2 * block], w[r, :, : 2 * block])
        total_decoded = total_decoded + dot_nt(
            pack[r, :, 2 * block : 5 * block], w[r, :, 2 * block : 5 * block]
        )
    pack_me[...] = pack[0]
    pack_chip[...] = pack[1]
    pack_cores[...] = pack[2:4]
    middle = 2 * block
    near[...] = sums[:, :middle]
    far[:8, :] = sums[:, middle:]
    far[8:9, :] = sums[5:6, :middle]
    far[9:10, :] = sums[5:6, middle:]
    far[10:, :] = jnp.zeros((6, middle), wide)
    grad_own[...] = jnp.where(first_chip, total_memory, total_decoded)
    grad_given[...] = jnp.where(first_chip, total_decoded, total_memory).astype(low)


def run_attend(
    places, kept, taken, smalls, vocab, vectors, vocab_bias, noise, lengths, labels, counted,
    frames,
):
    rows, width = kept.shape
    group = rows // frames
    full = vectors.shape[1]
    vocab_width = vocab[0].shape[1]
    cell = (frames * frames, group, 128)
    count = len(smalls[0])
    return pl.pallas_call(
        functools.partial(attend_kernel, count),
        out_shape=(
            jax.ShapeDtypeStruct((rows, width), wide),
            jax.ShapeDtypeStruct((rows, width), low),
            jax.ShapeDtypeStruct((rows, full // 4 * 6), low),
            jax.ShapeDtypeStruct((rows, full // 4 * 6), low),
            jax.ShapeDtypeStruct((2, rows, full // 4 * 6), low),
            jax.ShapeDtypeStruct((2, rows, vocab_width), low),
            jax.ShapeDtypeStruct((8, full // 2), wide),
            jax.ShapeDtypeStruct((16, full // 2), wide),
        ),
        in_specs=[in_smem] + [in_vmem] * 8 + [in_place] * (4 * count + 4),
        out_specs=[in_vmem] * 8,
        scratch_shapes=[
            pltpu.VMEM((rows, width), low),
            pltpu.VMEM((rows, width), low),
            pltpu.VMEM((rows, width), wide),
            pltpu.VMEM((4, rows, full // 4 * 6), low),
            pltpu.VMEM((8, full), wide),
            pltpu.VMEM((4, width, full // 4 * 6), low),
            pltpu.VMEM((4,) + vocab[0].shape, low),
            pltpu.SemaphoreType.DMA((4, places.shape[0] - 2)),
            pltpu.SemaphoreType.DMA((4,)),
        ]
        + [pltpu.VMEM((frames, group, full), wide)] * 4
        + [pltpu.VMEM(cell, wide)] * 7
        + [pltpu.VMEM((frames, group, 128), wide), pltpu.VMEM((rows, full), wide)]
        + [pltpu.VMEM((frames * frames, group, full), wide)] * 2,
        compiler_params=pltpu.CompilerParams(vmem_limit_bytes=56 << 20),
        name="attend",
    )(
        places, kept, taken, vectors, vocab_bias, noise, lengths, labels, counted,
        *sum(smalls, []), *vocab,
    )


def gradient_kernel(
    order, before, before_peer, normed, normed_peer, dz, dz_peer, states_own, states_core,
    seen, seen_core, far, far_core, pack_me, pack_core, pack_far, *refs
):
    outputs, paired = refs[:8], refs[8:12]
    a_rec, a_in, a_dz, states, a_context, a_grads, a_pack, block, paired_block, sems, out_sems = (
        refs[12:]
    )
    y = order[0]
    height = block.shape[1]
    wide_half = a_dz.shape[1]
    part = a_pack.shape[1] // 6
    width = a_rec.shape[1]
    jobs = []
    for sources, target in (
        ((dz, dz_peer), a_dz),
        ((before, before_peer), a_rec),
        ((normed, normed_peer), a_in),
        (
            (states_own.at[0], states_core.at[0], states_own.at[2], states_core.at[2]),
            states.at[y],
        ),
        (
            (
                states_own.at[1], states_core.at[1],
                states_own.at[3], states_core.at[3],
            ),
            states.at[1 - y],
        ),
        ((pack_me, pack_core.at[0], pack_far.at[0], pack_far.at[1]), a_pack),
        ((seen.at[0], seen_core.at[0], far.at[0, :, :width], far_core.at[0, :, :width]), a_context),
        ((seen.at[1], seen_core.at[1], far.at[1, :, :width], far_core.at[1, :, :width]), a_grads),
    ):
        rows = target.shape[0] // len(sources)
        for r, source in enumerate(sources):
            jobs.append(
                pltpu.make_async_copy(
                    source, target.at[r * rows : (r + 1) * rows, :], sems.at[len(jobs)]
                )
            )
    for job in jobs:
        job.start()
    for job in jobs[:6]:
        job.wait()
    both = 2 * wide_half

    def one(n, carried):
        cols = pl.ds(pl.multiple_of(order[1 + n] * height, height), height)
        pair = jnp.concatenate([a_rec[:, cols], a_in[:, cols]], axis=1)
        for at in range(0, wide_half, 1024):
            value = dot_tn(pair, a_dz[:, at : at + 1024]).astype(low)
            block[n, :, at : at + 1024] = value[:height]
            block[n, :, wide_half + at : wide_half + at + 1024] = value[height:]
        for m, output in enumerate(outputs):

            @pl.when(n == m)
            def _(m=m, output=output):
                pltpu.make_async_copy(
                    block.at[m, :, :both], output.at[:, :both], out_sems.at[m]
                ).start()

        return carried

    lax.fori_loop(0, 8, one, 0)
    for job in jobs[6:]:
        job.wait()

    def two(n, carried):
        cols = pl.ds(pl.multiple_of(order[1 + n] * height, height), height)
        for m in range(2):
            to = both + 2 * m * part
            block[n, :, to : to + 2 * part] = dot_tn(
                states[m, :, cols], a_pack[:, 2 * m * part : 2 * (m + 1) * part]
            ).astype(low)
        for m, output in enumerate(outputs):

            @pl.when(n == m)
            def _(m=m, output=output):
                pltpu.make_async_copy(
                    block.at[m, :, both:], output.at[:, both:], out_sems.at[12 + m]
                ).start()

        return carried

    lax.fori_loop(0, 8, two, 0)

    def pair(n, carried):
        cols = pl.ds(pl.multiple_of(order[9 + n] * 2 * height, 2 * height), 2 * height)
        grad_pre = a_pack[:, 4 * part : 5 * part]
        for m, (a, b) in enumerate(
            (
                (states[1, :, cols], grad_pre),
                (a_context[:, cols], grad_pre),
                (a_grads[:, cols], a_pack[:, 5 * part :]),
            )
        ):
            paired_block[n, :, m * part : (m + 1) * part] = dot_tn(a, b).astype(low)
        return carried

    lax.fori_loop(0, 4, pair, 0)
    for m, output in enumerate(paired):
        pltpu.make_async_copy(paired_block.at[m], output, out_sems.at[8 + m]).start()
    for m, output in enumerate(outputs):
        pltpu.make_async_copy(
            block.at[m, :, :both], output.at[:, :both], out_sems.at[m]
        ).wait()
        pltpu.make_async_copy(
            block.at[m, :, both:], output.at[:, both:], out_sems.at[12 + m]
        ).wait()
    for m, output in enumerate(paired):
        pltpu.make_async_copy(paired_block.at[m], output, out_sems.at[8 + m]).wait()


def run_gradients(order, *arrays):
    rows, width = arrays[0].shape
    wide_half = arrays[5].shape[1]
    part = arrays[12].shape[1] // 6
    columns = 2 * wide_half + 4 * part
    height = width // 8
    deep = 2 * rows
    return pl.pallas_call(
        gradient_kernel,
        out_shape=tuple(
            [jax.ShapeDtypeStruct((height, columns), low)] * 8
            + [jax.ShapeDtypeStruct((2 * height, 3 * part), low)] * 4
        ),
        in_specs=[in_smem] + [in_place] * 15,
        out_specs=[in_place] * 12,
        scratch_shapes=[
            pltpu.VMEM((deep, width), low),
            pltpu.VMEM((deep, width), low),
            pltpu.VMEM((deep, wide_half), low),
            pltpu.VMEM((2, deep, width), low),
            pltpu.VMEM((deep, width), low),
            pltpu.VMEM((deep, width), low),
            pltpu.VMEM((deep, 6 * part), low),
            pltpu.VMEM((8, height, columns), low),
            pltpu.VMEM((4, 2 * height, 3 * part), low),
            pltpu.SemaphoreType.DMA((26,)),
            pltpu.SemaphoreType.DMA((20,)),
        ],
        compiler_params=pltpu.CompilerParams(vmem_limit_bytes=56 << 20),
        name="weight_gradients",
    )(order, *arrays)


def local(
    dp,
    block_input, norm_gain, lstm_in, lstm_rec, lstm_bias,
    mono_mem, mono_dec, mono_bias, mono_vec, span_mem, span_dec, span_bias, span_vec,
    out_weight, out_bias, vocab_weight, vocab_bias, noise, enc_lengths, label_lengths, labels,
):
    ring = Ring(dp)
    s, y = lax.axis_index("section"), lax.axis_index("mp")
    _, utts, frames, width = block_input.shape
    half, quarter = utts // 2, utts // 4
    rows = frames * quarter
    shard_rows, _, unit_half = lstm_in.shape[1:]
    wide_half = 4 * unit_half
    block = mono_mem.shape[1]
    vocab_size = vocab_weight.shape[1]
    vocab_pad = 4 * block

    in_shard = lstm_in[0].reshape(shard_rows, wide_half)
    rec_shard = lstm_rec[0].reshape(shard_rows, wide_half)
    bias_shard = lstm_bias[0].reshape(1, wide_half)

    def of_section(array):
        return jnp.where(s == y, array, across_cores(array))

    inputs = of_section(jnp.swapaxes(block_input[0], 0, 1))
    gain = of_section(norm_gain[0])
    inputs_own = lax.dynamic_slice_in_dim(inputs, s * half, half, axis=1)
    inputs_other = lax.dynamic_slice_in_dim(inputs, (1 - s) * half, half, axis=1)
    normed_own = normalize(inputs_own.astype(wide), gain)
    normed_own = normed_own.astype(low).reshape(frames * half, width)
    normed_other = normalize(inputs_other.astype(wide), gain)
    normed_other = normed_other.astype(low).reshape(frames * half, width)

    start = s * half + y * quarter
    noise_part = jnp.transpose(
        lax.dynamic_slice_in_dim(noise, start, quarter, axis=0), (1, 2, 0)
    ).reshape(frames * frames, quarter, 1)
    noise_part = jnp.broadcast_to(noise_part, (frames * frames, quarter, 128))
    length_part = lax.dynamic_slice_in_dim(enc_lengths, start, quarter, axis=0)
    length_part = jnp.broadcast_to(length_part[:, None], (quarter, 128))
    label_part = lax.dynamic_slice_in_dim(labels, start, quarter, axis=0).T.reshape(rows, 1)
    count_part = lax.dynamic_slice_in_dim(label_lengths, start, quarter, axis=0)
    counted = (jnp.arange(frames)[:, None] < count_part[None, :]).astype(wide).reshape(rows, 1)
    bias_row = jnp.pad(vocab_bias, (0, vocab_pad - vocab_size), constant_values=-1e30)[None]

    vector_own = jnp.stack([mono_bias, mono_vec, span_bias, span_vec, out_bias])
    vocab_own = jnp.pad(vocab_weight, ((0, 0), (0, vocab_pad - vocab_size)))
    ready = (noise_part, length_part, label_part, counted, bias_row, normed_own, normed_other)
    places, in_own, rec_own, small_own, small_chip = [], [], [], [], []
    small = jnp.concatenate(
        [
            tie(mono_mem, in_shard, rec_shard), span_mem, mono_dec, span_dec,
            out_weight[0], out_weight[1],
        ],
        axis=1,
    )
    if ring.short:
        flow, across, onward = Flow(), ring.across, ring.onward
        both = 2 * wide_half
        corner_in, corner_rec, b_own = flow.step(
            (corners, in_shard), (corners, rec_shard), (corners, bias_shard)
        )
        small_far, small_next = across(small), onward(small)
        flow.landed += (small_far, small_next)
        b_own = b_own.astype(wide)
        small_own = [jnp.concatenate([small, small_far], axis=1)]
        small_chip, small_core = [], []
        held = jnp.concatenate([corner_in, corner_rec, small_next], axis=1)
        near, far, near_core, far_core = [], [], [], []
        for k in range(ring.outer):
            near.append(held)
            jobs = [(across, held), (across_chips, small_own[k])]
            if k < ring.outer - 1:
                jobs.append((onward, held[:, :both] if k == ring.outer - 2 else held))
            if k == 0:
                jobs += [(across_chips, vocab_own), (across_chips, vector_own)]
            results = flow.step(*jobs, also=ready if k == 1 else ())
            far.append(results[0])
            small_chip.append(results[1])
            if k == 0:
                vocab_chip, vector_pair = results[3:]
                vector_pair = jnp.concatenate([vector_own, vector_pair], axis=1)
            if k < ring.outer - 1:
                small_own.append(jnp.concatenate([held[:, both:], far[k][:, both:]], axis=1))
                held = results[2]
        for a, b in zip(near, far):
            near_core.append(across_cores(a))
            far_core.append(across_cores(b))
        small_core = [across_cores(a) for a in small_own]
        b_last, vocab_last, chip_last, vector_last = lax.optimization_barrier(
            (b_own, vocab_own, vocab_chip, vector_pair, held)
        )[:4]
        b_other = across_cores(b_last)
        vocab = [vocab_own, vocab_chip, across_cores(vocab_last), across_cores(chip_last)]
        vector_core = across_cores(vector_last)
        in_own = [a for pair in zip(near, far) for a in pair]
        in_other = [a for pair in zip(near_core, far_core) for a in pair]
        rec_own, rec_other, rec_column = in_own, in_other, wide_half
        for k in range(ring.outer):
            places += [ring.back(k) * 2 + ring.x, ring.back(k) * 2 + 1 - ring.x]
    else:
        vocab_chip = across_chips(vocab_own)
        small, in_block, rec_block = [
            lax.all_gather(a, "dp", axis=0, tiled=True)
            for a in (small, corners(in_shard), corners(rec_shard))
        ]
        places, in_own, rec_own = [jnp.int32(0)], [in_block], [rec_block]
        small_own, small_chip = [small], [across_chips(small)]
        vocab = [vocab_own, vocab_chip, across_cores(vocab_own), across_cores(vocab_chip)]
        in_other, rec_other, rec_column = [across_cores(in_block)], [across_cores(rec_block)], 0
        small_core = [across_cores(small)]
        b_own = corners(bias_shard).astype(wide)
        b_other = across_cores(b_own)
        vector_pair = across_chips(vector_own)
        vector_pair = jnp.concatenate([vector_own, vector_pair], axis=1)
        vector_core = across_cores(vector_pair)
    vectors = jnp.concatenate([vector_pair, vector_core], axis=1)
    vectors = jnp.pad(vectors, ((0, 3), (0, 0)))
    places = jnp.stack([s, y] + places).astype(jnp.int32)
    places = tie(places, vectors, *vocab, *ready, *small_chip[:-1], *small_core)

    kept, given, before, gates, cells = run_forward(
        places, normed_own, b_own, b_other, in_own, in_other, rec_own, rec_other, frames,
        rec_column,
    )

    kept, given = kept.reshape(rows, width), given.reshape(rows, width)
    taken = across_chips(given)
    small_chip[-1] = tie(small_chip[-1], kept)
    small_both = [across_cores(part) for part in small_chip]
    smalls = [small_own, small_chip, small_core, small_both]
    grad_own, grad_given, pack_me, pack_chip, pack_cores, seen, near, far = run_attend(
        places, kept, taken, smalls, vocab, vectors, bias_row, noise_part, length_part,
        label_part, counted, frames,
    )
    grad_given, kept_far = lax.optimization_barrier((grad_given, across_chips(tie(kept, taken))))
    grad_taken = across_chips(grad_given)
    pack_core = across_cores(pack_cores)
    pack_out = jnp.stack([pack_chip, pack_core[1]])
    far_peer = across_cores(far)
    vector_pair = (near[:5] + far_peer[:5]).reshape(5, 2, block)
    bias_pair = (far[8:10] + far_peer[8:10]).reshape(-1)
    vector_out = jnp.concatenate([vector_pair[:, 1].reshape(-1), bias_pair])
    vector_count = vector_out.shape[0] // (2 * rows)
    seen_out = jnp.concatenate(
        [seen, halves(vector_out, 2 * rows).reshape(2, rows, -1)], axis=2
    )
    before = before.reshape(frames * half, width)
    before_peer = across_cores(tie(before, taken))
    states = jnp.stack([tie(kept, grad_given), taken, given, kept_far])
    states_core, seen_core = across_cores(states), across_cores(seen)
    places_back, pack_out, seen_out = lax.optimization_barrier(
        (places, pack_out, seen_out, grad_taken, before_peer, states_core, seen_core)
    )[:3]
    dz_own, dz_other = run_backward(
        places_back, grad_own.reshape(frames, quarter, width),
        grad_taken.reshape(frames, quarter, width), gates, cells, rec_own, rec_other, rec_column,
    )
    pack_far = across_chips(pack_out)
    seen_far = across_chips(tie(seen_out, pack_out))

    dz_own, dz_other, pack_far, seen_far = lax.optimization_barrier(
        (
            dz_own.reshape(frames * half, wide_half), dz_other.reshape(frames * half, wide_half),
            pack_far, seen_far,
        )
    )
    dz_peer = across_cores(dz_other)
    grad_inputs, grad_gain = run_input(
        places, inputs_own.reshape(frames * half, width), gain[None], dz_own, dz_other,
        in_own, in_other,
    )
    grad_gain = grad_gain.reshape(width)
    z, x = ring.z, ring.x
    if ring.short:
        steps_back = [ring.back(k) for k in range(1, 5)]
        order = [at * 2 + 1 - x for at in steps_back] + [at * 2 + x for at in steps_back]
        order = [y] + order + steps_back
    else:
        order = [y] + [jnp.int32(k) for k in [*range(8), *range(4)]]
    totals = run_gradients(
        tie(jnp.stack(order).astype(jnp.int32), grad_gain), before, before_peer, normed_own, normed_other, dz_own,
        dz_peer, states, states_core, seen, seen_core, seen_far, across_cores(seen_far),
        pack_me, pack_core, pack_far,
    )
    grad_inputs = jnp.swapaxes(grad_inputs.reshape(frames, half, width), 0, 1)
    vector_far = joined(seen_far[:, :, width:].reshape(2 * rows, -1), vector_count).reshape(-1)

    sides_at = 5 * block + vocab_pad
    grad_peer = across_cores(grad_inputs)
    grad_section = jnp.concatenate(
        [
            jnp.where(s == 0, grad_inputs, grad_peer),
            jnp.where(s == 0, grad_peer, grad_inputs),
        ],
        axis=0,
    )
    gain_sum = grad_gain + across_cores(grad_gain)
    flat = jnp.concatenate(
        [
            vector_pair[:, 0].reshape(-1) + vector_far[: 5 * block],
            bias_pair + vector_far[5 * block :],
            jnp.sum(dz_own.astype(wide), axis=0) + jnp.sum(dz_peer.astype(wide), axis=0),
            gain_sum,
        ]
    )
    flat = jnp.pad(flat, (0, -flat.shape[0] % (8 * shard_rows)))

    def to_other_chip(section):
        return lax.ppermute(section, ("section", "mp"), [(0, 1), (3, 2)])

    if ring.short:
        r = shard_rows
        both, width_out = 2 * wide_half, 2 * block
        flow, across, onward = Flow(), ring.across, ring.onward
        theirs, mine, outputs = totals[:4], totals[4:8], totals[8:]

        def total(k, arrived, passed):
            value = mine[k - 1].astype(wide) + arrived.astype(wide)
            return value if passed is None else value + passed.astype(wide)

        def cornered(hop):
            index = lambda at, place, chip: (at * ring.dp + place) * 2 + chip
            pairs = [
                (index(p, a, q), index(q, b, p)) for a, b in hop for p in range(2) for q in range(2)
            ]
            return lambda array: lax.ppermute(array, ("section", "dp", "mp"), pairs)

        arrived, out_two, out_before = flow.step(
            (across, theirs[0]), (onward, outputs[1]), (ring.astern, outputs[0])
        )
        out_one = onward(
            tie((outputs[2].astype(wide) + out_two.astype(wide)).astype(low), arrived)
        )
        grad_far = to_other_chip(grad_section)
        flat = flat.reshape(8, -1)
        flat = (flat + across(flat)).reshape(-1)
        flat_width = flat.shape[0] // r
        flow.landed = (arrived,)
        value = total(1, arrived, None).astype(low)
        passed, arrived = flow.step((onward, value), (across, theirs[1]))
        out = outputs[3].astype(wide) + out_before.astype(wide) + out_one.astype(wide)
        vocab_rows = out[:, width_out:].astype(low)
        message = jnp.concatenate(
            [cut(out, 1 - x, r)[:, :width_out].astype(low), vocab_rows[:r], vocab_rows[r:]], axis=1
        )
        out_far = across(message)
        kept_rows = corners(tie(mine[3][:, :both], out_one))
        output_grad = cut(out, x, r)[:, :width_out] + out_far[:, :width_out].astype(wide)
        shard = jnp.concatenate([out[:r, width_out:], out[r:, width_out:]], axis=1)
        shard = (shard + out_far[:, width_out:].astype(wide)).astype(low)
        shard = jnp.concatenate([shard, halves(flat, r)], axis=1)
        value = total(2, arrived, passed).astype(low)
        passed, arrived = flow.step((onward, value), (across, theirs[2]), also=(grad_far,))
        next_one, next_three = onward(shard), ring.astern(shard)
        value = total(3, arrived, passed).astype(low)
        passed, arrived, energy_passed, energy_arrived = flow.step(
            (cornered(ring.ring), value[:, :both]), (cornered(ring.pair), theirs[3][:, :both]),
            (onward, value[:, both:]), (across, theirs[3][:, both:]),
            also=(kept_rows, next_one, next_three),
        )
        shards = {0: shard, 1: next_one, 3: next_three, 2: onward(next_one)}
        flat = sum(joined(a[:, 2 * block :], flat_width).reshape(-1) for a in shards.values())
        sides = corners(flat[sides_at : sides_at + wide_half + width])
        moved = kept_rows.astype(wide) + arrived.astype(wide) + passed.astype(wide)
        energy_grad = mine[3][:, both:].astype(wide) + energy_arrived.astype(wide)
        energy_grad = energy_grad + energy_passed.astype(wide)
        vocab_grad = jnp.zeros((vocab_pad, block), low)
        for k, held in shards.items():
            held = jnp.concatenate([held[:, :block], held[:, block : 2 * block]], axis=0)
            vocab_grad = lax.dynamic_update_slice(vocab_grad, held, (ring.back(k) * 2 * r, 0))
    else:
        grad_far = to_other_chip(grad_section)

        def scatter(parts):
            total = jnp.concatenate(parts, axis=0)
            return lax.psum_scatter(total, "dp", scatter_dimension=0, tiled=True).astype(wide)

        moved, output_grad = scatter(totals[:8]), scatter(totals[8:])
        moved, energy_grad = moved[:, : 2 * wide_half], moved[:, 2 * wide_half :]
        moved = corners(moved.astype(low)).astype(wide)
        flat = lax.psum(flat, "dp")
        sides = corners(flat[sides_at : sides_at + wide_half + width])
        vocab_grad = lax.all_gather(
            output_grad[:, 2 * block :].astype(low), "dp", axis=0, tiled=True
        )

    input_grad = jnp.where(s == y, grad_section, grad_far)
    vocab_grad = vocab_grad.T[:, :vocab_size].astype(wide)
    vector_sum = flat[: 5 * block].reshape(5, block)
    bias_sum = flat[5 * block : 5 * block + vocab_size]
    lstm_bias_sum = sides[:wide_half].reshape(1, 4, unit_half)
    gain_sum = sides[wide_half:][None]
    rec_grad = moved[:, :wide_half].reshape(1, shard_rows, 4, unit_half)
    in_grad = moved[:, wide_half:].reshape(1, shard_rows, 4, unit_half)
    mono_mem_grad, span_mem_grad, mono_dec_grad, span_dec_grad = [
        energy_grad[:, n * block : (n + 1) * block] for n in range(4)
    ]
    return (
        input_grad[None],
        gain_sum,
        in_grad,
        rec_grad,
        lstm_bias_sum,
        mono_mem_grad,
        mono_dec_grad,
        vector_sum[0],
        vector_sum[1],
        span_mem_grad,
        span_dec_grad,
        vector_sum[2],
        vector_sum[3],
        jnp.stack([output_grad[:, :block], output_grad[:, block : 2 * block]]),
        vector_sum[4],
        vocab_grad,
        bias_sum,
    )


def solution(mesh):
    both = ("section", "mp")
    in_specs = (
        P("section", "dp", None, None),
        P("section", None),
        P("section", "dp", None, "mp"),
        P("section", "dp", None, "mp"),
        P("section", None, "mp"),
        P("dp", both),
        P("dp", both),
        P(both),
        P(both),
        P("dp", both),
        P("dp", both),
        P(both),
        P(both),
        P(None, "dp", both),
        P(both),
        P(both, None),
        P(),
        P("dp", None, None),
        P("dp"),
        P("dp"),
        P("dp", None),
    )
    out_specs = (
        P("section", "dp", None, None),
        P("section", None),
        P("section", "dp", None, "mp"),
        P("section", "dp", None, "mp"),
        P("section", None, "mp"),
        P("dp", both),
        P("dp", both),
        P(both),
        P(both),
        P("dp", both),
        P("dp", both),
        P(both),
        P(both),
        P(None, "dp", both),
        P(both),
        P(both, None),
        P(),
    )
    dp = mesh.shape["dp"]

    def step(*arrays):
        return local(dp, *arrays)

    return jax.shard_map(step, mesh=mesh, in_specs=in_specs, out_specs=out_specs, check_vma=False)
```

```python
import functools

import jax
import jax.numpy as jnp
from jax import lax
from jax.experimental import pallas as pl
from jax.experimental.pallas import tpu as pltpu
from jax.sharding import PartitionSpec as P

epsilon = 1e-05
offset = -4.0
wide = jnp.float32
low = jnp.bfloat16
in_vmem = pl.BlockSpec(memory_space=pltpu.VMEM)
in_smem = pl.BlockSpec(memory_space=pltpu.SMEM)
in_place = pl.BlockSpec(memory_space=pl.ANY)
core_swap = [(0, 1), (1, 0)]
corner_swap = [(0, 0), (1, 2), (2, 1), (3, 3)]


def normalize(inputs, gain_row):
    average = jnp.mean(inputs, axis=-1, keepdims=True)
    centred = inputs - average
    spread = jnp.mean(centred * centred, axis=-1, keepdims=True)
    return centred * lax.rsqrt(spread + epsilon) * gain_row


def across_cores(array):
    return lax.ppermute(array, "section", core_swap)


def across_chips(array):
    return lax.ppermute(array, "mp", core_swap)


def corners(array):
    return lax.ppermute(array, ("section", "mp"), corner_swap)


def tie(value, *others):
    return lax.optimization_barrier((value,) + others)[0]


def cut(array, block, rows):
    return lax.dynamic_slice_in_dim(array, block * rows, rows, axis=0)


class Flow:
    def __init__(self):
        self.landed = ()

    def step(self, *jobs, also=()):
        operands = tuple(operand for _, operand in jobs)
        operands = lax.optimization_barrier(operands + self.landed + tuple(also))[: len(jobs)]
        results = [send(operand) for (send, _), operand in zip(jobs, operands)]
        self.landed = tuple(results)
        return results


class Ring:
    def __init__(self, dp):
        self.dp = dp
        self.outer = dp // 2
        self.short = dp % 2 == 0 and self.outer == 4
        pairs = [(z, x) for z in range(self.outer) for x in range(2)]
        self.pair = [(2 * z + x, 2 * z + 1 - x) for z, x in pairs]
        self.ring = [(2 * z + x, 2 * ((z + 1) % self.outer) + x) for z, x in pairs]
        self.turn = [(b, a) for a, b in self.ring]
        place = lax.axis_index("dp")
        self.z, self.x = place // 2, place % 2

    def across(self, array):
        return lax.ppermute(array, "dp", self.pair)

    def onward(self, array):
        return lax.ppermute(array, "dp", self.ring)

    def astern(self, array):
        return lax.ppermute(array, "dp", self.turn)

    def back(self, k):
        return lax.rem(self.z - k + self.outer, self.outer)


def halves(array, height):
    array = array.reshape(height, -1)
    upper = array.astype(low)
    lower = (array - upper.astype(wide)).astype(low)
    return jnp.pad(
        jnp.concatenate([upper, lower], axis=1), ((0, 0), (0, -2 * array.shape[1] % 128))
    )


def joined(array, count):
    return array[:, :count].astype(wide) + array[:, count : 2 * count].astype(wide)


def sigmoid(x):
    return 0.5 * jnp.tanh(0.5 * x) + 0.5


def fetch(blocks, places, side_blocks, target, sems, first=0, column=0):
    wide_half = target.shape[1] // 2
    columns = pl.ds(pl.multiple_of(side_blocks * wide_half, wide_half), wide_half)
    copies = []
    for k, block in enumerate(blocks):
        height = block.shape[0]
        span = pl.ds(pl.multiple_of(places[2 + k] * height, height), height)
        copies.append(
            pltpu.make_async_copy(
                block.at[:, column : column + wide_half],
                target.at[span, columns],
                sems.at[first + k],
            )
        )
    return copies


def forward_kernel(count, column, places, normed, b_own, b_other, *refs):
    in_own, in_other, w_own, w_other = [refs[n * count : (n + 1) * count] for n in range(4)]
    kept, given, before, gates, cells, wi, w, b, state, cell, sems = refs[4 * count :]
    steps, rows, wide_full = gates.shape
    wide_half = wide_full // 2
    unit_half = wide_half // 4
    chunk = min(256, unit_half)
    s = places[0]
    copies = fetch(in_own, places, s, wi, sems) + fetch(in_other, places, 1 - s, wi, sems, count)
    later = fetch(w_own, places, s, w, sems, 2 * count, column)
    later += fetch(w_other, places, 1 - s, w, sems, 3 * count, column)
    for copy in copies + later:
        copy.start()
    for source, at in ((b_own, s), (b_other, 1 - s)):
        b[:, pl.ds(pl.multiple_of(at * wide_half, wide_half), wide_half)] = source[...]
    state[...] = jnp.zeros_like(state)
    cell[...] = jnp.zeros_like(cell)
    for copy in copies:
        copy.wait()

    def project(g, carried):
        cols = pl.ds(pl.multiple_of(g * unit_half, unit_half), unit_half)
        value = jnp.dot(normed[...], wi[:, cols], preferred_element_type=wide) + b[:, cols]
        gates[:, :, cols] = value.reshape(steps, rows, unit_half)
        return carried

    lax.fori_loop(0, 8, project, 0)
    for copy in later:
        copy.wait()
    eighth = rows // 2
    first_chip = places[1] == 0

    def advance(t, carried):
        hidden = state[...]
        before[t] = hidden
        for at in range(0, 2 * unit_half, chunk):
            half, inside = at // unit_half, at % unit_half
            acts = []
            for g in range(4):
                cols = pl.ds(half * wide_half + g * unit_half + inside, chunk)
                value = gates[t, :, cols] + jnp.dot(
                    hidden, w[:, cols], preferred_element_type=wide
                )
                value = jnp.tanh(value) if g == 2 else sigmoid(value)
                gates[t, :, cols] = value
                acts.append(value)
            units = pl.ds(at, chunk)
            new_cell = acts[1] * cell[:, units] + acts[0] * acts[2]
            cell[:, units] = new_cell
            cells[t, :, units] = new_cell
            new_hidden = acts[3] * jnp.tanh(new_cell)
            state[:, units] = new_hidden.astype(low)
            upper, lower = new_hidden[:eighth], new_hidden[eighth:]
            kept[t, :, units] = jnp.where(first_chip, upper, lower).astype(low)
            given[t, :, units] = jnp.where(first_chip, lower, upper).astype(low)
        return carried

    lax.fori_loop(0, steps, advance, 0)


def run_forward(places, normed, b_own, b_other, in_own, in_other, w_own, w_other, steps, column):
    rows = normed.shape[0] // steps
    units = normed.shape[1]
    wide_half = b_own.shape[1]
    count = len(w_own)
    return pl.pallas_call(
        functools.partial(forward_kernel, count, column),
        out_shape=(
            jax.ShapeDtypeStruct((steps, rows // 2, units), low),
            jax.ShapeDtypeStruct((steps, rows // 2, units), low),
            jax.ShapeDtypeStruct((steps, rows, units), low),
            jax.ShapeDtypeStruct((steps, rows, 2 * wide_half), wide),
            jax.ShapeDtypeStruct((steps, rows, units), wide),
        ),
        in_specs=[in_smem] + [in_vmem] * 3 + [in_place] * (4 * count),
        out_specs=[in_vmem] * 5,
        scratch_shapes=[
            pltpu.VMEM((units, 2 * wide_half), low),
            pltpu.VMEM((units, 2 * wide_half), low),
            pltpu.VMEM((1, 2 * wide_half), wide),
            pltpu.VMEM((rows, units), low),
            pltpu.VMEM((rows, units), wide),
            pltpu.SemaphoreType.DMA((4 * count,)),
        ],
        compiler_params=pltpu.CompilerParams(vmem_limit_bytes=56 << 20),
        name="recur_forward",
    )(places, normed, b_own, b_other, *in_own, *in_other, *w_own, *w_other)


def backward_kernel(count, column, places, kept, taken, gates, cells, *refs):
    w_own, w_other = refs[:count], refs[count : 2 * count]
    dz_own, dz_other, dz, stage, w, dh, dc, sems = refs[2 * count :]
    steps, rows, wide_full = gates.shape
    wide_half = wide_full // 2
    unit_half = wide_half // 4
    chunk = min(256, unit_half)
    s = places[0]
    first_chip = places[1] == 0
    jobs = []
    for n, (sources, at) in enumerate(((w_own, s), (w_other, 1 - s))):
        for k, block in enumerate(sources):
            slot = n * count + k
            copy = pltpu.make_async_copy(
                block.at[:, column : column + wide_half], stage.at[slot], sems.at[slot]
            )
            copy.start()
            jobs.append((copy, slot, at, places[2 + k] * block.shape[0]))
    dh[...] = jnp.zeros_like(dh)
    dc[...] = jnp.zeros_like(dc)
    height = w_own[0].shape[0]
    piece = min(height, 128)
    for copy, slot, at, first in jobs:
        copy.wait()

        def turn(g, carried, slot=slot, at=at, first=first):
            columns = pl.ds(pl.multiple_of(g * unit_half, unit_half), unit_half)
            span = pl.ds(pl.multiple_of(at * wide_half + g * unit_half, unit_half), unit_half)
            for low_row in range(0, height, piece):
                into = pl.ds(pl.multiple_of(first + low_row, piece), piece)
                w[span, into] = stage[slot, low_row : low_row + piece, columns].T
            return carried

        lax.fori_loop(0, 4, turn, 0)

    def retreat(k, carried):
        t = steps - 1 - k
        earlier = jnp.maximum(t - 1, 0)
        live = jnp.where(t > 0, 1.0, 0.0).astype(wide)
        for at in range(0, 2 * unit_half, chunk):
            half, inside = at // unit_half, at % unit_half
            units = pl.ds(at, chunk)
            ours, theirs = kept[t, :, units], taken[t, :, units].astype(wide)
            grad = dh[:, units] + jnp.concatenate(
                [jnp.where(first_chip, ours, theirs), jnp.where(first_chip, theirs, ours)], axis=0
            )
            i, f, g, o = [
                gates[t, :, pl.ds(half * wide_half + n * unit_half + inside, chunk)]
                for n in range(4)
            ]
            squash = jnp.tanh(cells[t, :, units])
            total = dc[:, units] + grad * o * (1.0 - squash * squash)
            parts = (
                total * g * i * (1.0 - i),
                total * (cells[earlier, :, units] * live) * f * (1.0 - f),
                total * i * (1.0 - g * g),
                grad * squash * o * (1.0 - o),
            )
            for n, part in enumerate(parts):
                dz[half, :, pl.ds(n * unit_half + inside, chunk)] = part.astype(low)
            dc[:, units] = total * f
        dz_own[t] = dz[s]
        dz_other[t] = dz[1 - s]
        upper, lower = dz[0], dz[1]
        for at in range(0, 2 * unit_half, chunk):
            units = pl.ds(at, chunk)
            dh[:, units] = jnp.dot(
                upper, w[:wide_half, units], preferred_element_type=wide
            ) + jnp.dot(lower, w[wide_half:, units], preferred_element_type=wide)
        return carried

    lax.fori_loop(0, steps, retreat, 0)


def run_backward(places, kept, taken, gates, cells, w_own, w_other, column):
    steps, rows, wide_full = gates.shape
    units = cells.shape[2]
    count = len(w_own)
    return pl.pallas_call(
        functools.partial(backward_kernel, count, column),
        out_shape=(jax.ShapeDtypeStruct((steps, rows, wide_full // 2), low),) * 2,
        in_specs=[in_smem] + [in_vmem] * 4 + [in_place] * (2 * count),
        out_specs=[in_vmem] * 2,
        scratch_shapes=[
            pltpu.VMEM((2, rows, wide_full // 2), low),
            pltpu.VMEM((2 * count, units // count, wide_full // 2), low),
            pltpu.VMEM((wide_full, units), low),
            pltpu.VMEM((rows, units), wide),
            pltpu.VMEM((rows, units), wide),
            pltpu.SemaphoreType.DMA((2 * count,)),
        ],
        compiler_params=pltpu.CompilerParams(vmem_limit_bytes=56 << 20),
        name="recur_backward",
    )(places, kept, taken, gates, cells, *w_own, *w_other)


def input_kernel(count, places, inputs, gain, dz, dz_given, *refs):
    in_own, in_other = refs[:count], refs[count : 2 * count]
    grad_inputs, grad_gain, wi, sems = refs[2 * count :]
    s = places[0]
    copies = fetch(in_own, places, s, wi, sems) + fetch(in_other, places, 1 - s, wi, sems, count)
    for copy in copies:
        copy.start()
    x = inputs[...].astype(wide)
    centred = x - jnp.mean(x, axis=-1, keepdims=True)
    scale = lax.rsqrt(jnp.mean(centred * centred, axis=-1, keepdims=True) + epsilon)
    shape = centred * scale
    for copy in copies:
        copy.wait()
    wide_half = wi.shape[1] // 2
    own = pl.ds(pl.multiple_of(s * wide_half, wide_half), wide_half)
    other = pl.ds(pl.multiple_of((1 - s) * wide_half, wide_half), wide_half)
    grad = dot_nt(dz[...], wi[:, own]) + dot_nt(dz_given[...], wi[:, other])
    grad_gain[...] = jnp.sum(grad * shape, axis=0, keepdims=True)
    pulled = grad * gain[...]
    grad_inputs[...] = scale * (
        pulled
        - jnp.mean(pulled, axis=-1, keepdims=True)
        - shape * jnp.mean(pulled * shape, axis=-1, keepdims=True)
    )


def run_input(places, inputs, gain, dz, dz_given, in_own, in_other):
    count = len(in_own)
    rows, width = inputs.shape
    return pl.pallas_call(
        functools.partial(input_kernel, count),
        out_shape=(
            jax.ShapeDtypeStruct((rows, width), wide),
            jax.ShapeDtypeStruct((1, width), wide),
        ),
        in_specs=[in_smem] + [in_vmem] * 4 + [in_place] * (2 * count),
        out_specs=[in_vmem] * 2,
        scratch_shapes=[
            pltpu.VMEM((width, 2 * dz.shape[1]), low),
            pltpu.SemaphoreType.DMA((2 * count,)),
        ],
        compiler_params=pltpu.CompilerParams(vmem_limit_bytes=56 << 20),
        name="input_back",
    )(places, inputs, gain, dz, dz_given, *in_own, *in_other)


def dot_nt(a, b):
    return lax.dot_general(a, b, (((1,), (1,)), ((), ())), preferred_element_type=wide)


def dot_tn(a, b):
    return lax.dot_general(a, b, (((0,), (0,)), ((), ())), preferred_element_type=wide)


def attend_kernel(
    count, places, kept, taken, vectors, vocab_bias, noise, lengths, labels, counted, *refs
):
    small, vocab = refs[: 4 * count], refs[4 * count : 4 * count + 4]
    (
        grad_own, grad_given, pack_me, pack_chip, pack_cores, seen, near, far,
        memory, decoded, grad_memory, pack, sums, w, v, sems, v_sems, mk, sk, mq, sq, mono, span, keep, queue, scaled, ratio, window, mix, pre,
        mono_squash, span_squash,
    ) = refs[4 * count + 4 :]
    rows, _ = kept.shape
    frames, group, _ = mk.shape
    block = w.shape[2] // 6
    lanes = 128
    chunks = 4 * block // lanes
    copies = []
    for r in range(4):
        arrived = []
        for k in range(count):
            source = small[r * count + k]
            height = source.shape[0]
            for h in range(source.shape[1] // (6 * block)):
                to = pl.ds(pl.multiple_of(places[2 + len(arrived)] * height, height), height)
                arrived.append(
                    pltpu.make_async_copy(
                        source.at[:, 6 * block * h : 6 * block * (h + 1)],
                        w.at[r, to, :],
                        sems.at[r, len(arrived)],
                    )
                )
        copies.append(arrived)
    vocab_copies = [pltpu.make_async_copy(vocab[r], v.at[r], v_sems.at[r]) for r in range(4)]
    for copy in sum(copies, []) + vocab_copies:
        copy.start()

    first_chip = places[1] == 0

    @pl.when(first_chip)
    def _():
        memory[...] = kept[...]
        decoded[...] = taken[...]

    @pl.when(jnp.logical_not(first_chip))
    def _():
        memory[...] = taken[...]
        decoded[...] = kept[...]

    def split(value):
        return value.reshape(frames, group, value.shape[-1])

    mem, dec = memory[...], decoded[...]

    def lane(c):
        return pl.ds(c * lanes, lanes)

    def spread(row, c):
        return jnp.broadcast_to(vectors[row : row + 1, lane(c)], (group, lanes))

    def energies(queries, keys, vec_row, energy, kept_squash, r):
        mine = range(r * chunks // 4, (r + 1) * chunks // 4)
        weights = {c: spread(vec_row, c) for c in mine}

        def one(i, carried):
            query = {c: queries[i, :, lane(c)] for c in mine}
            for j in range(frames):
                total = None if r == 0 else energy[i * frames + j]
                for c in mine:
                    squash = jnp.tanh(query[c] + keys[j, :, lane(c)])
                    kept_squash[i * frames + j, :, lane(c)] = squash
                    part = squash * weights[c]
                    total = part if total is None else total + part
                if r == 3:
                    total = jnp.broadcast_to(
                        jnp.sum(total, axis=-1, keepdims=True), (group, lanes)
                    )
                energy[i * frames + j] = total
            return carried

        lax.fori_loop(0, frames, one, 0)

    for r in range(4):
        for copy in copies[r]:
            copy.wait()
        cols = pl.ds(r * block, block)
        keys = jnp.dot(mem, w[r, :, : 2 * block], preferred_element_type=wide)
        queries = jnp.dot(dec, w[r, :, 2 * block : 5 * block], preferred_element_type=wide)
        mk[:, :, cols] = split(keys[:, :block])
        sk[:, :, cols] = split(keys[:, block:])
        mq[:, :, cols] = split(queries[:, :block] + vectors[0:1, cols])
        sq[:, :, cols] = split(queries[:, block : 2 * block] + vectors[2:3, cols])
        pre[:, cols] = queries[:, 2 * block :] + vectors[4:5, cols]
        energies(mq, mk, 1, mono, mono_squash, r)
        energies(sq, sk, 3, span, span_squash, r)

    length = lengths[...]
    valid = [(length > j) for j in range(frames)]
    ones = jnp.ones((group, lanes), wide)
    zeros = jnp.zeros((group, lanes), wide)
    live = [jnp.where(valid[j], 1.0, 0.0).astype(wide) for j in range(frames)]
    diagonal = lax.broadcasted_iota(jnp.int32, (group, lanes), 1) - lax.broadcasted_iota(
        jnp.int32, (group, lanes), 0
    )

    def attend(i, previous):
        base = i * frames
        top = jnp.full((group, lanes), -1e30, wide)
        for j in range(frames):
            top = jnp.maximum(top, jnp.where(valid[j], span[base + j], -1e30))
        weight = [jnp.where(valid[j], jnp.exp(span[base + j] - top), 0.0) for j in range(frames)]
        current, ratios = [], []
        queued = previous[0]
        for j in range(frames):
            prob = sigmoid(mono[base + j] + offset + noise[base + j]) * live[j]
            keep[base + j] = prob
            queue[base + j] = queued
            alpha = prob * queued
            current.append(alpha)
            if j + 1 < frames:
                queued = (1.0 - prob) * queued + previous[j + 1]
            both = weight[j] + weight[j - 1] if j else weight[j]
            both = jnp.where(valid[j], both, 1.0)
            window[base + j] = both
            scaled[base + j] = weight[j]
            quotient = alpha / both
            ratio[base + j] = quotient
            ratios.append(quotient)
        row = zeros
        for j in range(frames):
            beta = weight[j] * (ratios[j] + (ratios[j + 1] if j + 1 < frames else zeros))
            row = jnp.where(diagonal == group * j, beta, row)
        mix[i] = row
        return tuple(current)

    lax.fori_loop(0, frames, attend, tuple([ones] + [zeros] * (frames - 1)))

    beta_low = mix[...].reshape(rows, lanes)[:, :rows].astype(low)
    context = jnp.dot(beta_low, mem, preferred_element_type=wide).astype(low)
    seen[0] = context
    for r in range(4):
        cols = pl.ds(r * block, block)
        value = jnp.tanh(
            pre[:, cols] + jnp.dot(context, w[r, :, 5 * block :], preferred_element_type=wide)
        )
        pre[:, cols] = value
        pack[r, :, 5 * block :] = value.astype(low)
    logits = vocab_bias[...]
    for r in range(4):
        vocab_copies[r].wait()
        logits = logits + jnp.dot(pack[r, :, 5 * block :], v[r], preferred_element_type=wide)
    shifted = jnp.exp(logits - jnp.max(logits, axis=-1, keepdims=True))
    softmax = shifted / jnp.sum(shifted, axis=-1, keepdims=True)
    onehot = (labels[...] == lax.broadcasted_iota(jnp.int32, softmax.shape, 1)).astype(wide)
    grad_logits = ((softmax - onehot) * counted[...]).astype(low)
    seen[1] = grad_logits
    sums[5:6, :] = jnp.sum(grad_logits.astype(wide), axis=0, keepdims=True)
    sums[6:8, :] = jnp.zeros((2, sums.shape[1]), wide)

    grad_context = jnp.zeros((rows, memory.shape[1]), wide)
    for r in range(4):
        cols = pl.ds(r * block, block)
        value = pre[:, cols]
        grad_pre = (dot_nt(grad_logits, v[r]) * (1.0 - value * value)).astype(low)
        pack[r, :, 4 * block : 5 * block] = grad_pre
        sums[4:5, cols] = jnp.sum(grad_pre.astype(wide), axis=0, keepdims=True)
        grad_context = grad_context + dot_nt(grad_pre, w[r, :, 5 * block :])
    upper = grad_context.astype(low)
    lower = (grad_context - upper.astype(wide)).astype(low)
    grad_memory[...] = dot_tn(beta_low, upper) + dot_tn(beta_low, lower)
    cross = dot_nt(upper, mem) + dot_nt(lower, mem)
    if rows < lanes:
        cross = jnp.concatenate([cross, jnp.zeros((rows, lanes - rows), wide)], axis=1)
    mix[...] = split(cross)

    def unattend(k, later):
        i = frames - 1 - k
        base = i * frames
        cross_row = mix[i]
        grad_beta = [
            jnp.broadcast_to(
                jnp.sum(
                    jnp.where(diagonal == group * j, cross_row, 0.0), axis=-1, keepdims=True
                ),
                (group, lanes),
            )
            for j in range(frames)
        ]
        weight = [scaled[base + j] for j in range(frames)]
        share = [ratio[base + j] for j in range(frames)]
        direct, from_window, grad_weight = [], [], []
        for j in range(frames):
            grad_ratio = grad_beta[j] * weight[j]
            if j:
                grad_ratio = grad_ratio + grad_beta[j - 1] * weight[j - 1]
            pull = grad_ratio / window[base + j]
            direct.append(pull)
            from_window.append(jnp.where(valid[j], -pull * share[j], 0.0))
            grad_weight.append(
                grad_beta[j] * (share[j] + (share[j + 1] if j + 1 < frames else zeros))
            )
        top = jnp.full((group, lanes), -1e30, wide)
        for j in range(frames):
            top = jnp.maximum(top, jnp.where(valid[j], span[base + j], -1e30))
        total, ties, at_top, through = zeros, zeros, [], []
        for j in range(frames):
            pulled = grad_weight[j] + from_window[j]
            if j + 1 < frames:
                pulled = pulled + from_window[j + 1]
            pulled = weight[j] * pulled
            through.append(pulled)
            total = total + pulled
            hit = jnp.where(span[base + j] == top, live[j], 0.0)
            at_top.append(hit)
            ties = ties + hit
        back = total / ties
        for j in range(frames):
            span[base + j] = through[j] - at_top[j] * back
        grad_queue = zeros
        now = [None] * frames
        for j in reversed(range(frames)):
            prob = keep[base + j]
            grad_alpha = direct[j] + later[j]
            mono[base + j] = queue[base + j] * (grad_alpha - grad_queue) * prob * (1.0 - prob)
            grad_queue = prob * grad_alpha + (1.0 - prob) * grad_queue
            now[j] = grad_queue
        return tuple(now)

    lax.fori_loop(0, frames, unattend, tuple([zeros] * frames))

    def energy_back(queries, keys, energy, kept_squash, bias_row, vec_row):
        def one_chunk(c, carried):
            at = pl.ds(pl.multiple_of(c * lanes, lanes), lanes)
            weight = jnp.broadcast_to(vectors[vec_row : vec_row + 1, at], (group, lanes))

            def one(i, carry):
                grad_keys, vec_total, bias_total = carry
                grad_query = zeros
                new_keys = []
                for j in range(frames):
                    squash = kept_squash[i * frames + j, :, at]
                    grad = energy[i * frames + j]
                    scaled_squash = grad * squash
                    vec_total = vec_total + scaled_squash
                    inner = grad - scaled_squash * squash
                    grad_query = grad_query + inner
                    new_keys.append(grad_keys[j] + inner)
                queries[i, :, at] = grad_query * weight
                return (tuple(new_keys), vec_total, bias_total + grad_query)

            grad_keys, vec_total, bias_total = lax.fori_loop(
                0, frames, one, (tuple([zeros] * frames), zeros, zeros)
            )
            for j in range(frames):
                keys[j, :, at] = grad_keys[j] * weight
            sums[bias_row : bias_row + 1, at] = jnp.sum(bias_total * weight, axis=0, keepdims=True)
            sums[vec_row : vec_row + 1, at] = jnp.sum(vec_total, axis=0, keepdims=True)
            return carried

        lax.fori_loop(0, chunks, one_chunk, 0)

    energy_back(mq, mk, mono, mono_squash, 0, 1)
    energy_back(sq, sk, span, span_squash, 2, 3)

    total_memory = grad_memory[...]
    total_decoded = jnp.zeros_like(total_memory)
    for r in range(4):
        cols = pl.ds(r * block, block)
        for n, source in enumerate((mk, sk, mq, sq)):
            pack[r, :, n * block : (n + 1) * block] = (
                source[:, :, cols].reshape(rows, block).astype(low)
            )
        total_memory = total_memory + dot_nt(pack[r, :, : 2 * block], w[r, :, : 2 * block])
        total_decoded = total_decoded + dot_nt(
            pack[r, :, 2 * block : 5 * block], w[r, :, 2 * block : 5 * block]
        )
    pack_me[...] = pack[0]
    pack_chip[...] = pack[1]
    pack_cores[...] = pack[2:4]
    middle = 2 * block
    near[...] = sums[:, :middle]
    far[:8, :] = sums[:, middle:]
    far[8:9, :] = sums[5:6, :middle]
    far[9:10, :] = sums[5:6, middle:]
    far[10:, :] = jnp.zeros((6, middle), wide)
    grad_own[...] = jnp.where(first_chip, total_memory, total_decoded)
    grad_given[...] = jnp.where(first_chip, total_decoded, total_memory).astype(low)


def run_attend(
    places, kept, taken, smalls, vocab, vectors, vocab_bias, noise, lengths, labels, counted,
    frames,
):
    rows, width = kept.shape
    group = rows // frames
    full = vectors.shape[1]
    vocab_width = vocab[0].shape[1]
    cell = (frames * frames, group, 128)
    count = len(smalls[0])
    return pl.pallas_call(
        functools.partial(attend_kernel, count),
        out_shape=(
            jax.ShapeDtypeStruct((rows, width), wide),
            jax.ShapeDtypeStruct((rows, width), low),
            jax.ShapeDtypeStruct((rows, full // 4 * 6), low),
            jax.ShapeDtypeStruct((rows, full // 4 * 6), low),
            jax.ShapeDtypeStruct((2, rows, full // 4 * 6), low),
            jax.ShapeDtypeStruct((2, rows, vocab_width), low),
            jax.ShapeDtypeStruct((8, full // 2), wide),
            jax.ShapeDtypeStruct((16, full // 2), wide),
        ),
        in_specs=[in_smem] + [in_vmem] * 8 + [in_place] * (4 * count + 4),
        out_specs=[in_vmem] * 8,
        scratch_shapes=[
            pltpu.VMEM((rows, width), low),
            pltpu.VMEM((rows, width), low),
            pltpu.VMEM((rows, width), wide),
            pltpu.VMEM((4, rows, full // 4 * 6), low),
            pltpu.VMEM((8, full), wide),
            pltpu.VMEM((4, width, full // 4 * 6), low),
            pltpu.VMEM((4,) + vocab[0].shape, low),
            pltpu.SemaphoreType.DMA((4, places.shape[0] - 2)),
            pltpu.SemaphoreType.DMA((4,)),
        ]
        + [pltpu.VMEM((frames, group, full), wide)] * 4
        + [pltpu.VMEM(cell, wide)] * 7
        + [pltpu.VMEM((frames, group, 128), wide), pltpu.VMEM((rows, full), wide)]
        + [pltpu.VMEM((frames * frames, group, full), wide)] * 2,
        compiler_params=pltpu.CompilerParams(vmem_limit_bytes=56 << 20),
        name="attend",
    )(
        places, kept, taken, vectors, vocab_bias, noise, lengths, labels, counted,
        *sum(smalls, []), *vocab,
    )


def gradient_kernel(
    order, before, before_peer, normed, normed_peer, dz, dz_peer, states_own, states_core,
    seen, seen_core, far, far_core, pack_me, pack_core, pack_far, *refs
):
    outputs, paired = refs[:8], refs[8:12]
    a_rec, a_in, a_dz, states, a_context, a_grads, a_pack, block, paired_block, sems, out_sems = (
        refs[12:]
    )
    y = order[0]
    height = block.shape[1]
    wide_half = a_dz.shape[1]
    part = a_pack.shape[1] // 6
    width = a_rec.shape[1]
    jobs = []
    for sources, target in (
        ((dz, dz_peer), a_dz),
        ((before, before_peer), a_rec),
        ((normed, normed_peer), a_in),
        (
            (states_own.at[0], states_core.at[0], states_own.at[2], states_core.at[2]),
            states.at[y],
        ),
        (
            (
                states_own.at[1], states_core.at[1],
                states_own.at[3], states_core.at[3],
            ),
            states.at[1 - y],
        ),
        ((pack_me, pack_core.at[0], pack_far.at[0], pack_far.at[1]), a_pack),
        ((seen.at[0], seen_core.at[0], far.at[0, :, :width], far_core.at[0, :, :width]), a_context),
        ((seen.at[1], seen_core.at[1], far.at[1, :, :width], far_core.at[1, :, :width]), a_grads),
    ):
        rows = target.shape[0] // len(sources)
        for r, source in enumerate(sources):
            jobs.append(
                pltpu.make_async_copy(
                    source, target.at[r * rows : (r + 1) * rows, :], sems.at[len(jobs)]
                )
            )
    for job in jobs:
        job.start()
    for job in jobs[:6]:
        job.wait()
    both = 2 * wide_half

    def one(n, carried):
        cols = pl.ds(pl.multiple_of(order[1 + n] * height, height), height)
        pair = jnp.concatenate([a_rec[:, cols], a_in[:, cols]], axis=1)
        for at in range(0, wide_half, 1024):
            value = dot_tn(pair, a_dz[:, at : at + 1024]).astype(low)
            block[n, :, at : at + 1024] = value[:height]
            block[n, :, wide_half + at : wide_half + at + 1024] = value[height:]
        for m, output in enumerate(outputs):

            @pl.when(n == m)
            def _(m=m, output=output):
                pltpu.make_async_copy(
                    block.at[m, :, :both], output.at[:, :both], out_sems.at[m]
                ).start()

        return carried

    lax.fori_loop(0, 8, one, 0)
    for job in jobs[6:]:
        job.wait()

    def two(n, carried):
        cols = pl.ds(pl.multiple_of(order[1 + n] * height, height), height)
        for m in range(2):
            to = both + 2 * m * part
            block[n, :, to : to + 2 * part] = dot_tn(
                states[m, :, cols], a_pack[:, 2 * m * part : 2 * (m + 1) * part]
            ).astype(low)
        for m, output in enumerate(outputs):

            @pl.when(n == m)
            def _(m=m, output=output):
                pltpu.make_async_copy(
                    block.at[m, :, both:], output.at[:, both:], out_sems.at[12 + m]
                ).start()

        return carried

    lax.fori_loop(0, 8, two, 0)

    def pair(n, carried):
        cols = pl.ds(pl.multiple_of(order[9 + n] * 2 * height, 2 * height), 2 * height)
        grad_pre = a_pack[:, 4 * part : 5 * part]
        for m, (a, b) in enumerate(
            (
                (states[1, :, cols], grad_pre),
                (a_context[:, cols], grad_pre),
                (a_grads[:, cols], a_pack[:, 5 * part :]),
            )
        ):
            paired_block[n, :, m * part : (m + 1) * part] = dot_tn(a, b).astype(low)
        return carried

    lax.fori_loop(0, 4, pair, 0)
    for m, output in enumerate(paired):
        pltpu.make_async_copy(paired_block.at[m], output, out_sems.at[8 + m]).start()
    for m, output in enumerate(outputs):
        pltpu.make_async_copy(
            block.at[m, :, :both], output.at[:, :both], out_sems.at[m]
        ).wait()
        pltpu.make_async_copy(
            block.at[m, :, both:], output.at[:, both:], out_sems.at[12 + m]
        ).wait()
    for m, output in enumerate(paired):
        pltpu.make_async_copy(paired_block.at[m], output, out_sems.at[8 + m]).wait()


def run_gradients(order, *arrays):
    rows, width = arrays[0].shape
    wide_half = arrays[5].shape[1]
    part = arrays[12].shape[1] // 6
    columns = 2 * wide_half + 4 * part
    height = width // 8
    deep = 2 * rows
    return pl.pallas_call(
        gradient_kernel,
        out_shape=tuple(
            [jax.ShapeDtypeStruct((height, columns), low)] * 8
            + [jax.ShapeDtypeStruct((2 * height, 3 * part), low)] * 4
        ),
        in_specs=[in_smem] + [in_place] * 15,
        out_specs=[in_place] * 12,
        scratch_shapes=[
            pltpu.VMEM((deep, width), low),
            pltpu.VMEM((deep, width), low),
            pltpu.VMEM((deep, wide_half), low),
            pltpu.VMEM((2, deep, width), low),
            pltpu.VMEM((deep, width), low),
            pltpu.VMEM((deep, width), low),
            pltpu.VMEM((deep, 6 * part), low),
            pltpu.VMEM((8, height, columns), low),
            pltpu.VMEM((4, 2 * height, 3 * part), low),
            pltpu.SemaphoreType.DMA((26,)),
            pltpu.SemaphoreType.DMA((20,)),
        ],
        compiler_params=pltpu.CompilerParams(vmem_limit_bytes=56 << 20),
        name="weight_gradients",
    )(order, *arrays)


def local(
    dp,
    block_input, norm_gain, lstm_in, lstm_rec, lstm_bias,
    mono_mem, mono_dec, mono_bias, mono_vec, span_mem, span_dec, span_bias, span_vec,
    out_weight, out_bias, vocab_weight, vocab_bias, noise, enc_lengths, label_lengths, labels,
):
    ring = Ring(dp)
    s, y = lax.axis_index("section"), lax.axis_index("mp")
    _, utts, frames, width = block_input.shape
    half, quarter = utts // 2, utts // 4
    rows = frames * quarter
    shard_rows, _, unit_half = lstm_in.shape[1:]
    wide_half = 4 * unit_half
    block = mono_mem.shape[1]
    vocab_size = vocab_weight.shape[1]
    vocab_pad = 4 * block

    in_shard = lstm_in[0].reshape(shard_rows, wide_half)
    rec_shard = lstm_rec[0].reshape(shard_rows, wide_half)
    bias_shard = lstm_bias[0].reshape(1, wide_half)

    def of_section(array):
        return jnp.where(s == y, array, across_cores(array))

    inputs = of_section(jnp.swapaxes(block_input[0], 0, 1))
    gain = of_section(norm_gain[0])
    inputs_own = lax.dynamic_slice_in_dim(inputs, s * half, half, axis=1)
    inputs_other = lax.dynamic_slice_in_dim(inputs, (1 - s) * half, half, axis=1)
    normed_own = normalize(inputs_own.astype(wide), gain)
    normed_own = normed_own.astype(low).reshape(frames * half, width)
    normed_other = normalize(inputs_other.astype(wide), gain)
    normed_other = normed_other.astype(low).reshape(frames * half, width)

    start = s * half + y * quarter
    noise_part = jnp.transpose(
        lax.dynamic_slice_in_dim(noise, start, quarter, axis=0), (1, 2, 0)
    ).reshape(frames * frames, quarter, 1)
    noise_part = jnp.broadcast_to(noise_part, (frames * frames, quarter, 128))
    length_part = lax.dynamic_slice_in_dim(enc_lengths, start, quarter, axis=0)
    length_part = jnp.broadcast_to(length_part[:, None], (quarter, 128))
    label_part = lax.dynamic_slice_in_dim(labels, start, quarter, axis=0).T.reshape(rows, 1)
    count_part = lax.dynamic_slice_in_dim(label_lengths, start, quarter, axis=0)
    counted = (jnp.arange(frames)[:, None] < count_part[None, :]).astype(wide).reshape(rows, 1)
    bias_row = jnp.pad(vocab_bias, (0, vocab_pad - vocab_size), constant_values=-1e30)[None]

    vector_own = jnp.stack([mono_bias, mono_vec, span_bias, span_vec, out_bias])
    vocab_own = jnp.pad(vocab_weight, ((0, 0), (0, vocab_pad - vocab_size)))
    ready = (noise_part, length_part, label_part, counted, bias_row, normed_own, normed_other)
    places, in_own, rec_own, small_own, small_chip = [], [], [], [], []
    small = jnp.concatenate(
        [
            tie(mono_mem, in_shard, rec_shard), span_mem, mono_dec, span_dec,
            out_weight[0], out_weight[1],
        ],
        axis=1,
    )
    if ring.short:
        flow, across, onward = Flow(), ring.across, ring.onward
        both = 2 * wide_half
        corner_in, corner_rec, b_own = flow.step(
            (corners, in_shard), (corners, rec_shard), (corners, bias_shard)
        )
        small_far, small_next = across(small), onward(small)
        flow.landed += (small_far, small_next)
        b_own = b_own.astype(wide)
        small_own = [jnp.concatenate([small, small_far], axis=1)]
        small_chip, small_core = [], []
        held = jnp.concatenate([corner_in, corner_rec, small_next], axis=1)
        near, far, near_core, far_core = [], [], [], []
        for k in range(ring.outer):
            near.append(held)
            jobs = [(across, held), (across_chips, small_own[k])]
            if k < ring.outer - 1:
                jobs.append((onward, held[:, :both] if k == ring.outer - 2 else held))
            if k == 0:
                jobs += [(across_chips, vocab_own), (across_chips, vector_own)]
            results = flow.step(*jobs, also=ready if k == 1 else ())
            far.append(results[0])
            small_chip.append(results[1])
            if k == 0:
                vocab_chip, vector_pair = results[3:]
                vector_pair = jnp.concatenate([vector_own, vector_pair], axis=1)
            if k < ring.outer - 1:
                small_own.append(jnp.concatenate([held[:, both:], far[k][:, both:]], axis=1))
                held = results[2]
        for a, b in zip(near, far):
            near_core.append(across_cores(a))
            far_core.append(across_cores(b))
        small_core = [across_cores(a) for a in small_own]
        b_last, vocab_last, chip_last, vector_last = lax.optimization_barrier(
            (b_own, vocab_own, vocab_chip, vector_pair, held)
        )[:4]
        b_other = across_cores(b_last)
        vocab = [vocab_own, vocab_chip, across_cores(vocab_last), across_cores(chip_last)]
        vector_core = across_cores(vector_last)
        in_own = [a for pair in zip(near, far) for a in pair]
        in_other = [a for pair in zip(near_core, far_core) for a in pair]
        rec_own, rec_other, rec_column = in_own, in_other, wide_half
        for k in range(ring.outer):
            places += [ring.back(k) * 2 + ring.x, ring.back(k) * 2 + 1 - ring.x]
    else:
        vocab_chip = across_chips(vocab_own)
        small, in_block, rec_block = [
            lax.all_gather(a, "dp", axis=0, tiled=True)
            for a in (small, corners(in_shard), corners(rec_shard))
        ]
        places, in_own, rec_own = [jnp.int32(0)], [in_block], [rec_block]
        small_own, small_chip = [small], [across_chips(small)]
        vocab = [vocab_own, vocab_chip, across_cores(vocab_own), across_cores(vocab_chip)]
        in_other, rec_other, rec_column = [across_cores(in_block)], [across_cores(rec_block)], 0
        small_core = [across_cores(small)]
        b_own = corners(bias_shard).astype(wide)
        b_other = across_cores(b_own)
        vector_pair = across_chips(vector_own)
        vector_pair = jnp.concatenate([vector_own, vector_pair], axis=1)
        vector_core = across_cores(vector_pair)
    vectors = jnp.concatenate([vector_pair, vector_core], axis=1)
    vectors = jnp.pad(vectors, ((0, 3), (0, 0)))
    places = jnp.stack([s, y] + places).astype(jnp.int32)
    z, x = ring.z, ring.x
    if ring.short:
        steps_back = [ring.back(k) for k in range(1, 5)]
        order = [at * 2 + 1 - x for at in steps_back] + [at * 2 + x for at in steps_back]
        order = [y] + order + steps_back
    else:
        order = [y] + [jnp.int32(k) for k in [*range(8), *range(4)]]
    order = jnp.stack(order).astype(jnp.int32)
    places = tie(places, order, vectors, *vocab, *ready, *small_chip[:-1], *small_core)

    kept, given, before, gates, cells = run_forward(
        places, normed_own, b_own, b_other, in_own, in_other, rec_own, rec_other, frames,
        rec_column,
    )

    kept, given = kept.reshape(rows, width), given.reshape(rows, width)
    taken = across_chips(given)
    small_chip[-1] = tie(small_chip[-1], kept)
    small_both = [across_cores(part) for part in small_chip]
    smalls = [small_own, small_chip, small_core, small_both]
    grad_own, grad_given, pack_me, pack_chip, pack_cores, seen, near, far = run_attend(
        places, kept, taken, smalls, vocab, vectors, bias_row, noise_part, length_part,
        label_part, counted, frames,
    )
    grad_given, kept_far = lax.optimization_barrier((grad_given, across_chips(tie(kept, taken))))
    grad_taken = across_chips(grad_given)
    pack_core = across_cores(pack_cores)
    pack_out = jnp.stack([pack_chip, pack_core[1]])
    far_peer = across_cores(far)
    vector_pair = (near[:5] + far_peer[:5]).reshape(5, 2, block)
    bias_pair = (far[8:10] + far_peer[8:10]).reshape(-1)
    vector_out = jnp.concatenate([vector_pair[:, 1].reshape(-1), bias_pair])
    vector_count = vector_out.shape[0] // (2 * rows)
    seen_out = jnp.concatenate(
        [seen, halves(vector_out, 2 * rows).reshape(2, rows, -1)], axis=2
    )
    before = before.reshape(frames * half, width)
    before_peer = across_cores(tie(before, taken))
    states = jnp.stack([tie(kept, grad_given), taken, given, kept_far])
    states_core, seen_core = across_cores(states), across_cores(seen)
    places_back, pack_out, seen_out = lax.optimization_barrier(
        (places, pack_out, seen_out, grad_taken, before_peer, states_core, seen_core)
    )[:3]
    dz_own, dz_other = run_backward(
        places_back, grad_own.reshape(frames, quarter, width),
        grad_taken.reshape(frames, quarter, width), gates, cells, rec_own, rec_other, rec_column,
    )
    pack_far = across_chips(pack_out)
    seen_far = across_chips(tie(seen_out, pack_out))

    dz_own, dz_other, pack_far, seen_far = lax.optimization_barrier(
        (
            dz_own.reshape(frames * half, wide_half), dz_other.reshape(frames * half, wide_half),
            pack_far, seen_far,
        )
    )
    dz_peer = across_cores(dz_other)
    totals = run_gradients(
        order, before, before_peer, normed_own, normed_other, dz_own,
        dz_peer, states, states_core, seen, seen_core, seen_far, across_cores(seen_far),
        pack_me, pack_core, pack_far,
    )
    vector_far = joined(seen_far[:, :, width:].reshape(2 * rows, -1), vector_count).reshape(-1)

    sides_at = 5 * block + vocab_pad
    def input_back(places):
        grad_inputs, grad_gain = run_input(
            places, inputs_own.reshape(frames * half, width), gain[None], dz_own, dz_other,
            in_own, in_other,
        )
        grad_gain = grad_gain.reshape(width)
        grad_inputs = jnp.swapaxes(grad_inputs.reshape(frames, half, width), 0, 1)
        grad_peer = across_cores(grad_inputs)
        grad_section = jnp.concatenate(
            [
                jnp.where(s == 0, grad_inputs, grad_peer),
                jnp.where(s == 0, grad_peer, grad_inputs),
            ],
            axis=0,
        )
        gain_sum = grad_gain + across_cores(grad_gain)
        flat = jnp.concatenate(
            [
                vector_pair[:, 0].reshape(-1) + vector_far[: 5 * block],
                bias_pair + vector_far[5 * block :],
                jnp.sum(dz_own.astype(wide), axis=0) + jnp.sum(dz_peer.astype(wide), axis=0),
                gain_sum,
            ]
        )
        return grad_section, jnp.pad(flat, (0, -flat.shape[0] % (8 * shard_rows)))

    def to_other_chip(section):
        return lax.ppermute(section, ("section", "mp"), [(0, 1), (3, 2)])

    if ring.short:
        r = shard_rows
        both, width_out = 2 * wide_half, 2 * block
        flow, across, onward = Flow(), ring.across, ring.onward
        theirs, mine, outputs = totals[:4], totals[4:8], totals[8:]

        def total(k, arrived, passed):
            value = mine[k - 1].astype(wide) + arrived.astype(wide)
            return value if passed is None else value + passed.astype(wide)

        def cornered(hop):
            index = lambda at, place, chip: (at * ring.dp + place) * 2 + chip
            pairs = [
                (index(p, a, q), index(q, b, p)) for a, b in hop for p in range(2) for q in range(2)
            ]
            return lambda array: lax.ppermute(array, ("section", "dp", "mp"), pairs)

        arrived, out_two, out_before = flow.step(
            (across, theirs[0]), (onward, outputs[1]), (ring.astern, outputs[0])
        )
        grad_section, flat = input_back(tie(places, out_two))
        out_one = onward(
            tie((outputs[2].astype(wide) + out_two.astype(wide)).astype(low), arrived)
        )
        grad_far = to_other_chip(grad_section)
        flat = flat.reshape(8, -1)
        flat = (flat + across(flat)).reshape(-1)
        flat_width = flat.shape[0] // r
        flow.landed = (arrived,)
        value = total(1, arrived, None).astype(low)
        passed, arrived = flow.step((onward, value), (across, theirs[1]))
        out = outputs[3].astype(wide) + out_before.astype(wide) + out_one.astype(wide)
        vocab_rows = out[:, width_out:].astype(low)
        message = jnp.concatenate(
            [cut(out, 1 - x, r)[:, :width_out].astype(low), vocab_rows[:r], vocab_rows[r:]], axis=1
        )
        kept_rows = corners(tie(mine[3][:, :both], out_one))
        value = total(2, arrived, passed).astype(low)
        passed, arrived, out_far = flow.step(
            (onward, value), (across, theirs[2]), (across, message), also=(grad_far,)
        )
        output_grad = cut(out, x, r)[:, :width_out] + out_far[:, :width_out].astype(wide)
        shard = jnp.concatenate([out[:r, width_out:], out[r:, width_out:]], axis=1)
        shard = (shard + out_far[:, width_out:].astype(wide)).astype(low)
        shard = jnp.concatenate([shard, halves(flat, r)], axis=1)
        next_one, next_three = onward(shard), ring.astern(shard)
        value = total(3, arrived, passed).astype(low)
        passed, arrived, energy_passed, energy_arrived, next_two = flow.step(
            (cornered(ring.ring), value[:, :both]), (cornered(ring.pair), theirs[3][:, :both]),
            (onward, value[:, both:]), (across, theirs[3][:, both:]), (onward, next_one),
            also=(kept_rows,),
        )
        shards = {0: shard, 1: next_one, 3: next_three, 2: next_two}
        flat = sum(joined(a[:, 2 * block :], flat_width).reshape(-1) for a in shards.values())
        sides = corners(flat[sides_at : sides_at + wide_half + width])
        moved = kept_rows.astype(wide) + arrived.astype(wide) + passed.astype(wide)
        energy_grad = mine[3][:, both:].astype(wide) + energy_arrived.astype(wide)
        energy_grad = energy_grad + energy_passed.astype(wide)
        vocab_grad = jnp.zeros((vocab_pad, block), low)
        for k, held in shards.items():
            held = jnp.concatenate([held[:, :block], held[:, block : 2 * block]], axis=0)
            vocab_grad = lax.dynamic_update_slice(vocab_grad, held, (ring.back(k) * 2 * r, 0))
    else:
        grad_section, flat = input_back(places)
        grad_far = to_other_chip(grad_section)

        def scatter(parts):
            total = jnp.concatenate(parts, axis=0)
            return lax.psum_scatter(total, "dp", scatter_dimension=0, tiled=True).astype(wide)

        moved, output_grad = scatter(totals[:8]), scatter(totals[8:])
        moved, energy_grad = moved[:, : 2 * wide_half], moved[:, 2 * wide_half :]
        moved = corners(moved.astype(low)).astype(wide)
        flat = lax.psum(flat, "dp")
        sides = corners(flat[sides_at : sides_at + wide_half + width])
        vocab_grad = lax.all_gather(
            output_grad[:, 2 * block :].astype(low), "dp", axis=0, tiled=True
        )

    input_grad = jnp.where(s == y, grad_section, grad_far)
    vocab_grad = vocab_grad.T[:, :vocab_size].astype(wide)
    vector_sum = flat[: 5 * block].reshape(5, block)
    bias_sum = flat[5 * block : 5 * block + vocab_size]
    lstm_bias_sum = sides[:wide_half].reshape(1, 4, unit_half)
    gain_sum = sides[wide_half:][None]
    rec_grad = moved[:, :wide_half].reshape(1, shard_rows, 4, unit_half)
    in_grad = moved[:, wide_half:].reshape(1, shard_rows, 4, unit_half)
    mono_mem_grad, span_mem_grad, mono_dec_grad, span_dec_grad = [
        energy_grad[:, n * block : (n + 1) * block] for n in range(4)
    ]
    return (
        input_grad[None],
        gain_sum,
        in_grad,
        rec_grad,
        lstm_bias_sum,
        mono_mem_grad,
        mono_dec_grad,
        vector_sum[0],
        vector_sum[1],
        span_mem_grad,
        span_dec_grad,
        vector_sum[2],
        vector_sum[3],
        jnp.stack([output_grad[:, :block], output_grad[:, block : 2 * block]]),
        vector_sum[4],
        vocab_grad,
        bias_sum,
    )


def solution(mesh):
    both = ("section", "mp")
    in_specs = (
        P("section", "dp", None, None),
        P("section", None),
        P("section", "dp", None, "mp"),
        P("section", "dp", None, "mp"),
        P("section", None, "mp"),
        P("dp", both),
        P("dp", both),
        P(both),
        P(both),
        P("dp", both),
        P("dp", both),
        P(both),
        P(both),
        P(None, "dp", both),
        P(both),
        P(both, None),
        P(),
        P("dp", None, None),
        P("dp"),
        P("dp"),
        P("dp", None),
    )
    out_specs = (
        P("section", "dp", None, None),
        P("section", None),
        P("section", "dp", None, "mp"),
        P("section", "dp", None, "mp"),
        P("section", None, "mp"),
        P("dp", both),
        P("dp", both),
        P(both),
        P(both),
        P("dp", both),
        P("dp", both),
        P(both),
        P(both),
        P(None, "dp", both),
        P(both),
        P(both, None),
        P(),
    )
    dp = mesh.shape["dp"]

    def step(*arrays):
        return local(dp, *arrays)

    return jax.shard_map(step, mesh=mesh, in_specs=in_specs, out_specs=out_specs, check_vma=False)
```

```python
import functools

import jax
import jax.numpy as jnp
from jax import lax
from jax.experimental import pallas as pl
from jax.experimental.pallas import tpu as pltpu
from jax.sharding import PartitionSpec as P

epsilon = 1e-05
offset = -4.0
wide = jnp.float32
low = jnp.bfloat16
in_vmem = pl.BlockSpec(memory_space=pltpu.VMEM)
in_smem = pl.BlockSpec(memory_space=pltpu.SMEM)
in_place = pl.BlockSpec(memory_space=pl.ANY)
core_swap = [(0, 1), (1, 0)]
corner_swap = [(0, 0), (1, 2), (2, 1), (3, 3)]


def normalize(inputs, gain_row):
    average = jnp.mean(inputs, axis=-1, keepdims=True)
    centred = inputs - average
    spread = jnp.mean(centred * centred, axis=-1, keepdims=True)
    return centred * lax.rsqrt(spread + epsilon) * gain_row


def across_cores(array):
    return lax.ppermute(array, "section", core_swap)


def across_chips(array):
    return lax.ppermute(array, "mp", core_swap)


def corners(array):
    return lax.ppermute(array, ("section", "mp"), corner_swap)


def tie(value, *others):
    return lax.optimization_barrier((value,) + others)[0]


def cut(array, block, rows):
    return lax.dynamic_slice_in_dim(array, block * rows, rows, axis=0)


class Flow:
    def __init__(self):
        self.landed = ()

    def step(self, *jobs, also=()):
        operands = tuple(operand for _, operand in jobs)
        operands = lax.optimization_barrier(operands + self.landed + tuple(also))[: len(jobs)]
        results = [send(operand) for (send, _), operand in zip(jobs, operands)]
        self.landed = tuple(results)
        return results


class Ring:
    def __init__(self, dp):
        self.dp = dp
        self.outer = dp // 2
        self.short = dp % 2 == 0 and self.outer == 4
        pairs = [(z, x) for z in range(self.outer) for x in range(2)]
        self.pair = [(2 * z + x, 2 * z + 1 - x) for z, x in pairs]
        self.ring = [(2 * z + x, 2 * ((z + 1) % self.outer) + x) for z, x in pairs]
        self.turn = [(b, a) for a, b in self.ring]
        place = lax.axis_index("dp")
        self.z, self.x = place // 2, place % 2

    def across(self, array):
        return lax.ppermute(array, "dp", self.pair)

    def onward(self, array):
        return lax.ppermute(array, "dp", self.ring)

    def astern(self, array):
        return lax.ppermute(array, "dp", self.turn)

    def back(self, k):
        return lax.rem(self.z - k + self.outer, self.outer)


def halves(array, height):
    array = array.reshape(height, -1)
    upper = array.astype(low)
    lower = (array - upper.astype(wide)).astype(low)
    return jnp.pad(
        jnp.concatenate([upper, lower], axis=1), ((0, 0), (0, -2 * array.shape[1] % 128))
    )


def joined(array, count):
    return array[:, :count].astype(wide) + array[:, count : 2 * count].astype(wide)


def sigmoid(x):
    return 0.5 * jnp.tanh(0.5 * x) + 0.5


def fetch(blocks, places, side_blocks, target, sems, first=0, column=0):
    wide_half = target.shape[1] // 2
    columns = pl.ds(pl.multiple_of(side_blocks * wide_half, wide_half), wide_half)
    copies = []
    for k, block in enumerate(blocks):
        height = block.shape[0]
        span = pl.ds(pl.multiple_of(places[2 + k] * height, height), height)
        copies.append(
            pltpu.make_async_copy(
                block.at[:, column : column + wide_half],
                target.at[span, columns],
                sems.at[first + k],
            )
        )
    return copies


def forward_kernel(count, column, places, normed, b_own, b_other, *refs):
    in_own, in_other, w_own, w_other = [refs[n * count : (n + 1) * count] for n in range(4)]
    (
        kept, given, before, gates_out, cells_out, gates, cells, wi, w, b, state, cell, sems,
        gate_sems, cell_sems,
    ) = refs[4 * count :]
    steps, rows, wide_full = gates.shape
    wide_half = wide_full // 2
    unit_half = wide_half // 4
    chunk = min(256, unit_half)
    s = places[0]
    copies = fetch(in_own, places, s, wi, sems) + fetch(in_other, places, 1 - s, wi, sems, count)
    later = fetch(w_own, places, s, w, sems, 2 * count, column)
    later += fetch(w_other, places, 1 - s, w, sems, 3 * count, column)
    for copy in copies + later:
        copy.start()
    for source, at in ((b_own, s), (b_other, 1 - s)):
        b[:, pl.ds(pl.multiple_of(at * wide_half, wide_half), wide_half)] = source[...]
    state[...] = jnp.zeros_like(state)
    cell[...] = jnp.zeros_like(cell)
    for copy in copies:
        copy.wait()

    def project(g, carried):
        cols = pl.ds(pl.multiple_of(g * unit_half, unit_half), unit_half)
        value = jnp.dot(normed[...], wi[:, cols], preferred_element_type=wide) + b[:, cols]
        gates[:, :, cols] = value.reshape(steps, rows, unit_half)
        return carried

    lax.fori_loop(0, 8, project, 0)
    for copy in later:
        copy.wait()
    eighth = rows // 2
    first_chip = places[1] == 0

    def advance(t, carried):
        hidden = state[...]
        before[t] = hidden
        for at in range(0, 2 * unit_half, chunk):
            half, inside = at // unit_half, at % unit_half
            acts = []
            for g in range(4):
                cols = pl.ds(half * wide_half + g * unit_half + inside, chunk)
                value = gates[t, :, cols] + jnp.dot(
                    hidden, w[:, cols], preferred_element_type=wide
                )
                value = jnp.tanh(value) if g == 2 else sigmoid(value)
                gates[t, :, cols] = value
                acts.append(value)
            units = pl.ds(at, chunk)
            new_cell = acts[1] * cell[:, units] + acts[0] * acts[2]
            cell[:, units] = new_cell
            cells[t, :, units] = new_cell
            new_hidden = acts[3] * jnp.tanh(new_cell)
            state[:, units] = new_hidden.astype(low)
            upper, lower = new_hidden[:eighth], new_hidden[eighth:]
            kept[t, :, units] = jnp.where(first_chip, upper, lower).astype(low)
            given[t, :, units] = jnp.where(first_chip, lower, upper).astype(low)
        pltpu.make_async_copy(gates.at[t], gates_out.at[t], gate_sems.at[t]).start()
        pltpu.make_async_copy(cells.at[t], cells_out.at[t], cell_sems.at[t]).start()
        return carried

    lax.fori_loop(0, steps, advance, 0)

    def settle(t, carried):
        pltpu.make_async_copy(gates.at[t], gates_out.at[t], gate_sems.at[t]).wait()
        pltpu.make_async_copy(cells.at[t], cells_out.at[t], cell_sems.at[t]).wait()
        return carried

    lax.fori_loop(0, steps, settle, 0)


def run_forward(places, normed, b_own, b_other, in_own, in_other, w_own, w_other, steps, column):
    rows = normed.shape[0] // steps
    units = normed.shape[1]
    wide_half = b_own.shape[1]
    count = len(w_own)
    return pl.pallas_call(
        functools.partial(forward_kernel, count, column),
        out_shape=(
            jax.ShapeDtypeStruct((steps, rows // 2, units), low),
            jax.ShapeDtypeStruct((steps, rows // 2, units), low),
            jax.ShapeDtypeStruct((steps, rows, units), low),
            jax.ShapeDtypeStruct((steps, rows, 2 * wide_half), wide),
            jax.ShapeDtypeStruct((steps, rows, units), wide),
        ),
        in_specs=[in_smem] + [in_vmem] * 3 + [in_place] * (4 * count),
        out_specs=[in_vmem] * 3 + [in_place] * 2,
        scratch_shapes=[
            pltpu.VMEM((steps, rows, 2 * wide_half), wide),
            pltpu.VMEM((steps, rows, units), wide),
            pltpu.VMEM((units, 2 * wide_half), low),
            pltpu.VMEM((units, 2 * wide_half), low),
            pltpu.VMEM((1, 2 * wide_half), wide),
            pltpu.VMEM((rows, units), low),
            pltpu.VMEM((rows, units), wide),
            pltpu.SemaphoreType.DMA((4 * count,)),
            pltpu.SemaphoreType.DMA((steps,)),
            pltpu.SemaphoreType.DMA((steps,)),
        ],
        compiler_params=pltpu.CompilerParams(vmem_limit_bytes=56 << 20),
        name="recur_forward",
    )(places, normed, b_own, b_other, *in_own, *in_other, *w_own, *w_other)


def backward_kernel(count, column, places, kept, taken, gates_in, cells_in, *refs):
    w_own, w_other = refs[:count], refs[count : 2 * count]
    dz_own, dz_other, gates, cells, dz, stage, w, dh, dc, sems, gate_sems, cell_sems = refs[
        2 * count :
    ]
    steps, rows, wide_full = gates.shape
    wide_half = wide_full // 2
    unit_half = wide_half // 4
    chunk = min(256, unit_half)
    s = places[0]
    first_chip = places[1] == 0

    def gate_copy(t):
        return pltpu.make_async_copy(gates_in.at[t], gates.at[t], gate_sems.at[t])

    def cell_copy(t):
        return pltpu.make_async_copy(cells_in.at[t], cells.at[t], cell_sems.at[t])

    gate_copy(steps - 1).start()
    cell_copy(steps - 1).start()
    jobs = []
    for n, (sources, at) in enumerate(((w_own, s), (w_other, 1 - s))):
        for k, block in enumerate(sources):
            slot = n * count + k
            copy = pltpu.make_async_copy(
                block.at[:, column : column + wide_half], stage.at[slot], sems.at[slot]
            )
            copy.start()
            jobs.append((copy, slot, at, places[2 + k] * block.shape[0]))
    for t in range(steps - 2, -1, -1):
        cell_copy(t).start()
        gate_copy(t).start()
    dh[...] = jnp.zeros_like(dh)
    dc[...] = jnp.zeros_like(dc)
    height = w_own[0].shape[0]
    piece = min(height, 128)
    for copy, slot, at, first in jobs:
        copy.wait()

        def turn(g, carried, slot=slot, at=at, first=first):
            columns = pl.ds(pl.multiple_of(g * unit_half, unit_half), unit_half)
            span = pl.ds(pl.multiple_of(at * wide_half + g * unit_half, unit_half), unit_half)
            for low_row in range(0, height, piece):
                into = pl.ds(pl.multiple_of(first + low_row, piece), piece)
                w[span, into] = stage[slot, low_row : low_row + piece, columns].T
            return carried

        lax.fori_loop(0, 4, turn, 0)

    cell_copy(steps - 1).wait()

    def retreat(k, carried):
        t = steps - 1 - k
        earlier = jnp.maximum(t - 1, 0)
        gate_copy(t).wait()

        @pl.when(t > 0)
        def _():
            cell_copy(earlier).wait()

        live = jnp.where(t > 0, 1.0, 0.0).astype(wide)
        for at in range(0, 2 * unit_half, chunk):
            half, inside = at // unit_half, at % unit_half
            units = pl.ds(at, chunk)
            ours, theirs = kept[t, :, units], taken[t, :, units].astype(wide)
            grad = dh[:, units] + jnp.concatenate(
                [jnp.where(first_chip, ours, theirs), jnp.where(first_chip, theirs, ours)], axis=0
            )
            i, f, g, o = [
                gates[t, :, pl.ds(half * wide_half + n * unit_half + inside, chunk)]
                for n in range(4)
            ]
            squash = jnp.tanh(cells[t, :, units])
            total = dc[:, units] + grad * o * (1.0 - squash * squash)
            parts = (
                total * g * i * (1.0 - i),
                total * (cells[earlier, :, units] * live) * f * (1.0 - f),
                total * i * (1.0 - g * g),
                grad * squash * o * (1.0 - o),
            )
            for n, part in enumerate(parts):
                dz[half, :, pl.ds(n * unit_half + inside, chunk)] = part.astype(low)
            dc[:, units] = total * f
        dz_own[t] = dz[s]
        dz_other[t] = dz[1 - s]
        upper, lower = dz[0], dz[1]
        for at in range(0, 2 * unit_half, chunk):
            units = pl.ds(at, chunk)
            dh[:, units] = jnp.dot(
                upper, w[:wide_half, units], preferred_element_type=wide
            ) + jnp.dot(lower, w[wide_half:, units], preferred_element_type=wide)
        return carried

    lax.fori_loop(0, steps, retreat, 0)


def run_backward(places, kept, taken, gates, cells, w_own, w_other, column):
    steps, rows, wide_full = gates.shape
    units = cells.shape[2]
    count = len(w_own)
    return pl.pallas_call(
        functools.partial(backward_kernel, count, column),
        out_shape=(jax.ShapeDtypeStruct((steps, rows, wide_full // 2), low),) * 2,
        in_specs=[in_smem] + [in_vmem] * 2 + [in_place] * (2 + 2 * count),
        out_specs=[in_vmem] * 2,
        scratch_shapes=[
            pltpu.VMEM((steps, rows, wide_full), wide),
            pltpu.VMEM((steps, rows, units), wide),
            pltpu.VMEM((2, rows, wide_full // 2), low),
            pltpu.VMEM((2 * count, units // count, wide_full // 2), low),
            pltpu.VMEM((wide_full, units), low),
            pltpu.VMEM((rows, units), wide),
            pltpu.VMEM((rows, units), wide),
            pltpu.SemaphoreType.DMA((2 * count,)),
            pltpu.SemaphoreType.DMA((steps,)),
            pltpu.SemaphoreType.DMA((steps,)),
        ],
        compiler_params=pltpu.CompilerParams(vmem_limit_bytes=56 << 20),
        name="recur_backward",
    )(places, kept, taken, gates, cells, *w_own, *w_other)


def input_kernel(count, places, inputs, gain, dz, dz_given, *refs):
    in_own, in_other = refs[:count], refs[count : 2 * count]
    grad_inputs, grad_gain, wi, sems = refs[2 * count :]
    s = places[0]
    copies = fetch(in_own, places, s, wi, sems) + fetch(in_other, places, 1 - s, wi, sems, count)
    for copy in copies:
        copy.start()
    x = inputs[...].astype(wide)
    centred = x - jnp.mean(x, axis=-1, keepdims=True)
    scale = lax.rsqrt(jnp.mean(centred * centred, axis=-1, keepdims=True) + epsilon)
    shape = centred * scale
    for copy in copies:
        copy.wait()
    wide_half = wi.shape[1] // 2
    own = pl.ds(pl.multiple_of(s * wide_half, wide_half), wide_half)
    other = pl.ds(pl.multiple_of((1 - s) * wide_half, wide_half), wide_half)
    grad = dot_nt(dz[...], wi[:, own]) + dot_nt(dz_given[...], wi[:, other])
    grad_gain[...] = jnp.sum(grad * shape, axis=0, keepdims=True)
    pulled = grad * gain[...]
    grad_inputs[...] = scale * (
        pulled
        - jnp.mean(pulled, axis=-1, keepdims=True)
        - shape * jnp.mean(pulled * shape, axis=-1, keepdims=True)
    )


def run_input(places, inputs, gain, dz, dz_given, in_own, in_other):
    count = len(in_own)
    rows, width = inputs.shape
    return pl.pallas_call(
        functools.partial(input_kernel, count),
        out_shape=(
            jax.ShapeDtypeStruct((rows, width), wide),
            jax.ShapeDtypeStruct((1, width), wide),
        ),
        in_specs=[in_smem] + [in_vmem] * 4 + [in_place] * (2 * count),
        out_specs=[in_vmem] * 2,
        scratch_shapes=[
            pltpu.VMEM((width, 2 * dz.shape[1]), low),
            pltpu.SemaphoreType.DMA((2 * count,)),
        ],
        compiler_params=pltpu.CompilerParams(vmem_limit_bytes=56 << 20),
        name="input_back",
    )(places, inputs, gain, dz, dz_given, *in_own, *in_other)


def dot_nt(a, b):
    return lax.dot_general(a, b, (((1,), (1,)), ((), ())), preferred_element_type=wide)


def dot_tn(a, b):
    return lax.dot_general(a, b, (((0,), (0,)), ((), ())), preferred_element_type=wide)


def attend_kernel(
    count, places, kept, taken, vectors, vocab_bias, noise, lengths, labels, counted, *refs
):
    small, vocab = refs[: 4 * count], refs[4 * count : 4 * count + 4]
    (
        grad_own, grad_given, pack_me, pack_chip, pack_cores, seen, near, far,
        memory, decoded, grad_memory, pack, sums, w, v, sems, v_sems, mk, sk, mq, sq, mono, span, keep, queue, scaled, ratio, window, mix, pre,
        mono_squash, span_squash,
    ) = refs[4 * count + 4 :]
    rows, _ = kept.shape
    frames, group, _ = mk.shape
    block = w.shape[2] // 6
    lanes = 128
    chunks = 4 * block // lanes
    copies = []
    for r in range(4):
        arrived = []
        for k in range(count):
            source = small[r * count + k]
            height = source.shape[0]
            for h in range(source.shape[1] // (6 * block)):
                to = pl.ds(pl.multiple_of(places[2 + len(arrived)] * height, height), height)
                arrived.append(
                    pltpu.make_async_copy(
                        source.at[:, 6 * block * h : 6 * block * (h + 1)],
                        w.at[r, to, :],
                        sems.at[r, len(arrived)],
                    )
                )
        copies.append(arrived)
    vocab_copies = [pltpu.make_async_copy(vocab[r], v.at[r], v_sems.at[r]) for r in range(4)]
    for copy in sum(copies, []) + vocab_copies:
        copy.start()

    first_chip = places[1] == 0

    @pl.when(first_chip)
    def _():
        memory[...] = kept[...]
        decoded[...] = taken[...]

    @pl.when(jnp.logical_not(first_chip))
    def _():
        memory[...] = taken[...]
        decoded[...] = kept[...]

    def split(value):
        return value.reshape(frames, group, value.shape[-1])

    mem, dec = memory[...], decoded[...]

    def lane(c):
        return pl.ds(c * lanes, lanes)

    def spread(row, c):
        return jnp.broadcast_to(vectors[row : row + 1, lane(c)], (group, lanes))

    def energies(queries, keys, vec_row, energy, kept_squash, r):
        mine = range(r * chunks // 4, (r + 1) * chunks // 4)
        weights = {c: spread(vec_row, c) for c in mine}

        def one(i, carried):
            query = {c: queries[i, :, lane(c)] for c in mine}
            for j in range(frames):
                total = None if r == 0 else energy[i * frames + j]
                for c in mine:
                    squash = jnp.tanh(query[c] + keys[j, :, lane(c)])
                    kept_squash[i * frames + j, :, lane(c)] = squash
                    part = squash * weights[c]
                    total = part if total is None else total + part
                if r == 3:
                    total = jnp.broadcast_to(
                        jnp.sum(total, axis=-1, keepdims=True), (group, lanes)
                    )
                energy[i * frames + j] = total
            return carried

        lax.fori_loop(0, frames, one, 0)

    for r in range(4):
        for copy in copies[r]:
            copy.wait()
        cols = pl.ds(r * block, block)
        keys = jnp.dot(mem, w[r, :, : 2 * block], preferred_element_type=wide)
        queries = jnp.dot(dec, w[r, :, 2 * block : 5 * block], preferred_element_type=wide)
        mk[:, :, cols] = split(keys[:, :block])
        sk[:, :, cols] = split(keys[:, block:])
        mq[:, :, cols] = split(queries[:, :block] + vectors[0:1, cols])
        sq[:, :, cols] = split(queries[:, block : 2 * block] + vectors[2:3, cols])
        pre[:, cols] = queries[:, 2 * block :] + vectors[4:5, cols]
        energies(mq, mk, 1, mono, mono_squash, r)
        energies(sq, sk, 3, span, span_squash, r)

    length = lengths[...]
    valid = [(length > j) for j in range(frames)]
    ones = jnp.ones((group, lanes), wide)
    zeros = jnp.zeros((group, lanes), wide)
    live = [jnp.where(valid[j], 1.0, 0.0).astype(wide) for j in range(frames)]
    diagonal = lax.broadcasted_iota(jnp.int32, (group, lanes), 1) - lax.broadcasted_iota(
        jnp.int32, (group, lanes), 0
    )

    def attend(i, previous):
        base = i * frames
        top = jnp.full((group, lanes), -1e30, wide)
        for j in range(frames):
            top = jnp.maximum(top, jnp.where(valid[j], span[base + j], -1e30))
        weight = [jnp.where(valid[j], jnp.exp(span[base + j] - top), 0.0) for j in range(frames)]
        current, ratios = [], []
        queued = previous[0]
        for j in range(frames):
            prob = sigmoid(mono[base + j] + offset + noise[base + j]) * live[j]
            keep[base + j] = prob
            queue[base + j] = queued
            alpha = prob * queued
            current.append(alpha)
            if j + 1 < frames:
                queued = (1.0 - prob) * queued + previous[j + 1]
            both = weight[j] + weight[j - 1] if j else weight[j]
            both = jnp.where(valid[j], both, 1.0)
            window[base + j] = both
            scaled[base + j] = weight[j]
            quotient = alpha / both
            ratio[base + j] = quotient
            ratios.append(quotient)
        row = zeros
        for j in range(frames):
            beta = weight[j] * (ratios[j] + (ratios[j + 1] if j + 1 < frames else zeros))
            row = jnp.where(diagonal == group * j, beta, row)
        mix[i] = row
        return tuple(current)

    lax.fori_loop(0, frames, attend, tuple([ones] + [zeros] * (frames - 1)))

    beta_low = mix[...].reshape(rows, lanes)[:, :rows].astype(low)
    context = jnp.dot(beta_low, mem, preferred_element_type=wide).astype(low)
    seen[0] = context
    for r in range(4):
        cols = pl.ds(r * block, block)
        value = jnp.tanh(
            pre[:, cols] + jnp.dot(context, w[r, :, 5 * block :], preferred_element_type=wide)
        )
        pre[:, cols] = value
        pack[r, :, 5 * block :] = value.astype(low)
    logits = vocab_bias[...]
    for r in range(4):
        vocab_copies[r].wait()
        logits = logits + jnp.dot(pack[r, :, 5 * block :], v[r], preferred_element_type=wide)
    shifted = jnp.exp(logits - jnp.max(logits, axis=-1, keepdims=True))
    softmax = shifted / jnp.sum(shifted, axis=-1, keepdims=True)
    onehot = (labels[:, :1] == lax.broadcasted_iota(jnp.int32, softmax.shape, 1)).astype(wide)
    grad_logits = ((softmax - onehot) * counted[:, :1]).astype(low)
    seen[1] = grad_logits
    sums[5:6, :] = jnp.sum(grad_logits.astype(wide), axis=0, keepdims=True)
    sums[6:8, :] = jnp.zeros((2, sums.shape[1]), wide)

    grad_context = jnp.zeros((rows, memory.shape[1]), wide)
    for r in range(4):
        cols = pl.ds(r * block, block)
        value = pre[:, cols]
        grad_pre = (dot_nt(grad_logits, v[r]) * (1.0 - value * value)).astype(low)
        pack[r, :, 4 * block : 5 * block] = grad_pre
        sums[4:5, cols] = jnp.sum(grad_pre.astype(wide), axis=0, keepdims=True)
        grad_context = grad_context + dot_nt(grad_pre, w[r, :, 5 * block :])
    upper = grad_context.astype(low)
    lower = (grad_context - upper.astype(wide)).astype(low)
    grad_memory[...] = dot_tn(beta_low, upper) + dot_tn(beta_low, lower)
    cross = dot_nt(upper, mem) + dot_nt(lower, mem)
    if rows < lanes:
        cross = jnp.concatenate([cross, jnp.zeros((rows, lanes - rows), wide)], axis=1)
    mix[...] = split(cross)

    def unattend(k, later):
        i = frames - 1 - k
        base = i * frames
        cross_row = mix[i]
        grad_beta = [
            jnp.broadcast_to(
                jnp.sum(
                    jnp.where(diagonal == group * j, cross_row, 0.0), axis=-1, keepdims=True
                ),
                (group, lanes),
            )
            for j in range(frames)
        ]
        weight = [scaled[base + j] for j in range(frames)]
        share = [ratio[base + j] for j in range(frames)]
        direct, from_window, grad_weight = [], [], []
        for j in range(frames):
            grad_ratio = grad_beta[j] * weight[j]
            if j:
                grad_ratio = grad_ratio + grad_beta[j - 1] * weight[j - 1]
            pull = grad_ratio / window[base + j]
            direct.append(pull)
            from_window.append(jnp.where(valid[j], -pull * share[j], 0.0))
            grad_weight.append(
                grad_beta[j] * (share[j] + (share[j + 1] if j + 1 < frames else zeros))
            )
        top = jnp.full((group, lanes), -1e30, wide)
        for j in range(frames):
            top = jnp.maximum(top, jnp.where(valid[j], span[base + j], -1e30))
        total, ties, at_top, through = zeros, zeros, [], []
        for j in range(frames):
            pulled = grad_weight[j] + from_window[j]
            if j + 1 < frames:
                pulled = pulled + from_window[j + 1]
            pulled = weight[j] * pulled
            through.append(pulled)
            total = total + pulled
            hit = jnp.where(span[base + j] == top, live[j], 0.0)
            at_top.append(hit)
            ties = ties + hit
        back = total / ties
        for j in range(frames):
            span[base + j] = through[j] - at_top[j] * back
        grad_queue = zeros
        now = [None] * frames
        for j in reversed(range(frames)):
            prob = keep[base + j]
            grad_alpha = direct[j] + later[j]
            mono[base + j] = queue[base + j] * (grad_alpha - grad_queue) * prob * (1.0 - prob)
            grad_queue = prob * grad_alpha + (1.0 - prob) * grad_queue
            now[j] = grad_queue
        return tuple(now)

    lax.fori_loop(0, frames, unattend, tuple([zeros] * frames))

    def energy_back(queries, keys, energy, kept_squash, bias_row, vec_row):
        def one_chunk(c, carried):
            at = pl.ds(pl.multiple_of(c * lanes, lanes), lanes)
            weight = jnp.broadcast_to(vectors[vec_row : vec_row + 1, at], (group, lanes))

            def one(i, carry):
                grad_keys, vec_total, bias_total = carry
                grad_query = zeros
                new_keys = []
                for j in range(frames):
                    squash = kept_squash[i * frames + j, :, at]
                    grad = energy[i * frames + j]
                    scaled_squash = grad * squash
                    vec_total = vec_total + scaled_squash
                    inner = grad - scaled_squash * squash
                    grad_query = grad_query + inner
                    new_keys.append(grad_keys[j] + inner)
                queries[i, :, at] = grad_query * weight
                return (tuple(new_keys), vec_total, bias_total + grad_query)

            grad_keys, vec_total, bias_total = lax.fori_loop(
                0, frames, one, (tuple([zeros] * frames), zeros, zeros)
            )
            for j in range(frames):
                keys[j, :, at] = grad_keys[j] * weight
            sums[bias_row : bias_row + 1, at] = jnp.sum(bias_total * weight, axis=0, keepdims=True)
            sums[vec_row : vec_row + 1, at] = jnp.sum(vec_total, axis=0, keepdims=True)
            return carried

        lax.fori_loop(0, chunks, one_chunk, 0)

    energy_back(mq, mk, mono, mono_squash, 0, 1)
    energy_back(sq, sk, span, span_squash, 2, 3)

    total_memory = grad_memory[...]
    total_decoded = jnp.zeros_like(total_memory)
    for r in range(4):
        cols = pl.ds(r * block, block)
        for n, source in enumerate((mk, sk, mq, sq)):
            pack[r, :, n * block : (n + 1) * block] = (
                source[:, :, cols].reshape(rows, block).astype(low)
            )
        total_memory = total_memory + dot_nt(pack[r, :, : 2 * block], w[r, :, : 2 * block])
        total_decoded = total_decoded + dot_nt(
            pack[r, :, 2 * block : 5 * block], w[r, :, 2 * block : 5 * block]
        )
    pack_me[...] = pack[0]
    pack_chip[...] = pack[1]
    pack_cores[...] = pack[2:4]
    middle = 2 * block
    near[...] = sums[:, :middle]
    far[:8, :] = sums[:, middle:]
    far[8:9, :] = sums[5:6, :middle]
    far[9:10, :] = sums[5:6, middle:]
    far[10:, :] = jnp.zeros((6, middle), wide)
    grad_own[...] = jnp.where(first_chip, total_memory, total_decoded)
    grad_given[...] = jnp.where(first_chip, total_decoded, total_memory).astype(low)


def run_attend(
    places, kept, taken, smalls, vocab, vectors, vocab_bias, noise, lengths, labels, counted,
    frames,
):
    rows, width = kept.shape
    group = rows // frames
    full = vectors.shape[1]
    vocab_width = vocab[0].shape[1]
    cell = (frames * frames, group, 128)
    count = len(smalls[0])
    return pl.pallas_call(
        functools.partial(attend_kernel, count),
        out_shape=(
            jax.ShapeDtypeStruct((rows, width), wide),
            jax.ShapeDtypeStruct((rows, width), low),
            jax.ShapeDtypeStruct((rows, full // 4 * 6), low),
            jax.ShapeDtypeStruct((rows, full // 4 * 6), low),
            jax.ShapeDtypeStruct((2, rows, full // 4 * 6), low),
            jax.ShapeDtypeStruct((2, rows, vocab_width), low),
            jax.ShapeDtypeStruct((8, full // 2), wide),
            jax.ShapeDtypeStruct((16, full // 2), wide),
        ),
        in_specs=[in_smem] + [in_vmem] * 8 + [in_place] * (4 * count + 4),
        out_specs=[in_vmem] * 8,
        scratch_shapes=[
            pltpu.VMEM((rows, width), low),
            pltpu.VMEM((rows, width), low),
            pltpu.VMEM((rows, width), wide),
            pltpu.VMEM((4, rows, full // 4 * 6), low),
            pltpu.VMEM((8, full), wide),
            pltpu.VMEM((4, width, full // 4 * 6), low),
            pltpu.VMEM((4,) + vocab[0].shape, low),
            pltpu.SemaphoreType.DMA((4, places.shape[0] - 2)),
            pltpu.SemaphoreType.DMA((4,)),
        ]
        + [pltpu.VMEM((frames, group, full), wide)] * 4
        + [pltpu.VMEM(cell, wide)] * 7
        + [pltpu.VMEM((frames, group, 128), wide), pltpu.VMEM((rows, full), wide)]
        + [pltpu.VMEM((frames * frames, group, full), wide)] * 2,
        compiler_params=pltpu.CompilerParams(vmem_limit_bytes=56 << 20),
        name="attend",
    )(
        places, kept, taken, vectors, vocab_bias, noise, lengths, labels, counted,
        *sum(smalls, []), *vocab,
    )


def gradient_kernel(
    order, before, before_peer, normed, normed_peer, dz, dz_peer, states_own, states_core,
    seen, seen_core, far, far_core, pack_me, pack_core, pack_far, *refs
):
    outputs, paired = refs[:8], refs[8:12]
    a_rec, a_in, a_dz, states, a_context, a_grads, a_pack, block, paired_block, sems, out_sems = (
        refs[12:]
    )
    y = order[0]
    height = block.shape[1]
    wide_half = a_dz.shape[1]
    part = a_pack.shape[1] // 6
    width = a_rec.shape[1]
    jobs = []
    for sources, target in (
        ((dz, dz_peer), a_dz),
        ((before, before_peer), a_rec),
        ((normed, normed_peer), a_in),
        (
            (states_own.at[0], states_core.at[0], states_own.at[2], states_core.at[2]),
            states.at[y],
        ),
        (
            (
                states_own.at[1], states_core.at[1],
                states_own.at[3], states_core.at[3],
            ),
            states.at[1 - y],
        ),
        ((pack_me, pack_core.at[0], pack_far.at[0], pack_far.at[1]), a_pack),
        ((seen.at[0], seen_core.at[0], far.at[0, :, :width], far_core.at[0, :, :width]), a_context),
        ((seen.at[1], seen_core.at[1], far.at[1, :, :width], far_core.at[1, :, :width]), a_grads),
    ):
        rows = target.shape[0] // len(sources)
        for r, source in enumerate(sources):
            jobs.append(
                pltpu.make_async_copy(
                    source, target.at[r * rows : (r + 1) * rows, :], sems.at[len(jobs)]
                )
            )
    for job in jobs:
        job.start()
    for job in jobs[:6]:
        job.wait()
    both = 2 * wide_half

    def one(n, carried):
        cols = pl.ds(pl.multiple_of(order[1 + n] * height, height), height)
        pair = jnp.concatenate([a_rec[:, cols], a_in[:, cols]], axis=1)
        for at in range(0, wide_half, 1024):
            value = dot_tn(pair, a_dz[:, at : at + 1024]).astype(low)
            block[n, :, at : at + 1024] = value[:height]
            block[n, :, wide_half + at : wide_half + at + 1024] = value[height:]
        for m, output in enumerate(outputs):

            @pl.when(n == m)
            def _(m=m, output=output):
                pltpu.make_async_copy(
                    block.at[m, :, :both], output.at[:, :both], out_sems.at[m]
                ).start()

        return carried

    lax.fori_loop(0, 8, one, 0)
    for job in jobs[6:]:
        job.wait()

    def two(n, carried):
        cols = pl.ds(pl.multiple_of(order[1 + n] * height, height), height)
        for m in range(2):
            to = both + 2 * m * part
            block[n, :, to : to + 2 * part] = dot_tn(
                states[m, :, cols], a_pack[:, 2 * m * part : 2 * (m + 1) * part]
            ).astype(low)
        for m, output in enumerate(outputs):

            @pl.when(n == m)
            def _(m=m, output=output):
                pltpu.make_async_copy(
                    block.at[m, :, both:], output.at[:, both:], out_sems.at[12 + m]
                ).start()

        return carried

    lax.fori_loop(0, 8, two, 0)

    def pair(n, carried):
        cols = pl.ds(pl.multiple_of(order[9 + n] * 2 * height, 2 * height), 2 * height)
        grad_pre = a_pack[:, 4 * part : 5 * part]
        for m, (a, b) in enumerate(
            (
                (states[1, :, cols], grad_pre),
                (a_context[:, cols], grad_pre),
                (a_grads[:, cols], a_pack[:, 5 * part :]),
            )
        ):
            paired_block[n, :, m * part : (m + 1) * part] = dot_tn(a, b).astype(low)
        return carried

    lax.fori_loop(0, 4, pair, 0)
    for m, output in enumerate(paired):
        pltpu.make_async_copy(paired_block.at[m], output, out_sems.at[8 + m]).start()
    for m, output in enumerate(outputs):
        pltpu.make_async_copy(
            block.at[m, :, :both], output.at[:, :both], out_sems.at[m]
        ).wait()
        pltpu.make_async_copy(
            block.at[m, :, both:], output.at[:, both:], out_sems.at[12 + m]
        ).wait()
    for m, output in enumerate(paired):
        pltpu.make_async_copy(paired_block.at[m], output, out_sems.at[8 + m]).wait()


def run_gradients(order, *arrays):
    rows, width = arrays[0].shape
    wide_half = arrays[5].shape[1]
    part = arrays[12].shape[1] // 6
    columns = 2 * wide_half + 4 * part
    height = width // 8
    deep = 2 * rows
    return pl.pallas_call(
        gradient_kernel,
        out_shape=tuple(
            [jax.ShapeDtypeStruct((height, columns), low)] * 8
            + [jax.ShapeDtypeStruct((2 * height, 3 * part), low)] * 4
        ),
        in_specs=[in_smem] + [in_place] * 15,
        out_specs=[in_place] * 12,
        scratch_shapes=[
            pltpu.VMEM((deep, width), low),
            pltpu.VMEM((deep, width), low),
            pltpu.VMEM((deep, wide_half), low),
            pltpu.VMEM((2, deep, width), low),
            pltpu.VMEM((deep, width), low),
            pltpu.VMEM((deep, width), low),
            pltpu.VMEM((deep, 6 * part), low),
            pltpu.VMEM((8, height, columns), low),
            pltpu.VMEM((4, 2 * height, 3 * part), low),
            pltpu.SemaphoreType.DMA((26,)),
            pltpu.SemaphoreType.DMA((20,)),
        ],
        compiler_params=pltpu.CompilerParams(vmem_limit_bytes=56 << 20),
        name="weight_gradients",
    )(order, *arrays)


def local(
    dp,
    block_input, norm_gain, lstm_in, lstm_rec, lstm_bias,
    mono_mem, mono_dec, mono_bias, mono_vec, span_mem, span_dec, span_bias, span_vec,
    out_weight, out_bias, vocab_weight, vocab_bias, noise, enc_lengths, label_lengths, labels,
):
    ring = Ring(dp)
    s, y = lax.axis_index("section"), lax.axis_index("mp")
    _, utts, frames, width = block_input.shape
    half, quarter = utts // 2, utts // 4
    rows = frames * quarter
    shard_rows, _, unit_half = lstm_in.shape[1:]
    wide_half = 4 * unit_half
    block = mono_mem.shape[1]
    vocab_size = vocab_weight.shape[1]
    vocab_pad = 4 * block

    in_shard = lstm_in[0].reshape(shard_rows, wide_half)
    rec_shard = lstm_rec[0].reshape(shard_rows, wide_half)
    bias_shard = lstm_bias[0].reshape(1, wide_half)

    def of_section(array):
        return jnp.where(s == y, array, across_cores(array))

    inputs = of_section(jnp.swapaxes(block_input[0], 0, 1))
    gain = of_section(norm_gain[0])
    inputs_own = lax.dynamic_slice_in_dim(inputs, s * half, half, axis=1)
    inputs_other = lax.dynamic_slice_in_dim(inputs, (1 - s) * half, half, axis=1)
    normed_own = normalize(inputs_own.astype(wide), gain)
    normed_own = normed_own.astype(low).reshape(frames * half, width)
    normed_other = normalize(inputs_other.astype(wide), gain)
    normed_other = normed_other.astype(low).reshape(frames * half, width)

    start = s * half + y * quarter
    noise_part = jnp.transpose(
        lax.dynamic_slice_in_dim(noise, start, quarter, axis=0), (1, 2, 0)
    ).reshape(frames * frames, quarter, 1)
    noise_part = jnp.broadcast_to(noise_part, (frames * frames, quarter, 128))
    length_part = lax.dynamic_slice_in_dim(enc_lengths, start, quarter, axis=0)
    length_part = jnp.broadcast_to(length_part[:, None], (quarter, 128))
    label_part = lax.dynamic_slice_in_dim(labels, start, quarter, axis=0).T.reshape(rows, 1)
    label_part = jnp.broadcast_to(label_part, (rows, 128))
    count_part = lax.dynamic_slice_in_dim(label_lengths, start, quarter, axis=0)
    counted = (jnp.arange(frames)[:, None] < count_part[None, :]).astype(wide).reshape(rows, 1)
    counted = jnp.broadcast_to(counted, (rows, 128))
    bias_row = jnp.pad(vocab_bias, (0, vocab_pad - vocab_size), constant_values=-1e30)[None]

    vector_own = jnp.stack([mono_bias, mono_vec, span_bias, span_vec, out_bias])
    vocab_own = jnp.pad(vocab_weight, ((0, 0), (0, vocab_pad - vocab_size)))
    ready = (noise_part, length_part, label_part, counted, bias_row, normed_own, normed_other)
    places, in_own, rec_own, small_own, small_chip = [], [], [], [], []
    small = jnp.concatenate(
        [
            tie(mono_mem, in_shard, rec_shard), span_mem, mono_dec, span_dec,
            out_weight[0], out_weight[1],
        ],
        axis=1,
    )
    if ring.short:
        flow, across, onward = Flow(), ring.across, ring.onward
        both = 2 * wide_half
        corner_in, corner_rec, b_own = flow.step(
            (corners, in_shard), (corners, rec_shard), (corners, bias_shard)
        )
        small_far, small_next = across(small), onward(small)
        flow.landed += (small_far, small_next)
        b_own = b_own.astype(wide)
        small_own = [jnp.concatenate([small, small_far], axis=1)]
        small_chip, small_core = [], []
        held = jnp.concatenate([corner_in, corner_rec, small_next], axis=1)
        near, far, near_core, far_core = [], [], [], []
        for k in range(ring.outer):
            near.append(held)
            jobs = [(across, held), (across_chips, small_own[k])]
            if k < ring.outer - 1:
                jobs.append((onward, held[:, :both] if k == ring.outer - 2 else held))
            if k == 0:
                jobs += [(across_chips, vocab_own), (across_chips, vector_own)]
            results = flow.step(*jobs, also=ready if k == 1 else ())
            far.append(results[0])
            small_chip.append(results[1])
            if k == 0:
                vocab_chip, vector_pair = results[3:]
                vector_pair = jnp.concatenate([vector_own, vector_pair], axis=1)
            if k < ring.outer - 1:
                small_own.append(jnp.concatenate([held[:, both:], far[k][:, both:]], axis=1))
                held = results[2]
        for a, b in zip(near, far):
            near_core.append(across_cores(a))
            far_core.append(across_cores(b))
        small_core = [across_cores(a) for a in small_own]
        b_last, vocab_last, chip_last, vector_last = lax.optimization_barrier(
            (b_own, vocab_own, vocab_chip, vector_pair, held)
        )[:4]
        b_other = across_cores(b_last)
        vocab = [vocab_own, vocab_chip, across_cores(vocab_last), across_cores(chip_last)]
        vector_core = across_cores(vector_last)
        in_own = [a for pair in zip(near, far) for a in pair]
        in_other = [a for pair in zip(near_core, far_core) for a in pair]
        rec_own, rec_other, rec_column = in_own, in_other, wide_half
        for k in range(ring.outer):
            places += [ring.back(k) * 2 + ring.x, ring.back(k) * 2 + 1 - ring.x]
    else:
        vocab_chip = across_chips(vocab_own)
        small, in_block, rec_block = [
            lax.all_gather(a, "dp", axis=0, tiled=True)
            for a in (small, corners(in_shard), corners(rec_shard))
        ]
        places, in_own, rec_own = [jnp.int32(0)], [in_block], [rec_block]
        small_own, small_chip = [small], [across_chips(small)]
        vocab = [vocab_own, vocab_chip, across_cores(vocab_own), across_cores(vocab_chip)]
        in_other, rec_other, rec_column = [across_cores(in_block)], [across_cores(rec_block)], 0
        small_core = [across_cores(small)]
        b_own = corners(bias_shard).astype(wide)
        b_other = across_cores(b_own)
        vector_pair = across_chips(vector_own)
        vector_pair = jnp.concatenate([vector_own, vector_pair], axis=1)
        vector_core = across_cores(vector_pair)
    vectors = jnp.concatenate([vector_pair, vector_core], axis=1)
    vectors = jnp.pad(vectors, ((0, 3), (0, 0)))
    places = jnp.stack([s, y] + places).astype(jnp.int32)
    z, x = ring.z, ring.x
    if ring.short:
        steps_back = [ring.back(k) for k in range(1, 5)]
        order = [at * 2 + 1 - x for at in steps_back] + [at * 2 + x for at in steps_back]
        order = [y] + order + steps_back
    else:
        order = [y] + [jnp.int32(k) for k in [*range(8), *range(4)]]
    order = jnp.stack(order).astype(jnp.int32)
    places = tie(places, order, vectors, *vocab, *ready, *small_chip[:-1], *small_core)

    kept, given, before, gates, cells = run_forward(
        places, normed_own, b_own, b_other, in_own, in_other, rec_own, rec_other, frames,
        rec_column,
    )

    kept, given = kept.reshape(rows, width), given.reshape(rows, width)
    taken = across_chips(given)
    small_chip[-1] = tie(small_chip[-1], kept)
    small_both = [across_cores(part) for part in small_chip]
    smalls = [small_own, small_chip, small_core, small_both]
    grad_own, grad_given, pack_me, pack_chip, pack_cores, seen, near, far = run_attend(
        places, kept, taken, smalls, vocab, vectors, bias_row, noise_part, length_part,
        label_part, counted, frames,
    )
    grad_given, kept_far = lax.optimization_barrier((grad_given, across_chips(tie(kept, taken))))
    grad_taken = across_chips(grad_given)
    pack_core = across_cores(pack_cores)
    pack_out = jnp.stack([pack_chip, pack_core[1]])
    far_peer = across_cores(far)
    vector_pair = (near[:5] + far_peer[:5]).reshape(5, 2, block)
    bias_pair = (far[8:10] + far_peer[8:10]).reshape(-1)
    vector_out = jnp.concatenate([vector_pair[:, 1].reshape(-1), bias_pair])
    vector_count = vector_out.shape[0] // (2 * rows)
    seen_out = jnp.concatenate(
        [seen, halves(vector_out, 2 * rows).reshape(2, rows, -1)], axis=2
    )
    before = before.reshape(frames * half, width)
    before_peer = across_cores(tie(before, taken))
    states = jnp.stack([tie(kept, grad_given), taken, given, kept_far])
    states_core, seen_core = across_cores(states), across_cores(seen)
    places_back, pack_out, seen_out = lax.optimization_barrier(
        (places, pack_out, seen_out, grad_taken, before_peer, states_core, seen_core)
    )[:3]
    dz_own, dz_other = run_backward(
        places_back, grad_own.reshape(frames, quarter, width),
        grad_taken.reshape(frames, quarter, width), gates, cells, rec_own, rec_other, rec_column,
    )
    pack_far = across_chips(pack_out)
    seen_far = across_chips(tie(seen_out, pack_out))

    dz_own, dz_other, pack_far, seen_far = lax.optimization_barrier(
        (
            dz_own.reshape(frames * half, wide_half), dz_other.reshape(frames * half, wide_half),
            pack_far, seen_far,
        )
    )
    dz_peer = across_cores(dz_other)
    totals = run_gradients(
        order, before, before_peer, normed_own, normed_other, dz_own,
        dz_peer, states, states_core, seen, seen_core, seen_far, across_cores(seen_far),
        pack_me, pack_core, pack_far,
    )
    vector_far = joined(seen_far[:, :, width:].reshape(2 * rows, -1), vector_count).reshape(-1)

    sides_at = 5 * block + vocab_pad
    def input_back(places):
        grad_inputs, grad_gain = run_input(
            places, inputs_own.reshape(frames * half, width), gain[None], dz_own, dz_other,
            in_own, in_other,
        )
        grad_gain = grad_gain.reshape(width)
        grad_inputs = jnp.swapaxes(grad_inputs.reshape(frames, half, width), 0, 1)
        grad_peer = across_cores(grad_inputs)
        grad_section = jnp.concatenate(
            [
                jnp.where(s == 0, grad_inputs, grad_peer),
                jnp.where(s == 0, grad_peer, grad_inputs),
            ],
            axis=0,
        )
        gain_sum = grad_gain + across_cores(grad_gain)
        flat = jnp.concatenate(
            [
                vector_pair[:, 0].reshape(-1) + vector_far[: 5 * block],
                bias_pair + vector_far[5 * block :],
                jnp.sum(dz_own.astype(wide), axis=0) + jnp.sum(dz_peer.astype(wide), axis=0),
                gain_sum,
            ]
        )
        return grad_section, jnp.pad(flat, (0, -flat.shape[0] % (8 * shard_rows)))

    def to_other_chip(section):
        return lax.ppermute(section, ("section", "mp"), [(0, 1), (3, 2)])

    if ring.short:
        r = shard_rows
        both, width_out = 2 * wide_half, 2 * block
        flow, across, onward = Flow(), ring.across, ring.onward
        theirs, mine, outputs = totals[:4], totals[4:8], totals[8:]

        def total(k, arrived, passed):
            value = mine[k - 1].astype(wide) + arrived.astype(wide)
            return value if passed is None else value + passed.astype(wide)

        def cornered(hop):
            index = lambda at, place, chip: (at * ring.dp + place) * 2 + chip
            pairs = [
                (index(p, a, q), index(q, b, p)) for a, b in hop for p in range(2) for q in range(2)
            ]
            return lambda array: lax.ppermute(array, ("section", "dp", "mp"), pairs)

        arrived, out_two, out_before = flow.step(
            (across, theirs[0]), (onward, outputs[1]), (ring.astern, outputs[0])
        )
        grad_section, flat = input_back(tie(places, out_two))
        out_one = onward(
            tie((outputs[2].astype(wide) + out_two.astype(wide)).astype(low), arrived)
        )
        grad_far = to_other_chip(grad_section)
        flat = flat.reshape(8, -1)
        flat = (flat + across(flat)).reshape(-1)
        flat_width = flat.shape[0] // r
        flow.landed = (arrived,)
        value = total(1, arrived, None).astype(low)
        passed, arrived = flow.step((onward, value), (across, theirs[1]))
        out = outputs[3].astype(wide) + out_before.astype(wide) + out_one.astype(wide)
        vocab_rows = out[:, width_out:].astype(low)
        message = jnp.concatenate(
            [cut(out, 1 - x, r)[:, :width_out].astype(low), vocab_rows[:r], vocab_rows[r:]], axis=1
        )
        kept_rows = corners(tie(mine[3][:, :both], out_one))
        value = total(2, arrived, passed).astype(low)
        passed, arrived, out_far = flow.step(
            (onward, value), (across, theirs[2]), (across, message), also=(grad_far,)
        )
        output_grad = cut(out, x, r)[:, :width_out] + out_far[:, :width_out].astype(wide)
        shard = jnp.concatenate([out[:r, width_out:], out[r:, width_out:]], axis=1)
        shard = (shard + out_far[:, width_out:].astype(wide)).astype(low)
        shard = jnp.concatenate([shard, halves(flat, r)], axis=1)
        next_one, next_three = onward(shard), ring.astern(shard)
        value = total(3, arrived, passed).astype(low)
        passed, arrived, energy_passed, energy_arrived, next_two = flow.step(
            (cornered(ring.ring), value[:, :both]), (cornered(ring.pair), theirs[3][:, :both]),
            (onward, value[:, both:]), (across, theirs[3][:, both:]), (onward, next_one),
            also=(kept_rows,),
        )
        shards = {0: shard, 1: next_one, 3: next_three, 2: next_two}
        flat = sum(joined(a[:, 2 * block :], flat_width).reshape(-1) for a in shards.values())
        sides = corners(flat[sides_at : sides_at + wide_half + width])
        moved = kept_rows.astype(wide) + arrived.astype(wide) + passed.astype(wide)
        energy_grad = mine[3][:, both:].astype(wide) + energy_arrived.astype(wide)
        energy_grad = energy_grad + energy_passed.astype(wide)
        vocab_grad = jnp.zeros((vocab_pad, block), low)
        for k, held in shards.items():
            held = jnp.concatenate([held[:, :block], held[:, block : 2 * block]], axis=0)
            vocab_grad = lax.dynamic_update_slice(vocab_grad, held, (ring.back(k) * 2 * r, 0))
    else:
        grad_section, flat = input_back(places)
        grad_far = to_other_chip(grad_section)

        def scatter(parts):
            total = jnp.concatenate(parts, axis=0)
            return lax.psum_scatter(total, "dp", scatter_dimension=0, tiled=True).astype(wide)

        moved, output_grad = scatter(totals[:8]), scatter(totals[8:])
        moved, energy_grad = moved[:, : 2 * wide_half], moved[:, 2 * wide_half :]
        moved = corners(moved.astype(low)).astype(wide)
        flat = lax.psum(flat, "dp")
        sides = corners(flat[sides_at : sides_at + wide_half + width])
        vocab_grad = lax.all_gather(
            output_grad[:, 2 * block :].astype(low), "dp", axis=0, tiled=True
        )

    input_grad = jnp.where(s == y, grad_section, grad_far)
    vocab_grad = vocab_grad.T[:, :vocab_size].astype(wide)
    vector_sum = flat[: 5 * block].reshape(5, block)
    bias_sum = flat[5 * block : 5 * block + vocab_size]
    lstm_bias_sum = sides[:wide_half].reshape(1, 4, unit_half)
    gain_sum = sides[wide_half:][None]
    rec_grad = moved[:, :wide_half].reshape(1, shard_rows, 4, unit_half)
    in_grad = moved[:, wide_half:].reshape(1, shard_rows, 4, unit_half)
    mono_mem_grad, span_mem_grad, mono_dec_grad, span_dec_grad = [
        energy_grad[:, n * block : (n + 1) * block] for n in range(4)
    ]
    return (
        input_grad[None],
        gain_sum,
        in_grad,
        rec_grad,
        lstm_bias_sum,
        mono_mem_grad,
        mono_dec_grad,
        vector_sum[0],
        vector_sum[1],
        span_mem_grad,
        span_dec_grad,
        vector_sum[2],
        vector_sum[3],
        jnp.stack([output_grad[:, :block], output_grad[:, block : 2 * block]]),
        vector_sum[4],
        vocab_grad,
        bias_sum,
    )


def solution(mesh):
    both = ("section", "mp")
    in_specs = (
        P("section", "dp", None, None),
        P("section", None),
        P("section", "dp", None, "mp"),
        P("section", "dp", None, "mp"),
        P("section", None, "mp"),
        P("dp", both),
        P("dp", both),
        P(both),
        P(both),
        P("dp", both),
        P("dp", both),
        P(both),
        P(both),
        P(None, "dp", both),
        P(both),
        P(both, None),
        P(),
        P("dp", None, None),
        P("dp"),
        P("dp"),
        P("dp", None),
    )
    out_specs = (
        P("section", "dp", None, None),
        P("section", None),
        P("section", "dp", None, "mp"),
        P("section", "dp", None, "mp"),
        P("section", None, "mp"),
        P("dp", both),
        P("dp", both),
        P(both),
        P(both),
        P("dp", both),
        P("dp", both),
        P(both),
        P(both),
        P(None, "dp", both),
        P(both),
        P(both, None),
        P(),
    )
    dp = mesh.shape["dp"]

    def step(*arrays):
        return local(dp, *arrays)

    return jax.shard_map(step, mesh=mesh, in_specs=in_specs, out_specs=out_specs, check_vma=False)
```

```python
import functools

import jax
import jax.numpy as jnp
from jax import lax
from jax.experimental import pallas as pl
from jax.experimental.pallas import tpu as pltpu
from jax.sharding import PartitionSpec as P

epsilon = 1e-05
offset = -4.0
wide = jnp.float32
low = jnp.bfloat16
in_vmem = pl.BlockSpec(memory_space=pltpu.VMEM)
in_smem = pl.BlockSpec(memory_space=pltpu.SMEM)
in_place = pl.BlockSpec(memory_space=pl.ANY)
core_swap = [(0, 1), (1, 0)]
corner_swap = [(0, 0), (1, 2), (2, 1), (3, 3)]


def normalize(inputs, gain_row):
    average = jnp.mean(inputs, axis=-1, keepdims=True)
    centred = inputs - average
    spread = jnp.mean(centred * centred, axis=-1, keepdims=True)
    return centred * lax.rsqrt(spread + epsilon) * gain_row


def across_cores(array):
    return lax.ppermute(array, "section", core_swap)


def across_chips(array):
    return lax.ppermute(array, "mp", core_swap)


def corners(array):
    return lax.ppermute(array, ("section", "mp"), corner_swap)


def tie(value, *others):
    return lax.optimization_barrier((value,) + others)[0]


def cut(array, block, rows):
    return lax.dynamic_slice_in_dim(array, block * rows, rows, axis=0)


class Flow:
    def __init__(self):
        self.landed = ()

    def step(self, *jobs, also=()):
        operands = tuple(operand for _, operand in jobs)
        operands = lax.optimization_barrier(operands + self.landed + tuple(also))[: len(jobs)]
        results = [send(operand) for (send, _), operand in zip(jobs, operands)]
        self.landed = tuple(results)
        return results


class Ring:
    def __init__(self, dp):
        self.dp = dp
        self.outer = dp // 2
        self.short = dp % 2 == 0 and self.outer == 4
        pairs = [(z, x) for z in range(self.outer) for x in range(2)]
        self.pair = [(2 * z + x, 2 * z + 1 - x) for z, x in pairs]
        self.ring = [(2 * z + x, 2 * ((z + 1) % self.outer) + x) for z, x in pairs]
        self.turn = [(b, a) for a, b in self.ring]
        place = lax.axis_index("dp")
        self.z, self.x = place // 2, place % 2

    def across(self, array):
        return lax.ppermute(array, "dp", self.pair)

    def onward(self, array):
        return lax.ppermute(array, "dp", self.ring)

    def astern(self, array):
        return lax.ppermute(array, "dp", self.turn)

    def back(self, k):
        return lax.rem(self.z - k + self.outer, self.outer)


def halves(array, height):
    array = array.reshape(height, -1)
    upper = array.astype(low)
    lower = (array - upper.astype(wide)).astype(low)
    return jnp.pad(
        jnp.concatenate([upper, lower], axis=1), ((0, 0), (0, -2 * array.shape[1] % 128))
    )


def joined(array, count):
    return array[:, :count].astype(wide) + array[:, count : 2 * count].astype(wide)


def sigmoid(x):
    return 0.5 * jnp.tanh(0.5 * x) + 0.5


def fetch(blocks, places, side_blocks, target, sems, first=0, column=0):
    wide_half = target.shape[1] // 2
    columns = pl.ds(pl.multiple_of(side_blocks * wide_half, wide_half), wide_half)
    copies = []
    for k, block in enumerate(blocks):
        height = block.shape[0]
        span = pl.ds(pl.multiple_of(places[2 + k] * height, height), height)
        copies.append(
            pltpu.make_async_copy(
                block.at[:, column : column + wide_half],
                target.at[span, columns],
                sems.at[first + k],
            )
        )
    return copies


def forward_kernel(count, column, places, normed, b_own, b_other, *refs):
    in_own, in_other, w_own, w_other = [refs[n * count : (n + 1) * count] for n in range(4)]
    (
        kept, given, before, gates_out, cells_out, gates, cells, wi, w, b, state, cell, sems,
        gate_sems, cell_sems,
    ) = refs[4 * count :]
    steps, rows, wide_full = gates.shape
    wide_half = wide_full // 2
    unit_half = wide_half // 4
    chunk = min(256, unit_half)
    s = places[0]
    copies = fetch(in_own, places, s, wi, sems) + fetch(in_other, places, 1 - s, wi, sems, count)
    later = fetch(w_own, places, s, w, sems, 2 * count, column)
    later += fetch(w_other, places, 1 - s, w, sems, 3 * count, column)
    for copy in copies + later:
        copy.start()
    for source, at in ((b_own, s), (b_other, 1 - s)):
        b[:, pl.ds(pl.multiple_of(at * wide_half, wide_half), wide_half)] = source[...]
    state[...] = jnp.zeros_like(state)
    cell[...] = jnp.zeros_like(cell)
    for copy in copies:
        copy.wait()

    def project(g, carried):
        cols = pl.ds(pl.multiple_of(g * unit_half, unit_half), unit_half)
        value = jnp.dot(normed[...], wi[:, cols], preferred_element_type=wide) + b[:, cols]
        gates[:, :, cols] = value.reshape(steps, rows, unit_half)
        return carried

    lax.fori_loop(0, 8, project, 0)
    for copy in later:
        copy.wait()
    eighth = rows // 2
    first_chip = places[1] == 0

    def advance(t, carried):
        hidden = state[...]
        before[t] = hidden
        for at in range(0, 2 * unit_half, chunk):
            half, inside = at // unit_half, at % unit_half
            acts = []
            for g in range(4):
                cols = pl.ds(half * wide_half + g * unit_half + inside, chunk)
                value = gates[t, :, cols] + jnp.dot(
                    hidden, w[:, cols], preferred_element_type=wide
                )
                value = jnp.tanh(value) if g == 2 else sigmoid(value)
                gates[t, :, cols] = value
                acts.append(value)
            units = pl.ds(at, chunk)
            new_cell = acts[1] * cell[:, units] + acts[0] * acts[2]
            cell[:, units] = new_cell
            cells[t, :, units] = new_cell
            new_hidden = acts[3] * jnp.tanh(new_cell)
            state[:, units] = new_hidden.astype(low)
            upper, lower = new_hidden[:eighth], new_hidden[eighth:]
            kept[t, :, units] = jnp.where(first_chip, upper, lower).astype(low)
            given[t, :, units] = jnp.where(first_chip, lower, upper).astype(low)
        pltpu.make_async_copy(gates.at[t], gates_out.at[t], gate_sems.at[t]).start()
        pltpu.make_async_copy(cells.at[t], cells_out.at[t], cell_sems.at[t]).start()
        return carried

    lax.fori_loop(0, steps, advance, 0)

    def settle(t, carried):
        pltpu.make_async_copy(gates.at[t], gates_out.at[t], gate_sems.at[t]).wait()
        pltpu.make_async_copy(cells.at[t], cells_out.at[t], cell_sems.at[t]).wait()
        return carried

    lax.fori_loop(0, steps, settle, 0)


def run_forward(places, normed, b_own, b_other, in_own, in_other, w_own, w_other, steps, column):
    rows = normed.shape[0] // steps
    units = normed.shape[1]
    wide_half = b_own.shape[1]
    count = len(w_own)
    return pl.pallas_call(
        functools.partial(forward_kernel, count, column),
        out_shape=(
            jax.ShapeDtypeStruct((steps, rows // 2, units), low),
            jax.ShapeDtypeStruct((steps, rows // 2, units), low),
            jax.ShapeDtypeStruct((steps, rows, units), low),
            jax.ShapeDtypeStruct((steps, rows, 2 * wide_half), wide),
            jax.ShapeDtypeStruct((steps, rows, units), wide),
        ),
        in_specs=[in_smem] + [in_vmem] * 3 + [in_place] * (4 * count),
        out_specs=[in_vmem] * 3 + [in_place] * 2,
        scratch_shapes=[
            pltpu.VMEM((steps, rows, 2 * wide_half), wide),
            pltpu.VMEM((steps, rows, units), wide),
            pltpu.VMEM((units, 2 * wide_half), low),
            pltpu.VMEM((units, 2 * wide_half), low),
            pltpu.VMEM((1, 2 * wide_half), wide),
            pltpu.VMEM((rows, units), low),
            pltpu.VMEM((rows, units), wide),
            pltpu.SemaphoreType.DMA((4 * count,)),
            pltpu.SemaphoreType.DMA((steps,)),
            pltpu.SemaphoreType.DMA((steps,)),
        ],
        compiler_params=pltpu.CompilerParams(vmem_limit_bytes=56 << 20),
        name="recur_forward",
    )(places, normed, b_own, b_other, *in_own, *in_other, *w_own, *w_other)


def backward_kernel(count, column, places, kept, taken, gates_in, cells_in, *refs):
    w_own, w_other = refs[:count], refs[count : 2 * count]
    dz_own, dz_other, gates, cells, dz, stage, w, dh, dc, sems, gate_sems, cell_sems = refs[
        2 * count :
    ]
    steps, rows, wide_full = gates.shape
    wide_half = wide_full // 2
    unit_half = wide_half // 4
    chunk = min(256, unit_half)
    s = places[0]
    first_chip = places[1] == 0

    def gate_copy(t):
        return pltpu.make_async_copy(gates_in.at[t], gates.at[t], gate_sems.at[t])

    def cell_copy(t):
        return pltpu.make_async_copy(cells_in.at[t], cells.at[t], cell_sems.at[t])

    gate_copy(steps - 1).start()
    cell_copy(steps - 1).start()
    jobs = []
    for n, (sources, at) in enumerate(((w_own, s), (w_other, 1 - s))):
        for k, block in enumerate(sources):
            slot = n * count + k
            copy = pltpu.make_async_copy(
                block.at[:, column : column + wide_half], stage.at[slot], sems.at[slot]
            )
            copy.start()
            jobs.append((copy, slot, at, places[2 + k] * block.shape[0]))
    for t in range(steps - 2, -1, -1):
        cell_copy(t).start()
        gate_copy(t).start()
    dh[...] = jnp.zeros_like(dh)
    dc[...] = jnp.zeros_like(dc)
    height = w_own[0].shape[0]
    piece = min(height, 128)
    for copy, slot, at, first in jobs:
        copy.wait()

        def turn(g, carried, slot=slot, at=at, first=first):
            columns = pl.ds(pl.multiple_of(g * unit_half, unit_half), unit_half)
            span = pl.ds(pl.multiple_of(at * wide_half + g * unit_half, unit_half), unit_half)
            for low_row in range(0, height, piece):
                into = pl.ds(pl.multiple_of(first + low_row, piece), piece)
                w[span, into] = stage[slot, low_row : low_row + piece, columns].T
            return carried

        lax.fori_loop(0, 4, turn, 0)

    cell_copy(steps - 1).wait()

    def retreat(k, carried):
        t = steps - 1 - k
        earlier = jnp.maximum(t - 1, 0)
        gate_copy(t).wait()

        @pl.when(t > 0)
        def _():
            cell_copy(earlier).wait()

        live = jnp.where(t > 0, 1.0, 0.0).astype(wide)
        for at in range(0, 2 * unit_half, chunk):
            half, inside = at // unit_half, at % unit_half
            units = pl.ds(at, chunk)
            ours, theirs = kept[t, :, units], taken[t, :, units].astype(wide)
            grad = dh[:, units] + jnp.concatenate(
                [jnp.where(first_chip, ours, theirs), jnp.where(first_chip, theirs, ours)], axis=0
            )
            i, f, g, o = [
                gates[t, :, pl.ds(half * wide_half + n * unit_half + inside, chunk)]
                for n in range(4)
            ]
            squash = jnp.tanh(cells[t, :, units])
            total = dc[:, units] + grad * o * (1.0 - squash * squash)
            parts = (
                total * g * i * (1.0 - i),
                total * (cells[earlier, :, units] * live) * f * (1.0 - f),
                total * i * (1.0 - g * g),
                grad * squash * o * (1.0 - o),
            )
            for n, part in enumerate(parts):
                dz[half, :, pl.ds(n * unit_half + inside, chunk)] = part.astype(low)
            dc[:, units] = total * f
        dz_own[t] = dz[s]
        dz_other[t] = dz[1 - s]
        upper, lower = dz[0], dz[1]
        for at in range(0, 2 * unit_half, chunk):
            units = pl.ds(at, chunk)
            dh[:, units] = jnp.dot(
                upper, w[:wide_half, units], preferred_element_type=wide
            ) + jnp.dot(lower, w[wide_half:, units], preferred_element_type=wide)
        return carried

    lax.fori_loop(0, steps, retreat, 0)


def run_backward(places, kept, taken, gates, cells, w_own, w_other, column):
    steps, rows, wide_full = gates.shape
    units = cells.shape[2]
    count = len(w_own)
    return pl.pallas_call(
        functools.partial(backward_kernel, count, column),
        out_shape=(jax.ShapeDtypeStruct((steps, rows, wide_full // 2), low),) * 2,
        in_specs=[in_smem] + [in_vmem] * 2 + [in_place] * (2 + 2 * count),
        out_specs=[in_vmem] * 2,
        scratch_shapes=[
            pltpu.VMEM((steps, rows, wide_full), wide),
            pltpu.VMEM((steps, rows, units), wide),
            pltpu.VMEM((2, rows, wide_full // 2), low),
            pltpu.VMEM((2 * count, units // count, wide_full // 2), low),
            pltpu.VMEM((wide_full, units), low),
            pltpu.VMEM((rows, units), wide),
            pltpu.VMEM((rows, units), wide),
            pltpu.SemaphoreType.DMA((2 * count,)),
            pltpu.SemaphoreType.DMA((steps,)),
            pltpu.SemaphoreType.DMA((steps,)),
        ],
        compiler_params=pltpu.CompilerParams(vmem_limit_bytes=56 << 20),
        name="recur_backward",
    )(places, kept, taken, gates, cells, *w_own, *w_other)


def input_kernel(count, places, inputs, gain, dz, dz_given, *refs):
    in_own, in_other = refs[:count], refs[count : 2 * count]
    grad_inputs, grad_gain, wi, sems = refs[2 * count :]
    s = places[0]
    copies = fetch(in_own, places, s, wi, sems) + fetch(in_other, places, 1 - s, wi, sems, count)
    for copy in copies:
        copy.start()
    x = inputs[...].astype(wide)
    centred = x - jnp.mean(x, axis=-1, keepdims=True)
    scale = lax.rsqrt(jnp.mean(centred * centred, axis=-1, keepdims=True) + epsilon)
    shape = centred * scale
    for copy in copies:
        copy.wait()
    wide_half = wi.shape[1] // 2
    own = pl.ds(pl.multiple_of(s * wide_half, wide_half), wide_half)
    other = pl.ds(pl.multiple_of((1 - s) * wide_half, wide_half), wide_half)
    grad = dot_nt(dz[...], wi[:, own]) + dot_nt(dz_given[...], wi[:, other])
    grad_gain[...] = jnp.sum(grad * shape, axis=0, keepdims=True)
    pulled = grad * gain[...]
    grad_inputs[...] = scale * (
        pulled
        - jnp.mean(pulled, axis=-1, keepdims=True)
        - shape * jnp.mean(pulled * shape, axis=-1, keepdims=True)
    )


def run_input(places, inputs, gain, dz, dz_given, in_own, in_other):
    count = len(in_own)
    rows, width = inputs.shape
    return pl.pallas_call(
        functools.partial(input_kernel, count),
        out_shape=(
            jax.ShapeDtypeStruct((rows, width), wide),
            jax.ShapeDtypeStruct((1, width), wide),
        ),
        in_specs=[in_smem] + [in_vmem] * 4 + [in_place] * (2 * count),
        out_specs=[in_vmem] * 2,
        scratch_shapes=[
            pltpu.VMEM((width, 2 * dz.shape[1]), low),
            pltpu.SemaphoreType.DMA((2 * count,)),
        ],
        compiler_params=pltpu.CompilerParams(vmem_limit_bytes=56 << 20),
        name="input_back",
    )(places, inputs, gain, dz, dz_given, *in_own, *in_other)


def dot_nt(a, b):
    return lax.dot_general(a, b, (((1,), (1,)), ((), ())), preferred_element_type=wide)


def dot_tn(a, b):
    return lax.dot_general(a, b, (((0,), (0,)), ((), ())), preferred_element_type=wide)


def attend_kernel(
    count, places, kept, taken, vectors, vocab_bias, noise, lengths, labels, counted, *refs
):
    small, vocab = refs[: 4 * count], refs[4 * count : 4 * count + 4]
    (
        grad_own, grad_given, pack_me, pack_chip, pack_cores, seen, near, far,
        memory, decoded, grad_memory, pack, sums, w, v, sems, v_sems, mk, sk, mq, sq, mono, span, keep, queue, scaled, ratio, window, mix, pre,
        mono_squash, span_squash,
    ) = refs[4 * count + 4 :]
    rows, _ = kept.shape
    frames, group, _ = mk.shape
    block = w.shape[2] // 6
    lanes = 128
    chunks = 4 * block // lanes
    copies = []
    for r in range(4):
        arrived = []
        for k in range(count):
            source = small[r * count + k]
            height = source.shape[0]
            for h in range(source.shape[1] // (6 * block)):
                to = pl.ds(pl.multiple_of(places[2 + len(arrived)] * height, height), height)
                arrived.append(
                    pltpu.make_async_copy(
                        source.at[:, 6 * block * h : 6 * block * (h + 1)],
                        w.at[r, to, :],
                        sems.at[r, len(arrived)],
                    )
                )
        copies.append(arrived)
    vocab_copies = [pltpu.make_async_copy(vocab[r], v.at[r], v_sems.at[r]) for r in range(4)]
    for copy in sum(copies, []) + vocab_copies:
        copy.start()

    first_chip = places[1] == 0

    @pl.when(first_chip)
    def _():
        memory[...] = kept[...]
        decoded[...] = taken[...]

    @pl.when(jnp.logical_not(first_chip))
    def _():
        memory[...] = taken[...]
        decoded[...] = kept[...]

    def split(value):
        return value.reshape(frames, group, value.shape[-1])

    mem, dec = memory[...], decoded[...]

    def lane(c):
        return pl.ds(c * lanes, lanes)

    def spread(row, c):
        return jnp.broadcast_to(vectors[row : row + 1, lane(c)], (group, lanes))

    def energies(queries, keys, vec_row, energy, kept_squash, r):
        mine = range(r * chunks // 4, (r + 1) * chunks // 4)
        weights = {c: spread(vec_row, c) for c in mine}

        def one(i, carried):
            query = {c: queries[i, :, lane(c)] for c in mine}
            for j in range(frames):
                total = None if r == 0 else energy[i * frames + j]
                for c in mine:
                    squash = jnp.tanh(query[c] + keys[j, :, lane(c)])
                    kept_squash[i * frames + j, :, lane(c)] = squash
                    part = squash * weights[c]
                    total = part if total is None else total + part
                if r == 3:
                    total = jnp.broadcast_to(
                        jnp.sum(total, axis=-1, keepdims=True), (group, lanes)
                    )
                energy[i * frames + j] = total
            return carried

        lax.fori_loop(0, frames, one, 0)

    for r in range(4):
        for copy in copies[r]:
            copy.wait()
        cols = pl.ds(r * block, block)
        keys = jnp.dot(mem, w[r, :, : 2 * block], preferred_element_type=wide)
        queries = jnp.dot(dec, w[r, :, 2 * block : 5 * block], preferred_element_type=wide)
        mk[:, :, cols] = split(keys[:, :block])
        sk[:, :, cols] = split(keys[:, block:])
        mq[:, :, cols] = split(queries[:, :block] + vectors[0:1, cols])
        sq[:, :, cols] = split(queries[:, block : 2 * block] + vectors[2:3, cols])
        pre[:, cols] = queries[:, 2 * block :] + vectors[4:5, cols]
        energies(mq, mk, 1, mono, mono_squash, r)
        energies(sq, sk, 3, span, span_squash, r)

    length = lengths[...]
    valid = [(length > j) for j in range(frames)]
    ones = jnp.ones((group, lanes), wide)
    zeros = jnp.zeros((group, lanes), wide)
    live = [jnp.where(valid[j], 1.0, 0.0).astype(wide) for j in range(frames)]
    diagonal = lax.broadcasted_iota(jnp.int32, (group, lanes), 1) - lax.broadcasted_iota(
        jnp.int32, (group, lanes), 0
    )

    def attend(i, previous):
        base = i * frames
        top = jnp.full((group, lanes), -1e30, wide)
        for j in range(frames):
            top = jnp.maximum(top, jnp.where(valid[j], span[base + j], -1e30))
        weight = [jnp.where(valid[j], jnp.exp(span[base + j] - top), 0.0) for j in range(frames)]
        current, ratios = [], []
        queued = previous[0]
        for j in range(frames):
            prob = sigmoid(mono[base + j] + offset + noise[base + j]) * live[j]
            keep[base + j] = prob
            queue[base + j] = queued
            alpha = prob * queued
            current.append(alpha)
            if j + 1 < frames:
                queued = (1.0 - prob) * queued + previous[j + 1]
            both = weight[j] + weight[j - 1] if j else weight[j]
            both = jnp.where(valid[j], both, 1.0)
            window[base + j] = both
            scaled[base + j] = weight[j]
            quotient = alpha / both
            ratio[base + j] = quotient
            ratios.append(quotient)
        row = zeros
        for j in range(frames):
            beta = weight[j] * (ratios[j] + (ratios[j + 1] if j + 1 < frames else zeros))
            row = jnp.where(diagonal == group * j, beta, row)
        mix[i] = row
        return tuple(current)

    lax.fori_loop(0, frames, attend, tuple([ones] + [zeros] * (frames - 1)))

    beta_low = mix[...].reshape(rows, lanes)[:, :rows].astype(low)
    context = jnp.dot(beta_low, mem, preferred_element_type=wide).astype(low)
    seen[0] = context
    for r in range(4):
        cols = pl.ds(r * block, block)
        value = jnp.tanh(
            pre[:, cols] + jnp.dot(context, w[r, :, 5 * block :], preferred_element_type=wide)
        )
        pre[:, cols] = value
        pack[r, :, 5 * block :] = value.astype(low)
    logits = vocab_bias[...]
    for r in range(4):
        vocab_copies[r].wait()
        logits = logits + jnp.dot(pack[r, :, 5 * block :], v[r], preferred_element_type=wide)
    shifted = jnp.exp(logits - jnp.max(logits, axis=-1, keepdims=True))
    softmax = shifted / jnp.sum(shifted, axis=-1, keepdims=True)
    onehot = (labels[:, :1] == lax.broadcasted_iota(jnp.int32, softmax.shape, 1)).astype(wide)
    grad_logits = ((softmax - onehot) * counted[:, :1]).astype(low)
    seen[1] = grad_logits
    sums[5:6, :] = jnp.sum(grad_logits.astype(wide), axis=0, keepdims=True)
    sums[6:8, :] = jnp.zeros((2, sums.shape[1]), wide)

    grad_context = jnp.zeros((rows, memory.shape[1]), wide)
    for r in range(4):
        cols = pl.ds(r * block, block)
        value = pre[:, cols]
        grad_pre = (dot_nt(grad_logits, v[r]) * (1.0 - value * value)).astype(low)
        pack[r, :, 4 * block : 5 * block] = grad_pre
        sums[4:5, cols] = jnp.sum(grad_pre.astype(wide), axis=0, keepdims=True)
        grad_context = grad_context + dot_nt(grad_pre, w[r, :, 5 * block :])
    upper = grad_context.astype(low)
    lower = (grad_context - upper.astype(wide)).astype(low)
    grad_memory[...] = dot_tn(beta_low, upper) + dot_tn(beta_low, lower)
    cross = dot_nt(upper, mem) + dot_nt(lower, mem)
    if rows < lanes:
        cross = jnp.concatenate([cross, jnp.zeros((rows, lanes - rows), wide)], axis=1)
    mix[...] = split(cross)

    def unattend(k, later):
        i = frames - 1 - k
        base = i * frames
        cross_row = mix[i]
        grad_beta = [
            jnp.broadcast_to(
                jnp.sum(
                    jnp.where(diagonal == group * j, cross_row, 0.0), axis=-1, keepdims=True
                ),
                (group, lanes),
            )
            for j in range(frames)
        ]
        weight = [scaled[base + j] for j in range(frames)]
        share = [ratio[base + j] for j in range(frames)]
        direct, from_window, grad_weight = [], [], []
        for j in range(frames):
            grad_ratio = grad_beta[j] * weight[j]
            if j:
                grad_ratio = grad_ratio + grad_beta[j - 1] * weight[j - 1]
            pull = grad_ratio / window[base + j]
            direct.append(pull)
            from_window.append(jnp.where(valid[j], -pull * share[j], 0.0))
            grad_weight.append(
                grad_beta[j] * (share[j] + (share[j + 1] if j + 1 < frames else zeros))
            )
        top = jnp.full((group, lanes), -1e30, wide)
        for j in range(frames):
            top = jnp.maximum(top, jnp.where(valid[j], span[base + j], -1e30))
        total, ties, at_top, through = zeros, zeros, [], []
        for j in range(frames):
            pulled = grad_weight[j] + from_window[j]
            if j + 1 < frames:
                pulled = pulled + from_window[j + 1]
            pulled = weight[j] * pulled
            through.append(pulled)
            total = total + pulled
            hit = jnp.where(span[base + j] == top, live[j], 0.0)
            at_top.append(hit)
            ties = ties + hit
        back = total / ties
        for j in range(frames):
            span[base + j] = through[j] - at_top[j] * back
        grad_queue = zeros
        now = [None] * frames
        for j in reversed(range(frames)):
            prob = keep[base + j]
            grad_alpha = direct[j] + later[j]
            mono[base + j] = queue[base + j] * (grad_alpha - grad_queue) * prob * (1.0 - prob)
            grad_queue = prob * grad_alpha + (1.0 - prob) * grad_queue
            now[j] = grad_queue
        return tuple(now)

    lax.fori_loop(0, frames, unattend, tuple([zeros] * frames))

    def energy_back(queries, keys, energy, kept_squash, bias_row, vec_row):
        def one_chunk(c, carried):
            at = pl.ds(pl.multiple_of(c * lanes, lanes), lanes)
            weight = jnp.broadcast_to(vectors[vec_row : vec_row + 1, at], (group, lanes))

            def one(i, carry):
                grad_keys, vec_total, bias_total = carry
                grad_query = zeros
                new_keys = []
                for j in range(frames):
                    squash = kept_squash[i * frames + j, :, at]
                    grad = energy[i * frames + j]
                    scaled_squash = grad * squash
                    vec_total = vec_total + scaled_squash
                    inner = grad - scaled_squash * squash
                    grad_query = grad_query + inner
                    new_keys.append(grad_keys[j] + inner)
                queries[i, :, at] = grad_query * weight
                return (tuple(new_keys), vec_total, bias_total + grad_query)

            grad_keys, vec_total, bias_total = lax.fori_loop(
                0, frames, one, (tuple([zeros] * frames), zeros, zeros)
            )
            for j in range(frames):
                keys[j, :, at] = grad_keys[j] * weight
            sums[bias_row : bias_row + 1, at] = jnp.sum(bias_total * weight, axis=0, keepdims=True)
            sums[vec_row : vec_row + 1, at] = jnp.sum(vec_total, axis=0, keepdims=True)
            return carried

        lax.fori_loop(0, chunks, one_chunk, 0)

    energy_back(mq, mk, mono, mono_squash, 0, 1)
    energy_back(sq, sk, span, span_squash, 2, 3)

    total_memory = grad_memory[...]
    total_decoded = jnp.zeros_like(total_memory)
    for r in range(4):
        cols = pl.ds(r * block, block)
        for n, source in enumerate((mk, sk, mq, sq)):
            pack[r, :, n * block : (n + 1) * block] = (
                source[:, :, cols].reshape(rows, block).astype(low)
            )
        total_memory = total_memory + dot_nt(pack[r, :, : 2 * block], w[r, :, : 2 * block])
        total_decoded = total_decoded + dot_nt(
            pack[r, :, 2 * block : 5 * block], w[r, :, 2 * block : 5 * block]
        )
    pack_me[...] = pack[0]
    pack_chip[...] = pack[1]
    pack_cores[...] = pack[2:4]
    middle = 2 * block
    near[...] = sums[:, :middle]
    far[:8, :] = sums[:, middle:]
    far[8:9, :] = sums[5:6, :middle]
    far[9:10, :] = sums[5:6, middle:]
    far[10:, :] = jnp.zeros((6, middle), wide)
    grad_own[...] = jnp.where(first_chip, total_memory, total_decoded)
    grad_given[...] = jnp.where(first_chip, total_decoded, total_memory).astype(low)


def run_attend(
    places, kept, taken, smalls, vocab, vectors, vocab_bias, noise, lengths, labels, counted,
    frames,
):
    rows, width = kept.shape
    group = rows // frames
    full = vectors.shape[1]
    vocab_width = vocab[0].shape[1]
    cell = (frames * frames, group, 128)
    count = len(smalls[0])
    return pl.pallas_call(
        functools.partial(attend_kernel, count),
        out_shape=(
            jax.ShapeDtypeStruct((rows, width), wide),
            jax.ShapeDtypeStruct((rows, width), low),
            jax.ShapeDtypeStruct((rows, full // 4 * 6), low),
            jax.ShapeDtypeStruct((rows, full // 4 * 6), low),
            jax.ShapeDtypeStruct((2, rows, full // 4 * 6), low),
            jax.ShapeDtypeStruct((2, rows, vocab_width), low),
            jax.ShapeDtypeStruct((8, full // 2), wide),
            jax.ShapeDtypeStruct((16, full // 2), wide),
        ),
        in_specs=[in_smem] + [in_vmem] * 8 + [in_place] * (4 * count + 4),
        out_specs=[in_vmem] * 8,
        scratch_shapes=[
            pltpu.VMEM((rows, width), low),
            pltpu.VMEM((rows, width), low),
            pltpu.VMEM((rows, width), wide),
            pltpu.VMEM((4, rows, full // 4 * 6), low),
            pltpu.VMEM((8, full), wide),
            pltpu.VMEM((4, width, full // 4 * 6), low),
            pltpu.VMEM((4,) + vocab[0].shape, low),
            pltpu.SemaphoreType.DMA((4, places.shape[0] - 2)),
            pltpu.SemaphoreType.DMA((4,)),
        ]
        + [pltpu.VMEM((frames, group, full), wide)] * 4
        + [pltpu.VMEM(cell, wide)] * 7
        + [pltpu.VMEM((frames, group, 128), wide), pltpu.VMEM((rows, full), wide)]
        + [pltpu.VMEM((frames * frames, group, full), wide)] * 2,
        compiler_params=pltpu.CompilerParams(vmem_limit_bytes=56 << 20),
        name="attend",
    )(
        places, kept, taken, vectors, vocab_bias, noise, lengths, labels, counted,
        *sum(smalls, []), *vocab,
    )


def gradient_kernel(
    order, before, before_peer, normed, normed_peer, dz, dz_peer, states_own, states_core,
    seen, seen_core, far, far_core, pack_me, pack_core, pack_far, *refs
):
    outputs, paired = refs[:8], refs[8:12]
    a_rec, a_in, a_dz, states, a_context, a_grads, a_pack, block, paired_block, sems, out_sems = (
        refs[12:]
    )
    y = order[0]
    height = block.shape[1]
    wide_half = a_dz.shape[1]
    part = a_pack.shape[1] // 6
    width = a_rec.shape[1]
    jobs = []
    for sources, target in (
        ((dz, dz_peer), a_dz),
        ((before, before_peer), a_rec),
        ((normed, normed_peer), a_in),
        (
            (states_own.at[0], states_core.at[0], states_own.at[2], states_core.at[2]),
            states.at[y],
        ),
        (
            (
                states_own.at[1], states_core.at[1],
                states_own.at[3], states_core.at[3],
            ),
            states.at[1 - y],
        ),
        ((pack_me, pack_core.at[0], pack_far.at[0], pack_far.at[1]), a_pack),
        ((seen.at[0], seen_core.at[0], far.at[0, :, :width], far_core.at[0, :, :width]), a_context),
        ((seen.at[1], seen_core.at[1], far.at[1, :, :width], far_core.at[1, :, :width]), a_grads),
    ):
        rows = target.shape[0] // len(sources)
        for r, source in enumerate(sources):
            jobs.append(
                pltpu.make_async_copy(
                    source, target.at[r * rows : (r + 1) * rows, :], sems.at[len(jobs)]
                )
            )
    for job in jobs:
        job.start()
    for job in jobs[:6]:
        job.wait()
    both = 2 * wide_half

    def one(n, carried):
        cols = pl.ds(pl.multiple_of(order[1 + n] * height, height), height)
        pair = jnp.concatenate([a_rec[:, cols], a_in[:, cols]], axis=1)
        for at in range(0, wide_half, 1024):
            value = dot_tn(pair, a_dz[:, at : at + 1024]).astype(low)
            block[n, :, at : at + 1024] = value[:height]
            block[n, :, wide_half + at : wide_half + at + 1024] = value[height:]
        for m, output in enumerate(outputs):

            @pl.when(n == m)
            def _(m=m, output=output):
                pltpu.make_async_copy(
                    block.at[m, :, :both], output.at[:, :both], out_sems.at[m]
                ).start()

        return carried

    lax.fori_loop(0, 8, one, 0)
    for job in jobs[6:]:
        job.wait()

    def two(n, carried):
        cols = pl.ds(pl.multiple_of(order[1 + n] * height, height), height)
        for m in range(2):
            to = both + 2 * m * part
            block[n, :, to : to + 2 * part] = dot_tn(
                states[m, :, cols], a_pack[:, 2 * m * part : 2 * (m + 1) * part]
            ).astype(low)
        for m, output in enumerate(outputs):

            @pl.when(n == m)
            def _(m=m, output=output):
                pltpu.make_async_copy(
                    block.at[m, :, both:], output.at[:, both:], out_sems.at[12 + m]
                ).start()

        return carried

    lax.fori_loop(0, 8, two, 0)

    def pair(n, carried):
        cols = pl.ds(pl.multiple_of(order[9 + n] * 2 * height, 2 * height), 2 * height)
        grad_pre = a_pack[:, 4 * part : 5 * part]
        for m, (a, b) in enumerate(
            (
                (states[1, :, cols], grad_pre),
                (a_context[:, cols], grad_pre),
                (a_grads[:, cols], a_pack[:, 5 * part :]),
            )
        ):
            paired_block[n, :, m * part : (m + 1) * part] = dot_tn(a, b).astype(low)
        return carried

    lax.fori_loop(0, 4, pair, 0)
    for m, output in enumerate(paired):
        pltpu.make_async_copy(paired_block.at[m], output, out_sems.at[8 + m]).start()
    for m, output in enumerate(outputs):
        pltpu.make_async_copy(
            block.at[m, :, :both], output.at[:, :both], out_sems.at[m]
        ).wait()
        pltpu.make_async_copy(
            block.at[m, :, both:], output.at[:, both:], out_sems.at[12 + m]
        ).wait()
    for m, output in enumerate(paired):
        pltpu.make_async_copy(paired_block.at[m], output, out_sems.at[8 + m]).wait()


def run_gradients(order, *arrays):
    rows, width = arrays[0].shape
    wide_half = arrays[5].shape[1]
    part = arrays[12].shape[1] // 6
    columns = 2 * wide_half + 4 * part
    height = width // 8
    deep = 2 * rows
    return pl.pallas_call(
        gradient_kernel,
        out_shape=tuple(
            [jax.ShapeDtypeStruct((height, columns), low)] * 8
            + [jax.ShapeDtypeStruct((2 * height, 3 * part), low)] * 4
        ),
        in_specs=[in_smem] + [in_place] * 15,
        out_specs=[in_place] * 12,
        scratch_shapes=[
            pltpu.VMEM((deep, width), low),
            pltpu.VMEM((deep, width), low),
            pltpu.VMEM((deep, wide_half), low),
            pltpu.VMEM((2, deep, width), low),
            pltpu.VMEM((deep, width), low),
            pltpu.VMEM((deep, width), low),
            pltpu.VMEM((deep, 6 * part), low),
            pltpu.VMEM((8, height, columns), low),
            pltpu.VMEM((4, 2 * height, 3 * part), low),
            pltpu.SemaphoreType.DMA((26,)),
            pltpu.SemaphoreType.DMA((20,)),
        ],
        compiler_params=pltpu.CompilerParams(vmem_limit_bytes=56 << 20),
        name="weight_gradients",
    )(order, *arrays)


def local(
    dp,
    block_input, norm_gain, lstm_in, lstm_rec, lstm_bias,
    mono_mem, mono_dec, mono_bias, mono_vec, span_mem, span_dec, span_bias, span_vec,
    out_weight, out_bias, vocab_weight, vocab_bias, noise, enc_lengths, label_lengths, labels,
):
    ring = Ring(dp)
    s, y = lax.axis_index("section"), lax.axis_index("mp")
    _, utts, frames, width = block_input.shape
    half, quarter = utts // 2, utts // 4
    rows = frames * quarter
    shard_rows, _, unit_half = lstm_in.shape[1:]
    wide_half = 4 * unit_half
    block = mono_mem.shape[1]
    vocab_size = vocab_weight.shape[1]
    vocab_pad = 4 * block

    in_shard = lstm_in[0].reshape(shard_rows, wide_half)
    rec_shard = lstm_rec[0].reshape(shard_rows, wide_half)
    bias_shard = lstm_bias[0].reshape(1, wide_half)

    def of_section(array):
        return jnp.where(s == y, array, across_cores(array))

    inputs = of_section(jnp.swapaxes(block_input[0], 0, 1))
    gain = of_section(norm_gain[0])
    inputs_own = lax.dynamic_slice_in_dim(inputs, s * half, half, axis=1)
    inputs_other = lax.dynamic_slice_in_dim(inputs, (1 - s) * half, half, axis=1)
    normed_own = normalize(inputs_own.astype(wide), gain)
    normed_own = normed_own.astype(low).reshape(frames * half, width)
    normed_other = normalize(inputs_other.astype(wide), gain)
    normed_other = normed_other.astype(low).reshape(frames * half, width)

    start = s * half + y * quarter
    noise_part = jnp.transpose(
        lax.dynamic_slice_in_dim(noise, start, quarter, axis=0), (1, 2, 0)
    ).reshape(frames * frames, quarter, 1)
    noise_part = jnp.broadcast_to(noise_part, (frames * frames, quarter, 128))
    length_part = lax.dynamic_slice_in_dim(enc_lengths, start, quarter, axis=0)
    length_part = jnp.broadcast_to(length_part[:, None], (quarter, 128))
    label_part = lax.dynamic_slice_in_dim(labels, start, quarter, axis=0).T.reshape(rows, 1)
    label_part = jnp.broadcast_to(label_part, (rows, 128))
    count_part = lax.dynamic_slice_in_dim(label_lengths, start, quarter, axis=0)
    counted = (jnp.arange(frames)[:, None] < count_part[None, :]).astype(wide).reshape(rows, 1)
    counted = jnp.broadcast_to(counted, (rows, 128))
    bias_row = jnp.pad(vocab_bias, (0, vocab_pad - vocab_size), constant_values=-1e30)[None]

    vector_own = jnp.stack([mono_bias, mono_vec, span_bias, span_vec, out_bias])
    vocab_own = jnp.pad(vocab_weight, ((0, 0), (0, vocab_pad - vocab_size)))
    ready = (noise_part, length_part, label_part, counted, bias_row, normed_own, normed_other)
    places, in_own, rec_own, small_own, small_chip = [], [], [], [], []
    small = jnp.concatenate(
        [
            tie(mono_mem, in_shard, rec_shard), span_mem, mono_dec, span_dec,
            out_weight[0], out_weight[1],
        ],
        axis=1,
    )
    if ring.short:
        flow, across, onward = Flow(), ring.across, ring.onward
        both = 2 * wide_half
        corner_in, corner_rec, b_own = flow.step(
            (corners, in_shard), (corners, rec_shard), (corners, bias_shard)
        )
        small_far, small_next = across(small), onward(small)
        flow.landed += (small_far, small_next)
        b_own = b_own.astype(wide)
        small_own = [jnp.concatenate([small, small_far], axis=1)]
        small_chip, small_core = [], []
        held = jnp.concatenate([corner_in, corner_rec, small_next], axis=1)
        near, far, near_core, far_core = [], [], [], []
        for k in range(ring.outer):
            near.append(held)
            jobs = [(across, held), (across_chips, small_own[k])]
            if k < ring.outer - 1:
                jobs.append((onward, held[:, :both] if k == ring.outer - 2 else held))
            if k == 0:
                jobs.append((across_chips, vocab_own))
            if k == 1:
                jobs.append((across_chips, vector_own))
            results = flow.step(*jobs)
            far.append(results[0])
            small_chip.append(results[1])
            if k == 0:
                vocab_chip = results[3]
            if k == 1:
                vector_pair = jnp.concatenate([vector_own, results[3]], axis=1)
            if k < ring.outer - 1:
                small_own.append(jnp.concatenate([held[:, both:], far[k][:, both:]], axis=1))
                held = results[2]
        for k, (a, b) in enumerate(zip(near, far)):
            near_core.append(across_cores(a if k else tie(a, near[1], *ready)))
            far_core.append(across_cores(b))
        b_last, vocab_last, chip_last, vector_last = lax.optimization_barrier(
            (b_own, vocab_own, vocab_chip, vector_pair, held)
        )[:4]
        b_other = across_cores(b_last)
        vocab = [vocab_own, vocab_chip, across_cores(vocab_last), across_cores(chip_last)]
        vector_core = across_cores(vector_last)
        for k in range(ring.outer):
            places += [ring.back(k) * 2 + ring.x, ring.back(k) * 2 + 1 - ring.x]
        places = jnp.stack([s, y] + places).astype(jnp.int32)
        vectors = jnp.concatenate([vector_pair, vector_core], axis=1)
        vectors = jnp.pad(vectors, ((0, 3), (0, 0)))
        small_core = [across_cores(a) for a in small_own[:-1]]
        small_core.append(across_cores(tie(small_own[-1], vectors, places)))
        in_own = [a for pair in zip(near, far) for a in pair]
        in_other = [a for pair in zip(near_core, far_core) for a in pair]
        rec_own, rec_other, rec_column = in_own, in_other, wide_half
    else:
        vocab_chip = across_chips(vocab_own)
        small, in_block, rec_block = [
            lax.all_gather(a, "dp", axis=0, tiled=True)
            for a in (small, corners(in_shard), corners(rec_shard))
        ]
        places, in_own, rec_own = [jnp.int32(0)], [in_block], [rec_block]
        small_own, small_chip = [small], [across_chips(small)]
        vocab = [vocab_own, vocab_chip, across_cores(vocab_own), across_cores(vocab_chip)]
        in_other, rec_other, rec_column = [across_cores(in_block)], [across_cores(rec_block)], 0
        small_core = [across_cores(small)]
        b_own = corners(bias_shard).astype(wide)
        b_other = across_cores(b_own)
        vector_pair = across_chips(vector_own)
        vector_pair = jnp.concatenate([vector_own, vector_pair], axis=1)
        vector_core = across_cores(vector_pair)
        vectors = jnp.concatenate([vector_pair, vector_core], axis=1)
        vectors = jnp.pad(vectors, ((0, 3), (0, 0)))
        places = jnp.stack([s, y] + places).astype(jnp.int32)
    z, x = ring.z, ring.x
    if ring.short:
        steps_back = [ring.back(k) for k in range(1, 5)]
        order = [at * 2 + 1 - x for at in steps_back] + [at * 2 + x for at in steps_back]
        order = [y] + order + steps_back
    else:
        order = [y] + [jnp.int32(k) for k in [*range(8), *range(4)]]
    order = jnp.stack(order).astype(jnp.int32)
    places = tie(places, order, vectors, *vocab, *ready, *small_chip[:-1], *small_core)

    kept, given, before, gates, cells = run_forward(
        places, normed_own, b_own, b_other, in_own, in_other, rec_own, rec_other, frames,
        rec_column,
    )

    kept, given = kept.reshape(rows, width), given.reshape(rows, width)
    taken = across_chips(given)
    small_chip[-1] = tie(small_chip[-1], kept)
    small_both = [across_cores(part) for part in small_chip]
    smalls = [small_own, small_chip, small_core, small_both]
    grad_own, grad_given, pack_me, pack_chip, pack_cores, seen, near, far = run_attend(
        places, kept, taken, smalls, vocab, vectors, bias_row, noise_part, length_part,
        label_part, counted, frames,
    )
    grad_given, kept_far = lax.optimization_barrier((grad_given, across_chips(tie(kept, taken))))
    grad_taken = across_chips(grad_given)
    pack_core = across_cores(pack_cores)
    pack_out = jnp.stack([pack_chip, pack_core[1]])
    far_peer = across_cores(far)
    vector_pair = (near[:5] + far_peer[:5]).reshape(5, 2, block)
    bias_pair = (far[8:10] + far_peer[8:10]).reshape(-1)
    vector_out = jnp.concatenate([vector_pair[:, 1].reshape(-1), bias_pair])
    vector_count = vector_out.shape[0] // (2 * rows)
    seen_out = jnp.concatenate(
        [seen, halves(vector_out, 2 * rows).reshape(2, rows, -1)], axis=2
    )
    before = before.reshape(frames * half, width)
    before_peer = across_cores(tie(before, taken))
    states = jnp.stack([tie(kept, grad_given), taken, given, kept_far])
    states_core, seen_core = across_cores(states), across_cores(seen)
    places_back, pack_out, seen_out = lax.optimization_barrier(
        (places, pack_out, seen_out, grad_taken, before_peer, states_core, seen_core)
    )[:3]
    dz_own, dz_other = run_backward(
        places_back, grad_own.reshape(frames, quarter, width),
        grad_taken.reshape(frames, quarter, width), gates, cells, rec_own, rec_other, rec_column,
    )
    pack_far = across_chips(pack_out)
    seen_far = across_chips(tie(seen_out, pack_out))

    dz_own, dz_other, pack_far, seen_far = lax.optimization_barrier(
        (
            dz_own.reshape(frames * half, wide_half), dz_other.reshape(frames * half, wide_half),
            pack_far, seen_far,
        )
    )
    dz_peer = across_cores(dz_other)
    totals = run_gradients(
        order, before, before_peer, normed_own, normed_other, dz_own,
        dz_peer, states, states_core, seen, seen_core, seen_far, across_cores(seen_far),
        pack_me, pack_core, pack_far,
    )
    vector_far = joined(seen_far[:, :, width:].reshape(2 * rows, -1), vector_count).reshape(-1)

    sides_at = 5 * block + vocab_pad
    def input_back(places):
        grad_inputs, grad_gain = run_input(
            places, inputs_own.reshape(frames * half, width), gain[None], dz_own, dz_other,
            in_own, in_other,
        )
        grad_gain = grad_gain.reshape(width)
        grad_inputs = jnp.swapaxes(grad_inputs.reshape(frames, half, width), 0, 1)
        grad_peer = across_cores(grad_inputs)
        grad_section = jnp.concatenate(
            [
                jnp.where(s == 0, grad_inputs, grad_peer),
                jnp.where(s == 0, grad_peer, grad_inputs),
            ],
            axis=0,
        )
        gain_sum = grad_gain + across_cores(grad_gain)
        flat = jnp.concatenate(
            [
                vector_pair[:, 0].reshape(-1) + vector_far[: 5 * block],
                bias_pair + vector_far[5 * block :],
                jnp.sum(dz_own.astype(wide), axis=0) + jnp.sum(dz_peer.astype(wide), axis=0),
                gain_sum,
            ]
        )
        return grad_section, jnp.pad(flat, (0, -flat.shape[0] % (8 * shard_rows)))

    def to_other_chip(section):
        return lax.ppermute(section, ("section", "mp"), [(0, 1), (3, 2)])

    if ring.short:
        r = shard_rows
        both, width_out = 2 * wide_half, 2 * block
        flow, across, onward = Flow(), ring.across, ring.onward
        theirs, mine, outputs = totals[:4], totals[4:8], totals[8:]

        def total(k, arrived, passed):
            value = mine[k - 1].astype(wide) + arrived.astype(wide)
            return value if passed is None else value + passed.astype(wide)

        def cornered(hop):
            index = lambda at, place, chip: (at * ring.dp + place) * 2 + chip
            pairs = [
                (index(p, a, q), index(q, b, p)) for a, b in hop for p in range(2) for q in range(2)
            ]
            return lambda array: lax.ppermute(array, ("section", "dp", "mp"), pairs)

        arrived, out_two, out_before = flow.step(
            (across, theirs[0]), (onward, outputs[1]), (ring.astern, outputs[0])
        )
        grad_section, flat = input_back(tie(places, out_two))
        out_one = onward(
            tie((outputs[2].astype(wide) + out_two.astype(wide)).astype(low), arrived)
        )
        grad_far = to_other_chip(grad_section)
        flat = flat.reshape(8, -1)
        flat = (flat + across(flat)).reshape(-1)
        flat_width = flat.shape[0] // r
        flow.landed = (arrived,)
        value = total(1, arrived, None).astype(low)
        passed, arrived = flow.step((onward, value), (across, theirs[1]))
        out = outputs[3].astype(wide) + out_before.astype(wide) + out_one.astype(wide)
        vocab_rows = out[:, width_out:].astype(low)
        message = jnp.concatenate(
            [cut(out, 1 - x, r)[:, :width_out].astype(low), vocab_rows[:r], vocab_rows[r:]], axis=1
        )
        kept_rows = corners(tie(mine[3][:, :both], out_one))
        value = total(2, arrived, passed).astype(low)
        passed, arrived, out_far = flow.step(
            (onward, value), (across, theirs[2]), (across, message), also=(grad_far,)
        )
        output_grad = cut(out, x, r)[:, :width_out] + out_far[:, :width_out].astype(wide)
        shard = jnp.concatenate([out[:r, width_out:], out[r:, width_out:]], axis=1)
        shard = (shard + out_far[:, width_out:].astype(wide)).astype(low)
        shard = jnp.concatenate([shard, halves(flat, r)], axis=1)
        next_one, next_three = onward(shard), ring.astern(shard)
        value = total(3, arrived, passed).astype(low)
        passed, arrived, energy_passed, energy_arrived, next_two = flow.step(
            (cornered(ring.ring), value[:, :both]), (cornered(ring.pair), theirs[3][:, :both]),
            (onward, value[:, both:]), (across, theirs[3][:, both:]), (onward, next_one),
            also=(kept_rows,),
        )
        shards = {0: shard, 1: next_one, 3: next_three, 2: next_two}
        flat = sum(joined(a[:, 2 * block :], flat_width).reshape(-1) for a in shards.values())
        sides = corners(flat[sides_at : sides_at + wide_half + width])
        moved = kept_rows.astype(wide) + arrived.astype(wide) + passed.astype(wide)
        energy_grad = mine[3][:, both:].astype(wide) + energy_arrived.astype(wide)
        energy_grad = energy_grad + energy_passed.astype(wide)
        vocab_grad = jnp.zeros((vocab_pad, block), low)
        for k, held in shards.items():
            held = jnp.concatenate([held[:, :block], held[:, block : 2 * block]], axis=0)
            vocab_grad = lax.dynamic_update_slice(vocab_grad, held, (ring.back(k) * 2 * r, 0))
    else:
        grad_section, flat = input_back(places)
        grad_far = to_other_chip(grad_section)

        def scatter(parts):
            total = jnp.concatenate(parts, axis=0)
            return lax.psum_scatter(total, "dp", scatter_dimension=0, tiled=True).astype(wide)

        moved, output_grad = scatter(totals[:8]), scatter(totals[8:])
        moved, energy_grad = moved[:, : 2 * wide_half], moved[:, 2 * wide_half :]
        moved = corners(moved.astype(low)).astype(wide)
        flat = lax.psum(flat, "dp")
        sides = corners(flat[sides_at : sides_at + wide_half + width])
        vocab_grad = lax.all_gather(
            output_grad[:, 2 * block :].astype(low), "dp", axis=0, tiled=True
        )

    input_grad = jnp.where(s == y, grad_section, grad_far)
    vocab_grad = vocab_grad.T[:, :vocab_size].astype(wide)
    vector_sum = flat[: 5 * block].reshape(5, block)
    bias_sum = flat[5 * block : 5 * block + vocab_size]
    lstm_bias_sum = sides[:wide_half].reshape(1, 4, unit_half)
    gain_sum = sides[wide_half:][None]
    rec_grad = moved[:, :wide_half].reshape(1, shard_rows, 4, unit_half)
    in_grad = moved[:, wide_half:].reshape(1, shard_rows, 4, unit_half)
    mono_mem_grad, span_mem_grad, mono_dec_grad, span_dec_grad = [
        energy_grad[:, n * block : (n + 1) * block] for n in range(4)
    ]
    return (
        input_grad[None],
        gain_sum,
        in_grad,
        rec_grad,
        lstm_bias_sum,
        mono_mem_grad,
        mono_dec_grad,
        vector_sum[0],
        vector_sum[1],
        span_mem_grad,
        span_dec_grad,
        vector_sum[2],
        vector_sum[3],
        jnp.stack([output_grad[:, :block], output_grad[:, block : 2 * block]]),
        vector_sum[4],
        vocab_grad,
        bias_sum,
    )


def solution(mesh):
    both = ("section", "mp")
    in_specs = (
        P("section", "dp", None, None),
        P("section", None),
        P("section", "dp", None, "mp"),
        P("section", "dp", None, "mp"),
        P("section", None, "mp"),
        P("dp", both),
        P("dp", both),
        P(both),
        P(both),
        P("dp", both),
        P("dp", both),
        P(both),
        P(both),
        P(None, "dp", both),
        P(both),
        P(both, None),
        P(),
        P("dp", None, None),
        P("dp"),
        P("dp"),
        P("dp", None),
    )
    out_specs = (
        P("section", "dp", None, None),
        P("section", None),
        P("section", "dp", None, "mp"),
        P("section", "dp", None, "mp"),
        P("section", None, "mp"),
        P("dp", both),
        P("dp", both),
        P(both),
        P(both),
        P("dp", both),
        P("dp", both),
        P(both),
        P(both),
        P(None, "dp", both),
        P(both),
        P(both, None),
        P(),
    )
    dp = mesh.shape["dp"]

    def step(*arrays):
        return local(dp, *arrays)

    return jax.shard_map(step, mesh=mesh, in_specs=in_specs, out_specs=out_specs, check_vma=False)
```

```python
import functools

import jax
import jax.numpy as jnp
from jax import lax
from jax.experimental import pallas as pl
from jax.experimental.pallas import tpu as pltpu
from jax.sharding import PartitionSpec as P

epsilon = 1e-05
offset = -4.0
wide = jnp.float32
low = jnp.bfloat16
in_vmem = pl.BlockSpec(memory_space=pltpu.VMEM)
in_smem = pl.BlockSpec(memory_space=pltpu.SMEM)
in_place = pl.BlockSpec(memory_space=pl.ANY)
core_swap = [(0, 1), (1, 0)]
corner_swap = [(0, 0), (1, 2), (2, 1), (3, 3)]


def normalize(inputs, gain_row):
    average = jnp.mean(inputs, axis=-1, keepdims=True)
    centred = inputs - average
    spread = jnp.mean(centred * centred, axis=-1, keepdims=True)
    return centred * lax.rsqrt(spread + epsilon) * gain_row


def across_cores(array):
    return lax.ppermute(array, "section", core_swap)


def across_chips(array):
    return lax.ppermute(array, "mp", core_swap)


def corners(array):
    return lax.ppermute(array, ("section", "mp"), corner_swap)


def tie(value, *others):
    return lax.optimization_barrier((value,) + others)[0]


def cut(array, block, rows):
    return lax.dynamic_slice_in_dim(array, block * rows, rows, axis=0)


class Flow:
    def __init__(self):
        self.landed = ()

    def step(self, *jobs, also=()):
        operands = tuple(operand for _, operand in jobs)
        operands = lax.optimization_barrier(operands + self.landed + tuple(also))[: len(jobs)]
        results = [send(operand) for (send, _), operand in zip(jobs, operands)]
        self.landed = tuple(results)
        return results


class Ring:
    def __init__(self, dp):
        self.dp = dp
        self.outer = dp // 2
        self.short = dp % 2 == 0 and self.outer == 4
        pairs = [(z, x) for z in range(self.outer) for x in range(2)]
        self.pair = [(2 * z + x, 2 * z + 1 - x) for z, x in pairs]
        self.ring = [(2 * z + x, 2 * ((z + 1) % self.outer) + x) for z, x in pairs]
        self.turn = [(b, a) for a, b in self.ring]
        place = lax.axis_index("dp")
        self.z, self.x = place // 2, place % 2

    def across(self, array):
        return lax.ppermute(array, "dp", self.pair)

    def onward(self, array):
        return lax.ppermute(array, "dp", self.ring)

    def astern(self, array):
        return lax.ppermute(array, "dp", self.turn)

    def back(self, k):
        return lax.rem(self.z - k + self.outer, self.outer)


def halves(array, height):
    array = array.reshape(height, -1)
    upper = array.astype(low)
    lower = (array - upper.astype(wide)).astype(low)
    return jnp.pad(
        jnp.concatenate([upper, lower], axis=1), ((0, 0), (0, -2 * array.shape[1] % 128))
    )


def joined(array, count):
    return array[:, :count].astype(wide) + array[:, count : 2 * count].astype(wide)


def sigmoid(x):
    return 0.5 * jnp.tanh(0.5 * x) + 0.5


def fetch(blocks, places, side_blocks, target, sems, first=0, column=0):
    wide_half = target.shape[1] // 2
    columns = pl.ds(pl.multiple_of(side_blocks * wide_half, wide_half), wide_half)
    copies = []
    for k, block in enumerate(blocks):
        height = block.shape[0]
        span = pl.ds(pl.multiple_of(places[2 + k] * height, height), height)
        copies.append(
            pltpu.make_async_copy(
                block.at[:, column : column + wide_half],
                target.at[span, columns],
                sems.at[first + k],
            )
        )
    return copies


def forward_kernel(count, column, places, normed, b_own, b_other, *refs):
    in_own, in_other, w_own, w_other = [refs[n * count : (n + 1) * count] for n in range(4)]
    (
        kept, given, before, gates_out, cells_out, gates, cells, wi, w, b, state, cell, sems,
        gate_sems, cell_sems,
    ) = refs[4 * count :]
    steps, rows, wide_full = gates.shape
    wide_half = wide_full // 2
    unit_half = wide_half // 4
    chunk = min(256, unit_half)
    s = places[0]
    copies = fetch(in_own, places, s, wi, sems) + fetch(in_other, places, 1 - s, wi, sems, count)
    later = fetch(w_own, places, s, w, sems, 2 * count, column)
    later += fetch(w_other, places, 1 - s, w, sems, 3 * count, column)
    for copy in copies + later:
        copy.start()
    for source, at in ((b_own, s), (b_other, 1 - s)):
        b[:, pl.ds(pl.multiple_of(at * wide_half, wide_half), wide_half)] = source[...]
    state[...] = jnp.zeros_like(state)
    cell[...] = jnp.zeros_like(cell)
    for copy in copies:
        copy.wait()

    def project(g, carried):
        cols = pl.ds(pl.multiple_of(g * unit_half, unit_half), unit_half)
        value = jnp.dot(normed[...], wi[:, cols], preferred_element_type=wide) + b[:, cols]
        gates[:, :, cols] = value.reshape(steps, rows, unit_half)
        return carried

    lax.fori_loop(0, 8, project, 0)
    for copy in later:
        copy.wait()
    eighth = rows // 2
    first_chip = places[1] == 0

    def advance(t, carried):
        hidden = state[...]
        before[t] = hidden
        for at in range(0, 2 * unit_half, chunk):
            half, inside = at // unit_half, at % unit_half
            acts = []
            for g in range(4):
                cols = pl.ds(half * wide_half + g * unit_half + inside, chunk)
                value = gates[t, :, cols] + jnp.dot(
                    hidden, w[:, cols], preferred_element_type=wide
                )
                value = jnp.tanh(value) if g == 2 else sigmoid(value)
                gates[t, :, cols] = value
                acts.append(value)
            units = pl.ds(at, chunk)
            new_cell = acts[1] * cell[:, units] + acts[0] * acts[2]
            cell[:, units] = new_cell
            cells[t, :, units] = new_cell
            new_hidden = acts[3] * jnp.tanh(new_cell)
            state[:, units] = new_hidden.astype(low)
            upper, lower = new_hidden[:eighth], new_hidden[eighth:]
            kept[t, :, units] = jnp.where(first_chip, upper, lower).astype(low)
            given[t, :, units] = jnp.where(first_chip, lower, upper).astype(low)
        pltpu.make_async_copy(gates.at[t], gates_out.at[t], gate_sems.at[t]).start()
        pltpu.make_async_copy(cells.at[t], cells_out.at[t], cell_sems.at[t]).start()
        return carried

    lax.fori_loop(0, steps, advance, 0)

    def settle(t, carried):
        pltpu.make_async_copy(gates.at[t], gates_out.at[t], gate_sems.at[t]).wait()
        pltpu.make_async_copy(cells.at[t], cells_out.at[t], cell_sems.at[t]).wait()
        return carried

    lax.fori_loop(0, steps, settle, 0)


def run_forward(places, normed, b_own, b_other, in_own, in_other, w_own, w_other, steps, column):
    rows = normed.shape[0] // steps
    units = normed.shape[1]
    wide_half = b_own.shape[1]
    count = len(w_own)
    return pl.pallas_call(
        functools.partial(forward_kernel, count, column),
        out_shape=(
            jax.ShapeDtypeStruct((steps, rows // 2, units), low),
            jax.ShapeDtypeStruct((steps, rows // 2, units), low),
            jax.ShapeDtypeStruct((steps, rows, units), low),
            jax.ShapeDtypeStruct((steps, rows, 2 * wide_half), wide),
            jax.ShapeDtypeStruct((steps, rows, units), wide),
        ),
        in_specs=[in_smem] + [in_vmem] * 3 + [in_place] * (4 * count),
        out_specs=[in_vmem] * 3 + [in_place] * 2,
        scratch_shapes=[
            pltpu.VMEM((steps, rows, 2 * wide_half), wide),
            pltpu.VMEM((steps, rows, units), wide),
            pltpu.VMEM((units, 2 * wide_half), low),
            pltpu.VMEM((units, 2 * wide_half), low),
            pltpu.VMEM((1, 2 * wide_half), wide),
            pltpu.VMEM((rows, units), low),
            pltpu.VMEM((rows, units), wide),
            pltpu.SemaphoreType.DMA((4 * count,)),
            pltpu.SemaphoreType.DMA((steps,)),
            pltpu.SemaphoreType.DMA((steps,)),
        ],
        compiler_params=pltpu.CompilerParams(vmem_limit_bytes=56 << 20),
        name="recur_forward",
    )(places, normed, b_own, b_other, *in_own, *in_other, *w_own, *w_other)


def backward_kernel(count, column, places, kept, taken, gates_in, cells_in, *refs):
    w_own, w_other = refs[:count], refs[count : 2 * count]
    dz_own, dz_other, gates, cells, dz, stage, w, dh, dc, sems, gate_sems, cell_sems = refs[
        2 * count :
    ]
    steps, rows, wide_full = gates.shape
    wide_half = wide_full // 2
    unit_half = wide_half // 4
    chunk = min(256, unit_half)
    s = places[0]
    first_chip = places[1] == 0

    def gate_copy(t):
        return pltpu.make_async_copy(gates_in.at[t], gates.at[t], gate_sems.at[t])

    def cell_copy(t):
        return pltpu.make_async_copy(cells_in.at[t], cells.at[t], cell_sems.at[t])

    gate_copy(steps - 1).start()
    cell_copy(steps - 1).start()
    jobs = []
    for n, (sources, at) in enumerate(((w_own, s), (w_other, 1 - s))):
        for k, block in enumerate(sources):
            slot = n * count + k
            copy = pltpu.make_async_copy(
                block.at[:, column : column + wide_half], stage.at[slot], sems.at[slot]
            )
            copy.start()
            jobs.append((copy, slot, at, places[2 + k] * block.shape[0]))
    for t in range(steps - 2, -1, -1):
        cell_copy(t).start()
        gate_copy(t).start()
    dh[...] = jnp.zeros_like(dh)
    dc[...] = jnp.zeros_like(dc)
    height = w_own[0].shape[0]
    piece = min(height, 128)
    for copy, slot, at, first in jobs:
        copy.wait()

        def turn(g, carried, slot=slot, at=at, first=first):
            columns = pl.ds(pl.multiple_of(g * unit_half, unit_half), unit_half)
            span = pl.ds(pl.multiple_of(at * wide_half + g * unit_half, unit_half), unit_half)
            for low_row in range(0, height, piece):
                into = pl.ds(pl.multiple_of(first + low_row, piece), piece)
                w[span, into] = stage[slot, low_row : low_row + piece, columns].T
            return carried

        lax.fori_loop(0, 4, turn, 0)

    cell_copy(steps - 1).wait()

    def retreat(k, carried):
        t = steps - 1 - k
        earlier = jnp.maximum(t - 1, 0)
        gate_copy(t).wait()

        @pl.when(t > 0)
        def _():
            cell_copy(earlier).wait()

        live = jnp.where(t > 0, 1.0, 0.0).astype(wide)
        for at in range(0, 2 * unit_half, chunk):
            half, inside = at // unit_half, at % unit_half
            units = pl.ds(at, chunk)
            ours, theirs = kept[t, :, units], taken[t, :, units].astype(wide)
            grad = dh[:, units] + jnp.concatenate(
                [jnp.where(first_chip, ours, theirs), jnp.where(first_chip, theirs, ours)], axis=0
            )
            i, f, g, o = [
                gates[t, :, pl.ds(half * wide_half + n * unit_half + inside, chunk)]
                for n in range(4)
            ]
            squash = jnp.tanh(cells[t, :, units])
            total = dc[:, units] + grad * o * (1.0 - squash * squash)
            parts = (
                total * g * i * (1.0 - i),
                total * (cells[earlier, :, units] * live) * f * (1.0 - f),
                total * i * (1.0 - g * g),
                grad * squash * o * (1.0 - o),
            )
            for n, part in enumerate(parts):
                dz[half, :, pl.ds(n * unit_half + inside, chunk)] = part.astype(low)
            dc[:, units] = total * f
        dz_own[t] = dz[s]
        dz_other[t] = dz[1 - s]
        upper, lower = dz[0], dz[1]
        for at in range(0, 2 * unit_half, chunk):
            units = pl.ds(at, chunk)
            dh[:, units] = jnp.dot(
                upper, w[:wide_half, units], preferred_element_type=wide
            ) + jnp.dot(lower, w[wide_half:, units], preferred_element_type=wide)
        return carried

    lax.fori_loop(0, steps, retreat, 0)


def run_backward(places, kept, taken, gates, cells, w_own, w_other, column):
    steps, rows, wide_full = gates.shape
    units = cells.shape[2]
    count = len(w_own)
    return pl.pallas_call(
        functools.partial(backward_kernel, count, column),
        out_shape=(jax.ShapeDtypeStruct((steps, rows, wide_full // 2), low),) * 2,
        in_specs=[in_smem] + [in_vmem] * 2 + [in_place] * (2 + 2 * count),
        out_specs=[in_vmem] * 2,
        scratch_shapes=[
            pltpu.VMEM((steps, rows, wide_full), wide),
            pltpu.VMEM((steps, rows, units), wide),
            pltpu.VMEM((2, rows, wide_full // 2), low),
            pltpu.VMEM((2 * count, units // count, wide_full // 2), low),
            pltpu.VMEM((wide_full, units), low),
            pltpu.VMEM((rows, units), wide),
            pltpu.VMEM((rows, units), wide),
            pltpu.SemaphoreType.DMA((2 * count,)),
            pltpu.SemaphoreType.DMA((steps,)),
            pltpu.SemaphoreType.DMA((steps,)),
        ],
        compiler_params=pltpu.CompilerParams(vmem_limit_bytes=56 << 20),
        name="recur_backward",
    )(places, kept, taken, gates, cells, *w_own, *w_other)


def input_kernel(count, places, inputs, gain, dz, dz_given, *refs):
    in_own, in_other = refs[:count], refs[count : 2 * count]
    grad_inputs, grad_gain, wi, sems = refs[2 * count :]
    s = places[0]
    copies = fetch(in_own, places, s, wi, sems) + fetch(in_other, places, 1 - s, wi, sems, count)
    for copy in copies:
        copy.start()
    x = inputs[...].astype(wide)
    centred = x - jnp.mean(x, axis=-1, keepdims=True)
    scale = lax.rsqrt(jnp.mean(centred * centred, axis=-1, keepdims=True) + epsilon)
    shape = centred * scale
    for copy in copies:
        copy.wait()
    wide_half = wi.shape[1] // 2
    own = pl.ds(pl.multiple_of(s * wide_half, wide_half), wide_half)
    other = pl.ds(pl.multiple_of((1 - s) * wide_half, wide_half), wide_half)
    grad = dot_nt(dz[...], wi[:, own]) + dot_nt(dz_given[...], wi[:, other])
    grad_gain[...] = jnp.sum(grad * shape, axis=0, keepdims=True)
    pulled = grad * gain[...]
    grad_inputs[...] = scale * (
        pulled
        - jnp.mean(pulled, axis=-1, keepdims=True)
        - shape * jnp.mean(pulled * shape, axis=-1, keepdims=True)
    )


def run_input(places, inputs, gain, dz, dz_given, in_own, in_other):
    count = len(in_own)
    rows, width = inputs.shape
    return pl.pallas_call(
        functools.partial(input_kernel, count),
        out_shape=(
            jax.ShapeDtypeStruct((rows, width), wide),
            jax.ShapeDtypeStruct((1, width), wide),
        ),
        in_specs=[in_smem] + [in_vmem] * 4 + [in_place] * (2 * count),
        out_specs=[in_vmem] * 2,
        scratch_shapes=[
            pltpu.VMEM((width, 2 * dz.shape[1]), low),
            pltpu.SemaphoreType.DMA((2 * count,)),
        ],
        compiler_params=pltpu.CompilerParams(vmem_limit_bytes=56 << 20),
        name="input_back",
    )(places, inputs, gain, dz, dz_given, *in_own, *in_other)


def dot_nt(a, b):
    return lax.dot_general(a, b, (((1,), (1,)), ((), ())), preferred_element_type=wide)


def dot_tn(a, b):
    return lax.dot_general(a, b, (((0,), (0,)), ((), ())), preferred_element_type=wide)


def attend_kernel(
    count, places, kept, taken, vectors, vocab_bias, noise, lengths, labels, counted, *refs
):
    small, vocab = refs[: 4 * count], refs[4 * count : 4 * count + 4]
    (
        grad_own, grad_given, pack_me, pack_chip, pack_cores, seen, near, far,
        memory, decoded, grad_memory, pack, sums, w, v, sems, v_sems, mk, sk, mq, sq, mono, span, keep, queue, scaled, ratio, window, mix, pre,
        mono_squash, span_squash,
    ) = refs[4 * count + 4 :]
    rows, _ = kept.shape
    frames, group, _ = mk.shape
    block = w.shape[2] // 6
    lanes = 128
    chunks = 4 * block // lanes
    copies = []
    for r in range(4):
        arrived = []
        for k in range(count):
            source = small[r * count + k]
            height = source.shape[0]
            for h in range(source.shape[1] // (6 * block)):
                to = pl.ds(pl.multiple_of(places[2 + len(arrived)] * height, height), height)
                arrived.append(
                    pltpu.make_async_copy(
                        source.at[:, 6 * block * h : 6 * block * (h + 1)],
                        w.at[r, to, :],
                        sems.at[r, len(arrived)],
                    )
                )
        copies.append(arrived)
    vocab_copies = [pltpu.make_async_copy(vocab[r], v.at[r], v_sems.at[r]) for r in range(4)]
    for copy in sum(copies, []) + vocab_copies:
        copy.start()

    first_chip = places[1] == 0

    @pl.when(first_chip)
    def _():
        memory[...] = kept[...]
        decoded[...] = taken[...]

    @pl.when(jnp.logical_not(first_chip))
    def _():
        memory[...] = taken[...]
        decoded[...] = kept[...]

    def split(value):
        return value.reshape(frames, group, value.shape[-1])

    mem, dec = memory[...], decoded[...]

    def lane(c):
        return pl.ds(c * lanes, lanes)

    def spread(row, c):
        return jnp.broadcast_to(vectors[row : row + 1, lane(c)], (group, lanes))

    def energies(queries, keys, vec_row, energy, kept_squash, r):
        mine = range(r * chunks // 4, (r + 1) * chunks // 4)
        weights = {c: spread(vec_row, c) for c in mine}

        def one(i, carried):
            query = {c: queries[i, :, lane(c)] for c in mine}
            for j in range(frames):
                total = None if r == 0 else energy[i * frames + j]
                for c in mine:
                    squash = jnp.tanh(query[c] + keys[j, :, lane(c)])
                    kept_squash[i * frames + j, :, lane(c)] = squash
                    part = squash * weights[c]
                    total = part if total is None else total + part
                if r == 3:
                    total = jnp.broadcast_to(
                        jnp.sum(total, axis=-1, keepdims=True), (group, lanes)
                    )
                energy[i * frames + j] = total
            return carried

        lax.fori_loop(0, frames, one, 0)

    for r in range(4):
        for copy in copies[r]:
            copy.wait()
        cols = pl.ds(r * block, block)
        keys = jnp.dot(mem, w[r, :, : 2 * block], preferred_element_type=wide)
        queries = jnp.dot(dec, w[r, :, 2 * block : 5 * block], preferred_element_type=wide)
        mk[:, :, cols] = split(keys[:, :block])
        sk[:, :, cols] = split(keys[:, block:])
        mq[:, :, cols] = split(queries[:, :block] + vectors[0:1, cols])
        sq[:, :, cols] = split(queries[:, block : 2 * block] + vectors[2:3, cols])
        pre[:, cols] = queries[:, 2 * block :] + vectors[4:5, cols]
        energies(mq, mk, 1, mono, mono_squash, r)
        energies(sq, sk, 3, span, span_squash, r)

    length = lengths[...]
    valid = [(length > j) for j in range(frames)]
    ones = jnp.ones((group, lanes), wide)
    zeros = jnp.zeros((group, lanes), wide)
    live = [jnp.where(valid[j], 1.0, 0.0).astype(wide) for j in range(frames)]
    diagonal = lax.broadcasted_iota(jnp.int32, (group, lanes), 1) - lax.broadcasted_iota(
        jnp.int32, (group, lanes), 0
    )

    def attend(i, previous):
        base = i * frames
        top = jnp.full((group, lanes), -1e30, wide)
        for j in range(frames):
            top = jnp.maximum(top, jnp.where(valid[j], span[base + j], -1e30))
        weight = [jnp.where(valid[j], jnp.exp(span[base + j] - top), 0.0) for j in range(frames)]
        current, ratios = [], []
        queued = previous[0]
        for j in range(frames):
            prob = sigmoid(mono[base + j] + offset + noise[base + j]) * live[j]
            keep[base + j] = prob
            queue[base + j] = queued
            alpha = prob * queued
            current.append(alpha)
            if j + 1 < frames:
                queued = (1.0 - prob) * queued + previous[j + 1]
            both = weight[j] + weight[j - 1] if j else weight[j]
            both = jnp.where(valid[j], both, 1.0)
            window[base + j] = both
            scaled[base + j] = weight[j]
            quotient = alpha / both
            ratio[base + j] = quotient
            ratios.append(quotient)
        row = zeros
        for j in range(frames):
            beta = weight[j] * (ratios[j] + (ratios[j + 1] if j + 1 < frames else zeros))
            row = jnp.where(diagonal == group * j, beta, row)
        mix[i] = row
        return tuple(current)

    lax.fori_loop(0, frames, attend, tuple([ones] + [zeros] * (frames - 1)))

    beta_low = mix[...].reshape(rows, lanes)[:, :rows].astype(low)
    context = jnp.dot(beta_low, mem, preferred_element_type=wide).astype(low)
    seen[0] = context
    for r in range(4):
        cols = pl.ds(r * block, block)
        value = jnp.tanh(
            pre[:, cols] + jnp.dot(context, w[r, :, 5 * block :], preferred_element_type=wide)
        )
        pre[:, cols] = value
        pack[r, :, 5 * block :] = value.astype(low)
    logits = vocab_bias[...]
    for r in range(4):
        vocab_copies[r].wait()
        logits = logits + jnp.dot(pack[r, :, 5 * block :], v[r], preferred_element_type=wide)
    shifted = jnp.exp(logits - jnp.max(logits, axis=-1, keepdims=True))
    softmax = shifted / jnp.sum(shifted, axis=-1, keepdims=True)
    onehot = (labels[:, :1] == lax.broadcasted_iota(jnp.int32, softmax.shape, 1)).astype(wide)
    grad_logits = ((softmax - onehot) * counted[:, :1]).astype(low)
    seen[1] = grad_logits
    sums[5:6, :] = jnp.sum(grad_logits.astype(wide), axis=0, keepdims=True)
    sums[6:8, :] = jnp.zeros((2, sums.shape[1]), wide)

    grad_context = jnp.zeros((rows, memory.shape[1]), wide)
    for r in range(4):
        cols = pl.ds(r * block, block)
        value = pre[:, cols]
        grad_pre = (dot_nt(grad_logits, v[r]) * (1.0 - value * value)).astype(low)
        pack[r, :, 4 * block : 5 * block] = grad_pre
        sums[4:5, cols] = jnp.sum(grad_pre.astype(wide), axis=0, keepdims=True)
        grad_context = grad_context + dot_nt(grad_pre, w[r, :, 5 * block :])
    upper = grad_context.astype(low)
    lower = (grad_context - upper.astype(wide)).astype(low)
    grad_memory[...] = dot_tn(beta_low, upper) + dot_tn(beta_low, lower)
    cross = dot_nt(upper, mem) + dot_nt(lower, mem)
    if rows < lanes:
        cross = jnp.concatenate([cross, jnp.zeros((rows, lanes - rows), wide)], axis=1)
    mix[...] = split(cross)

    def unattend(k, later):
        i = frames - 1 - k
        base = i * frames
        cross_row = mix[i]
        grad_beta = [
            jnp.broadcast_to(
                jnp.sum(
                    jnp.where(diagonal == group * j, cross_row, 0.0), axis=-1, keepdims=True
                ),
                (group, lanes),
            )
            for j in range(frames)
        ]
        weight = [scaled[base + j] for j in range(frames)]
        share = [ratio[base + j] for j in range(frames)]
        direct, from_window, grad_weight = [], [], []
        for j in range(frames):
            grad_ratio = grad_beta[j] * weight[j]
            if j:
                grad_ratio = grad_ratio + grad_beta[j - 1] * weight[j - 1]
            pull = grad_ratio / window[base + j]
            direct.append(pull)
            from_window.append(jnp.where(valid[j], -pull * share[j], 0.0))
            grad_weight.append(
                grad_beta[j] * (share[j] + (share[j + 1] if j + 1 < frames else zeros))
            )
        top = jnp.full((group, lanes), -1e30, wide)
        for j in range(frames):
            top = jnp.maximum(top, jnp.where(valid[j], span[base + j], -1e30))
        total, ties, at_top, through = zeros, zeros, [], []
        for j in range(frames):
            pulled = grad_weight[j] + from_window[j]
            if j + 1 < frames:
                pulled = pulled + from_window[j + 1]
            pulled = weight[j] * pulled
            through.append(pulled)
            total = total + pulled
            hit = jnp.where(span[base + j] == top, live[j], 0.0)
            at_top.append(hit)
            ties = ties + hit
        back = total / ties
        for j in range(frames):
            span[base + j] = through[j] - at_top[j] * back
        grad_queue = zeros
        now = [None] * frames
        for j in reversed(range(frames)):
            prob = keep[base + j]
            grad_alpha = direct[j] + later[j]
            mono[base + j] = queue[base + j] * (grad_alpha - grad_queue) * prob * (1.0 - prob)
            grad_queue = prob * grad_alpha + (1.0 - prob) * grad_queue
            now[j] = grad_queue
        return tuple(now)

    lax.fori_loop(0, frames, unattend, tuple([zeros] * frames))

    def energy_back(queries, keys, energy, kept_squash, bias_row, vec_row):
        def one_chunk(c, carried):
            at = pl.ds(pl.multiple_of(c * lanes, lanes), lanes)
            weight = jnp.broadcast_to(vectors[vec_row : vec_row + 1, at], (group, lanes))

            def one(i, carry):
                grad_keys, vec_total, bias_total = carry
                grad_query = zeros
                new_keys = []
                for j in range(frames):
                    squash = kept_squash[i * frames + j, :, at]
                    grad = energy[i * frames + j]
                    scaled_squash = grad * squash
                    vec_total = vec_total + scaled_squash
                    inner = grad - scaled_squash * squash
                    grad_query = grad_query + inner
                    new_keys.append(grad_keys[j] + inner)
                queries[i, :, at] = grad_query * weight
                return (tuple(new_keys), vec_total, bias_total + grad_query)

            grad_keys, vec_total, bias_total = lax.fori_loop(
                0, frames, one, (tuple([zeros] * frames), zeros, zeros)
            )
            for j in range(frames):
                keys[j, :, at] = grad_keys[j] * weight
            sums[bias_row : bias_row + 1, at] = jnp.sum(bias_total * weight, axis=0, keepdims=True)
            sums[vec_row : vec_row + 1, at] = jnp.sum(vec_total, axis=0, keepdims=True)
            return carried

        lax.fori_loop(0, chunks, one_chunk, 0)

    energy_back(mq, mk, mono, mono_squash, 0, 1)
    energy_back(sq, sk, span, span_squash, 2, 3)

    total_memory = grad_memory[...]
    total_decoded = jnp.zeros_like(total_memory)
    for r in range(4):
        cols = pl.ds(r * block, block)
        for n, source in enumerate((mk, sk, mq, sq)):
            pack[r, :, n * block : (n + 1) * block] = (
                source[:, :, cols].reshape(rows, block).astype(low)
            )
        total_memory = total_memory + dot_nt(pack[r, :, : 2 * block], w[r, :, : 2 * block])
        total_decoded = total_decoded + dot_nt(
            pack[r, :, 2 * block : 5 * block], w[r, :, 2 * block : 5 * block]
        )
    pack_me[...] = pack[0]
    pack_chip[...] = pack[1]
    pack_cores[...] = pack[2:4]
    middle = 2 * block
    near[...] = sums[:, :middle]
    far[:8, :] = sums[:, middle:]
    far[8:9, :] = sums[5:6, :middle]
    far[9:10, :] = sums[5:6, middle:]
    far[10:, :] = jnp.zeros((6, middle), wide)
    grad_own[...] = jnp.where(first_chip, total_memory, total_decoded)
    grad_given[...] = jnp.where(first_chip, total_decoded, total_memory).astype(low)


def run_attend(
    places, kept, taken, smalls, vocab, vectors, vocab_bias, noise, lengths, labels, counted,
    frames,
):
    rows, width = kept.shape
    group = rows // frames
    full = vectors.shape[1]
    vocab_width = vocab[0].shape[1]
    cell = (frames * frames, group, 128)
    count = len(smalls[0])
    return pl.pallas_call(
        functools.partial(attend_kernel, count),
        out_shape=(
            jax.ShapeDtypeStruct((rows, width), wide),
            jax.ShapeDtypeStruct((rows, width), low),
            jax.ShapeDtypeStruct((rows, full // 4 * 6), low),
            jax.ShapeDtypeStruct((rows, full // 4 * 6), low),
            jax.ShapeDtypeStruct((2, rows, full // 4 * 6), low),
            jax.ShapeDtypeStruct((2, rows, vocab_width), low),
            jax.ShapeDtypeStruct((8, full // 2), wide),
            jax.ShapeDtypeStruct((16, full // 2), wide),
        ),
        in_specs=[in_smem] + [in_vmem] * 8 + [in_place] * (4 * count + 4),
        out_specs=[in_vmem] * 8,
        scratch_shapes=[
            pltpu.VMEM((rows, width), low),
            pltpu.VMEM((rows, width), low),
            pltpu.VMEM((rows, width), wide),
            pltpu.VMEM((4, rows, full // 4 * 6), low),
            pltpu.VMEM((8, full), wide),
            pltpu.VMEM((4, width, full // 4 * 6), low),
            pltpu.VMEM((4,) + vocab[0].shape, low),
            pltpu.SemaphoreType.DMA((4, places.shape[0] - 2)),
            pltpu.SemaphoreType.DMA((4,)),
        ]
        + [pltpu.VMEM((frames, group, full), wide)] * 4
        + [pltpu.VMEM(cell, wide)] * 7
        + [pltpu.VMEM((frames, group, 128), wide), pltpu.VMEM((rows, full), wide)]
        + [pltpu.VMEM((frames * frames, group, full), wide)] * 2,
        compiler_params=pltpu.CompilerParams(vmem_limit_bytes=56 << 20),
        name="attend",
    )(
        places, kept, taken, vectors, vocab_bias, noise, lengths, labels, counted,
        *sum(smalls, []), *vocab,
    )


def gradient_kernel(
    order, before, before_peer, normed, normed_peer, dz, dz_peer, states_own, states_core,
    seen, seen_core, far, far_core, pack_me, pack_core, pack_far, *refs
):
    outputs, paired = refs[:8], refs[8:12]
    a_rec, a_in, a_dz, states, a_context, a_grads, a_pack, block, paired_block, sems, out_sems = (
        refs[12:]
    )
    y = order[0]
    height = block.shape[1]
    wide_half = a_dz.shape[1]
    part = a_pack.shape[1] // 6
    width = a_rec.shape[1]
    jobs = []
    for sources, target in (
        ((dz, dz_peer), a_dz),
        ((before, before_peer), a_rec),
        ((normed, normed_peer), a_in),
        (
            (states_own.at[0], states_core.at[0], states_own.at[2], states_core.at[2]),
            states.at[y],
        ),
        (
            (
                states_own.at[1], states_core.at[1],
                states_own.at[3], states_core.at[3],
            ),
            states.at[1 - y],
        ),
        ((pack_me, pack_core.at[0], pack_far.at[0], pack_far.at[1]), a_pack),
        ((seen.at[0], seen_core.at[0], far.at[0, :, :width], far_core.at[0, :, :width]), a_context),
        ((seen.at[1], seen_core.at[1], far.at[1, :, :width], far_core.at[1, :, :width]), a_grads),
    ):
        rows = target.shape[0] // len(sources)
        for r, source in enumerate(sources):
            jobs.append(
                pltpu.make_async_copy(
                    source, target.at[r * rows : (r + 1) * rows, :], sems.at[len(jobs)]
                )
            )
    for job in jobs:
        job.start()
    for job in jobs[:6]:
        job.wait()
    both = 2 * wide_half

    def one(n, carried):
        cols = pl.ds(pl.multiple_of(order[1 + n] * height, height), height)
        pair = jnp.concatenate([a_rec[:, cols], a_in[:, cols]], axis=1)
        for at in range(0, wide_half, 1024):
            value = dot_tn(pair, a_dz[:, at : at + 1024]).astype(low)
            block[n, :, at : at + 1024] = value[:height]
            block[n, :, wide_half + at : wide_half + at + 1024] = value[height:]
        for m, output in enumerate(outputs):

            @pl.when(n == m)
            def _(m=m, output=output):
                pltpu.make_async_copy(
                    block.at[m, :, :both], output.at[:, :both], out_sems.at[m]
                ).start()

        return carried

    lax.fori_loop(0, 8, one, 0)
    for job in jobs[6:]:
        job.wait()

    def two(n, carried):
        cols = pl.ds(pl.multiple_of(order[1 + n] * height, height), height)
        for m in range(2):
            to = both + 2 * m * part
            block[n, :, to : to + 2 * part] = dot_tn(
                states[m, :, cols], a_pack[:, 2 * m * part : 2 * (m + 1) * part]
            ).astype(low)
        for m, output in enumerate(outputs):

            @pl.when(n == m)
            def _(m=m, output=output):
                pltpu.make_async_copy(
                    block.at[m, :, both:], output.at[:, both:], out_sems.at[12 + m]
                ).start()

        return carried

    lax.fori_loop(0, 8, two, 0)

    def pair(n, carried):
        cols = pl.ds(pl.multiple_of(order[9 + n] * 2 * height, 2 * height), 2 * height)
        grad_pre = a_pack[:, 4 * part : 5 * part]
        for m, (a, b) in enumerate(
            (
                (states[1, :, cols], grad_pre),
                (a_context[:, cols], grad_pre),
                (a_grads[:, cols], a_pack[:, 5 * part :]),
            )
        ):
            paired_block[n, :, m * part : (m + 1) * part] = dot_tn(a, b).astype(low)
        return carried

    lax.fori_loop(0, 4, pair, 0)
    for m, output in enumerate(paired):
        pltpu.make_async_copy(paired_block.at[m], output, out_sems.at[8 + m]).start()
    for m, output in enumerate(outputs):
        pltpu.make_async_copy(
            block.at[m, :, :both], output.at[:, :both], out_sems.at[m]
        ).wait()
        pltpu.make_async_copy(
            block.at[m, :, both:], output.at[:, both:], out_sems.at[12 + m]
        ).wait()
    for m, output in enumerate(paired):
        pltpu.make_async_copy(paired_block.at[m], output, out_sems.at[8 + m]).wait()


def run_gradients(order, *arrays):
    rows, width = arrays[0].shape
    wide_half = arrays[5].shape[1]
    part = arrays[12].shape[1] // 6
    columns = 2 * wide_half + 4 * part
    height = width // 8
    deep = 2 * rows
    return pl.pallas_call(
        gradient_kernel,
        out_shape=tuple(
            [jax.ShapeDtypeStruct((height, columns), low)] * 8
            + [jax.ShapeDtypeStruct((2 * height, 3 * part), low)] * 4
        ),
        in_specs=[in_smem] + [in_place] * 15,
        out_specs=[in_place] * 12,
        scratch_shapes=[
            pltpu.VMEM((deep, width), low),
            pltpu.VMEM((deep, width), low),
            pltpu.VMEM((deep, wide_half), low),
            pltpu.VMEM((2, deep, width), low),
            pltpu.VMEM((deep, width), low),
            pltpu.VMEM((deep, width), low),
            pltpu.VMEM((deep, 6 * part), low),
            pltpu.VMEM((8, height, columns), low),
            pltpu.VMEM((4, 2 * height, 3 * part), low),
            pltpu.SemaphoreType.DMA((26,)),
            pltpu.SemaphoreType.DMA((20,)),
        ],
        compiler_params=pltpu.CompilerParams(vmem_limit_bytes=56 << 20),
        name="weight_gradients",
    )(order, *arrays)


def local(
    dp,
    block_input, norm_gain, lstm_in, lstm_rec, lstm_bias,
    mono_mem, mono_dec, mono_bias, mono_vec, span_mem, span_dec, span_bias, span_vec,
    out_weight, out_bias, vocab_weight, vocab_bias, noise, enc_lengths, label_lengths, labels,
):
    ring = Ring(dp)
    s, y = lax.axis_index("section"), lax.axis_index("mp")
    _, utts, frames, width = block_input.shape
    half, quarter = utts // 2, utts // 4
    rows = frames * quarter
    shard_rows, _, unit_half = lstm_in.shape[1:]
    wide_half = 4 * unit_half
    block = mono_mem.shape[1]
    vocab_size = vocab_weight.shape[1]
    vocab_pad = 4 * block

    in_shard = lstm_in[0].reshape(shard_rows, wide_half)
    rec_shard = lstm_rec[0].reshape(shard_rows, wide_half)
    bias_shard = lstm_bias[0].reshape(1, wide_half)

    def of_section(array):
        return jnp.where(s == y, array, across_cores(array))

    inputs = of_section(jnp.swapaxes(block_input[0], 0, 1))
    gain = of_section(norm_gain[0])
    inputs_own = lax.dynamic_slice_in_dim(inputs, s * half, half, axis=1)
    inputs_other = lax.dynamic_slice_in_dim(inputs, (1 - s) * half, half, axis=1)
    normed_own = normalize(inputs_own.astype(wide), gain)
    normed_own = normed_own.astype(low).reshape(frames * half, width)
    normed_other = normalize(inputs_other.astype(wide), gain)
    normed_other = normed_other.astype(low).reshape(frames * half, width)

    start = s * half + y * quarter
    noise_part = jnp.transpose(
        lax.dynamic_slice_in_dim(noise, start, quarter, axis=0), (1, 2, 0)
    ).reshape(frames * frames, quarter, 1)
    noise_part = jnp.broadcast_to(noise_part, (frames * frames, quarter, 128))
    length_part = lax.dynamic_slice_in_dim(enc_lengths, start, quarter, axis=0)
    length_part = jnp.broadcast_to(length_part[:, None], (quarter, 128))
    label_part = lax.dynamic_slice_in_dim(labels, start, quarter, axis=0).T.reshape(rows, 1)
    label_part = jnp.broadcast_to(label_part, (rows, 128))
    count_part = lax.dynamic_slice_in_dim(label_lengths, start, quarter, axis=0)
    counted = (jnp.arange(frames)[:, None] < count_part[None, :]).astype(wide).reshape(rows, 1)
    counted = jnp.broadcast_to(counted, (rows, 128))
    bias_row = jnp.pad(vocab_bias, (0, vocab_pad - vocab_size), constant_values=-1e30)[None]

    vector_own = jnp.stack([mono_bias, mono_vec, span_bias, span_vec, out_bias])
    vocab_own = jnp.pad(vocab_weight, ((0, 0), (0, vocab_pad - vocab_size)))
    ready = (noise_part, length_part, label_part, counted, bias_row, normed_own, normed_other)
    places, in_own, rec_own, small_own, small_chip = [], [], [], [], []
    z, x = ring.z, ring.x
    if ring.short:
        steps_back = [ring.back(k) for k in range(1, 5)]
        order = [at * 2 + 1 - x for at in steps_back] + [at * 2 + x for at in steps_back]
        order = [y] + order + steps_back
    else:
        order = [y] + [jnp.int32(k) for k in [*range(8), *range(4)]]
    order = jnp.stack(order).astype(jnp.int32)
    small = jnp.concatenate(
        [
            tie(mono_mem, in_shard, rec_shard), span_mem, mono_dec, span_dec,
            out_weight[0], out_weight[1],
        ],
        axis=1,
    )
    if ring.short:
        flow, across, onward = Flow(), ring.across, ring.onward
        both = 2 * wide_half
        corner_in, corner_rec, b_own = flow.step(
            (corners, in_shard), (corners, rec_shard), (corners, bias_shard)
        )
        small_far, small_next = across(small), onward(small)
        flow.landed += (small_far, small_next)
        b_own = b_own.astype(wide)
        small_own = [jnp.concatenate([small, small_far], axis=1)]
        small_chip, small_core = [], []
        held = jnp.concatenate([corner_in, corner_rec, small_next], axis=1)
        near, far, near_core, far_core = [], [], [], []
        for k in range(ring.outer):
            near.append(held)
            jobs = [(across, held)]
            if k < ring.outer - 1:
                jobs.append((onward, held[:, :both] if k == ring.outer - 2 else held))
            if k == 0:
                jobs.append((across_chips, vocab_own))
            if k == 1:
                jobs.append((across_chips, vector_own))
            results = flow.step(*jobs, also=tuple(small_chip[-1:]))
            far.append(results[0])
            small_chip.append(across_chips(small_own[k]))
            if k == 0:
                vocab_chip = results[2]
            if k == 1:
                vector_pair = jnp.concatenate([vector_own, results[2]], axis=1)
            if k < ring.outer - 1:
                small_own.append(jnp.concatenate([held[:, both:], far[k][:, both:]], axis=1))
                held = results[1]
        for k, (a, b) in enumerate(zip(near, far)):
            near_core.append(across_cores(a if k else tie(a, near[1], *ready)))
            far_core.append(across_cores(b))
        b_last, vocab_last, chip_last, vector_last = lax.optimization_barrier(
            (b_own, vocab_own, vocab_chip, vector_pair, held)
        )[:4]
        b_other = across_cores(b_last)
        vocab = [vocab_own, vocab_chip, across_cores(vocab_last), across_cores(chip_last)]
        vector_core = across_cores(vector_last)
        for k in range(ring.outer):
            places += [ring.back(k) * 2 + ring.x, ring.back(k) * 2 + 1 - ring.x]
        places = jnp.stack([s, y] + places).astype(jnp.int32)
        vectors = jnp.concatenate([vector_pair, vector_core], axis=1)
        vectors = jnp.pad(vectors, ((0, 3), (0, 0)))
        small_core = [across_cores(a) for a in small_own[:-1]]
        small_core.append(across_cores(tie(small_own[-1], vectors, places, order)))
        in_own = [a for pair in zip(near, far) for a in pair]
        in_other = [a for pair in zip(near_core, far_core) for a in pair]
        rec_own, rec_other, rec_column = in_own, in_other, wide_half
    else:
        vocab_chip = across_chips(vocab_own)
        small, in_block, rec_block = [
            lax.all_gather(a, "dp", axis=0, tiled=True)
            for a in (small, corners(in_shard), corners(rec_shard))
        ]
        places, in_own, rec_own = [jnp.int32(0)], [in_block], [rec_block]
        small_own, small_chip = [small], [across_chips(small)]
        vocab = [vocab_own, vocab_chip, across_cores(vocab_own), across_cores(vocab_chip)]
        in_other, rec_other, rec_column = [across_cores(in_block)], [across_cores(rec_block)], 0
        small_core = [across_cores(small)]
        b_own = corners(bias_shard).astype(wide)
        b_other = across_cores(b_own)
        vector_pair = across_chips(vector_own)
        vector_pair = jnp.concatenate([vector_own, vector_pair], axis=1)
        vector_core = across_cores(vector_pair)
        vectors = jnp.concatenate([vector_pair, vector_core], axis=1)
        vectors = jnp.pad(vectors, ((0, 3), (0, 0)))
        places = jnp.stack([s, y] + places).astype(jnp.int32)
    places = tie(places, order, vectors, *vocab, *ready, *small_chip[:-1], *small_core)

    kept, given, before, gates, cells = run_forward(
        places, normed_own, b_own, b_other, in_own, in_other, rec_own, rec_other, frames,
        rec_column,
    )

    kept, given = kept.reshape(rows, width), given.reshape(rows, width)
    taken = across_chips(given)
    small_chip[-1] = tie(small_chip[-1], kept)
    small_both = [across_cores(part) for part in small_chip]
    smalls = [small_own, small_chip, small_core, small_both]
    grad_own, grad_given, pack_me, pack_chip, pack_cores, seen, near, far = run_attend(
        places, kept, taken, smalls, vocab, vectors, bias_row, noise_part, length_part,
        label_part, counted, frames,
    )
    grad_given, kept_far = lax.optimization_barrier((grad_given, across_chips(tie(kept, taken))))
    grad_taken = across_chips(grad_given)
    pack_core = across_cores(pack_cores)
    pack_out = jnp.stack([pack_chip, pack_core[1]])
    far_peer = across_cores(far)
    vector_pair = (near[:5] + far_peer[:5]).reshape(5, 2, block)
    bias_pair = (far[8:10] + far_peer[8:10]).reshape(-1)
    vector_out = jnp.concatenate([vector_pair[:, 1].reshape(-1), bias_pair])
    vector_count = vector_out.shape[0] // (2 * rows)
    seen_out = jnp.concatenate(
        [seen, halves(vector_out, 2 * rows).reshape(2, rows, -1)], axis=2
    )
    before = before.reshape(frames * half, width)
    before_peer = across_cores(tie(before, taken))
    states = jnp.stack([tie(kept, grad_given), taken, given, kept_far])
    states_core, seen_core = across_cores(states), across_cores(seen)
    places_back, pack_out, seen_out = lax.optimization_barrier(
        (places, pack_out, seen_out, grad_taken, before_peer, states_core, seen_core)
    )[:3]
    dz_own, dz_other = run_backward(
        places_back, grad_own.reshape(frames, quarter, width),
        grad_taken.reshape(frames, quarter, width), gates, cells, rec_own, rec_other, rec_column,
    )
    pack_far = across_chips(pack_out)
    seen_far = across_chips(tie(seen_out, pack_out))

    dz_own, dz_other, pack_far, seen_far = lax.optimization_barrier(
        (
            dz_own.reshape(frames * half, wide_half), dz_other.reshape(frames * half, wide_half),
            pack_far, seen_far,
        )
    )
    dz_peer = across_cores(dz_other)
    totals = run_gradients(
        order, before, before_peer, normed_own, normed_other, dz_own,
        dz_peer, states, states_core, seen, seen_core, seen_far, across_cores(seen_far),
        pack_me, pack_core, pack_far,
    )
    vector_far = joined(seen_far[:, :, width:].reshape(2 * rows, -1), vector_count).reshape(-1)

    sides_at = 5 * block + vocab_pad
    def input_back(places):
        grad_inputs, grad_gain = run_input(
            places, inputs_own.reshape(frames * half, width), gain[None], dz_own, dz_other,
            in_own, in_other,
        )
        grad_gain = grad_gain.reshape(width)
        grad_inputs = jnp.swapaxes(grad_inputs.reshape(frames, half, width), 0, 1)
        grad_peer = across_cores(grad_inputs)
        grad_section = jnp.concatenate(
            [
                jnp.where(s == 0, grad_inputs, grad_peer),
                jnp.where(s == 0, grad_peer, grad_inputs),
            ],
            axis=0,
        )
        gain_sum = grad_gain + across_cores(grad_gain)
        flat = jnp.concatenate(
            [
                vector_pair[:, 0].reshape(-1) + vector_far[: 5 * block],
                bias_pair + vector_far[5 * block :],
                jnp.sum(dz_own.astype(wide), axis=0) + jnp.sum(dz_peer.astype(wide), axis=0),
                gain_sum,
            ]
        )
        return grad_section, jnp.pad(flat, (0, -flat.shape[0] % (8 * shard_rows)))

    def to_other_chip(section):
        return lax.ppermute(section, ("section", "mp"), [(0, 1), (3, 2)])

    if ring.short:
        r = shard_rows
        both, width_out = 2 * wide_half, 2 * block
        flow, across, onward = Flow(), ring.across, ring.onward
        theirs, mine, outputs = totals[:4], totals[4:8], totals[8:]

        def total(k, arrived, passed):
            value = mine[k - 1].astype(wide) + arrived.astype(wide)
            return value if passed is None else value + passed.astype(wide)

        def cornered(hop):
            index = lambda at, place, chip: (at * ring.dp + place) * 2 + chip
            pairs = [
                (index(p, a, q), index(q, b, p)) for a, b in hop for p in range(2) for q in range(2)
            ]
            return lambda array: lax.ppermute(array, ("section", "dp", "mp"), pairs)

        arrived, out_two, out_before = flow.step(
            (across, theirs[0]), (onward, outputs[1]), (ring.astern, outputs[0])
        )
        grad_section, flat = input_back(tie(places, out_two))
        out_one = onward(
            tie((outputs[2].astype(wide) + out_two.astype(wide)).astype(low), arrived)
        )
        grad_far = to_other_chip(grad_section)
        flat = flat.reshape(8, -1)
        flat = (flat + across(flat)).reshape(-1)
        flat_width = flat.shape[0] // r
        flow.landed = (arrived,)
        value = total(1, arrived, None).astype(low)
        passed, arrived = flow.step((onward, value), (across, theirs[1]))
        out = outputs[3].astype(wide) + out_before.astype(wide) + out_one.astype(wide)
        vocab_rows = out[:, width_out:].astype(low)
        message = jnp.concatenate(
            [cut(out, 1 - x, r)[:, :width_out].astype(low), vocab_rows[:r], vocab_rows[r:]], axis=1
        )
        kept_rows = corners(tie(mine[3][:, :both], out_one))
        value = total(2, arrived, passed).astype(low)
        passed, arrived, out_far = flow.step(
            (onward, value), (across, theirs[2]), (across, message), also=(grad_far,)
        )
        output_grad = cut(out, x, r)[:, :width_out] + out_far[:, :width_out].astype(wide)
        shard = jnp.concatenate([out[:r, width_out:], out[r:, width_out:]], axis=1)
        shard = (shard + out_far[:, width_out:].astype(wide)).astype(low)
        shard = jnp.concatenate([shard, halves(flat, r)], axis=1)
        next_one, next_three = onward(shard), ring.astern(shard)
        value = total(3, arrived, passed).astype(low)
        passed, arrived, energy_passed, energy_arrived, next_two = flow.step(
            (cornered(ring.ring), value[:, :both]), (cornered(ring.pair), theirs[3][:, :both]),
            (onward, value[:, both:]), (across, theirs[3][:, both:]), (onward, next_one),
            also=(kept_rows,),
        )
        shards = {0: shard, 1: next_one, 3: next_three, 2: next_two}
        flat = sum(joined(a[:, 2 * block :], flat_width).reshape(-1) for a in shards.values())
        sides = corners(flat[sides_at : sides_at + wide_half + width])
        moved = kept_rows.astype(wide) + arrived.astype(wide) + passed.astype(wide)
        energy_grad = mine[3][:, both:].astype(wide) + energy_arrived.astype(wide)
        energy_grad = energy_grad + energy_passed.astype(wide)
        vocab_grad = jnp.zeros((vocab_pad, block), low)
        for k, held in shards.items():
            held = jnp.concatenate([held[:, :block], held[:, block : 2 * block]], axis=0)
            vocab_grad = lax.dynamic_update_slice(vocab_grad, held, (ring.back(k) * 2 * r, 0))
    else:
        grad_section, flat = input_back(places)
        grad_far = to_other_chip(grad_section)

        def scatter(parts):
            total = jnp.concatenate(parts, axis=0)
            return lax.psum_scatter(total, "dp", scatter_dimension=0, tiled=True).astype(wide)

        moved, output_grad = scatter(totals[:8]), scatter(totals[8:])
        moved, energy_grad = moved[:, : 2 * wide_half], moved[:, 2 * wide_half :]
        moved = corners(moved.astype(low)).astype(wide)
        flat = lax.psum(flat, "dp")
        sides = corners(flat[sides_at : sides_at + wide_half + width])
        vocab_grad = lax.all_gather(
            output_grad[:, 2 * block :].astype(low), "dp", axis=0, tiled=True
        )

    input_grad = jnp.where(s == y, grad_section, grad_far)
    vocab_grad = vocab_grad.T[:, :vocab_size].astype(wide)
    vector_sum = flat[: 5 * block].reshape(5, block)
    bias_sum = flat[5 * block : 5 * block + vocab_size]
    lstm_bias_sum = sides[:wide_half].reshape(1, 4, unit_half)
    gain_sum = sides[wide_half:][None]
    rec_grad = moved[:, :wide_half].reshape(1, shard_rows, 4, unit_half)
    in_grad = moved[:, wide_half:].reshape(1, shard_rows, 4, unit_half)
    mono_mem_grad, span_mem_grad, mono_dec_grad, span_dec_grad = [
        energy_grad[:, n * block : (n + 1) * block] for n in range(4)
    ]
    return (
        input_grad[None],
        gain_sum,
        in_grad,
        rec_grad,
        lstm_bias_sum,
        mono_mem_grad,
        mono_dec_grad,
        vector_sum[0],
        vector_sum[1],
        span_mem_grad,
        span_dec_grad,
        vector_sum[2],
        vector_sum[3],
        jnp.stack([output_grad[:, :block], output_grad[:, block : 2 * block]]),
        vector_sum[4],
        vocab_grad,
        bias_sum,
    )


def solution(mesh):
    both = ("section", "mp")
    in_specs = (
        P("section", "dp", None, None),
        P("section", None),
        P("section", "dp", None, "mp"),
        P("section", "dp", None, "mp"),
        P("section", None, "mp"),
        P("dp", both),
        P("dp", both),
        P(both),
        P(both),
        P("dp", both),
        P("dp", both),
        P(both),
        P(both),
        P(None, "dp", both),
        P(both),
        P(both, None),
        P(),
        P("dp", None, None),
        P("dp"),
        P("dp"),
        P("dp", None),
    )
    out_specs = (
        P("section", "dp", None, None),
        P("section", None),
        P("section", "dp", None, "mp"),
        P("section", "dp", None, "mp"),
        P("section", None, "mp"),
        P("dp", both),
        P("dp", both),
        P(both),
        P(both),
        P("dp", both),
        P("dp", both),
        P(both),
        P(both),
        P(None, "dp", both),
        P(both),
        P(both, None),
        P(),
    )
    dp = mesh.shape["dp"]

    def step(*arrays):
        return local(dp, *arrays)

    return jax.shard_map(step, mesh=mesh, in_specs=in_specs, out_specs=out_specs, check_vma=False)
```
